32 devices in a mesh: dp: 8 (over y, x, core), tensor: 4 (over z).
Axes of the slice: x: 2, y: 2, z: 4, core: 2. Of those that a mesh axis runs over, the one named last changes fastest.
Arguments:
- char_inputs: bfloat16 [131072, 256], P(('dp', 'tensor')), may hold values from -6 to 6
- char_counts: int32 [8192], P(('dp', 'tensor')), may hold values from 1 to 16
- doc_ids: int32 [8, 1024], P('dp'), may hold values from 0 to 3, never falling along the last dimension, each value on 1 to 512 neighbouring positions
- cotangent: bfloat16 [8192, 512], P('dp'), may hold values from -6 to 6
- char_norm_one: float32 [256], replicated, may hold values from 0.5 to 1.5
- char_query: bfloat16 [256, 256], replicated, may hold values from -0.375 to 0.375
- char_key: bfloat16 [256, 256], replicated, may hold values from -0.375 to 0.375
- char_value: bfloat16 [256, 256], replicated, may hold values from -0.375 to 0.375
- char_out: bfloat16 [256, 256], replicated, may hold values from -0.75 to 0.75
- char_norm_two: float32 [256], replicated, may hold values from 0.5 to 1.5
- char_up: bfloat16 [256, 1024], replicated, may hold values from -0.375 to 0.375
- char_down: bfloat16 [1024, 256], replicated, may hold values from -0.1875 to 0.1875
- char_proj: bfloat16 [256, 512], replicated, may hold values from -1.5 to 1.5
- word_norm_one: float32 [512], replicated, may hold values from 0.5 to 1.5
- word_query: bfloat16 [512, 512], P(None, 'tensor'), may hold values from -0.25 to 0.25
- word_key: bfloat16 [512, 512], P(None, 'tensor'), may hold values from -0.25 to 0.25
- word_value: bfloat16 [512, 512], P(None, 'tensor'), may hold values from -0.25 to 0.25
- word_out_proj: bfloat16 [512, 512], P('tensor'), may hold values from -1 to 1
- word_norm_two: float32 [512], replicated, may hold values from 0.5 to 1.5
- word_up: bfloat16 [512, 2048], P(None, 'tensor'), may hold values from -0.25 to 0.25
- word_down: bfloat16 [2048, 512], P('tensor'), may hold values from -0.125 to 0.125
Outputs:
- word_output: bfloat16 [8192, 512], P(('dp', 'tensor'))
- char_input_gradient: float32 [131072, 256], P(('dp', 'tensor'))
- char_norm_one_gradient: float32 [256], replicated
- char_query_gradient: float32 [256, 256], replicated
- char_key_gradient: float32 [256, 256], replicated
- char_value_gradient: float32 [256, 256], replicated
- char_out_gradient: float32 [256, 256], replicated
- char_norm_two_gradient: float32 [256], replicated
- char_up_gradient: float32 [256, 1024], replicated
- char_down_gradient: float32 [1024, 256], replicated
- char_proj_gradient: float32 [256, 512], replicated
- word_norm_one_gradient: float32 [512], replicated
- word_query_gradient: float32 [512, 512], P(None, 'tensor')
- word_key_gradient: float32 [512, 512], P(None, 'tensor')
- word_value_gradient: float32 [512, 512], P(None, 'tensor')
- word_out_proj_gradient: float32 [512, 512], P('tensor')
- word_norm_two_gradient: float32 [512], replicated
- word_up_gradient: float32 [512, 2048], P(None, 'tensor')
- word_down_gradient: float32 [2048, 512], P('tensor')
The draws below stay inside these ranges and needn't reach their ends.
Inputs may be any that keep to these rules, and one draw needn't show every extreme that they name: Slots of a word from char_counts on are padding. `doc_ids`: ids never fall along a sequence; each document covers 1 to 512 consecutive words, one exactly that many.
All inputs are finite; a program needn't handle non-finite values.
Results may differ from the reference program's by a relative error of at most 0.018.
Values may be sent and summed in bfloat16 or wider, within the bound.
A program may use at most 192 MiB of HBM per device.

```python
import math
import jax
import jax.numpy as jnp
import numpy as np
from jax import lax

D = 512
HEADS = 8
HD = 64
FF = 2048
CW = 256
CHEADS = 4
CHD = 64
CFF = 1024
CHARS = 16
LEN = 1024
DOCS = 4
SEQS = 8
WORDS = 8192


def plant(result, rng, smallest, high):
    longest = result.shape.index(max(result.shape))
    spots = []
    for shift in (0, 1):
        where = [jax.random.randint(jax.random.fold_in(rng, axis), (), 0, length) for axis, length in enumerate(result.shape)]
        where[longest] = (where[longest] + shift) % result.shape[longest]
        spots.append(tuple(where))
    return result.at[spots[0]].set(smallest).at[spots[1]].set(high)


def shard_levels(rng, shape, pieces, low, high):
    factor_of = 1.0
    for axis_at, parts in pieces:
        draws = jax.random.uniform(jax.random.fold_in(jax.random.fold_in(rng, 6), axis_at), (parts,), jnp.float32, low / len(pieces), high / len(pieces))
        factor_of = factor_of * jnp.repeat(jnp.exp(draws), shape[axis_at] // parts).reshape((-1,) + (1,) * (len(shape) - 1 - axis_at))
    return factor_of


def profile(amount, total, bound, slope):
    loads = [(1 << 20) // math.isqrt(standing ** slope) + 1 for standing in range(2, amount + 1)]
    rest, holding = total - bound - (amount - 1), [1] * (amount - 1)
    while rest > 0:
        movable = [i for i in range(amount - 1) if holding[i] < bound]
        whole, left = sum([loads[i] for i in movable]), rest
        for i in movable:
            extra = min(bound - holding[i], max(1, left * loads[i] // whole), rest)
            holding[i] = holding[i] + extra
            rest = rest - extra
    return np.array([bound] + holding)


def ragged_sizes(key, number_of, total, reach, slope):
    if number_of == 2:
        one = jax.random.randint(key, (), max(1, total - reach), min(reach, total - 1) + 1)
        return jnp.stack([one, total - one])
    sizes = jnp.asarray(profile(number_of, total, reach, slope), jnp.int32)
    couples = (number_of - 1) // 2
    donor, sink = sizes[1:1 + 2 * couples:2], sizes[2:2 + 2 * couples:2]
    margin = jnp.minimum(donor - 1, reach - sink)
    moved = jax.random.randint(jax.random.fold_in(key, 1), (couples,), 0, 1 << 20) % (margin + 1)
    sizes = sizes.at[1:1 + 2 * couples:2].set(donor - moved).at[2:2 + 2 * couples:2].set(sink + moved)
    return sizes[jax.random.permutation(jax.random.fold_in(key, 2), number_of)]


def noise(rng, dims, width, limit, cuts=(), held_as=jnp.bfloat16):
    drawn = width * jax.random.normal(rng, dims, jnp.float32)
    if cuts:
        drawn = drawn * shard_levels(rng, dims, cuts, -0.22, 0.18)
    return jnp.clip(drawn, -limit, limit).astype(held_as)


def setup_inputs(seed: int = 0) -> dict:
    keys = jax.random.split(jax.random.key(seed), 22)
    return {
        "char_inputs": noise(keys[0], (WORDS * CHARS, CW), 1.0, 6.0, ((0, 32),)),
        "char_counts": plant(jax.random.randint(keys[1], (WORDS,), 1, CHARS + 1), jax.random.fold_in(keys[1], 1), 1, CHARS).astype(jnp.int32),
        "doc_ids": jax.vmap(lambda own: jnp.searchsorted(jnp.cumsum(ragged_sizes(own, DOCS, LEN, LEN // 2, 1)), jnp.arange(LEN), side="right"))(jax.random.split(keys[2], SEQS)).reshape((SEQS, LEN)).astype(jnp.int32),
        "cotangent": noise(keys[3], (WORDS, D), 1.0, 6.0, ((0, 8),)),
        "char_norm_one": jnp.clip(1.0 + 0.1 * jax.random.normal(keys[4], (CW,), jnp.float32), 0.5, 1.5),
        "char_query": noise(keys[5], (CW, CW), CW ** -0.5, 0.375),
        "char_key": noise(keys[6], (CW, CW), CW ** -0.5, 0.375),
        "char_value": noise(keys[7], (CW, CW), CW ** -0.5, 0.375),
        "char_out": noise(keys[8], (CW, CW), (CW // 4) ** -0.5, 0.75),
        "char_norm_two": jnp.clip(1.0 + 0.1 * jax.random.normal(keys[9], (CW,), jnp.float32), 0.5, 1.5),
        "char_up": noise(keys[10], (CW, CFF), CW ** -0.5, 0.375),
        "char_down": noise(keys[11], (CFF, CW), CFF ** -0.5, 0.1875),
        "char_proj": noise(keys[12], (CW, D), (CW // 16) ** -0.5, 1.5),
        "word_norm_one": jnp.clip(1.0 + 0.1 * jax.random.normal(keys[13], (D,), jnp.float32), 0.5, 1.5),
        "word_query": noise(keys[14], (D, D), D ** -0.5, 0.25, ((1, 4),)),
        "word_key": noise(keys[15], (D, D), D ** -0.5, 0.25, ((1, 4),)),
        "word_value": noise(keys[16], (D, D), D ** -0.5, 0.25, ((1, 4),)),
        "word_out_proj": noise(keys[17], (D, D), (D // 16) ** -0.5, 1.0, ((0, 4),)),
        "word_norm_two": jnp.clip(1.0 + 0.1 * jax.random.normal(keys[18], (D,), jnp.float32), 0.5, 1.5),
        "word_up": noise(keys[19], (D, FF), D ** -0.5, 0.25, ((1, 4),)),
        "word_down": noise(keys[20], (FF, D), FF ** -0.5, 0.125, ((0, 4),)),
    }


EPSILON = 1e-05
NEG_LARGE = -1e+30
HIGHEST = lax.Precision.HIGHEST

@jax.custom_vjp
def low(v):
    return lax.optimization_barrier(v.astype(jnp.bfloat16)).astype(jnp.float32)

@jax.custom_vjp
def low_back(v):
    return v

def low_keep(v):
    return (low(v), None)

def low_pass(kept, grad):
    return (grad,)

def back_keep(v):
    return (v, None)

def back_low(kept, grad):
    return (low(grad),)
low.defvjp(low_keep, low_pass)
low_back.defvjp(back_keep, back_low)

def layer_norm(values, gain_vector):
    centre = values - lax.optimization_barrier(jnp.mean(values, axis=-1, keepdims=True))
    spread = lax.optimization_barrier(jnp.mean(centre * centre, axis=-1, keepdims=True))
    return centre * lax.rsqrt(spread + EPSILON) * gain_vector

def product(left, right):
    return jnp.dot(left, right, precision=HIGHEST)

def char_block(char_params, char_rows, word_counts):
    norm_one, query_w, key_w, value_w, out_w, norm_two, up_w, down_w, proj_w = char_params
    word_total = word_counts.shape[0]
    flat_rows = char_rows.reshape(word_total * CHARS, CW)
    shape_four = (word_total, CHARS, CHEADS, CHD)
    normed = low(layer_norm(flat_rows, norm_one))
    queries = low_back(low(product(normed, query_w))).reshape(shape_four)
    key_rows = low_back(low(product(normed, key_w))).reshape(shape_four)
    value_rows = low_back(low(product(normed, value_w))).reshape(shape_four)
    scores = low_back(jnp.einsum('wqhd,wkhd->whqk', queries, key_rows, precision=HIGHEST) * CHD ** (-0.5))
    valid = jnp.arange(CHARS)[None, :] < word_counts[:, None]
    scores = jnp.where(valid[:, None, None, :], scores, NEG_LARGE)
    attention_probs = low(jax.nn.softmax(scores, axis=-1))
    mixed_rows = low_back(low(jnp.einsum('whqk,wkhd->wqhd', attention_probs, value_rows, precision=HIGHEST)))
    mixed_rows = mixed_rows.reshape(word_total * CHARS, CW)
    first_sum = flat_rows + low_back(product(mixed_rows, out_w))
    normed_two = low(layer_norm(first_sum, norm_two))
    activation = low(jax.nn.gelu(low_back(product(normed_two, up_w)), approximate=True))
    second_sum = first_sum + low_back(product(activation, down_w))
    slot_weights = valid.astype(jnp.float32)
    pooled = lax.optimization_barrier(jnp.sum(second_sum.reshape(word_total, CHARS, CW) * slot_weights[:, :, None], axis=1))
    pooled = low(pooled / word_counts.astype(jnp.float32)[:, None])
    return low_back(low(product(pooled, proj_w)))

def word_block(word_params, inputs, seq_docs):
    norm_one, query_w, key_w, value_w, out_w, norm_two, up_w, down_w = word_params
    length = seq_docs.shape[0]
    shape_three = (length, HEADS, HD)
    normed = low(layer_norm(inputs, norm_one))
    queries = low_back(low(product(normed, query_w))).reshape(shape_three)
    key_rows = low_back(low(product(normed, key_w))).reshape(shape_three)
    value_rows = low_back(low(product(normed, value_w))).reshape(shape_three)
    scores = low_back(jnp.einsum('qhd,khd->hqk', queries, key_rows, precision=HIGHEST) * HD ** (-0.5))
    positions = jnp.arange(length)
    allowed = (seq_docs[:, None] == seq_docs[None, :]) & (positions[None, :] <= positions[:, None])
    scores = jnp.where(allowed[None], scores, NEG_LARGE)
    attention_probs = low(jax.nn.softmax(scores, axis=-1))
    mixed_rows = low_back(low(jnp.einsum('hqk,khd->qhd', attention_probs, value_rows, precision=HIGHEST)))
    mixed_rows = mixed_rows.reshape(length, D)
    middle = inputs + low_back(product(mixed_rows, out_w))
    normed_two = low(layer_norm(middle, norm_two))
    activation = low(jax.nn.gelu(low_back(product(normed_two, up_w)), approximate=True))
    return middle + low_back(product(activation, down_w))

def one_sequence(char_params, word_params, seq_chars, seq_counts, seq_docs):
    return word_block(word_params, char_block(char_params, seq_chars, seq_counts), seq_docs)

def reference(char_inputs, char_counts, doc_ids, cotangent, char_norm_one, char_query, char_key, char_value, char_out, char_norm_two, char_up, char_down, char_proj, word_norm_one, word_query, word_key, word_value, word_out_proj, word_norm_two, word_up, word_down):
    char_params = (char_norm_one.astype(jnp.float32), char_query.astype(jnp.float32), char_key.astype(jnp.float32), char_value.astype(jnp.float32), char_out.astype(jnp.float32), char_norm_two.astype(jnp.float32), char_up.astype(jnp.float32), char_down.astype(jnp.float32), char_proj.astype(jnp.float32))
    word_params = (word_norm_one.astype(jnp.float32), word_query.astype(jnp.float32), word_key.astype(jnp.float32), word_value.astype(jnp.float32), word_out_proj.astype(jnp.float32), word_norm_two.astype(jnp.float32), word_up.astype(jnp.float32), word_down.astype(jnp.float32))
    sequences = doc_ids.shape[0]
    char_whole = char_inputs.astype(jnp.float32).reshape(sequences, LEN, CHARS, CW)
    counts_whole = char_counts.reshape(sequences, LEN)
    checked = jax.checkpoint(one_sequence)

    def whole_layer(char_weights, word_weights, char_values):
        return lax.map(lambda members: checked(char_weights, word_weights, members[0], members[1], members[2]), (char_values, counts_whole, doc_ids))
    outputs, pull_back = jax.vjp(whole_layer, char_params, word_params, char_whole)
    char_grads, word_grads, input_grad = pull_back(cotangent.astype(jnp.float32).reshape(sequences, LEN, D))
    return (outputs.reshape(WORDS, D).astype(jnp.bfloat16), input_grad.reshape(WORDS * CHARS, CW), char_grads[0], char_grads[1], char_grads[2], char_grads[3], char_grads[4], char_grads[5], char_grads[6], char_grads[7], char_grads[8], word_grads[0], word_grads[1], word_grads[2], word_grads[3], word_grads[4], word_grads[5], word_grads[6], word_grads[7])
```

```python
import functools

import jax
import jax.numpy as jnp
from jax import lax
from jax.experimental import pallas as pl
from jax.experimental.pallas import tpu as pltpu

from jax.sharding import PartitionSpec as P

BF = jnp.bfloat16
F32 = jnp.float32
EPSILON = 1e-05
NEG_LARGE = -1e30
CHEADS = 4
CHD = 64
TILE = 128
CSTEP = 512
GELU_C = 0.7978845608028654
GELU_A = 0.044715


def nn(left, right):
    return lax.dot_general(left, right, (((1,), (0,)), ((), ())), preferred_element_type=F32)


def nt(left, right):
    return lax.dot_general(left, right, (((1,), (1,)), ((), ())), preferred_element_type=F32)


def tn(left, right):
    return lax.dot_general(left, right, (((0,), (0,)), ((), ())), preferred_element_type=F32)


def norm_parts(values):
    centre = values - jnp.mean(values, axis=-1, keepdims=True)
    spread = jnp.mean(centre * centre, axis=-1, keepdims=True)
    rate = lax.rsqrt(spread + EPSILON)
    return centre * rate, rate


def norm_back(upstream, gain, unit, rate):
    scaled = upstream * gain
    first = jnp.mean(scaled, axis=-1, keepdims=True)
    second = jnp.mean(scaled * unit, axis=-1, keepdims=True)
    return rate * (scaled - first - unit * second)


def gelu_parts(values):
    square = values * values
    inner = values * (GELU_C + (GELU_C * GELU_A) * square)
    half = 0.5 + 0.5 * jnp.tanh(inner)
    active = values * half
    slope = half + (active * (1.0 - half)) * (2.0 * GELU_C + (6.0 * GELU_C * GELU_A) * square)
    return active, slope


def split_heads(pair):
    low_half = lax.broadcasted_iota(jnp.int32, pair.shape, 1) < CHD
    zero = jnp.zeros_like(pair)
    return jnp.concatenate([jnp.where(low_half, pair, zero), jnp.where(low_half, zero, pair)], axis=0)


def word_of_lane(shape, slots):
    lane = lax.broadcasted_iota(jnp.int32, shape, 1)
    return jnp.bitwise_and(lane, TILE - 1) // slots


def compact(scores, slots):
    words = word_of_lane((slots, scores.shape[1]), slots)
    result = scores[0:slots]
    for word in range(1, TILE // slots):
        result = jnp.where(words == word, scores[word * slots:(word + 1) * slots], result)
    return result


def expand(packed, slots):
    words = word_of_lane(packed.shape, slots)
    zero = jnp.zeros_like(packed)
    return jnp.concatenate(
        [jnp.where(words == word, packed, zero) for word in range(TILE // slots)], axis=0
    )


def stack_lanes(pair):
    return jnp.concatenate([pair[:, :TILE], pair[:, TILE:]], axis=0)


def pool_matrix(rows, slots, counts_col):
    words = rows // slots
    row = lax.broadcasted_iota(jnp.int32, (rows, words), 0)
    word = lax.broadcasted_iota(jnp.int32, (rows, words), 1)
    mine = (row // slots == word) & (jnp.bitwise_and(row, slots - 1) < counts_col)
    return jnp.where(mine, 1.0 / counts_col.astype(F32), 0.0)


def char_forward_kernel(slots, x_ref, cnt_lane_ref, cnt_col_ref, gain1_ref, wqkv_ref, wout_ref,
                        gain2_ref, wup_ref, wdown_ref, wproj_ref,
                        vec_ref, pooled_ref, qkv_ref, probs_ref, mixed_ref, first_ref,
                        slope_ref, act_pool_ref):
    rows = x_ref.shape[0]
    width = x_ref.shape[1]
    base = x_ref[...].astype(F32)
    unit, _ = norm_parts(base)
    normed = (unit * gain1_ref[...]).astype(BF)
    qkv_ref[...] = nn(normed, wqkv_ref[...]).astype(BF)
    for tile in range(rows // TILE):
        at = pl.ds(tile * TILE, TILE)
        valid = (lax.broadcasted_iota(jnp.int32, (slots, TILE), 0)
                 < cnt_lane_ref[:, tile * TILE:(tile + 1) * TILE])
        for pair in range(CHEADS // 2):
            c0 = pair * TILE
            queries = split_heads(qkv_ref[at, c0:c0 + TILE])
            keys = qkv_ref[at, width + c0:width + c0 + TILE]
            values = split_heads(qkv_ref[at, 2 * width + c0:2 * width + c0 + TILE])
            scores = compact(nt(keys, queries), slots)
            parts = []
            for head in range(2):
                own = jnp.where(valid, scores[:, head * TILE:(head + 1) * TILE], NEG_LARGE)
                top = jnp.max(own, axis=0, keepdims=True)
                weight = jnp.exp((own - top) * (CHD ** -0.5))
                parts.append(weight / jnp.sum(weight, axis=0, keepdims=True))
            probs = jnp.concatenate(parts, axis=1).astype(BF)
            probs_ref[tile, pair] = probs
            mixed_ref[at, c0:c0 + TILE] = tn(stack_lanes(expand(probs, slots)), values).astype(BF)
    first = base + nn(mixed_ref[...], wout_ref[...])
    first_ref[...] = first
    unit2, _ = norm_parts(first)
    normed2 = (unit2 * gain2_ref[...]).astype(BF)
    counts_col = cnt_col_ref[...]
    slot = jnp.bitwise_and(lax.broadcasted_iota(jnp.int32, (rows, 1), 0), slots - 1)
    valid_col = slot < counts_col
    pool = pool_matrix(rows, slots, counts_col).astype(BF)
    chunk = 256
    for part in range(wup_ref.shape[1] // chunk):
        cols = slice(part * chunk, (part + 1) * chunk)
        active, slope = gelu_parts(nn(normed2, wup_ref[:, cols]))
        slope_ref[:, cols] = jnp.where(valid_col, slope, 0.0).astype(BF)
        act_pool_ref[:, cols] = tn(pool, active.astype(BF)).astype(BF)
    pooled = tn(pool, first.astype(BF)) + nn(act_pool_ref[...], wdown_ref[...])
    pooled = pooled.astype(BF)
    pooled_ref[...] = pooled
    vec_ref[...] = nn(pooled, wproj_ref[...]).astype(BF)


def char_forward(x, counts, gain1, wqkv, wout, gain2, wup, wdown, wproj):
    rows, width = x.shape
    words = counts.shape[0]
    slots = rows // words
    hidden = wup.shape[1]
    wide = wproj.shape[1]
    step = min(CSTEP, rows)
    step_words = step // slots
    spread = jnp.repeat(counts, slots)
    row_block = lambda cols: pl.BlockSpec((step, cols), lambda i: (i, 0))
    word_block = lambda cols: pl.BlockSpec((step_words, cols), lambda i: (i, 0))
    whole = lambda shape: pl.BlockSpec(shape, lambda i: (0, 0))
    tiles = step // TILE
    return pl.pallas_call(
        functools.partial(char_forward_kernel, slots),
        grid=(rows // step,),
        in_specs=[
            row_block(width),
            pl.BlockSpec((1, step), lambda i: (0, i)),
            row_block(1),
            whole((1, width)),
            whole((width, 3 * width)),
            whole((width, width)),
            whole((1, width)),
            whole((width, hidden)),
            whole((hidden, width)),
            whole((width, wide)),
        ],
        out_specs=[
            word_block(wide),
            word_block(width),
            row_block(3 * width),
            pl.BlockSpec((tiles, CHEADS // 2, slots, 2 * TILE), lambda i: (i, 0, 0, 0)),
            row_block(width),
            row_block(width),
            row_block(hidden),
            word_block(hidden),
        ],
        out_shape=[
            jax.ShapeDtypeStruct((words, wide), BF),
            jax.ShapeDtypeStruct((words, width), BF),
            jax.ShapeDtypeStruct((rows, 3 * width), BF),
            jax.ShapeDtypeStruct((rows // TILE, CHEADS // 2, slots, 2 * TILE), BF),
            jax.ShapeDtypeStruct((rows, width), BF),
            jax.ShapeDtypeStruct((rows, width), F32),
            jax.ShapeDtypeStruct((rows, hidden), BF),
            jax.ShapeDtypeStruct((words, hidden), BF),
        ],
        compiler_params=pltpu.CompilerParams(vmem_limit_bytes=60 << 20),
        name="char_forward",
    )(x, spread[None, :], spread[:, None], gain1[None, :], wqkv, wout, gain2[None, :], wup, wdown, wproj)


def char_backward_kernel(slots, x_ref, cnt_col_ref, inv_ref, gain1_ref, wqkv_ref, wout_ref, gain2_ref,
                         wup_ref, wdown_ref, gpl_ref, act_pool_ref, qkv_ref, probs_ref,
                         mixed_ref, first_ref, slope_ref,
                         dx_ref, dgain_ref, dqkv_ref, dout_ref, dup_ref, ddown_ref,
                         down_ref, gq_ref, gmix_ref, gup_ref, spread_ref):
    step = pl.program_id(0)
    rows, width = x_ref.shape
    words = rows // slots

    @pl.when(step == 0)
    def _():
        dgain_ref[...] = jnp.zeros_like(dgain_ref)
        dqkv_ref[...] = jnp.zeros_like(dqkv_ref)
        dout_ref[...] = jnp.zeros_like(dout_ref)
        dup_ref[...] = jnp.zeros_like(dup_ref)
        low = gpl_ref[...].astype(BF)
        ddown_ref[...] = tn(act_pool_ref[...], low)
        scaled = gpl_ref[...] * inv_ref[...]
        down_ref[:, width:] = nt(scaled.astype(BF), wdown_ref[...])
        down_ref[:, :width] = scaled

    for word in range(words):
        line = down_ref[pl.ds(step * words + word, 1), :width]
        spread_ref[word * slots:(word + 1) * slots, :] = jnp.broadcast_to(line, (slots, width))
        line = down_ref[pl.ds(step * words + word, 1), width:]
        at = slice(word * slots, (word + 1) * slots)
        gup_ref[at, :] = (jnp.broadcast_to(line, (slots, line.shape[1])) * slope_ref[at, :].astype(F32)).astype(BF)

    slot = jnp.bitwise_and(lax.broadcasted_iota(jnp.int32, (rows, 1), 0), slots - 1)
    valid_col = slot < cnt_col_ref[...]
    first = first_ref[...]
    unit2, rate2 = norm_parts(first)
    dup_ref[...] += tn((unit2 * gain2_ref[...]).astype(BF), gup_ref[...])
    upstream = nt(gup_ref[...], wup_ref[...])
    dgain_ref[1:2, :] += jnp.sum(upstream * unit2, axis=0, keepdims=True)
    grad_first = jnp.where(valid_col, spread_ref[...], 0.0) + norm_back(upstream, gain2_ref[...], unit2, rate2)
    spread_ref[...] = grad_first
    low = grad_first.astype(BF)
    dout_ref[...] += tn(mixed_ref[...], low)
    gmix_ref[...] = nt(low, wout_ref[...]).astype(BF)
    for tile in range(rows // TILE):
        at = pl.ds(tile * TILE, TILE)
        for pair in range(CHEADS // 2):
            c0 = pair * TILE
            queries = split_heads(qkv_ref[at, c0:c0 + TILE])
            keys = split_heads(qkv_ref[at, width + c0:width + c0 + TILE])
            values = qkv_ref[at, 2 * width + c0:2 * width + c0 + TILE]
            grads = split_heads(gmix_ref[at, c0:c0 + TILE])
            probs_low = probs_ref[tile, pair]
            probs = probs_low.astype(F32)
            grad_probs = compact(nt(values, grads), slots)
            inner = jnp.sum(probs * grad_probs, axis=0, keepdims=True)
            grad_scores = (probs * (grad_probs - inner) * (CHD ** -0.5)).astype(BF)
            wide_scores = expand(grad_scores, slots)
            wide_probs = expand(probs_low, slots)
            gq_ref[at, c0:c0 + TILE] = tn(stack_lanes(wide_scores), keys).astype(BF)
            gq_ref[at, width + c0:width + c0 + TILE] = nn(wide_scores, queries).astype(BF)
            gq_ref[at, 2 * width + c0:2 * width + c0 + TILE] = nn(wide_probs, grads).astype(BF)
    unit1, rate1 = norm_parts(x_ref[...].astype(F32))
    dqkv_ref[...] += tn((unit1 * gain1_ref[...]).astype(BF), gq_ref[...])
    upstream1 = nt(gq_ref[...], wqkv_ref[...])
    dgain_ref[0:1, :] += jnp.sum(upstream1 * unit1, axis=0, keepdims=True)
    dx_ref[...] = spread_ref[...] + norm_back(upstream1, gain1_ref[...], unit1, rate1)


def char_backward(x, counts, gain1, wqkv, wout, gain2, wup, wdown, grad_pooled, saved):
    qkv, probs, mixed, first, slope, act_pool = saved
    rows, width = x.shape
    words = counts.shape[0]
    slots = rows // words
    hidden = wup.shape[1]
    step = min(CSTEP, rows)
    spread = jnp.repeat(counts, slots)
    row_block = lambda cols: pl.BlockSpec((step, cols), lambda i: (i, 0))
    whole = lambda shape: pl.BlockSpec(shape, lambda i: (0, 0))
    tiles = step // TILE
    return pl.pallas_call(
        functools.partial(char_backward_kernel, slots),
        grid=(rows // step,),
        in_specs=[
            row_block(width),
            row_block(1),
            whole((words, 1)),
            whole((1, width)),
            whole((width, 3 * width)),
            whole((width, width)),
            whole((1, width)),
            whole((width, hidden)),
            whole((hidden, width)),
            whole((words, width)),
            whole((words, hidden)),
            row_block(3 * width),
            pl.BlockSpec((tiles, CHEADS // 2, slots, 2 * TILE), lambda i: (i, 0, 0, 0)),
            row_block(width),
            row_block(width),
            row_block(hidden),
        ],
        out_specs=[
            row_block(width),
            whole((8, width)),
            whole((width, 3 * width)),
            whole((width, width)),
            whole((width, hidden)),
            whole((hidden, width)),
        ],
        out_shape=[
            jax.ShapeDtypeStruct((rows, width), F32),
            jax.ShapeDtypeStruct((8, width), F32),
            jax.ShapeDtypeStruct((width, 3 * width), F32),
            jax.ShapeDtypeStruct((width, width), F32),
            jax.ShapeDtypeStruct((width, hidden), F32),
            jax.ShapeDtypeStruct((hidden, width), F32),
        ],
        scratch_shapes=[
            pltpu.VMEM((words, width + hidden), F32),
            pltpu.VMEM((step, 3 * width), BF),
            pltpu.VMEM((step, width), BF),
            pltpu.VMEM((step, hidden), BF),
            pltpu.VMEM((step, width), F32),
        ],
        compiler_params=pltpu.CompilerParams(vmem_limit_bytes=60 << 20),
        name="char_backward",
    )(x, spread[:, None], (1.0 / counts.astype(F32))[:, None], gain1[None, :], wqkv, wout, gain2[None, :],
      wup, wdown, grad_pooled, act_pool, qkv, probs, mixed, first, slope)


HD = 64


def layer_norm(values, gain_vector):
    centre = values - jnp.mean(values, axis=-1, keepdims=True)
    spread = jnp.mean(centre * centre, axis=-1, keepdims=True)
    return centre * lax.rsqrt(spread + EPSILON) * gain_vector


def gelu_tanh(values):
    return jax.nn.gelu(values, approximate=True)


def matmul(left, right):
    return jnp.dot(left, right, preferred_element_type=jnp.float32)


def contract_rows(left, right):
    return lax.dot_general(
        left, right, (((0,), (0,)), ((), ())), preferred_element_type=jnp.float32
    )


def contract_cols(left, right):
    return lax.dot_general(
        left, right, (((1,), (1,)), ((), ())), preferred_element_type=jnp.float32
    )


def block_mask(seq_docs, first_row, block_rows):
    length = seq_docs.shape[0]
    block_docs = lax.dynamic_slice_in_dim(seq_docs, first_row, block_rows, 0)
    row_ids = first_row + jnp.arange(block_rows)
    key_ids = jnp.arange(length)
    return (block_docs[:, None] == seq_docs[None, :]) & (key_ids[None, :] <= row_ids[:, None])


def attention_forward(queries, key_rows, value_rows, doc_ids, block_rows):
    length = queries.shape[1]
    score_scale = queries.shape[3] ** (-0.5)
    block_count = length // block_rows

    def sequence_pass(members):
        seq_q, seq_k, seq_v, seq_docs = members

        def block_pass(block_index):
            first_row = block_index * block_rows
            block_q = lax.dynamic_slice_in_dim(seq_q, first_row, block_rows, 0)
            allowed = block_mask(seq_docs, first_row, block_rows)
            scores = (
                jnp.einsum("qhd,khd->hqk", block_q, seq_k, preferred_element_type=jnp.float32)
                * score_scale
            )
            scores = jnp.where(allowed[None], scores, NEG_LARGE)
            row_max = jnp.max(scores, axis=-1, keepdims=True)
            exponent = jnp.exp(scores - row_max)
            row_total = jnp.sum(exponent, axis=-1, keepdims=True)
            weights_low = (exponent / row_total).astype(jnp.bfloat16)
            mixed_rows = jnp.einsum(
                "hqk,khd->qhd", weights_low, seq_v, preferred_element_type=jnp.float32
            ).astype(jnp.bfloat16)
            return (mixed_rows, (row_max + jnp.log(row_total))[..., 0])

        mixed_rows, log_totals = lax.map(block_pass, jnp.arange(block_count))
        return (mixed_rows.reshape(seq_q.shape), log_totals)

    return lax.map(sequence_pass, (queries, key_rows, value_rows, doc_ids))


def attention_backward(queries, key_rows, value_rows, doc_ids, log_totals, grad_mixed, block_rows):
    length = queries.shape[1]
    score_scale = queries.shape[3] ** (-0.5)
    block_count = length // block_rows

    def sequence_pass(members):
        seq_q, seq_k, seq_v, seq_docs, seq_logs, seq_grad = members

        def block_pass(carried, block_index):
            key_acc, value_acc = carried
            first_row = block_index * block_rows
            block_q = lax.dynamic_slice_in_dim(seq_q, first_row, block_rows, 0)
            block_grad = lax.dynamic_slice_in_dim(seq_grad, first_row, block_rows, 0)
            allowed = block_mask(seq_docs, first_row, block_rows)
            scores = (
                jnp.einsum("qhd,khd->hqk", block_q, seq_k, preferred_element_type=jnp.float32)
                * score_scale
            )
            scores = jnp.where(allowed[None], scores, NEG_LARGE)
            weights_full = jnp.exp(scores - seq_logs[block_index][..., None])
            weights_low = weights_full.astype(jnp.bfloat16)
            value_acc = value_acc + jnp.einsum(
                "hqk,qhd->khd", weights_low, block_grad, preferred_element_type=jnp.float32
            )
            grad_weights = jnp.einsum(
                "qhd,khd->hqk", block_grad, seq_v, preferred_element_type=jnp.float32
            )
            inner_sum = jnp.sum(weights_full * grad_weights, axis=-1, keepdims=True)
            grad_scores = (weights_full * (grad_weights - inner_sum)).astype(jnp.bfloat16)
            grad_block_q = (
                jnp.einsum("hqk,khd->qhd", grad_scores, seq_k, preferred_element_type=jnp.float32)
                * score_scale
            ).astype(jnp.bfloat16)
            key_acc = (
                key_acc
                + jnp.einsum(
                    "hqk,qhd->khd", grad_scores, block_q, preferred_element_type=jnp.float32
                )
                * score_scale
            )
            return ((key_acc, value_acc), grad_block_q)

        zero_rows = jnp.zeros(seq_k.shape, jnp.float32)
        (key_acc, value_acc), grad_q = lax.scan(
            block_pass, (zero_rows, zero_rows), jnp.arange(block_count)
        )
        return (
            grad_q.reshape(seq_q.shape),
            key_acc.astype(jnp.bfloat16),
            value_acc.astype(jnp.bfloat16),
        )

    return lax.map(sequence_pass, (queries, key_rows, value_rows, doc_ids, log_totals, grad_mixed))


def per_device(
    char_inputs,
    char_counts,
    doc_ids,
    cotangent,
    char_norm_one,
    char_query,
    char_key,
    char_value,
    char_out,
    char_norm_two,
    char_up,
    char_down,
    char_proj,
    word_norm_one,
    word_query,
    word_key,
    word_value,
    word_out_proj,
    word_norm_two,
    word_up,
    word_down,
):
    word_count = char_counts.shape[0]
    tensor_rank = lax.axis_index("tensor")
    char_qkv = jnp.concatenate([char_query, char_key, char_value], axis=1)
    word_vectors, pooled, *saved = char_forward(
        char_inputs, char_counts, char_norm_one, char_qkv, char_out, char_norm_two, char_up, char_down, char_proj
    )
    input_whole = lax.all_gather(word_vectors, "tensor", axis=0, tiled=True).astype(jnp.float32)
    normed_whole, pull_first = jax.vjp(layer_norm, input_whole, word_norm_one)
    normed = normed_whole.astype(jnp.bfloat16)
    sequences = doc_ids.shape[0]
    seq_len = doc_ids.shape[1]
    token_count = sequences * seq_len
    head_count = word_query.shape[1] // HD
    shape_heads = (sequences, seq_len, head_count, HD)
    block_rows = min(512, seq_len)
    queries = matmul(normed, word_query).astype(jnp.bfloat16).reshape(shape_heads)
    key_rows = matmul(normed, word_key).astype(jnp.bfloat16).reshape(shape_heads)
    value_rows = matmul(normed, word_value).astype(jnp.bfloat16).reshape(shape_heads)
    mixed_heads, log_totals = attention_forward(queries, key_rows, value_rows, doc_ids, block_rows)
    mixed_flat = mixed_heads.reshape(token_count, head_count * HD)
    attention_part = matmul(mixed_flat, word_out_proj)
    middle = input_whole + lax.psum(attention_part.astype(jnp.bfloat16), "tensor").astype(
        jnp.float32
    )
    normed_mid, pull_mid = jax.vjp(layer_norm, middle, word_norm_two)
    normed_mid = normed_mid.astype(jnp.bfloat16)
    hidden, pull_gelu = jax.vjp(gelu_tanh, matmul(normed_mid, word_up))
    hidden = hidden.astype(jnp.bfloat16)
    feedforward_part = matmul(hidden, word_down)
    full_output = middle + lax.psum(feedforward_part.astype(jnp.bfloat16), "tensor").astype(
        jnp.float32
    )
    word_output = lax.dynamic_slice_in_dim(full_output, tensor_rank * word_count, word_count, 0)
    word_output = word_output.astype(jnp.bfloat16)
    grad_down = contract_rows(hidden, cotangent)
    grad_pre = pull_gelu(contract_cols(cotangent, word_down))[0].astype(jnp.bfloat16)
    grad_up = contract_rows(normed_mid, grad_pre)
    mid_part = contract_cols(grad_pre, word_up)
    cotangent_full = cotangent.astype(jnp.float32)
    back_mid, grad_gain_two = pull_mid(
        lax.psum(mid_part.astype(jnp.bfloat16), "tensor").astype(jnp.float32)
    )
    grad_middle = cotangent_full + back_mid
    grad_middle_low = grad_middle.astype(jnp.bfloat16)
    grad_out_proj = contract_rows(mixed_flat, grad_middle_low)
    grad_mixed = (
        contract_cols(grad_middle_low, word_out_proj).astype(jnp.bfloat16).reshape(shape_heads)
    )
    grad_q, grad_k, grad_v = attention_backward(
        queries, key_rows, value_rows, doc_ids, log_totals, grad_mixed, block_rows
    )
    flat_shape = (token_count, head_count * HD)
    grad_q = grad_q.reshape(flat_shape)
    grad_k = grad_k.reshape(flat_shape)
    grad_v = grad_v.reshape(flat_shape)
    grad_query = contract_rows(normed, grad_q)
    grad_key = contract_rows(normed, grad_k)
    grad_value = contract_rows(normed, grad_v)
    first_part = (
        contract_cols(grad_q, word_query)
        + contract_cols(grad_k, word_key)
        + contract_cols(grad_v, word_value)
    )
    back_first, grad_gain_one = pull_first(
        lax.psum(first_part.astype(jnp.bfloat16), "tensor").astype(jnp.float32)
    )
    grad_input = lax.dynamic_slice_in_dim(
        grad_middle + back_first, tensor_rank * word_count, word_count, 0
    )
    gain_share = (tensor_rank == 0).astype(jnp.float32)
    grad_vectors = grad_input.astype(jnp.bfloat16)
    grad_proj = contract_rows(pooled, grad_vectors)
    grad_pooled = contract_cols(grad_vectors, char_proj)
    char_input_gradient, grad_gains, grad_char_qkv, grad_char_out, grad_char_up, grad_char_down = char_backward(
        char_inputs, char_counts, char_norm_one, char_qkv, char_out, char_norm_two, char_up, char_down,
        grad_pooled, saved
    )
    grad_char_gain_one, grad_char_gain_two = grad_gains[0], grad_gains[1]
    grad_char_query, grad_char_key, grad_char_value = jnp.split(grad_char_qkv, 3, axis=1)
    word_sums = lax.psum(
        (grad_query, grad_key, grad_value, grad_out_proj, grad_up, grad_down), "dp"
    )
    char_sums = lax.psum(
        (
            grad_char_gain_one,
            grad_char_query,
            grad_char_key,
            grad_char_value,
            grad_char_out,
            grad_char_gain_two,
            grad_char_up,
            grad_char_down,
            grad_proj,
            grad_gain_one * gain_share,
            grad_gain_two * gain_share,
        ),
        ("dp", "tensor"),
    )
    return (
        word_output,
        char_input_gradient,
        char_sums[0],
        char_sums[1],
        char_sums[2],
        char_sums[3],
        char_sums[4],
        char_sums[5],
        char_sums[6],
        char_sums[7],
        char_sums[8],
        char_sums[9],
        word_sums[0],
        word_sums[1],
        word_sums[2],
        word_sums[3],
        char_sums[10],
        word_sums[4],
        word_sums[5],
    )


def solution(mesh):
    in_specs = (
        P(("dp", "tensor"), None),
        P(("dp", "tensor")),
        P("dp", None),
        P("dp", None),
        P(),
        P(),
        P(),
        P(),
        P(),
        P(),
        P(),
        P(),
        P(),
        P(),
        P(None, "tensor"),
        P(None, "tensor"),
        P(None, "tensor"),
        P("tensor", None),
        P(),
        P(None, "tensor"),
        P("tensor", None),
    )
    out_specs = (
        P(("dp", "tensor"), None),
        P(("dp", "tensor"), None),
        P(),
        P(),
        P(),
        P(),
        P(),
        P(),
        P(),
        P(),
        P(),
        P(),
        P(None, "tensor"),
        P(None, "tensor"),
        P(None, "tensor"),
        P("tensor", None),
        P(),
        P(None, "tensor"),
        P("tensor", None),
    )
    return jax.shard_map(
        per_device, mesh=mesh, in_specs=in_specs, out_specs=out_specs, check_vma=False
    )
```

```python
import functools

import jax
import jax.numpy as jnp
from jax import lax
from jax.experimental import pallas as pl
from jax.experimental.pallas import tpu as pltpu
from jax.sharding import PartitionSpec as P

BF = jnp.bfloat16
F32 = jnp.float32
EPSILON = 1e-05
NEG_LARGE = -1e30
RANKS = 4
CHEADS = 4
CHD = 64
TILE = 128
CHAR_STEPS = 8
GELU_C = 0.7978845608028654
GELU_A = 0.044715


def nn(left, right):
    return lax.dot_general(left, right, (((1,), (0,)), ((), ())), preferred_element_type=F32)


def nt(left, right):
    return lax.dot_general(left, right, (((1,), (1,)), ((), ())), preferred_element_type=F32)


def tn(left, right):
    return lax.dot_general(left, right, (((0,), (0,)), ((), ())), preferred_element_type=F32)


def norm_parts(values):
    centre = values - jnp.mean(values, axis=-1, keepdims=True)
    spread = jnp.mean(centre * centre, axis=-1, keepdims=True)
    rate = lax.rsqrt(spread + EPSILON)
    return centre * rate, rate


def norm_back(upstream, gain, unit, rate):
    scaled = upstream * gain
    first = jnp.mean(scaled, axis=-1, keepdims=True)
    second = jnp.mean(scaled * unit, axis=-1, keepdims=True)
    return rate * (scaled - first - unit * second)


def gelu_parts(values):
    square = values * values
    inner = values * (GELU_C + (GELU_C * GELU_A) * square)
    half = 0.5 + 0.5 * jnp.tanh(inner)
    active = values * half
    slope = half + (active * (1.0 - half)) * (2.0 * GELU_C + (6.0 * GELU_C * GELU_A) * square)
    return active, slope


def split_heads(pair):
    low_half = lax.broadcasted_iota(jnp.int32, pair.shape, 1) < CHD
    zero = jnp.zeros_like(pair)
    return jnp.concatenate([jnp.where(low_half, pair, zero), jnp.where(low_half, zero, pair)], axis=0)


def word_of_lane(shape, slots):
    lane = lax.broadcasted_iota(jnp.int32, shape, 1)
    return jnp.bitwise_and(lane, TILE - 1) // slots


def compact(scores, slots):
    words = word_of_lane((slots, scores.shape[1]), slots)
    result = scores[0:slots]
    for word in range(1, TILE // slots):
        result = jnp.where(words == word, scores[word * slots:(word + 1) * slots], result)
    return result


def expand(packed, slots):
    words = word_of_lane(packed.shape, slots)
    zero = jnp.zeros_like(packed)
    return jnp.concatenate(
        [jnp.where(words == word, packed, zero) for word in range(TILE // slots)], axis=0
    )


def stack_lanes(pair):
    return jnp.concatenate([pair[:, :TILE], pair[:, TILE:]], axis=0)


def pool_matrix(rows, slots, counts_col):
    words = rows // slots
    row = lax.broadcasted_iota(jnp.int32, (rows, words), 0)
    word = lax.broadcasted_iota(jnp.int32, (rows, words), 1)
    mine = (row // slots == word) & (jnp.bitwise_and(row, slots - 1) < counts_col)
    return jnp.where(mine, 1.0 / counts_col.astype(F32), 0.0)


MESH = pl.DeviceIdType.MESH
LANE_SPLIT = 256


class Place:
    def __init__(self):
        self.dp = lax.axis_index("dp")
        self.rank = lax.axis_index("tensor")
        self.core = lax.rem(self.dp, 2)
        self.x = lax.rem(self.dp // 2, 2)
        self.y = lax.rem(self.dp // 4, 2)
        self.core_mate = (self.dp + 1 - 2 * self.core, self.rank)
        self.x_mate = (self.dp + 2 - 4 * self.x, self.rank)
        self.y_mate = (self.dp + 4 - 8 * self.y, self.rank)

    def ring(self, offset):
        return lax.rem(self.rank + offset, RANKS)

    def ring_device(self, offset):
        return (self.dp, self.ring(offset))

    def bit_mate(self, bit):
        size = 1 << bit
        mine = lax.rem(self.dp // size, 2)
        return (self.dp + size - 2 * size * mine, self.rank)

    def mates(self, bits):
        extra = [self.bit_mate(bit) for bit in range(3, bits)]
        return [self.core_mate, self.x_mate, self.y_mate] + extra


def meet(devices):
    barrier = pltpu.get_barrier_semaphore()
    for device in devices:
        pl.semaphore_signal(barrier, inc=1, device_id=device, device_id_type=MESH)
    pl.semaphore_wait(barrier, len(devices))


def remote(source, target, sems, device):
    return pltpu.make_async_remote_copy(
        src_ref=source, dst_ref=target, send_sem=sems[0], recv_sem=sems[1],
        device_id=device, device_id_type=MESH,
    )


class Sems:
    def __init__(self, send, recv, start=0):
        self.send, self.recv, self.next = send, recv, start

    def take(self):
        at = self.next
        self.next += 1
        return self.send.at[at], self.recv.at[at]


def rows_at(start, size):
    return pl.ds(pl.multiple_of(start, 16), size)


def halves(width):
    return (slice(0, LANE_SPLIT), slice(LANE_SPLIT, width))


class Gather:
    def __init__(self, place, local, whole, sems):
        self.stages = [[], [], [], []]
        rows = local.shape[0]
        unit = rows // 8
        p = place
        left, right = halves(local.shape[1])
        left_at = p.core * 4 + p.x * 2 + p.y
        right_at = p.core * 4 + p.y * 2 + p.x
        for offset in range(1, RANKS):
            for lanes, at in ((left, left_at), (right, right_at)):
                at = rows_at(at * unit, unit)
                self.stages[0].append(remote(
                    local.at[at, lanes], whole.at[p.rank, at, lanes], sems.take(), p.ring_device(offset)))
        for offset in range(1, RANKS):
            rank = p.ring(offset)
            for lanes, at, first, second, mate_first, mate_second in (
                (left, left_at, p.x, None, p.y_mate, p.x_mate),
                (right, right_at, p.y, None, p.x_mate, p.y_mate),
            ):
                one = rows_at(at * unit, unit)
                two = rows_at((p.core * 4 + first * 2) * unit, 2 * unit)
                self.stages[1].append(remote(
                    whole.at[rank, one, lanes], whole.at[rank, one, lanes], sems.take(), mate_first))
                self.stages[2].append(remote(
                    whole.at[rank, two, lanes], whole.at[rank, two, lanes], sems.take(), mate_second))
            four = rows_at(p.core * 4 * unit, 4 * unit)
            self.stages[3].append(remote(
                whole.at[rank, four], whole.at[rank, four], sems.take(), p.core_mate))

    def start(self, stage):
        for copy in self.stages[stage]:
            copy.start()

    def wait(self, stage):
        for copy in self.stages[stage]:
            copy.wait()


def gather_copies():
    return 2 * (RANKS - 1) * 3 + (RANKS - 1)


class Reduce:
    def __init__(self, place, bits, buf, out, got_core, got_one, got_two, got_more, got_rank, sems, everywhere):
        p = place
        self.p, self.buf, self.everywhere = p, buf, everywhere
        self.mine = out.at[p.rank] if everywhere else out
        self.got = (got_core, got_one, got_two, got_more, got_rank)
        rows = buf.shape[1]
        unit = rows // 8
        self.unit = unit
        left, right = halves(buf.shape[2])
        self.lanes = (left, right)
        half = lambda core: rows_at(core * 4 * unit, 4 * unit)
        self.core_copy = [remote(buf.at[:, half(1 - p.core)], got_core, sems.take(), p.core_mate)]
        self.core_rows = half(p.core)
        quarter_left = lambda x: rows_at((p.core * 4 + x * 2) * unit, 2 * unit)
        quarter_right = lambda y: rows_at((p.core * 4 + y * 2) * unit, 2 * unit)
        self.one_copy = [
            remote(buf.at[:, quarter_left(1 - p.x), left], got_one.at[:, :, left], sems.take(), p.x_mate),
            remote(buf.at[:, quarter_right(1 - p.y), right], got_one.at[:, :, right], sems.take(), p.y_mate),
        ]
        self.one_rows = (quarter_left(p.x), quarter_right(p.y))
        eighth_left = lambda y: rows_at((p.core * 4 + p.x * 2 + y) * unit, unit)
        eighth_right = lambda x: rows_at((p.core * 4 + p.y * 2 + x) * unit, unit)
        self.two_copy = [
            remote(buf.at[:, eighth_left(1 - p.y), left], got_two.at[:, :, left], sems.take(), p.y_mate),
            remote(buf.at[:, eighth_right(1 - p.x), right], got_two.at[:, :, right], sems.take(), p.x_mate),
        ]
        self.two_rows = (eighth_left(p.y), eighth_right(p.x))
        self.more_copy = []
        for bit in range(3, bits):
            mate = p.bit_mate(bit)
            self.more_copy.append([
                remote(buf.at[:, at, lanes], got_more.at[bit - 3, :, :, lanes], sems.take(), mate)
                for at, lanes in zip(self.two_rows, self.lanes)
            ])
        self.rank_copy, self.rank_back = [], []
        for offset in range(1, RANKS):
            for at, lanes in zip(self.two_rows, self.lanes):
                self.rank_copy.append(remote(
                    buf.at[p.ring(offset), at, lanes], got_rank.at[offset - 1, :, lanes],
                    sems.take(), p.ring_device(offset)))
        if everywhere:
            for offset in range(1, RANKS):
                for at, lanes in zip(self.two_rows, self.lanes):
                    self.rank_back.append(remote(
                        out.at[p.rank, at, lanes], out.at[p.rank, at, lanes], sems.take(), p.ring_device(offset)))

        def back(at, lanes, mate):
            part = out.at[:, at, lanes] if everywhere else out.at[at, lanes]
            return remote(part, part, sems.take(), mate)

        self.back_two = [back(self.two_rows[0], left, p.y_mate), back(self.two_rows[1], right, p.x_mate)]
        self.back_one = [back(self.one_rows[0], left, p.x_mate), back(self.one_rows[1], right, p.y_mate)]
        self.back_core = [back(self.core_rows, slice(None), p.core_mate)]
        names = ["core", "one", "two"] + list(range(len(self.more_copy))) + ["rank"]
        names += ["rank_back"] if everywhere else []
        self.names = names + ["back_two", "back_one", "back_core"]

    def copies(self, name):
        if isinstance(name, int):
            return self.more_copy[name]
        return {"core": self.core_copy, "one": self.one_copy, "two": self.two_copy, "rank": self.rank_copy,
                "rank_back": self.rank_back, "back_two": self.back_two, "back_one": self.back_one,
                "back_core": self.back_core}[name]

    def add(self, at, lanes, terms, who=slice(None)):
        total = self.buf[who, at, lanes].astype(F32)
        for term in terms:
            total = total + term.astype(F32)
        self.buf[who, at, lanes] = total.astype(BF)

    def start(self, index):
        for copy in self.copies(self.names[index]):
            copy.start()

    def finish(self, index):
        name = self.names[index]
        for copy in self.copies(name):
            copy.wait()
        got_core, got_one, got_two, got_more, got_rank = self.got
        if name == "core":
            for quarter in range(RANKS):
                self.add(self.core_rows, slice(None), [got_core[quarter]], quarter)
        elif name == "one":
            for at, lanes in zip(self.one_rows, self.lanes):
                for quarter in range(RANKS):
                    self.add(at, lanes, [got_one[quarter, :, lanes]], quarter)
        elif name == "two":
            for at, lanes in zip(self.two_rows, self.lanes):
                for quarter in range(RANKS):
                    self.add(at, lanes, [got_two[quarter, :, lanes]], quarter)
        elif name == "rank":
            for at, lanes in zip(self.two_rows, self.lanes):
                total = self.buf[self.p.rank, at, lanes].astype(F32)
                for k in range(RANKS - 1):
                    total = total + got_rank[k, :, lanes].astype(F32)
                self.mine[at, lanes] = total.astype(BF)
        elif isinstance(name, int):
            for at, lanes in zip(self.two_rows, self.lanes):
                for quarter in range(RANKS):
                    self.add(at, lanes, [got_more[name, quarter, :, lanes]], quarter)

    def run(self, index):
        self.start(index)
        self.finish(index)


def reduce_copies(bits, everywhere):
    pairs = 2 * (RANKS - 1)
    return 1 + 2 + 2 + 2 * (bits - 3) + pairs + (pairs if everywhere else 0) + 2 + 2 + 1


def reduce_scratch(bits, rows, lanes):
    unit = rows // 8
    return [
        pltpu.VMEM((RANKS, 4 * unit, lanes), BF),
        pltpu.VMEM((RANKS, 2 * unit, lanes), BF),
        pltpu.VMEM((RANKS, unit, lanes), BF),
        pltpu.VMEM((max(bits - 3, 1), RANKS, unit, lanes), BF),
        pltpu.VMEM((RANKS - 1, unit, lanes), BF),
    ]


def char_forward_kernel(slots, x_ref, cnt_lane_ref, cnt_col_ref, gain1_ref, wqkv_ref, wout_ref,
                        gain2_ref, wup_ref, wdown_ref, wproj_ref,
                        lqkv_ref, lout_ref, lup_ref, ldown_ref,
                        vec_ref, pooled_ref, qkv_ref, probs_ref, mixed_ref, first_ref,
                        slope_ref, act_pool_ref, near_ref, wqkv_all, wout_all, wup_all, wdown_all,
                        own_sem, send_sem, recv_sem):
    rows = x_ref.shape[0]
    width = x_ref.shape[1]
    step = pl.program_id(0)
    steps = pl.num_programs(0)
    words = rows // slots
    p = Place()
    pairs = ((lqkv_ref, wqkv_all), (lout_ref, wout_all), (lup_ref, wup_all), (ldown_ref, wdown_all))
    gathers = [Gather(p, mine, whole, Sems(send_sem, recv_sem, gather_copies() * index))
               for index, (mine, whole) in enumerate(pairs)]
    own_copies = [pltpu.make_async_copy(mine, whole.at[p.rank], own_sem.at[index])
                  for index, (mine, whole) in enumerate(pairs)]
    vec_base = gather_copies() * len(pairs)

    def vec_copies(at):
        copies = []
        for slot, offset in ((1, 1), (0, 2)):
            sem = vec_base + 2 * at + slot
            part = rows_at(at * words, words)
            copies.append(remote(vec_ref.at[part], near_ref.at[slot, part],
                                 (send_sem.at[sem], recv_sem.at[sem]), p.ring_device(offset)))
        return copies

    @pl.when(step == 0)
    def _():
        meet([p.ring_device(offset) for offset in (1, 2, 3)] + [p.core_mate, p.x_mate, p.y_mate])
        for copy in own_copies:
            copy.start()

    plan = {at: [] for at in range(CHAR_STEPS)}
    for group, (members, begin) in enumerate((((0, 1), (0, 2, 3, 4)), ((2,), (0, 3, 4, 5)), ((3,), (0, 4, 5, 6)))):
        for stage in range(4):
            for member in members:
                plan[begin[stage]].append((member, stage))
    for at, todo in plan.items():
        if todo:
            @pl.when(step == at)
            def _(todo=todo):
                for member, stage in todo:
                    if stage:
                        gathers[member].wait(stage - 1)
                    gathers[member].start(stage)

    @pl.when(step > 0)
    def _():
        for copy in vec_copies(step - 1):
            copy.start()

    base = x_ref[...].astype(F32)
    unit, _ = norm_parts(base)
    normed = (unit * gain1_ref[...]).astype(BF)
    qkv_ref[...] = nn(normed, wqkv_ref[...]).astype(BF)
    for tile in range(rows // TILE):
        at = pl.ds(tile * TILE, TILE)
        valid = (lax.broadcasted_iota(jnp.int32, (slots, TILE), 0)
                 < cnt_lane_ref[:, tile * TILE:(tile + 1) * TILE])
        for pair in range(CHEADS // 2):
            c0 = pair * TILE
            queries = split_heads(qkv_ref[at, c0:c0 + TILE])
            keys = qkv_ref[at, width + c0:width + c0 + TILE]
            values = split_heads(qkv_ref[at, 2 * width + c0:2 * width + c0 + TILE])
            scores = compact(nt(keys, queries), slots)
            parts = []
            for head in range(2):
                own = jnp.where(valid, scores[:, head * TILE:(head + 1) * TILE], NEG_LARGE)
                top = jnp.max(own, axis=0, keepdims=True)
                weight = jnp.exp((own - top) * (CHD ** -0.5))
                parts.append(weight / jnp.sum(weight, axis=0, keepdims=True))
            probs = jnp.concatenate(parts, axis=1).astype(BF)
            probs_ref[tile, pair] = probs
            mixed_ref[at, c0:c0 + TILE] = tn(stack_lanes(expand(probs, slots)), values).astype(BF)
    first = base + nn(mixed_ref[...], wout_ref[...])
    first_ref[...] = first
    unit2, _ = norm_parts(first)
    normed2 = (unit2 * gain2_ref[...]).astype(BF)
    counts_col = cnt_col_ref[...]
    slot = jnp.bitwise_and(lax.broadcasted_iota(jnp.int32, (rows, 1), 0), slots - 1)
    valid_col = slot < counts_col
    pool = pool_matrix(rows, slots, counts_col).astype(BF)
    chunk = 256
    for part in range(wup_ref.shape[1] // chunk):
        cols = slice(part * chunk, (part + 1) * chunk)
        active, slope = gelu_parts(nn(normed2, wup_ref[:, cols]))
        slope_ref[:, cols] = jnp.where(valid_col, slope, 0.0).astype(BF)
        act_pool_ref[:, cols] = tn(pool, active.astype(BF)).astype(BF)
    pooled = tn(pool, first.astype(BF)) + nn(act_pool_ref[...], wdown_ref[...])
    pooled = pooled.astype(BF)
    pooled_ref[...] = pooled
    vec_ref[rows_at(step * words, words), :] = nn(pooled, wproj_ref[...]).astype(BF)

    @pl.when(step == steps - 1)
    def _():
        for copy in vec_copies(step):
            copy.start()
        for copy in own_copies:
            copy.wait()
        for gather in gathers:
            gather.wait(3)
        for at in range(CHAR_STEPS):
            for copy in vec_copies(at):
                copy.wait()


def char_forward(x, counts, gain1, wqkv, wout, gain2, wup, wdown, wproj, lqkv, lout, lup, ldown):
    rows, width = x.shape
    words = counts.shape[0]
    slots = rows // words
    hidden = wup.shape[1]
    wide = wproj.shape[1]
    step = rows // CHAR_STEPS
    step_words = step // slots
    spread = jnp.repeat(counts, slots)
    row_block = lambda cols: pl.BlockSpec((step, cols), lambda i: (i, 0))
    word_block = lambda cols: pl.BlockSpec((step_words, cols), lambda i: (i, 0))
    whole = lambda shape: pl.BlockSpec(shape, lambda i: (0, 0))
    tiles = step // TILE
    return pl.pallas_call(
        functools.partial(char_forward_kernel, slots),
        grid=(rows // step,),
        in_specs=[
            row_block(width),
            pl.BlockSpec((1, step), lambda i: (0, i)),
            row_block(1),
            whole((1, width)),
            whole((width, 3 * width)),
            whole((width, width)),
            whole((1, width)),
            whole((width, hidden)),
            whole((hidden, width)),
            whole((width, wide)),
            whole(lqkv.shape),
            whole(lout.shape),
            whole(lup.shape),
            whole(ldown.shape),
        ],
        out_specs=[
            whole((words, wide)),
            word_block(width),
            row_block(3 * width),
            pl.BlockSpec((tiles, CHEADS // 2, slots, 2 * TILE), lambda i: (i, 0, 0, 0)),
            row_block(width),
            row_block(width),
            row_block(hidden),
            word_block(hidden),
        ] + [pl.BlockSpec(memory_space=pl.ANY)] * 5,
        out_shape=[
            jax.ShapeDtypeStruct((words, wide), BF),
            jax.ShapeDtypeStruct((words, width), BF),
            jax.ShapeDtypeStruct((rows, 3 * width), BF),
            jax.ShapeDtypeStruct((rows // TILE, CHEADS // 2, slots, 2 * TILE), BF),
            jax.ShapeDtypeStruct((rows, width), BF),
            jax.ShapeDtypeStruct((rows, width), F32),
            jax.ShapeDtypeStruct((rows, hidden), BF),
            jax.ShapeDtypeStruct((words, hidden), BF),
            jax.ShapeDtypeStruct((2, words, wide), BF),
            jax.ShapeDtypeStruct((RANKS,) + lqkv.shape, BF),
            jax.ShapeDtypeStruct((RANKS,) + lout.shape, BF),
            jax.ShapeDtypeStruct((RANKS,) + lup.shape, BF),
            jax.ShapeDtypeStruct((RANKS,) + ldown.shape, BF),
        ],
        scratch_shapes=[
            pltpu.SemaphoreType.DMA((4,)),
            pltpu.SemaphoreType.DMA((gather_copies() * 4 + 2 * CHAR_STEPS,)),
            pltpu.SemaphoreType.DMA((gather_copies() * 4 + 2 * CHAR_STEPS,)),
        ],
        compiler_params=pltpu.CompilerParams(
            vmem_limit_bytes=60 << 20, collective_id=0, has_side_effects=True),
        name="char_forward",
    )(x, spread[None, :], spread[:, None], gain1[None, :], wqkv, wout, gain2[None, :], wup, wdown, wproj,
      lqkv, lout, lup, ldown)


UP, DOWN, OUT, QKV, WORD_ROWS = 0, 512, 1024, 1152, 1536


def word_kernel(bits, vec_ref, near_ref, row_docs_ref, key_docs_ref, cot_ref, wqkv_ref, wout_ref, wup_ref,
                wdown_ref, gain1_ref, gain2_ref, wproj_ref, pooled_ref,
                out_ref, gpl_ref, dproj_ref, dgain_ref, grads_ref,
                n1_ref, q_ref, kv_ref, probs_ref, o_ref, act_ref, slope_ref, go_ref, gq_ref, gkv_ref,
                back_ref, cot_own, cot_sem, part_ref, got_ref, send_sem, recv_sem):
    p = Place()
    words, wide = vec_ref.shape
    window = 3 * words
    fetch = pltpu.make_async_copy(cot_ref.at[rows_at(p.rank * words, words)], cot_own, cot_sem)
    fetch.start()
    meet([p.ring_device(offset) for offset in (1, 2, 3)])

    own = vec_ref[...].astype(F32)
    unit1, rate1 = norm_parts(own)
    n1_ref[2 * words:, :] = (unit1 * gain1_ref[...]).astype(BF)
    for slot in range(2):
        unit, _ = norm_parts(near_ref[slot].astype(F32))
        n1_ref[slot * words:(slot + 1) * words, :] = (unit * gain1_ref[...]).astype(BF)

    def project(rank, carry):
        q_ref[rank] = nn(n1_ref[2 * words:, :], wqkv_ref[rank, :, 0:TILE]).astype(BF)
        kv_ref[rank] = nn(n1_ref[...], wqkv_ref[rank, :, TILE:]).astype(BF)
        scores = nt(split_heads(q_ref[rank]), kv_ref[rank, :, 0:TILE]) * (CHD ** -0.5)
        row = lax.broadcasted_iota(jnp.int32, (words, window), 0)
        key = lax.broadcasted_iota(jnp.int32, (words, window), 1)
        allowed = (row_docs_ref[...] == key_docs_ref[...]) & (key <= row + 2 * words)
        for head in range(2):
            at = slice(head * words, (head + 1) * words)
            masked = jnp.where(allowed, scores[at], NEG_LARGE)
            top = jnp.max(masked, axis=-1, keepdims=True)
            weight = jnp.exp(masked - top)
            probs_ref[rank, at, :] = (weight * (1.0 / jnp.sum(weight, axis=-1, keepdims=True))).astype(BF)
        pair = jnp.concatenate([probs_ref[rank, 0:words, :], probs_ref[rank, words:, :]], axis=1)
        o_ref[rank] = nn(pair, split_heads(kv_ref[rank, :, TILE:])).astype(BF)
        back_ref[...] += nn(o_ref[rank], wout_ref[rank])
        return carry

    back_ref[...] = own
    lax.fori_loop(0, RANKS, project, 0)
    middle = back_ref[...]
    unit2, rate2 = norm_parts(middle)
    normed2 = (unit2 * gain2_ref[...]).astype(BF)

    def feed(rank, carry):
        active, slope = gelu_parts(nn(normed2, wup_ref[rank]))
        act_ref[rank] = active.astype(BF)
        slope_ref[rank] = slope.astype(BF)
        back_ref[...] += nn(act_ref[rank], wdown_ref[rank])
        return carry

    lax.fori_loop(0, RANKS, feed, 0)
    out_ref[...] = back_ref[...].astype(BF)
    fetch.wait()
    back_ref[...] = jnp.zeros_like(back_ref)

    def feed_back(rank, carry):
        upstream = (nt(cot_own[...], wdown_ref[rank]) * slope_ref[rank].astype(F32)).astype(BF)
        back_ref[...] += nt(upstream, wup_ref[rank])
        grads_ref[rank, UP:DOWN, :] = tn(normed2, upstream).astype(BF)
        grads_ref[rank, DOWN:OUT, :] = tn(act_ref[rank], cot_own[...]).astype(BF)
        return carry

    lax.fori_loop(0, RANKS, feed_back, 0)
    upstream2 = back_ref[...]
    dgain_ref[...] = jnp.zeros_like(dgain_ref)
    dgain_ref[1:2, :] = jnp.sum(upstream2 * unit2, axis=0, keepdims=True)
    grad_middle = cot_own[...].astype(F32) + norm_back(upstream2, gain2_ref[...], unit2, rate2)
    middle_low = grad_middle.astype(BF)

    back_ref[...] = jnp.zeros_like(back_ref)
    part_ref[...] = jnp.zeros_like(part_ref)

    def attend_back(rank, carry):
        go_ref[...] = nt(middle_low, wout_ref[rank]).astype(BF)
        grads_ref[rank, OUT:QKV, :] = tn(o_ref[rank], middle_low).astype(BF)
        go_pair = split_heads(go_ref[...])
        grad_probs = nt(go_pair, kv_ref[rank, :, TILE:])
        probs = probs_ref[rank].astype(F32)
        inner = jnp.sum(probs * grad_probs, axis=-1, keepdims=True)
        grad_scores = (probs * (grad_probs - inner) * (CHD ** -0.5)).astype(BF)
        q_pair = split_heads(q_ref[rank])
        gkv_ref[:, 0:TILE] = tn(grad_scores, q_pair).astype(BF)
        gkv_ref[:, TILE:] = tn(probs_ref[rank], go_pair).astype(BF)
        pair = jnp.concatenate([grad_scores[0:words], grad_scores[words:]], axis=1)
        gq_ref[...] = nn(pair, split_heads(kv_ref[rank, :, 0:TILE])).astype(BF)
        part_ref[...] += nt(gkv_ref[0:2 * words, :], wqkv_ref[rank, :, TILE:])
        back_ref[...] += nt(gkv_ref[2 * words:, :], wqkv_ref[rank, :, TILE:])
        back_ref[...] += nt(gq_ref[...], wqkv_ref[rank, :, 0:TILE])
        grads_ref[rank, QKV:QKV + TILE, :] = tn(gq_ref[...], n1_ref[2 * words:, :]).astype(BF)
        grads_ref[rank, QKV + TILE:WORD_ROWS, :] = tn(gkv_ref[...], n1_ref[...]).astype(BF)
        return carry

    lax.fori_loop(0, RANKS, attend_back, 0)
    near_ref_low = got_ref.at[2]
    near_ref_low[...] = part_ref[...].astype(BF).reshape(2, words, wide)
    sends = []
    for slot, offset in ((0, RANKS - 2), (1, RANKS - 1)):
        sends.append(remote(got_ref.at[2, slot], got_ref.at[slot, 0], (send_sem.at[slot], recv_sem.at[slot]),
                            p.ring_device(offset)))
    for copy in sends:
        copy.start()
    for copy in sends:
        copy.wait()
    upstream1 = back_ref[...] + got_ref[0, 0].astype(F32) + got_ref[1, 0].astype(F32)
    dgain_ref[0:1, :] = jnp.sum(upstream1 * unit1, axis=0, keepdims=True)
    grad_vec = (grad_middle + norm_back(upstream1, gain1_ref[...], unit1, rate1)).astype(BF)
    dproj_ref[...] = tn(pooled_ref[...], grad_vec)
    gpl_ref[...] = nt(grad_vec, wproj_ref[...])


def word_layer(bits, vec, near, doc_ids, cotangent, wqkv, wout, wup, wdown, gain1, gain2, wproj, pooled):
    words, wide = vec.shape
    width = pooled.shape[1]
    window = 3 * words
    rank = lax.axis_index("tensor")
    padded = jnp.concatenate([jnp.full((2 * words,), -1, jnp.int32), doc_ids[0]])
    key_docs = lax.dynamic_slice_in_dim(padded, rank * words, window, 0)
    hidden = wup.shape[2]
    vm = pl.BlockSpec(memory_space=pltpu.VMEM)
    return pl.pallas_call(
        functools.partial(word_kernel, bits),
        in_specs=[vm] * 4 + [pl.BlockSpec(memory_space=pl.ANY)] + [vm] * 8,
        out_specs=[vm] * 5,
        out_shape=[
            jax.ShapeDtypeStruct((words, wide), BF),
            jax.ShapeDtypeStruct((words, width), F32),
            jax.ShapeDtypeStruct((width, wide), F32),
            jax.ShapeDtypeStruct((8, wide), F32),
            jax.ShapeDtypeStruct((RANKS, WORD_ROWS, wide), BF),
        ],
        scratch_shapes=[
            pltpu.VMEM((window, wide), BF),
            pltpu.VMEM((RANKS, words, TILE), BF),
            pltpu.VMEM((RANKS, window, 2 * TILE), BF),
            pltpu.VMEM((RANKS, 2 * words, window), BF),
            pltpu.VMEM((RANKS, words, TILE), BF),
            pltpu.VMEM((RANKS, words, hidden), BF),
            pltpu.VMEM((RANKS, words, hidden), BF),
            pltpu.VMEM((words, TILE), BF),
            pltpu.VMEM((words, TILE), BF),
            pltpu.VMEM((window, 2 * TILE), BF),
            pltpu.VMEM((words, wide), F32),
            pltpu.VMEM((words, wide), BF),
            pltpu.SemaphoreType.DMA,
            pltpu.VMEM((2 * words, wide), F32),
            pltpu.VMEM((3, 2, words, wide), BF),
            pltpu.SemaphoreType.DMA((2,)),
            pltpu.SemaphoreType.DMA((2,)),
        ],
        compiler_params=pltpu.CompilerParams(
            vmem_limit_bytes=62 << 20, collective_id=1, has_side_effects=True),
        name="word_layer",
    )(vec, near, key_docs[2 * words:, None], key_docs[None, :], cotangent, wqkv, wout, wup, wdown,
      gain1[None, :], gain2[None, :], wproj, pooled)


def char_backward_kernel(slots, x_ref, cnt_col_ref, inv_ref, gain1_ref, wqkv_ref, wout_ref, gain2_ref,
                         wup_ref, wdown_ref, gpl_ref, act_pool_ref, qkv_ref, probs_ref,
                         mixed_ref, first_ref, slope_ref,
                         dx_ref, dgain_ref, dqkv_ref, dout_ref, dup_ref, ddown_ref,
                         down_ref, gq_ref, gmix_ref, gup_ref, spread_ref):
    step = pl.program_id(0)
    rows, width = x_ref.shape
    words = rows // slots

    @pl.when(step == 0)
    def _():
        dgain_ref[...] = jnp.zeros_like(dgain_ref)
        dqkv_ref[...] = jnp.zeros_like(dqkv_ref)
        dout_ref[...] = jnp.zeros_like(dout_ref)
        dup_ref[...] = jnp.zeros_like(dup_ref)
        low = gpl_ref[...].astype(BF)
        ddown_ref[...] = tn(act_pool_ref[...], low)
        scaled = gpl_ref[...] * inv_ref[...]
        down_ref[:, width:] = nt(scaled.astype(BF), wdown_ref[...])
        down_ref[:, :width] = scaled

    for word in range(words):
        line = down_ref[pl.ds(step * words + word, 1), :width]
        spread_ref[word * slots:(word + 1) * slots, :] = jnp.broadcast_to(line, (slots, width))
        line = down_ref[pl.ds(step * words + word, 1), width:]
        at = slice(word * slots, (word + 1) * slots)
        gup_ref[at, :] = (jnp.broadcast_to(line, (slots, line.shape[1])) * slope_ref[at, :].astype(F32)).astype(BF)

    slot = jnp.bitwise_and(lax.broadcasted_iota(jnp.int32, (rows, 1), 0), slots - 1)
    valid_col = slot < cnt_col_ref[...]
    first = first_ref[...]
    unit2, rate2 = norm_parts(first)
    dup_ref[...] += tn((unit2 * gain2_ref[...]).astype(BF), gup_ref[...])
    upstream = nt(gup_ref[...], wup_ref[...])
    dgain_ref[1:2, :] += jnp.sum(upstream * unit2, axis=0, keepdims=True)
    grad_first = jnp.where(valid_col, spread_ref[...], 0.0) + norm_back(upstream, gain2_ref[...], unit2, rate2)
    spread_ref[...] = grad_first
    low = grad_first.astype(BF)
    dout_ref[...] += tn(mixed_ref[...], low)
    gmix_ref[...] = nt(low, wout_ref[...]).astype(BF)
    for tile in range(rows // TILE):
        at = pl.ds(tile * TILE, TILE)
        for pair in range(CHEADS // 2):
            c0 = pair * TILE
            queries = split_heads(qkv_ref[at, c0:c0 + TILE])
            keys = split_heads(qkv_ref[at, width + c0:width + c0 + TILE])
            values = qkv_ref[at, 2 * width + c0:2 * width + c0 + TILE]
            grads = split_heads(gmix_ref[at, c0:c0 + TILE])
            probs_low = probs_ref[tile, pair]
            probs = probs_low.astype(F32)
            grad_probs = compact(nt(values, grads), slots)
            inner = jnp.sum(probs * grad_probs, axis=0, keepdims=True)
            grad_scores = (probs * (grad_probs - inner) * (CHD ** -0.5)).astype(BF)
            wide_scores = expand(grad_scores, slots)
            wide_probs = expand(probs_low, slots)
            gq_ref[at, c0:c0 + TILE] = tn(stack_lanes(wide_scores), keys).astype(BF)
            gq_ref[at, width + c0:width + c0 + TILE] = nn(wide_scores, queries).astype(BF)
            gq_ref[at, 2 * width + c0:2 * width + c0 + TILE] = nn(wide_probs, grads).astype(BF)
    unit1, rate1 = norm_parts(x_ref[...].astype(F32))
    dqkv_ref[...] += tn((unit1 * gain1_ref[...]).astype(BF), gq_ref[...])
    upstream1 = nt(gq_ref[...], wqkv_ref[...])
    dgain_ref[0:1, :] += jnp.sum(upstream1 * unit1, axis=0, keepdims=True)
    dx_ref[...] = spread_ref[...] + norm_back(upstream1, gain1_ref[...], unit1, rate1)


def char_backward(x, counts, gain1, wqkv, wout, gain2, wup, wdown, grad_pooled, saved):
    qkv, probs, mixed, first, slope, act_pool = saved
    rows, width = x.shape
    words = counts.shape[0]
    slots = rows // words
    hidden = wup.shape[1]
    step = rows // CHAR_STEPS
    spread = jnp.repeat(counts, slots)
    row_block = lambda cols: pl.BlockSpec((step, cols), lambda i: (i, 0))
    whole = lambda shape: pl.BlockSpec(shape, lambda i: (0, 0))
    tiles = step // TILE
    return pl.pallas_call(
        functools.partial(char_backward_kernel, slots),
        grid=(rows // step,),
        in_specs=[
            row_block(width),
            row_block(1),
            whole((words, 1)),
            whole((1, width)),
            whole((width, 3 * width)),
            whole((width, width)),
            whole((1, width)),
            whole((width, hidden)),
            whole((hidden, width)),
            whole((words, width)),
            whole((words, hidden)),
            row_block(3 * width),
            pl.BlockSpec((tiles, CHEADS // 2, slots, 2 * TILE), lambda i: (i, 0, 0, 0)),
            row_block(width),
            row_block(width),
            row_block(hidden),
        ],
        out_specs=[
            row_block(width),
            whole((8, width)),
            whole((width, 3 * width)),
            whole((width, width)),
            whole((width, hidden)),
            whole((hidden, width)),
        ],
        out_shape=[
            jax.ShapeDtypeStruct((rows, width), F32),
            jax.ShapeDtypeStruct((8, width), F32),
            jax.ShapeDtypeStruct((width, 3 * width), F32),
            jax.ShapeDtypeStruct((width, width), F32),
            jax.ShapeDtypeStruct((width, hidden), F32),
            jax.ShapeDtypeStruct((hidden, width), F32),
        ],
        scratch_shapes=[
            pltpu.VMEM((words, width + hidden), F32),
            pltpu.VMEM((step, 3 * width), BF),
            pltpu.VMEM((step, width), BF),
            pltpu.VMEM((step, hidden), BF),
            pltpu.VMEM((step, width), F32),
        ],
        compiler_params=pltpu.CompilerParams(vmem_limit_bytes=60 << 20),
        name="char_backward",
    )(x, spread[:, None], (1.0 / counts.astype(F32))[:, None], gain1[None, :], wqkv, wout, gain2[None, :],
      wup, wdown, grad_pooled, act_pool, qkv, probs, mixed, first, slope)

CHAR_ROWS = 512


def reduce_kernel(bits, word_ref, dgain_ref, dqkv_ref, dout_ref, dup_ref, ddown_ref, dproj_ref, wgain_ref,
                  word_out, char_out, word_buf, char_buf, w1, w2, w3, w4, w5, c1, c2, c3, c4, c5, send_sem, recv_sem, own_sem):
    p = Place()
    meet(p.mates(bits) + [p.ring_device(offset) for offset in (1, 2, 3)])
    fetch = pltpu.make_async_copy(word_ref, word_buf, own_sem)
    fetch.start()
    width = dout_ref.shape[0]
    low = lambda value: value.astype(BF)
    char_buf[0, :, :] = low(jnp.concatenate([dup_ref[:, 0:2 * width], dup_ref[:, 2 * width:]], axis=0))
    char_buf[1, :, :] = low(jnp.concatenate([ddown_ref[0:2 * width, :], ddown_ref[2 * width:, :]], axis=1))
    char_buf[2, 0:width, :] = low(dproj_ref[...])
    char_buf[2, width:, :] = low(dqkv_ref[:, 0:2 * width])
    half = width // 2
    char_buf[3, 0:half, :] = low(jnp.concatenate([dout_ref[0:half, :], dout_ref[half:, :]], axis=1))
    value = dqkv_ref[:, 2 * width:]
    char_buf[3, half:width, :] = low(jnp.concatenate([value[0:half, :], value[half:, :]], axis=1))
    char_buf[3, width:, :] = jnp.zeros_like(char_buf[3, width:, :])
    gains = jnp.concatenate([wgain_ref[...], jnp.concatenate([dgain_ref[...], dgain_ref[...]], axis=1)], axis=0)
    char_buf[3, width:width + 16, :] = low(gains)
    fetch.wait()
    word = Reduce(p, bits, word_buf, word_out, w1, w2, w3, w4, w5, Sems(send_sem, recv_sem), False)
    char = Reduce(p, bits, char_buf, char_out, c1, c2, c3, c4, c5,
                  Sems(send_sem, recv_sem, reduce_copies(bits, False)), True)
    last = len(char.names)
    word.start(0)
    for index in range(last):
        char.start(index)
        if index < len(word.names):
            word.finish(index)
            if index + 1 < len(word.names):
                word.start(index + 1)
        char.finish(index)


def reduce_all(bits, word_grads, dgain, dqkv, dout, dup, ddown, dproj, wgain):
    wide = word_grads.shape[2]
    vm = pl.BlockSpec(memory_space=pltpu.VMEM)
    copies = reduce_copies(bits, False) + reduce_copies(bits, True)
    return pl.pallas_call(
        functools.partial(reduce_kernel, bits),
        in_specs=[pl.BlockSpec(memory_space=pl.ANY)] + [vm] * 7,
        out_specs=[vm, vm],
        out_shape=[
            jax.ShapeDtypeStruct(word_grads.shape[1:], BF),
            jax.ShapeDtypeStruct((RANKS, CHAR_ROWS, wide), BF),
        ],
        scratch_shapes=[pltpu.VMEM(word_grads.shape, BF), pltpu.VMEM((RANKS, CHAR_ROWS, wide), BF)]
        + reduce_scratch(bits, word_grads.shape[1], wide) + reduce_scratch(bits, CHAR_ROWS, wide)
        + [pltpu.SemaphoreType.DMA((copies,)), pltpu.SemaphoreType.DMA((copies,)), pltpu.SemaphoreType.DMA],
        compiler_params=pltpu.CompilerParams(
            vmem_limit_bytes=62 << 20, collective_id=2, has_side_effects=True),
        name="reduce_all",
    )(word_grads, dgain, dqkv, dout, dup, ddown, dproj, wgain)


def per_device(
    bits,
    char_inputs,
    char_counts,
    doc_ids,
    cotangent,
    char_norm_one,
    char_query,
    char_key,
    char_value,
    char_out,
    char_norm_two,
    char_up,
    char_down,
    char_proj,
    word_norm_one,
    word_query,
    word_key,
    word_value,
    word_out_proj,
    word_norm_two,
    word_up,
    word_down,
):
    char_qkv = jnp.concatenate([char_query, char_key, char_value], axis=1)
    word_qkv = jnp.concatenate([word_query, word_key, word_value], axis=1)
    vec, pooled, *saved, near, qkv_all, out_all, up_all, down_all = char_forward(
        char_inputs, char_counts, char_norm_one, char_qkv, char_out, char_norm_two, char_up, char_down, char_proj,
        word_qkv, word_out_proj, word_up, word_down,
    )
    word_output, grad_pooled, grad_proj, word_gains, word_grads = word_layer(
        bits, vec, near, doc_ids, cotangent, qkv_all, out_all, up_all, down_all,
        word_norm_one, word_norm_two, char_proj, pooled,
    )
    char_input_gradient, char_gains, char_dqkv, char_dout, char_dup, char_ddown = char_backward(
        char_inputs, char_counts, char_norm_one, char_qkv, char_out, char_norm_two, char_up, char_down,
        grad_pooled, saved,
    )
    word_sum, char_sum = reduce_all(
        bits, word_grads, char_gains, char_dqkv, char_dout, char_dup, char_ddown, grad_proj, word_gains
    )
    word_sum = word_sum.astype(F32)
    char_sum = char_sum.astype(F32)
    width = char_out.shape[0]
    half = width // 2
    join = lambda rows: jnp.concatenate([rows[:, :width], rows[:, width:]], axis=0)
    gains = char_sum[3, width:]
    return (
        word_output,
        char_input_gradient,
        gains[8, :width],
        char_sum[2, width:, :width],
        char_sum[2, width:, width:],
        join(char_sum[3, half:width]),
        join(char_sum[3, :half]),
        gains[9, :width],
        jnp.concatenate([char_sum[0, :width], char_sum[0, width:]], axis=1),
        join(char_sum[1]),
        char_sum[2, :width],
        gains[0],
        word_sum[QKV:QKV + TILE].T,
        word_sum[QKV + TILE:QKV + 2 * TILE].T,
        word_sum[QKV + 2 * TILE:].T,
        word_sum[OUT:QKV],
        gains[1],
        word_sum[UP:DOWN],
        word_sum[DOWN:OUT],
    )


def solution(mesh):
    in_specs = (
        P(("dp", "tensor"), None),
        P(("dp", "tensor")),
        P("dp", None),
        P("dp", None),
        P(),
        P(),
        P(),
        P(),
        P(),
        P(),
        P(),
        P(),
        P(),
        P(),
        P(None, "tensor"),
        P(None, "tensor"),
        P(None, "tensor"),
        P("tensor", None),
        P(),
        P(None, "tensor"),
        P("tensor", None),
    )
    out_specs = (
        P(("dp", "tensor"), None),
        P(("dp", "tensor"), None),
        P(),
        P(),
        P(),
        P(),
        P(),
        P(),
        P(),
        P(),
        P(),
        P(),
        P(None, "tensor"),
        P(None, "tensor"),
        P(None, "tensor"),
        P("tensor", None),
        P(),
        P(None, "tensor"),
        P("tensor", None),
    )
    assert mesh.shape["tensor"] == RANKS
    bits = mesh.shape["dp"].bit_length() - 1
    assert bits >= 3 and mesh.shape["dp"] == 1 << bits
    return jax.shard_map(
        functools.partial(per_device, bits), mesh=mesh, in_specs=in_specs, out_specs=out_specs, check_vma=False
    )
```

```python
import functools

import jax
import jax.numpy as jnp
from jax import lax
from jax.experimental import pallas as pl
from jax.experimental.pallas import tpu as pltpu
from jax.sharding import PartitionSpec as P

BF = jnp.bfloat16
F32 = jnp.float32
EPSILON = 1e-05
NEG_LARGE = -1e30
RANKS = 4
CHEADS = 4
CHD = 64
TILE = 128
CHAR_STEPS = 8
GELU_C = 0.7978845608028654
GELU_A = 0.044715


def nn(left, right):
    return lax.dot_general(left, right, (((1,), (0,)), ((), ())), preferred_element_type=F32)


def nt(left, right):
    return lax.dot_general(left, right, (((1,), (1,)), ((), ())), preferred_element_type=F32)


def tn(left, right):
    return lax.dot_general(left, right, (((0,), (0,)), ((), ())), preferred_element_type=F32)


def norm_parts(values):
    centre = values - jnp.mean(values, axis=-1, keepdims=True)
    spread = jnp.mean(centre * centre, axis=-1, keepdims=True)
    rate = lax.rsqrt(spread + EPSILON)
    return centre * rate, rate


def norm_back(upstream, gain, unit, rate):
    scaled = upstream * gain
    first = jnp.mean(scaled, axis=-1, keepdims=True)
    second = jnp.mean(scaled * unit, axis=-1, keepdims=True)
    return rate * (scaled - first - unit * second)


def gelu_parts(values):
    square = values * values
    inner = values * (GELU_C + (GELU_C * GELU_A) * square)
    half = 0.5 + 0.5 * jnp.tanh(inner)
    active = values * half
    slope = half + (active * (1.0 - half)) * (2.0 * GELU_C + (6.0 * GELU_C * GELU_A) * square)
    return active, slope


def split_heads(pair):
    low_half = lax.broadcasted_iota(jnp.int32, pair.shape, 1) < CHD
    zero = jnp.zeros_like(pair)
    return jnp.concatenate([jnp.where(low_half, pair, zero), jnp.where(low_half, zero, pair)], axis=0)


def word_of_lane(shape, slots):
    lane = lax.broadcasted_iota(jnp.int32, shape, 1)
    return jnp.bitwise_and(lane, TILE - 1) // slots


def compact(scores, slots):
    words = word_of_lane((slots, scores.shape[1]), slots)
    result = scores[0:slots]
    for word in range(1, TILE // slots):
        result = jnp.where(words == word, scores[word * slots:(word + 1) * slots], result)
    return result


def expand(packed, slots):
    words = word_of_lane(packed.shape, slots)
    zero = jnp.zeros_like(packed)
    return jnp.concatenate(
        [jnp.where(words == word, packed, zero) for word in range(TILE // slots)], axis=0
    )


def stack_lanes(pair):
    return jnp.concatenate([pair[:, :TILE], pair[:, TILE:]], axis=0)


def pool_matrix(rows, slots, counts_col):
    words = rows // slots
    row = lax.broadcasted_iota(jnp.int32, (rows, words), 0)
    word = lax.broadcasted_iota(jnp.int32, (rows, words), 1)
    mine = (row // slots == word) & (jnp.bitwise_and(row, slots - 1) < counts_col)
    return jnp.where(mine, 1.0 / counts_col.astype(F32), 0.0)


MESH = pl.DeviceIdType.MESH
LANE_SPLIT = 256


class Place:
    def __init__(self):
        self.dp = lax.axis_index("dp")
        self.rank = lax.axis_index("tensor")
        self.core = lax.rem(self.dp, 2)
        self.x = lax.rem(self.dp // 2, 2)
        self.y = lax.rem(self.dp // 4, 2)
        self.core_mate = (self.dp + 1 - 2 * self.core, self.rank)
        self.x_mate = (self.dp + 2 - 4 * self.x, self.rank)
        self.y_mate = (self.dp + 4 - 8 * self.y, self.rank)

    def ring(self, offset):
        return lax.rem(self.rank + offset, RANKS)

    def ring_device(self, offset):
        return (self.dp, self.ring(offset))

    def bit_mate(self, bit):
        size = 1 << bit
        mine = lax.rem(self.dp // size, 2)
        return (self.dp + size - 2 * size * mine, self.rank)

    def mates(self, bits):
        extra = [self.bit_mate(bit) for bit in range(3, bits)]
        return [self.core_mate, self.x_mate, self.y_mate] + extra


def meet(devices):
    barrier = pltpu.get_barrier_semaphore()
    for device in devices:
        pl.semaphore_signal(barrier, inc=1, device_id=device, device_id_type=MESH)
    pl.semaphore_wait(barrier, len(devices))


def remote(source, target, sems, device):
    return pltpu.make_async_remote_copy(
        src_ref=source, dst_ref=target, send_sem=sems[0], recv_sem=sems[1],
        device_id=device, device_id_type=MESH,
    )


class Sems:
    def __init__(self, send, recv, start=0):
        self.send, self.recv, self.next = send, recv, start

    def take(self):
        at = self.next
        self.next += 1
        return self.send.at[at], self.recv.at[at]


def rows_at(start, size):
    return pl.ds(pl.multiple_of(start, 16), size)


def halves(width):
    return (slice(0, LANE_SPLIT), slice(LANE_SPLIT, width))


class Gather:
    def __init__(self, place, local, whole, sems):
        self.stages = [[], [], [], []]
        rows = local.shape[0]
        unit = rows // 8
        p = place
        left, right = halves(local.shape[1])
        left_at = p.core * 4 + p.x * 2 + p.y
        right_at = p.core * 4 + p.y * 2 + p.x
        for offset in range(1, RANKS):
            for lanes, at in ((left, left_at), (right, right_at)):
                at = rows_at(at * unit, unit)
                self.stages[0].append(remote(
                    local.at[at, lanes], whole.at[p.rank, at, lanes], sems.take(), p.ring_device(offset)))
        for offset in range(1, RANKS):
            rank = p.ring(offset)
            for lanes, at, first, second, mate_first, mate_second in (
                (left, left_at, p.x, None, p.y_mate, p.x_mate),
                (right, right_at, p.y, None, p.x_mate, p.y_mate),
            ):
                one = rows_at(at * unit, unit)
                two = rows_at((p.core * 4 + first * 2) * unit, 2 * unit)
                self.stages[1].append(remote(
                    whole.at[rank, one, lanes], whole.at[rank, one, lanes], sems.take(), mate_first))
                self.stages[2].append(remote(
                    whole.at[rank, two, lanes], whole.at[rank, two, lanes], sems.take(), mate_second))
            four = rows_at(p.core * 4 * unit, 4 * unit)
            self.stages[3].append(remote(
                whole.at[rank, four], whole.at[rank, four], sems.take(), p.core_mate))

    def start(self, stage):
        for copy in self.stages[stage]:
            copy.start()

    def wait(self, stage):
        for copy in self.stages[stage]:
            copy.wait()


def gather_copies():
    return 2 * (RANKS - 1) * 3 + (RANKS - 1)


class Chain:
    def __init__(self, place, bits, src, refs, sems, everywhere):
        p = place
        buf, got_core, got_one, got_two, got_more, got_rank, out = refs
        self.p, self.src, self.everywhere = p, src, everywhere
        self.buf, self.got_core, self.got_one, self.got_two = buf, got_core, got_one, got_two
        self.got_more, self.got_rank = got_more, got_rank
        self.mine = out.at[p.rank] if everywhere else out
        unit = src.shape[1] // 8
        lanes = left, right = halves(src.shape[2])
        self.lanes = lanes
        self.own = rows_at(p.core * 4 * unit, 4 * unit)
        stages = [("core", [remote(src.at[:, rows_at((1 - p.core) * 4 * unit, 4 * unit)], got_core,
                                   sems.take(), p.core_mate)])]
        first, second = (p.x, p.y), (p.y, p.x)
        first_mate, second_mate = (p.x_mate, p.y_mate), (p.y_mate, p.x_mate)
        one = lambda side, at: rows_at(at * 2 * unit, 2 * unit)
        two = lambda side, at: rows_at((first[side] * 2 + at) * unit, unit)
        self.one_rows = [one(side, first[side]) for side in (0, 1)]
        self.two_rows = [two(side, second[side]) for side in (0, 1)]
        stages.append(("one", [
            remote(buf.at[:, one(side, 1 - first[side]), lanes[side]], got_one.at[:, :, lanes[side]],
                   sems.take(), first_mate[side]) for side in (0, 1)]))
        stages.append(("two", [
            remote(buf.at[:, two(side, 1 - second[side]), lanes[side]], got_two.at[:, :, lanes[side]],
                   sems.take(), second_mate[side]) for side in (0, 1)]))
        for bit in range(3, bits):
            stages.append((bit - 3, [
                remote(buf.at[:, self.two_rows[side], lanes[side]], got_more.at[bit - 3, :, :, lanes[side]],
                       sems.take(), p.bit_mate(bit)) for side in (0, 1)]))
        stages.append(("rank", [
            remote(buf.at[p.ring(offset), self.two_rows[side], lanes[side]],
                   got_rank.at[offset - 1, :, lanes[side]], sems.take(), p.ring_device(offset))
            for offset in range(1, RANKS) for side in (0, 1)]))
        base = p.core * 4 * unit
        self.out_two = [rows_at(base + (first[side] * 2 + second[side]) * unit, unit) for side in (0, 1)]
        out_one = [rows_at(base + first[side] * 2 * unit, 2 * unit) for side in (0, 1)]
        if everywhere:
            stages.append(("rank_back", [
                remote(out.at[p.rank, self.out_two[side], lanes[side]], out.at[p.rank, self.out_two[side], lanes[side]],
                       sems.take(), p.ring_device(offset))
                for offset in range(1, RANKS) for side in (0, 1)]))

        def back(at, part_lanes, mate):
            part = out.at[:, at, part_lanes] if everywhere else out.at[at, part_lanes]
            return remote(part, part, sems.take(), mate)

        stages.append(("back_two", [back(self.out_two[side], lanes[side], second_mate[side]) for side in (0, 1)]))
        stages.append(("back_one", [back(out_one[side], lanes[side], first_mate[side]) for side in (0, 1)]))
        stages.append(("back_core", [back(self.own, slice(None), p.core_mate)]))
        self.stages = stages

    def fetch(self, sem):
        return pltpu.make_async_copy(self.src.at[:, self.own], self.buf, sem)

    def start(self, index):
        for copy in self.stages[index][1]:
            copy.start()

    def finish(self, index):
        name, copies = self.stages[index]
        for copy in copies:
            copy.wait()
        buf = self.buf
        if name == "core":
            own = self.src if self.everywhere else None
            for quarter in range(RANKS):
                mine = own[quarter, self.own, :] if self.everywhere else buf[quarter]
                buf[quarter] = mine + self.got_core[quarter]
        elif name == "one":
            for at, lanes in zip(self.one_rows, self.lanes):
                for quarter in range(RANKS):
                    buf[quarter, at, lanes] += self.got_one[quarter, :, lanes]
        elif name == "two":
            for at, lanes in zip(self.two_rows, self.lanes):
                for quarter in range(RANKS):
                    buf[quarter, at, lanes] += self.got_two[quarter, :, lanes]
        elif name == "rank":
            for side in (0, 1):
                at, lanes = self.two_rows[side], self.lanes[side]
                total = buf[self.p.rank, at, lanes].astype(F32)
                for k in range(RANKS - 1):
                    total = total + self.got_rank[k, :, lanes].astype(F32)
                self.mine[self.out_two[side], lanes] = total.astype(BF)
        elif isinstance(name, int):
            for at, lanes in zip(self.two_rows, self.lanes):
                for quarter in range(RANKS):
                    buf[quarter, at, lanes] += self.got_more[name, quarter, :, lanes]

    def step(self, index):
        if index:
            self.finish(index - 1)
        if index < len(self.stages):
            self.start(index)


def chain_copies(bits, everywhere):
    pairs = 2 * (RANKS - 1)
    return 1 + 2 + 2 + 2 * (bits - 3) + pairs + (pairs if everywhere else 0) + 2 + 2 + 1


def chain_scratch(bits, rows, lanes):
    unit = rows // 8
    return [
        pltpu.VMEM((RANKS, 4 * unit, lanes), BF),
        pltpu.VMEM((RANKS, 4 * unit, lanes), BF),
        pltpu.VMEM((RANKS, 2 * unit, lanes), BF),
        pltpu.VMEM((RANKS, unit, lanes), BF),
        pltpu.VMEM((max(bits - 3, 1), RANKS, unit, lanes), BF),
        pltpu.VMEM((RANKS - 1, unit, lanes), BF),
    ]


def char_forward_kernel(slots, x_ref, cnt_lane_ref, cnt_col_ref, gain1_ref, wqkv_ref, wout_ref,
                        gain2_ref, wup_ref, wdown_ref, wproj_ref,
                        lqkv_ref, lout_ref, lup_ref, ldown_ref,
                        vec_ref, pooled_ref, qkv_ref, probs_ref, mixed_ref, first_ref,
                        slope_ref, act_pool_ref, near_ref, wqkv_all, wout_all, wup_all, wdown_all,
                        own_sem, send_sem, recv_sem):
    rows = x_ref.shape[0]
    width = x_ref.shape[1]
    step = pl.program_id(0)
    steps = pl.num_programs(0)
    words = rows // slots
    p = Place()
    pairs = ((lqkv_ref, wqkv_all), (lout_ref, wout_all), (lup_ref, wup_all), (ldown_ref, wdown_all))
    gathers = [Gather(p, mine, whole, Sems(send_sem, recv_sem, gather_copies() * index))
               for index, (mine, whole) in enumerate(pairs)]
    own_copies = [pltpu.make_async_copy(mine, whole.at[p.rank], own_sem.at[index])
                  for index, (mine, whole) in enumerate(pairs)]
    vec_base = gather_copies() * len(pairs)

    def vec_copies(at):
        copies = []
        for slot, offset in ((1, 1), (0, 2)):
            sem = vec_base + 2 * at + slot
            part = rows_at(at * words, words)
            copies.append(remote(vec_ref.at[part], near_ref.at[slot, part],
                                 (send_sem.at[sem], recv_sem.at[sem]), p.ring_device(offset)))
        return copies

    @pl.when(step == 0)
    def _():
        meet([p.ring_device(offset) for offset in (1, 2, 3)] + [p.core_mate, p.x_mate, p.y_mate])
        for copy in own_copies:
            copy.start()

    plan = {at: [] for at in range(CHAR_STEPS)}
    for group, (members, begin) in enumerate((((0, 1), (0, 2, 3, 4)), ((2,), (0, 3, 4, 5)), ((3,), (0, 4, 5, 6)))):
        for stage in range(4):
            for member in members:
                plan[begin[stage]].append((member, stage))
    for at, todo in plan.items():
        if todo:
            @pl.when(step == at)
            def _(todo=todo):
                for member, stage in todo:
                    if stage:
                        gathers[member].wait(stage - 1)
                    gathers[member].start(stage)

    @pl.when(step > 0)
    def _():
        for copy in vec_copies(step - 1):
            copy.start()

    base = x_ref[...].astype(F32)
    unit, _ = norm_parts(base)
    normed = (unit * gain1_ref[...]).astype(BF)
    qkv_ref[...] = nn(normed, wqkv_ref[...]).astype(BF)
    for tile in range(rows // TILE):
        at = pl.ds(tile * TILE, TILE)
        valid = (lax.broadcasted_iota(jnp.int32, (slots, TILE), 0)
                 < cnt_lane_ref[:, tile * TILE:(tile + 1) * TILE])
        for pair in range(CHEADS // 2):
            c0 = pair * TILE
            queries = split_heads(qkv_ref[at, c0:c0 + TILE])
            keys = qkv_ref[at, width + c0:width + c0 + TILE]
            values = split_heads(qkv_ref[at, 2 * width + c0:2 * width + c0 + TILE])
            scores = compact(nt(keys, queries), slots)
            parts = []
            for head in range(2):
                own = jnp.where(valid, scores[:, head * TILE:(head + 1) * TILE], NEG_LARGE)
                top = jnp.max(own, axis=0, keepdims=True)
                weight = jnp.exp((own - top) * (CHD ** -0.5))
                parts.append(weight / jnp.sum(weight, axis=0, keepdims=True))
            probs = jnp.concatenate(parts, axis=1).astype(BF)
            probs_ref[tile, pair] = probs
            mixed_ref[at, c0:c0 + TILE] = tn(stack_lanes(expand(probs, slots)), values).astype(BF)
    first = base + nn(mixed_ref[...], wout_ref[...])
    first_ref[...] = first
    unit2, _ = norm_parts(first)
    normed2 = (unit2 * gain2_ref[...]).astype(BF)
    counts_col = cnt_col_ref[...]
    slot = jnp.bitwise_and(lax.broadcasted_iota(jnp.int32, (rows, 1), 0), slots - 1)
    valid_col = slot < counts_col
    pool = pool_matrix(rows, slots, counts_col).astype(BF)
    chunk = 256
    for part in range(wup_ref.shape[1] // chunk):
        cols = slice(part * chunk, (part + 1) * chunk)
        active, slope = gelu_parts(nn(normed2, wup_ref[:, cols]))
        slope_ref[:, cols] = jnp.where(valid_col, slope, 0.0).astype(BF)
        act_pool_ref[:, cols] = tn(pool, active.astype(BF)).astype(BF)
    pooled = tn(pool, first.astype(BF)) + nn(act_pool_ref[...], wdown_ref[...])
    pooled = pooled.astype(BF)
    pooled_ref[...] = pooled
    vec_ref[rows_at(step * words, words), :] = nn(pooled, wproj_ref[...]).astype(BF)

    @pl.when(step == steps - 1)
    def _():
        for copy in vec_copies(step):
            copy.start()
        for copy in own_copies:
            copy.wait()
        for gather in gathers:
            gather.wait(3)
        for at in range(CHAR_STEPS):
            for copy in vec_copies(at):
                copy.wait()


def char_forward(x, counts, gain1, wqkv, wout, gain2, wup, wdown, wproj, lqkv, lout, lup, ldown):
    rows, width = x.shape
    words = counts.shape[0]
    slots = rows // words
    hidden = wup.shape[1]
    wide = wproj.shape[1]
    step = rows // CHAR_STEPS
    step_words = step // slots
    spread = jnp.repeat(counts, slots)
    row_block = lambda cols: pl.BlockSpec((step, cols), lambda i: (i, 0))
    word_block = lambda cols: pl.BlockSpec((step_words, cols), lambda i: (i, 0))
    whole = lambda shape: pl.BlockSpec(shape, lambda i: (0, 0))
    tiles = step // TILE
    return pl.pallas_call(
        functools.partial(char_forward_kernel, slots),
        grid=(rows // step,),
        in_specs=[
            row_block(width),
            pl.BlockSpec((1, step), lambda i: (0, i)),
            row_block(1),
            whole((1, width)),
            whole((width, 3 * width)),
            whole((width, width)),
            whole((1, width)),
            whole((width, hidden)),
            whole((hidden, width)),
            whole((width, wide)),
            whole(lqkv.shape),
            whole(lout.shape),
            whole(lup.shape),
            whole(ldown.shape),
        ],
        out_specs=[
            whole((words, wide)),
            word_block(width),
            row_block(3 * width),
            pl.BlockSpec((tiles, CHEADS // 2, slots, 2 * TILE), lambda i: (i, 0, 0, 0)),
            row_block(width),
            row_block(width),
            row_block(hidden),
            word_block(hidden),
        ] + [pl.BlockSpec(memory_space=pl.ANY)] * 5,
        out_shape=[
            jax.ShapeDtypeStruct((words, wide), BF),
            jax.ShapeDtypeStruct((words, width), BF),
            jax.ShapeDtypeStruct((rows, 3 * width), BF),
            jax.ShapeDtypeStruct((rows // TILE, CHEADS // 2, slots, 2 * TILE), BF),
            jax.ShapeDtypeStruct((rows, width), BF),
            jax.ShapeDtypeStruct((rows, width), F32),
            jax.ShapeDtypeStruct((rows, hidden), BF),
            jax.ShapeDtypeStruct((words, hidden), BF),
            jax.ShapeDtypeStruct((2, words, wide), BF),
            jax.ShapeDtypeStruct((RANKS,) + lqkv.shape, BF),
            jax.ShapeDtypeStruct((RANKS,) + lout.shape, BF),
            jax.ShapeDtypeStruct((RANKS,) + lup.shape, BF),
            jax.ShapeDtypeStruct((RANKS,) + ldown.shape, BF),
        ],
        scratch_shapes=[
            pltpu.SemaphoreType.DMA((4,)),
            pltpu.SemaphoreType.DMA((gather_copies() * 4 + 2 * CHAR_STEPS,)),
            pltpu.SemaphoreType.DMA((gather_copies() * 4 + 2 * CHAR_STEPS,)),
        ],
        compiler_params=pltpu.CompilerParams(
            vmem_limit_bytes=60 << 20, collective_id=0, has_side_effects=True),
        name="char_forward",
    )(x, spread[None, :], spread[:, None], gain1[None, :], wqkv, wout, gain2[None, :], wup, wdown, wproj,
      lqkv, lout, lup, ldown)


def word_kernel(bits, vec_ref, near_ref, row_docs_ref, key_docs_ref, cot_ref, wqkv_ref, wout_ref, wup_ref,
                wdown_ref, gain1_ref, gain2_ref, wproj_ref, pooled_ref,
                out_ref, gpl_ref, dproj_ref, dgain_ref, up_grad_ref, down_grad_ref, mix_grad_ref,
                n1_ref, q_ref, kv_ref, probs_ref, o_ref, act_ref, slope_ref, go_ref, gq_ref, gkv_ref,
                back_ref, cot_own, cot_sem, part_ref, got_ref, send_sem, recv_sem):
    p = Place()
    words, wide = vec_ref.shape
    window = 3 * words
    fetch = pltpu.make_async_copy(cot_ref.at[rows_at(p.rank * words, words)], cot_own, cot_sem)
    fetch.start()
    meet([p.ring_device(offset) for offset in (1, 2, 3)])

    own = vec_ref[...].astype(F32)
    unit1, rate1 = norm_parts(own)
    n1_ref[2 * words:, :] = (unit1 * gain1_ref[...]).astype(BF)
    for slot in range(2):
        unit, _ = norm_parts(near_ref[slot].astype(F32))
        n1_ref[slot * words:(slot + 1) * words, :] = (unit * gain1_ref[...]).astype(BF)

    def project(rank, carry):
        q_ref[rank] = nn(n1_ref[2 * words:, :], wqkv_ref[rank, :, 0:TILE]).astype(BF)
        kv_ref[rank] = nn(n1_ref[...], wqkv_ref[rank, :, TILE:]).astype(BF)
        scores = nt(split_heads(q_ref[rank]), kv_ref[rank, :, 0:TILE]) * (CHD ** -0.5)
        row = lax.broadcasted_iota(jnp.int32, (words, window), 0)
        key = lax.broadcasted_iota(jnp.int32, (words, window), 1)
        allowed = (row_docs_ref[...] == key_docs_ref[...]) & (key <= row + 2 * words)
        for head in range(2):
            at = slice(head * words, (head + 1) * words)
            masked = jnp.where(allowed, scores[at], NEG_LARGE)
            top = jnp.max(masked, axis=-1, keepdims=True)
            weight = jnp.exp(masked - top)
            probs_ref[rank, at, :] = (weight * (1.0 / jnp.sum(weight, axis=-1, keepdims=True))).astype(BF)
        pair = jnp.concatenate([probs_ref[rank, 0:words, :], probs_ref[rank, words:, :]], axis=1)
        o_ref[rank] = nn(pair, split_heads(kv_ref[rank, :, TILE:])).astype(BF)
        back_ref[...] += nn(o_ref[rank], wout_ref[rank])
        return carry

    back_ref[...] = own
    lax.fori_loop(0, RANKS, project, 0)
    middle = back_ref[...]
    unit2, rate2 = norm_parts(middle)
    normed2 = (unit2 * gain2_ref[...]).astype(BF)

    def feed(rank, carry):
        active, slope = gelu_parts(nn(normed2, wup_ref[rank]))
        act_ref[rank] = active.astype(BF)
        slope_ref[rank] = slope.astype(BF)
        back_ref[...] += nn(act_ref[rank], wdown_ref[rank])
        return carry

    lax.fori_loop(0, RANKS, feed, 0)
    out_ref[...] = back_ref[...].astype(BF)
    fetch.wait()
    back_ref[...] = jnp.zeros_like(back_ref)

    def feed_back(rank, carry):
        upstream = (nt(cot_own[...], wdown_ref[rank]) * slope_ref[rank].astype(F32)).astype(BF)
        back_ref[...] += nt(upstream, wup_ref[rank])
        up_grad_ref[rank] = tn(normed2, upstream).astype(BF)
        down_grad_ref[rank] = tn(act_ref[rank], cot_own[...]).astype(BF)
        return carry

    lax.fori_loop(0, RANKS, feed_back, 0)
    upstream2 = back_ref[...]
    dgain_ref[...] = jnp.zeros_like(dgain_ref)
    dgain_ref[1:2, :] = jnp.sum(upstream2 * unit2, axis=0, keepdims=True)
    grad_middle = cot_own[...].astype(F32) + norm_back(upstream2, gain2_ref[...], unit2, rate2)
    middle_low = grad_middle.astype(BF)

    back_ref[...] = jnp.zeros_like(back_ref)
    part_ref[...] = jnp.zeros_like(part_ref)

    def attend_back(rank, carry):
        go_ref[...] = nt(middle_low, wout_ref[rank]).astype(BF)
        mix_grad_ref[rank, :, 3 * TILE:] = tn(middle_low, o_ref[rank]).astype(BF)
        go_pair = split_heads(go_ref[...])
        grad_probs = nt(go_pair, kv_ref[rank, :, TILE:])
        probs = probs_ref[rank].astype(F32)
        inner = jnp.sum(probs * grad_probs, axis=-1, keepdims=True)
        grad_scores = (probs * (grad_probs - inner) * (CHD ** -0.5)).astype(BF)
        q_pair = split_heads(q_ref[rank])
        gkv_ref[:, 0:TILE] = tn(grad_scores, q_pair).astype(BF)
        gkv_ref[:, TILE:] = tn(probs_ref[rank], go_pair).astype(BF)
        pair = jnp.concatenate([grad_scores[0:words], grad_scores[words:]], axis=1)
        gq_ref[...] = nn(pair, split_heads(kv_ref[rank, :, 0:TILE])).astype(BF)
        part_ref[...] += nt(gkv_ref[0:2 * words, :], wqkv_ref[rank, :, TILE:])
        back_ref[...] += nt(gkv_ref[2 * words:, :], wqkv_ref[rank, :, TILE:])
        back_ref[...] += nt(gq_ref[...], wqkv_ref[rank, :, 0:TILE])
        mix_grad_ref[rank, :, 0:TILE] = tn(n1_ref[2 * words:, :], gq_ref[...]).astype(BF)
        mix_grad_ref[rank, :, TILE:3 * TILE] = tn(n1_ref[...], gkv_ref[...]).astype(BF)
        return carry

    lax.fori_loop(0, RANKS, attend_back, 0)
    near_ref_low = got_ref.at[2]
    near_ref_low[...] = part_ref[...].astype(BF).reshape(2, words, wide)
    sends = []
    for slot, offset in ((0, RANKS - 2), (1, RANKS - 1)):
        sends.append(remote(got_ref.at[2, slot], got_ref.at[slot, 0], (send_sem.at[slot], recv_sem.at[slot]),
                            p.ring_device(offset)))
    for copy in sends:
        copy.start()
    for copy in sends:
        copy.wait()
    upstream1 = back_ref[...] + got_ref[0, 0].astype(F32) + got_ref[1, 0].astype(F32)
    dgain_ref[0:1, :] = jnp.sum(upstream1 * unit1, axis=0, keepdims=True)
    grad_vec = (grad_middle + norm_back(upstream1, gain1_ref[...], unit1, rate1)).astype(BF)
    dproj_ref[...] = tn(pooled_ref[...], grad_vec).astype(BF)
    gpl_ref[...] = nt(grad_vec, wproj_ref[...])


def word_layer(bits, vec, near, doc_ids, cotangent, wqkv, wout, wup, wdown, gain1, gain2, wproj, pooled):
    words, wide = vec.shape
    width = pooled.shape[1]
    window = 3 * words
    rank = lax.axis_index("tensor")
    padded = jnp.concatenate([jnp.full((2 * words,), -1, jnp.int32), doc_ids[0]])
    key_docs = lax.dynamic_slice_in_dim(padded, rank * words, window, 0)
    hidden = wup.shape[2]
    vm = pl.BlockSpec(memory_space=pltpu.VMEM)
    return pl.pallas_call(
        functools.partial(word_kernel, bits),
        in_specs=[vm] * 4 + [pl.BlockSpec(memory_space=pl.ANY)] + [vm] * 8,
        out_specs=[vm] * 7,
        out_shape=[
            jax.ShapeDtypeStruct((words, wide), BF),
            jax.ShapeDtypeStruct((words, width), F32),
            jax.ShapeDtypeStruct((width, wide), BF),
            jax.ShapeDtypeStruct((8, wide), F32),
        ] + [
            jax.ShapeDtypeStruct((RANKS, wide, wide), BF) for _ in range(3)
        ],
        scratch_shapes=[
            pltpu.VMEM((window, wide), BF),
            pltpu.VMEM((RANKS, words, TILE), BF),
            pltpu.VMEM((RANKS, window, 2 * TILE), BF),
            pltpu.VMEM((RANKS, 2 * words, window), BF),
            pltpu.VMEM((RANKS, words, TILE), BF),
            pltpu.VMEM((RANKS, words, hidden), BF),
            pltpu.VMEM((RANKS, words, hidden), BF),
            pltpu.VMEM((words, TILE), BF),
            pltpu.VMEM((words, TILE), BF),
            pltpu.VMEM((window, 2 * TILE), BF),
            pltpu.VMEM((words, wide), F32),
            pltpu.VMEM((words, wide), BF),
            pltpu.SemaphoreType.DMA,
            pltpu.VMEM((2 * words, wide), F32),
            pltpu.VMEM((3, 2, words, wide), BF),
            pltpu.SemaphoreType.DMA((2,)),
            pltpu.SemaphoreType.DMA((2,)),
        ],
        compiler_params=pltpu.CompilerParams(
            vmem_limit_bytes=62 << 20, collective_id=1, has_side_effects=True),
        name="word_layer",
    )(vec, near, key_docs[2 * words:, None], key_docs[None, :], cotangent, wqkv, wout, wup, wdown,
      gain1[None, :], gain2[None, :], wproj, pooled)


CHAINS = 6
PLAN = (
    (0, 2, 5, 7, 9, 10, 11),
    (0, 4, 7, 9, 11, 12, 13),
    (1, 6, 9, 11, 13, 14, 15),
    (1, 3, 6, 8, 10, 12, 13, 14),
    (8, 10, 12, 14, 15),
)


def char_backward_kernel(slots, bits, x_ref, cnt_col_ref, inv_ref, gain1_ref, wqkv_ref, wout_ref, gain2_ref,
                         wup_ref, wdown_ref, gpl_ref, act_pool_ref, dproj_ref, wgain_ref, qkv_ref, probs_ref,
                         mixed_ref, first_ref, slope_ref, up_grad_ref, down_grad_ref, mix_grad_ref,
                         dx_ref, up_out, down_out, mix_out, early_out, mid_out, late_out,
                         down_ref, gq_ref, gmix_ref, gup_ref, spread_ref, dgain_ref, dqkv_ref, dout_ref, dup_ref,
                         early_ref, mid_ref, late_ref, *rest):
    step = pl.program_id(0)
    steps = pl.num_programs(0)
    half_steps = CHAR_STEPS
    rows, width = x_ref.shape
    words = rows // slots
    p = Place()
    send_sem, recv_sem, own_sem = rest[-3:]
    sources = (up_grad_ref, down_grad_ref, mix_grad_ref, early_ref, mid_ref, late_ref)
    results = (up_out, down_out, mix_out, early_out, mid_out, late_out)
    outs = rest[6 * CHAINS:7 * CHAINS]
    leave = [pltpu.make_async_copy(out, result, own_sem.at[CHAINS + index])
             for index, (out, result) in enumerate(zip(outs, results))]
    word_chains = 3
    chains, first_sem = [], 0
    for index in range(CHAINS):
        everywhere = index >= word_chains
        refs = tuple(rest[6 * index:6 * index + 6]) + (outs[index],)
        chains.append(Chain(p, bits, sources[index], refs, Sems(send_sem, recv_sem, first_sem), everywhere))
        first_sem += chain_copies(bits, everywhere)

    @pl.when(step == 0)
    def _():
        meet(p.mates(bits) + [p.ring_device(offset) for offset in (1, 2, 3)])
        for index in range(word_chains):
            chains[index].fetch(own_sem.at[index]).start()

    for at in range(2 * half_steps):
        todo = [(index, stages.index(at)) for index, stages in enumerate(PLAN) if at in stages]
        if todo:
            @pl.when(step == at)
            def _(todo=todo):
                for index, stage in todo:
                    if stage == 1 and index < word_chains:
                        chains[index].fetch(own_sem.at[index]).wait()
                    chains[index].step(stage)

    low = lambda value: value.astype(BF)

    @pl.when(step == 0)
    def _():
        dgain_ref[...] = jnp.zeros_like(dgain_ref)
        dqkv_ref[...] = jnp.zeros_like(dqkv_ref)
        dout_ref[...] = jnp.zeros_like(dout_ref)
        dup_ref[...] = jnp.zeros_like(dup_ref)
        grad_down = low(tn(act_pool_ref[...], low(gpl_ref[...])))
        quarter = early_ref.shape[1]
        for index in range(RANKS):
            early_ref[index, :, 0:width] = grad_down[index * quarter:(index + 1) * quarter]
            early_ref[index, :, width:] = grad_down[(RANKS + index) * quarter:(RANKS + index + 1) * quarter]
        scaled = gpl_ref[...] * inv_ref[...]
        down_ref[:, width:] = nt(scaled.astype(BF), wdown_ref[...])
        down_ref[:, :width] = scaled

    @pl.when(step < half_steps)
    def _():
        here = rows_at(step * rows, rows)
        for word in range(words):
            line = down_ref[pl.ds(step * words + word, 1), :width]
            at = slice(word * slots, (word + 1) * slots)
            gq_ref[at, :width] = jnp.broadcast_to(line, (slots, width))
            line = down_ref[pl.ds(step * words + word, 1), width:]
            gup_ref[at, :] = (jnp.broadcast_to(line, (slots, line.shape[1])) * slope_ref[at, :].astype(F32)).astype(BF)

        slot = jnp.bitwise_and(lax.broadcasted_iota(jnp.int32, (rows, 1), 0), slots - 1)
        valid_col = slot < cnt_col_ref[...]
        unit2, rate2 = norm_parts(first_ref[...])
        dup_ref[...] += tn((unit2 * gain2_ref[...]).astype(BF), gup_ref[...])
        upstream = nt(gup_ref[...], wup_ref[...])
        dgain_ref[1:2, :] += jnp.sum(upstream * unit2, axis=0, keepdims=True)
        grad_first = jnp.where(valid_col, gq_ref[:, :width], 0.0) + norm_back(upstream, gain2_ref[...], unit2, rate2)
        spread_ref[here, :] = grad_first
        grad_low = low(grad_first)
        dout_ref[...] += tn(mixed_ref[...], grad_low)
        gmix_ref[here, :] = low(nt(grad_low, wout_ref[...]))

    @pl.when(step == half_steps - 1)
    def _():
        mid_ref[0] = low(dup_ref[:, 0:2 * width])
        mid_ref[1] = low(dup_ref[:, 2 * width:])
        mid_ref[2] = dproj_ref[...]
        half = width // 2
        mid_ref[3, 0:half, 0:width] = low(dout_ref[0:half, :])
        mid_ref[3, 0:half, width:] = low(dout_ref[half:, :])
        mid_ref[3, half:, :] = jnp.zeros_like(mid_ref[3, half:, :])
        both = jnp.concatenate([dgain_ref[...], dgain_ref[...]], axis=1)
        mid_ref[3, half:half + 16, :] = low(jnp.concatenate([wgain_ref[...], both], axis=0))

    @pl.when(step >= half_steps)
    def _():
        for tile in range(rows // TILE):
            at = pl.ds(tile * TILE, TILE)
            here = rows_at((step - half_steps) * rows + tile * TILE, TILE)
            for pair in range(CHEADS // 2):
                c0 = pair * TILE
                queries = split_heads(qkv_ref[at, c0:c0 + TILE])
                keys = split_heads(qkv_ref[at, width + c0:width + c0 + TILE])
                values = qkv_ref[at, 2 * width + c0:2 * width + c0 + TILE]
                grads = split_heads(gmix_ref[here, c0:c0 + TILE])
                probs_low = probs_ref[tile, pair]
                probs = probs_low.astype(F32)
                grad_probs = compact(nt(values, grads), slots)
                inner = jnp.sum(probs * grad_probs, axis=0, keepdims=True)
                grad_scores = (probs * (grad_probs - inner) * (CHD ** -0.5)).astype(BF)
                wide_scores = expand(grad_scores, slots)
                wide_probs = expand(probs_low, slots)
                gup_ref[at, c0:c0 + TILE] = tn(stack_lanes(wide_scores), keys).astype(BF)
                gup_ref[at, width + c0:width + c0 + TILE] = nn(wide_scores, queries).astype(BF)
                gup_ref[at, 2 * width + c0:2 * width + c0 + TILE] = nn(wide_probs, grads).astype(BF)
        unit1, rate1 = norm_parts(x_ref[...].astype(F32))
        grads = gup_ref[:, 0:3 * width]
        dqkv_ref[...] += tn((unit1 * gain1_ref[...]).astype(BF), grads)
        upstream1 = nt(grads, wqkv_ref[...])
        dgain_ref[0:1, :] += jnp.sum(upstream1 * unit1, axis=0, keepdims=True)
        here = rows_at((step - half_steps) * rows, rows)
        dx_ref[...] = low(spread_ref[here, :] + norm_back(upstream1, gain1_ref[...], unit1, rate1))

    @pl.when(step == steps - 1)
    def _():
        half = width // 2
        for index in range(2):
            late_ref[index] = low(dqkv_ref[index * half:(index + 1) * half, 0:2 * width])
            late_ref[2, :, index * width:(index + 1) * width] = low(dqkv_ref[index * half:(index + 1) * half, 2 * width:])
        late_ref[3] = jnp.zeros_like(late_ref[3])
        both = jnp.concatenate([dgain_ref[...], dgain_ref[...]], axis=1)
        late_ref[3, 0:16, :] = low(jnp.concatenate([both, both], axis=0))
        done = [len(stages) for stages in PLAN] + [0]
        while any(done[index] <= len(chains[index].stages) for index in range(CHAINS)):
            for index in reversed(range(CHAINS)):
                if done[index] <= len(chains[index].stages):
                    chains[index].step(done[index])
                    done[index] += 1
                    if done[index] > len(chains[index].stages):
                        leave[index].start()
        for copy in leave:
            copy.wait()


def char_backward(bits, x, counts, gain1, wqkv, wout, gain2, wup, wdown, grad_pooled, saved, grad_proj,
                  word_gains, word_grads):
    qkv, probs, mixed, first, slope, act_pool = saved
    rows, width = x.shape
    words = counts.shape[0]
    slots = rows // words
    hidden = wup.shape[1]
    wide = word_gains.shape[1]
    step = rows // CHAR_STEPS
    spread = jnp.repeat(counts, slots)
    last = CHAR_STEPS - 1
    ahead = lambda i: i - (i // CHAR_STEPS) * (i - last)
    behind = lambda i: (i // CHAR_STEPS) * (i - CHAR_STEPS)
    ahead_block = lambda cols: pl.BlockSpec((step, cols), lambda i: (ahead(i), 0))
    behind_block = lambda cols: pl.BlockSpec((step, cols), lambda i: (behind(i), 0))
    whole = lambda shape: pl.BlockSpec(shape, lambda i: (0,) * len(shape))
    tiles = step // TILE
    sum_shapes = [(wide, wide)] * 3 + [(RANKS, width // 2, wide), (RANKS, width, wide), (RANKS, width // 2, wide)]
    sources = [(RANKS,) + shape if len(shape) == 2 else shape for shape in sum_shapes]
    copies = sum(chain_copies(bits, index >= 3) for index in range(CHAINS))
    scratch = []
    for shape in sources:
        scratch += chain_scratch(bits, shape[1], wide)
    return pl.pallas_call(
        functools.partial(char_backward_kernel, slots, bits),
        grid=(2 * CHAR_STEPS,),
        in_specs=[
            behind_block(width),
            ahead_block(1),
            whole((words, 1)),
            whole((1, width)),
            whole((width, 3 * width)),
            whole((width, width)),
            whole((1, width)),
            whole((width, hidden)),
            whole((hidden, width)),
            whole((words, width)),
            whole((words, hidden)),
            whole((width, wide)),
            whole((8, wide)),
            behind_block(3 * width),
            pl.BlockSpec((tiles, CHEADS // 2, slots, 2 * TILE), lambda i: (behind(i), 0, 0, 0)),
            ahead_block(width),
            ahead_block(width),
            ahead_block(hidden),
        ] + [pl.BlockSpec(memory_space=pl.ANY)] * 3,
        out_specs=[behind_block(width)] + [pl.BlockSpec(memory_space=pl.ANY)] * CHAINS,
        out_shape=[jax.ShapeDtypeStruct((rows, width), BF)]
        + [jax.ShapeDtypeStruct(shape, BF) for shape in sum_shapes],
        scratch_shapes=[
            pltpu.VMEM((words, width + hidden), F32),
            pltpu.VMEM((step, width), F32),
            pltpu.VMEM((rows, width), BF),
            pltpu.VMEM((step, hidden), BF),
            pltpu.VMEM((rows, width), F32),
            pltpu.VMEM((8, width), F32),
            pltpu.VMEM((width, 3 * width), F32),
            pltpu.VMEM((width, width), F32),
            pltpu.VMEM((width, hidden), F32),
        ] + [pltpu.VMEM(shape, BF) for shape in sources[3:]] + scratch
        + [pltpu.VMEM(shape, BF) for shape in sum_shapes] + [pltpu.SemaphoreType.DMA((copies,)), pltpu.SemaphoreType.DMA((copies,)), pltpu.SemaphoreType.DMA((2 * CHAINS,))],
        compiler_params=pltpu.CompilerParams(
            vmem_limit_bytes=63 << 20, collective_id=2, has_side_effects=True),
        name="char_backward",
    )(x, spread[:, None], (1.0 / counts.astype(F32))[:, None], gain1[None, :], wqkv, wout, gain2[None, :],
      wup, wdown, grad_pooled, act_pool, grad_proj, word_gains, qkv, probs, mixed, first, slope, *word_grads)


def unpack_kernel(out_in, dx_in, up_in, down_in, mix_in, early_in, mid_in, late_in,
                  out_ref, dx_ref, gain1_ref, dq_ref, dk_ref, dv_ref, dout_ref, gain2_ref, dup_ref, ddown_ref, dproj_ref,
                  wgain1_ref, wq_ref, wk_ref, wv_ref, wout_ref, wgain2_ref, wup_ref, wdown_ref):
    dx_ref[...] = dx_in[...].astype(F32)
    out_ref[...] = out_in[...]
    width = dout_ref.shape[0]
    half = width // 2

    @pl.when(pl.program_id(0) == 0)
    def _():
        wup_ref[...] = up_in[...].astype(F32)
        wdown_ref[...] = down_in[...].astype(F32)
        wq_ref[...] = mix_in[:, 0:TILE].astype(F32)
        wk_ref[...] = mix_in[:, TILE:2 * TILE].astype(F32)
        wv_ref[...] = mix_in[:, 2 * TILE:3 * TILE].astype(F32)
        wout_ref[...] = mix_in[:, 3 * TILE:].astype(F32).T
        for index in range(RANKS):
            quarter = early_in.shape[1]
            ddown_ref[index * quarter:(index + 1) * quarter, :] = early_in[index, :, 0:width].astype(F32)
            ddown_ref[(RANKS + index) * quarter:(RANKS + index + 1) * quarter, :] = early_in[index, :, width:].astype(F32)
        dup_ref[:, 0:2 * width] = mid_in[0].astype(F32)
        dup_ref[:, 2 * width:] = mid_in[1].astype(F32)
        dproj_ref[...] = mid_in[2].astype(F32)
        gains = mid_in[3, half:half + 16, :].astype(F32)
        wgain1_ref[...] = gains[0:1]
        wgain2_ref[...] = gains[1:2]
        gain2_ref[...] = gains[9:10, 0:width]
        gain1_ref[...] = late_in[3, 0:16, 0:width].astype(F32)[0:1]
        for index in range(2):
            at = slice(index * half, (index + 1) * half)
            cols = slice(index * width, (index + 1) * width)
            dout_ref[at, :] = mid_in[3, 0:half, cols].astype(F32)
            dq_ref[at, :] = late_in[index, :, 0:width].astype(F32)
            dk_ref[at, :] = late_in[index, :, width:].astype(F32)
            dv_ref[at, :] = late_in[2, :, cols].astype(F32)


def unpack(word_output, grad_inputs, sums, width, hidden):
    steps = 8
    rows = grad_inputs.shape[0]
    words, wide = word_output.shape
    whole = lambda shape: pl.BlockSpec(shape, lambda i: (0,) * len(shape))
    split = lambda array: pl.BlockSpec((array.shape[0] // steps, array.shape[1]), lambda i: (i, 0))
    shapes = [(1, width), (width, width), (width, width), (width, width), (width, width), (1, width),
              (width, hidden), (hidden, width), (width, wide),
              (1, wide), (wide, TILE), (wide, TILE), (wide, TILE), (TILE, wide), (1, wide), (wide, wide), (wide, wide)]
    results = pl.pallas_call(
        unpack_kernel,
        grid=(steps,),
        in_specs=[split(word_output), split(grad_inputs)] + [whole(array.shape) for array in sums],
        out_specs=[split(word_output), split(grad_inputs)] + [whole(shape) for shape in shapes],
        out_shape=[jax.ShapeDtypeStruct(word_output.shape, BF), jax.ShapeDtypeStruct(grad_inputs.shape, F32)]
        + [jax.ShapeDtypeStruct(shape, F32) for shape in shapes],
        compiler_params=pltpu.CompilerParams(vmem_limit_bytes=60 << 20),
        name="unpack",
    )(word_output, grad_inputs, *sums)
    return tuple(array[0] if array.shape[0] == 1 else array for array in results)


def per_device(
    bits,
    char_inputs,
    char_counts,
    doc_ids,
    cotangent,
    char_norm_one,
    char_query,
    char_key,
    char_value,
    char_out,
    char_norm_two,
    char_up,
    char_down,
    char_proj,
    word_norm_one,
    word_query,
    word_key,
    word_value,
    word_out_proj,
    word_norm_two,
    word_up,
    word_down,
):
    char_qkv = jnp.concatenate([char_query, char_key, char_value], axis=1)
    word_qkv = jnp.concatenate([word_query, word_key, word_value], axis=1)
    vec, pooled, *saved, near, qkv_all, out_all, up_all, down_all = char_forward(
        char_inputs, char_counts, char_norm_one, char_qkv, char_out, char_norm_two, char_up, char_down, char_proj,
        word_qkv, word_out_proj, word_up, word_down,
    )
    word_output, grad_pooled, grad_proj, word_gains, *word_grads = word_layer(
        bits, vec, near, doc_ids, cotangent, qkv_all, out_all, up_all, down_all,
        word_norm_one, word_norm_two, char_proj, pooled,
    )
    grad_inputs, *sums = char_backward(
        bits, char_inputs, char_counts, char_norm_one, char_qkv, char_out, char_norm_two, char_up, char_down,
        grad_pooled, saved, grad_proj, word_gains, word_grads,
    )
    return unpack(word_output, grad_inputs, sums, char_out.shape[0], char_up.shape[1])


def solution(mesh):
    in_specs = (
        P(("dp", "tensor"), None),
        P(("dp", "tensor")),
        P("dp", None),
        P("dp", None),
        P(),
        P(),
        P(),
        P(),
        P(),
        P(),
        P(),
        P(),
        P(),
        P(),
        P(None, "tensor"),
        P(None, "tensor"),
        P(None, "tensor"),
        P("tensor", None),
        P(),
        P(None, "tensor"),
        P("tensor", None),
    )
    out_specs = (
        P(("dp", "tensor"), None),
        P(("dp", "tensor"), None),
        P(),
        P(),
        P(),
        P(),
        P(),
        P(),
        P(),
        P(),
        P(),
        P(),
        P(None, "tensor"),
        P(None, "tensor"),
        P(None, "tensor"),
        P("tensor", None),
        P(),
        P(None, "tensor"),
        P("tensor", None),
    )
    assert mesh.shape["tensor"] == RANKS
    bits = mesh.shape["dp"].bit_length() - 1
    assert bits >= 3 and mesh.shape["dp"] == 1 << bits
    return jax.shard_map(
        functools.partial(per_device, bits), mesh=mesh, in_specs=in_specs, out_specs=out_specs, check_vma=False
    )
```

```python
import functools

import jax
import jax.numpy as jnp
from jax import lax
from jax.experimental import pallas as pl
from jax.experimental.pallas import tpu as pltpu
from jax.sharding import PartitionSpec as P

BF = jnp.bfloat16
F32 = jnp.float32
EPSILON = 1e-05
NEG_LARGE = -1e30
RANKS = 4
CHEADS = 4
CHD = 64
TILE = 128
CHAR_STEPS = 8
GELU_C = 0.7978845608028654
GELU_A = 0.044715


def nn(left, right):
    return lax.dot_general(left, right, (((1,), (0,)), ((), ())), preferred_element_type=F32)


def nt(left, right):
    return lax.dot_general(left, right, (((1,), (1,)), ((), ())), preferred_element_type=F32)


def tn(left, right):
    return lax.dot_general(left, right, (((0,), (0,)), ((), ())), preferred_element_type=F32)


def norm_parts(values):
    centre = values - jnp.mean(values, axis=-1, keepdims=True)
    spread = jnp.mean(centre * centre, axis=-1, keepdims=True)
    rate = lax.rsqrt(spread + EPSILON)
    return centre * rate, rate


def norm_back(upstream, gain, unit, rate):
    scaled = upstream * gain
    first = jnp.mean(scaled, axis=-1, keepdims=True)
    second = jnp.mean(scaled * unit, axis=-1, keepdims=True)
    return rate * (scaled - first - unit * second)


def gelu_parts(values):
    square = values * values
    inner = values * (GELU_C + (GELU_C * GELU_A) * square)
    half = 0.5 + 0.5 * jnp.tanh(inner)
    active = values * half
    slope = half + (active * (1.0 - half)) * (2.0 * GELU_C + (6.0 * GELU_C * GELU_A) * square)
    return active, slope


def split_heads(pair):
    low_half = lax.broadcasted_iota(jnp.int32, pair.shape, 1) < CHD
    zero = jnp.zeros_like(pair)
    return jnp.concatenate([jnp.where(low_half, pair, zero), jnp.where(low_half, zero, pair)], axis=0)


def word_of_lane(shape, slots):
    lane = lax.broadcasted_iota(jnp.int32, shape, 1)
    return jnp.bitwise_and(lane, TILE - 1) // slots


def compact(scores, slots):
    words = word_of_lane((slots, scores.shape[1]), slots)
    result = scores[0:slots]
    for word in range(1, TILE // slots):
        result = jnp.where(words == word, scores[word * slots:(word + 1) * slots], result)
    return result


def expand(packed, slots):
    words = word_of_lane(packed.shape, slots)
    zero = jnp.zeros_like(packed)
    return jnp.concatenate(
        [jnp.where(words == word, packed, zero) for word in range(TILE // slots)], axis=0
    )


def stack_lanes(pair):
    return jnp.concatenate([pair[:, :TILE], pair[:, TILE:]], axis=0)


def pool_matrix(rows, slots, counts_col):
    words = rows // slots
    row = lax.broadcasted_iota(jnp.int32, (rows, words), 0)
    word = lax.broadcasted_iota(jnp.int32, (rows, words), 1)
    mine = (row // slots == word) & (jnp.bitwise_and(row, slots - 1) < counts_col)
    return jnp.where(mine, 1.0 / counts_col.astype(F32), 0.0)


MESH = pl.DeviceIdType.MESH
LANE_SPLIT = 256


class Place:
    def __init__(self):
        self.dp = lax.axis_index("dp")
        self.rank = lax.axis_index("tensor")
        self.core = lax.rem(self.dp, 2)
        self.x = lax.rem(self.dp // 2, 2)
        self.y = lax.rem(self.dp // 4, 2)
        self.core_mate = (self.dp + 1 - 2 * self.core, self.rank)
        self.x_mate = (self.dp + 2 - 4 * self.x, self.rank)
        self.y_mate = (self.dp + 4 - 8 * self.y, self.rank)

    def ring(self, offset):
        return lax.rem(self.rank + offset, RANKS)

    def ring_device(self, offset):
        return (self.dp, self.ring(offset))

    def bit_mate(self, bit):
        size = 1 << bit
        mine = lax.rem(self.dp // size, 2)
        return (self.dp + size - 2 * size * mine, self.rank)

    def mates(self, bits):
        extra = [self.bit_mate(bit) for bit in range(3, bits)]
        return [self.core_mate, self.x_mate, self.y_mate] + extra


def meet(devices):
    barrier = pltpu.get_barrier_semaphore()
    for device in devices:
        pl.semaphore_signal(barrier, inc=1, device_id=device, device_id_type=MESH)
    pl.semaphore_wait(barrier, len(devices))


def remote(source, target, sems, device):
    return pltpu.make_async_remote_copy(
        src_ref=source, dst_ref=target, send_sem=sems[0], recv_sem=sems[1],
        device_id=device, device_id_type=MESH,
    )


class Sems:
    def __init__(self, send, recv, start=0):
        self.send, self.recv, self.next = send, recv, start

    def take(self):
        at = self.next
        self.next += 1
        return self.send.at[at], self.recv.at[at]


def rows_at(start, size):
    return pl.ds(pl.multiple_of(start, 16), size)


def halves(width):
    return (slice(0, LANE_SPLIT), slice(LANE_SPLIT, width))


class Gather:
    def __init__(self, place, local, whole, sems):
        self.stages = [[], [], [], []]
        rows = local.shape[0]
        unit = rows // 8
        p = place
        left, right = halves(local.shape[1])
        left_at = p.core * 4 + p.x * 2 + p.y
        right_at = p.core * 4 + p.y * 2 + p.x
        for offset in range(1, RANKS):
            for lanes, at in ((left, left_at), (right, right_at)):
                at = rows_at(at * unit, unit)
                self.stages[0].append(remote(
                    local.at[at, lanes], whole.at[p.rank, at, lanes], sems.take(), p.ring_device(offset)))
        for offset in range(1, RANKS):
            rank = p.ring(offset)
            for lanes, at, first, second, mate_first, mate_second in (
                (left, left_at, p.x, None, p.y_mate, p.x_mate),
                (right, right_at, p.y, None, p.x_mate, p.y_mate),
            ):
                one = rows_at(at * unit, unit)
                two = rows_at((p.core * 4 + first * 2) * unit, 2 * unit)
                self.stages[1].append(remote(
                    whole.at[rank, one, lanes], whole.at[rank, one, lanes], sems.take(), mate_first))
                self.stages[2].append(remote(
                    whole.at[rank, two, lanes], whole.at[rank, two, lanes], sems.take(), mate_second))
            four = rows_at(p.core * 4 * unit, 4 * unit)
            self.stages[3].append(remote(
                whole.at[rank, four], whole.at[rank, four], sems.take(), p.core_mate))

    def start(self, stage):
        for copy in self.stages[stage]:
            copy.start()

    def wait(self, stage):
        for copy in self.stages[stage]:
            copy.wait()


def gather_copies():
    return 2 * (RANKS - 1) * 3 + (RANKS - 1)


class Chain:
    def __init__(self, place, bits, src, refs, sems, everywhere):
        p = place
        buf, got_core, got_one, got_two, got_more, got_rank, out = refs
        self.p, self.src, self.everywhere = p, src, everywhere
        self.buf, self.got_core, self.got_one, self.got_two = buf, got_core, got_one, got_two
        self.got_more, self.got_rank = got_more, got_rank
        self.mine = out.at[p.rank] if everywhere else out
        unit = src.shape[1] // 8
        lanes = left, right = halves(src.shape[2])
        self.lanes = lanes
        self.own = rows_at(p.core * 4 * unit, 4 * unit)
        stages = [("core", [remote(src.at[:, rows_at((1 - p.core) * 4 * unit, 4 * unit)], got_core,
                                   sems.take(), p.core_mate)])]
        first, second = (p.x, p.y), (p.y, p.x)
        first_mate, second_mate = (p.x_mate, p.y_mate), (p.y_mate, p.x_mate)
        one = lambda side, at: rows_at(at * 2 * unit, 2 * unit)
        two = lambda side, at: rows_at((first[side] * 2 + at) * unit, unit)
        self.one_rows = [one(side, first[side]) for side in (0, 1)]
        self.two_rows = [two(side, second[side]) for side in (0, 1)]
        stages.append(("one", [
            remote(buf.at[:, one(side, 1 - first[side]), lanes[side]], got_one.at[:, :, lanes[side]],
                   sems.take(), first_mate[side]) for side in (0, 1)]))
        stages.append(("two", [
            remote(buf.at[:, two(side, 1 - second[side]), lanes[side]], got_two.at[:, :, lanes[side]],
                   sems.take(), second_mate[side]) for side in (0, 1)]))
        for bit in range(3, bits):
            stages.append((bit - 3, [
                remote(buf.at[:, self.two_rows[side], lanes[side]], got_more.at[bit - 3, :, :, lanes[side]],
                       sems.take(), p.bit_mate(bit)) for side in (0, 1)]))
        stages.append(("rank", [
            remote(buf.at[p.ring(offset), self.two_rows[side], lanes[side]],
                   got_rank.at[offset - 1, :, lanes[side]], sems.take(), p.ring_device(offset))
            for offset in range(1, RANKS) for side in (0, 1)]))
        base = p.core * 4 * unit
        self.out_two = [rows_at(base + (first[side] * 2 + second[side]) * unit, unit) for side in (0, 1)]
        out_one = [rows_at(base + first[side] * 2 * unit, 2 * unit) for side in (0, 1)]
        if everywhere:
            stages.append(("rank_back", [
                remote(out.at[p.rank, self.out_two[side], lanes[side]], out.at[p.rank, self.out_two[side], lanes[side]],
                       sems.take(), p.ring_device(offset))
                for offset in range(1, RANKS) for side in (0, 1)]))

        def back(at, part_lanes, mate):
            part = out.at[:, at, part_lanes] if everywhere else out.at[at, part_lanes]
            return remote(part, part, sems.take(), mate)

        stages.append(("back_two", [back(self.out_two[side], lanes[side], second_mate[side]) for side in (0, 1)]))
        stages.append(("back_one", [back(out_one[side], lanes[side], first_mate[side]) for side in (0, 1)]))
        stages.append(("back_core", [back(self.own, slice(None), p.core_mate)]))
        self.stages = stages

    def fetch(self, sem):
        return pltpu.make_async_copy(self.src.at[:, self.own], self.buf, sem)

    def start(self, index):
        for copy in self.stages[index][1]:
            copy.start()

    def finish(self, index):
        name, copies = self.stages[index]
        for copy in copies:
            copy.wait()
        buf = self.buf
        if name == "core":
            own = self.src if self.everywhere else None
            for quarter in range(RANKS):
                mine = own[quarter, self.own, :] if self.everywhere else buf[quarter]
                buf[quarter] = mine + self.got_core[quarter]
        elif name == "one":
            for at, lanes in zip(self.one_rows, self.lanes):
                for quarter in range(RANKS):
                    buf[quarter, at, lanes] += self.got_one[quarter, :, lanes]
        elif name == "two":
            for at, lanes in zip(self.two_rows, self.lanes):
                for quarter in range(RANKS):
                    buf[quarter, at, lanes] += self.got_two[quarter, :, lanes]
        elif name == "rank":
            for side in (0, 1):
                at, lanes = self.two_rows[side], self.lanes[side]
                total = buf[self.p.rank, at, lanes].astype(F32)
                for k in range(RANKS - 1):
                    total = total + self.got_rank[k, :, lanes].astype(F32)
                self.mine[self.out_two[side], lanes] = total.astype(BF)
        elif isinstance(name, int):
            for at, lanes in zip(self.two_rows, self.lanes):
                for quarter in range(RANKS):
                    buf[quarter, at, lanes] += self.got_more[name, quarter, :, lanes]

    def step(self, index):
        if index:
            self.finish(index - 1)
        if index < len(self.stages):
            self.start(index)


def chain_copies(bits, everywhere):
    pairs = 2 * (RANKS - 1)
    return 1 + 2 + 2 + 2 * (bits - 3) + pairs + (pairs if everywhere else 0) + 2 + 2 + 1


def chain_scratch(bits, rows, lanes):
    unit = rows // 8
    return [
        pltpu.VMEM((RANKS, 4 * unit, lanes), BF),
        pltpu.VMEM((RANKS, 4 * unit, lanes), BF),
        pltpu.VMEM((RANKS, 2 * unit, lanes), BF),
        pltpu.VMEM((RANKS, unit, lanes), BF),
        pltpu.VMEM((max(bits - 3, 1), RANKS, unit, lanes), BF),
        pltpu.VMEM((RANKS - 1, unit, lanes), BF),
    ]


def char_forward_kernel(slots, x_ref, cnt_lane_ref, cnt_col_ref, gain1_ref, wqkv_ref, wout_ref,
                        gain2_ref, wup_ref, wdown_ref, wproj_ref,
                        lqkv_ref, lout_ref, lup_ref, ldown_ref,
                        vec_ref, pooled_ref, qkv_ref, probs_ref, mixed_ref, first_ref,
                        slope_ref, act_pool_ref, near_ref, wqkv_all, wout_all, wup_all, wdown_all,
                        own_sem, send_sem, recv_sem):
    rows = x_ref.shape[0]
    width = x_ref.shape[1]
    step = pl.program_id(0)
    steps = pl.num_programs(0)
    words = rows // slots
    p = Place()
    pairs = ((lqkv_ref, wqkv_all), (lout_ref, wout_all), (lup_ref, wup_all), (ldown_ref, wdown_all))
    gathers = [Gather(p, mine, whole, Sems(send_sem, recv_sem, gather_copies() * index))
               for index, (mine, whole) in enumerate(pairs)]
    own_copies = [pltpu.make_async_copy(mine, whole.at[p.rank], own_sem.at[index])
                  for index, (mine, whole) in enumerate(pairs)]
    vec_base = gather_copies() * len(pairs)

    def vec_copies(at):
        copies = []
        for slot, offset in ((1, 1), (0, 2)):
            sem = vec_base + 2 * at + slot
            part = rows_at(at * words, words)
            copies.append(remote(vec_ref.at[part], near_ref.at[slot, part],
                                 (send_sem.at[sem], recv_sem.at[sem]), p.ring_device(offset)))
        return copies

    @pl.when(step == 0)
    def _():
        meet([p.ring_device(offset) for offset in (1, 2, 3)] + [p.core_mate, p.x_mate, p.y_mate])
        for copy in own_copies:
            copy.start()

    plan = {at: [] for at in range(CHAR_STEPS)}
    for group, (members, begin) in enumerate((((0, 1), (0, 2, 3, 4)), ((2,), (0, 3, 4, 5)), ((3,), (0, 4, 5, 6)))):
        for stage in range(4):
            for member in members:
                plan[begin[stage]].append((member, stage))
    for at, todo in plan.items():
        if todo:
            @pl.when(step == at)
            def _(todo=todo):
                for member, stage in todo:
                    if stage:
                        gathers[member].wait(stage - 1)
                    gathers[member].start(stage)

    @pl.when(step > 0)
    def _():
        for copy in vec_copies(step - 1):
            copy.start()

    base = x_ref[...].astype(F32)
    unit, _ = norm_parts(base)
    normed = (unit * gain1_ref[...]).astype(BF)
    qkv_ref[...] = nn(normed, wqkv_ref[...]).astype(BF)
    for tile in range(rows // TILE):
        at = pl.ds(tile * TILE, TILE)
        valid = (lax.broadcasted_iota(jnp.int32, (slots, TILE), 0)
                 < cnt_lane_ref[:, tile * TILE:(tile + 1) * TILE])
        for pair in range(CHEADS // 2):
            c0 = pair * TILE
            queries = split_heads(qkv_ref[at, c0:c0 + TILE])
            keys = qkv_ref[at, width + c0:width + c0 + TILE]
            values = split_heads(qkv_ref[at, 2 * width + c0:2 * width + c0 + TILE])
            scores = compact(nt(keys, queries), slots)
            parts = []
            for head in range(2):
                own = jnp.where(valid, scores[:, head * TILE:(head + 1) * TILE], NEG_LARGE)
                top = jnp.max(own, axis=0, keepdims=True)
                weight = jnp.exp((own - top) * (CHD ** -0.5))
                parts.append(weight / jnp.sum(weight, axis=0, keepdims=True))
            probs = jnp.concatenate(parts, axis=1).astype(BF)
            probs_ref[tile, pair] = probs
            mixed_ref[at, c0:c0 + TILE] = tn(stack_lanes(expand(probs, slots)), values).astype(BF)
    first = base + nn(mixed_ref[...], wout_ref[...])
    first_ref[...] = first
    unit2, _ = norm_parts(first)
    normed2 = (unit2 * gain2_ref[...]).astype(BF)
    counts_col = cnt_col_ref[...]
    slot = jnp.bitwise_and(lax.broadcasted_iota(jnp.int32, (rows, 1), 0), slots - 1)
    valid_col = slot < counts_col
    pool = pool_matrix(rows, slots, counts_col).astype(BF)
    chunk = 256
    for part in range(wup_ref.shape[1] // chunk):
        cols = slice(part * chunk, (part + 1) * chunk)
        active, slope = gelu_parts(nn(normed2, wup_ref[:, cols]))
        slope_ref[:, cols] = jnp.where(valid_col, slope, 0.0).astype(BF)
        act_pool_ref[:, cols] = tn(pool, active.astype(BF)).astype(BF)
    pooled = tn(pool, first.astype(BF)) + nn(act_pool_ref[...], wdown_ref[...])
    pooled = pooled.astype(BF)
    pooled_ref[...] = pooled
    vec_ref[rows_at(step * words, words), :] = nn(pooled, wproj_ref[...]).astype(BF)

    @pl.when(step == steps - 1)
    def _():
        for copy in vec_copies(step):
            copy.start()
        for copy in own_copies:
            copy.wait()
        for gather in gathers:
            gather.wait(3)
        for at in range(CHAR_STEPS):
            for copy in vec_copies(at):
                copy.wait()


def char_forward(x, counts, gain1, wqkv, wout, gain2, wup, wdown, wproj, lqkv, lout, lup, ldown):
    rows, width = x.shape
    words = counts.shape[0]
    slots = rows // words
    hidden = wup.shape[1]
    wide = wproj.shape[1]
    step = rows // CHAR_STEPS
    step_words = step // slots
    spread = jnp.repeat(counts, slots)
    row_block = lambda cols: pl.BlockSpec((step, cols), lambda i: (i, 0))
    word_block = lambda cols: pl.BlockSpec((step_words, cols), lambda i: (i, 0))
    whole = lambda shape: pl.BlockSpec(shape, lambda i: (0, 0))
    tiles = step // TILE
    return pl.pallas_call(
        functools.partial(char_forward_kernel, slots),
        grid=(rows // step,),
        in_specs=[
            row_block(width),
            pl.BlockSpec((1, step), lambda i: (0, i)),
            row_block(1),
            whole((1, width)),
            whole((width, 3 * width)),
            whole((width, width)),
            whole((1, width)),
            whole((width, hidden)),
            whole((hidden, width)),
            whole((width, wide)),
            whole(lqkv.shape),
            whole(lout.shape),
            whole(lup.shape),
            whole(ldown.shape),
        ],
        out_specs=[
            whole((words, wide)),
            word_block(width),
            row_block(3 * width),
            pl.BlockSpec((tiles, CHEADS // 2, slots, 2 * TILE), lambda i: (i, 0, 0, 0)),
            row_block(width),
            row_block(width),
            row_block(hidden),
            word_block(hidden),
        ] + [pl.BlockSpec(memory_space=pl.ANY)] * 5,
        out_shape=[
            jax.ShapeDtypeStruct((words, wide), BF),
            jax.ShapeDtypeStruct((words, width), BF),
            jax.ShapeDtypeStruct((rows, 3 * width), BF),
            jax.ShapeDtypeStruct((rows // TILE, CHEADS // 2, slots, 2 * TILE), BF),
            jax.ShapeDtypeStruct((rows, width), BF),
            jax.ShapeDtypeStruct((rows, width), F32),
            jax.ShapeDtypeStruct((rows, hidden), BF),
            jax.ShapeDtypeStruct((words, hidden), BF),
            jax.ShapeDtypeStruct((2, words, wide), BF),
            jax.ShapeDtypeStruct((RANKS,) + lqkv.shape, BF),
            jax.ShapeDtypeStruct((RANKS,) + lout.shape, BF),
            jax.ShapeDtypeStruct((RANKS,) + lup.shape, BF),
            jax.ShapeDtypeStruct((RANKS,) + ldown.shape, BF),
        ],
        scratch_shapes=[
            pltpu.SemaphoreType.DMA((4,)),
            pltpu.SemaphoreType.DMA((gather_copies() * 4 + 2 * CHAR_STEPS,)),
            pltpu.SemaphoreType.DMA((gather_copies() * 4 + 2 * CHAR_STEPS,)),
        ],
        compiler_params=pltpu.CompilerParams(
            vmem_limit_bytes=60 << 20, collective_id=0, has_side_effects=True),
        name="char_forward",
    )(x, spread[None, :], spread[:, None], gain1[None, :], wqkv, wout, gain2[None, :], wup, wdown, wproj,
      lqkv, lout, lup, ldown)


def word_kernel(bits, vec_ref, near_ref, row_docs_ref, key_docs_ref, cot_ref, wqkv_ref, wout_ref, wup_ref,
                wdown_ref, gain1_ref, gain2_ref, wproj_ref, pooled_ref,
                out_ref, gpl_ref, dproj_ref, dgain_ref, up_grad_ref, down_grad_ref, mix_grad_ref,
                n1_ref, q_ref, kv_ref, probs_ref, o_ref, act_ref, slope_ref, go_ref, gq_ref, gkv_ref,
                back_ref, cot_own, cot_sem, part_ref, got_ref, send_sem, recv_sem):
    p = Place()
    words, wide = vec_ref.shape
    window = 3 * words
    fetch = pltpu.make_async_copy(cot_ref.at[rows_at(p.rank * words, words)], cot_own, cot_sem)
    fetch.start()
    meet([p.ring_device(offset) for offset in (1, 2, 3)])

    own = vec_ref[...].astype(F32)
    unit1, rate1 = norm_parts(own)
    n1_ref[2 * words:, :] = (unit1 * gain1_ref[...]).astype(BF)
    for slot in range(2):
        unit, _ = norm_parts(near_ref[slot].astype(F32))
        n1_ref[slot * words:(slot + 1) * words, :] = (unit * gain1_ref[...]).astype(BF)

    def project(rank, carry):
        q_ref[rank] = nn(n1_ref[2 * words:, :], wqkv_ref[rank, :, 0:TILE]).astype(BF)
        kv_ref[rank] = nn(n1_ref[...], wqkv_ref[rank, :, TILE:]).astype(BF)
        scores = nt(split_heads(q_ref[rank]), kv_ref[rank, :, 0:TILE]) * (CHD ** -0.5)
        row = lax.broadcasted_iota(jnp.int32, (words, window), 0)
        key = lax.broadcasted_iota(jnp.int32, (words, window), 1)
        allowed = (row_docs_ref[...] == key_docs_ref[...]) & (key <= row + 2 * words)
        for head in range(2):
            at = slice(head * words, (head + 1) * words)
            masked = jnp.where(allowed, scores[at], NEG_LARGE)
            top = jnp.max(masked, axis=-1, keepdims=True)
            weight = jnp.exp(masked - top)
            probs_ref[rank, at, :] = (weight * (1.0 / jnp.sum(weight, axis=-1, keepdims=True))).astype(BF)
        pair = jnp.concatenate([probs_ref[rank, 0:words, :], probs_ref[rank, words:, :]], axis=1)
        o_ref[rank] = nn(pair, split_heads(kv_ref[rank, :, TILE:])).astype(BF)
        back_ref[...] += nn(o_ref[rank], wout_ref[rank])
        return carry

    back_ref[...] = own
    lax.fori_loop(0, RANKS, project, 0)
    middle = back_ref[...]
    unit2, rate2 = norm_parts(middle)
    normed2 = (unit2 * gain2_ref[...]).astype(BF)

    def feed(rank, carry):
        active, slope = gelu_parts(nn(normed2, wup_ref[rank]))
        act_ref[rank] = active.astype(BF)
        slope_ref[rank] = slope.astype(BF)
        back_ref[...] += nn(act_ref[rank], wdown_ref[rank])
        return carry

    lax.fori_loop(0, RANKS, feed, 0)
    out_ref[...] = back_ref[...].astype(BF)
    fetch.wait()
    back_ref[...] = jnp.zeros_like(back_ref)

    def feed_back(rank, carry):
        upstream = (nt(cot_own[...], wdown_ref[rank]) * slope_ref[rank].astype(F32)).astype(BF)
        back_ref[...] += nt(upstream, wup_ref[rank])
        up_grad_ref[rank] = tn(normed2, upstream).astype(BF)
        down_grad_ref[rank] = tn(act_ref[rank], cot_own[...]).astype(BF)
        return carry

    lax.fori_loop(0, RANKS, feed_back, 0)
    upstream2 = back_ref[...]
    dgain_ref[...] = jnp.zeros_like(dgain_ref)
    dgain_ref[1:2, :] = jnp.sum(upstream2 * unit2, axis=0, keepdims=True)
    grad_middle = cot_own[...].astype(F32) + norm_back(upstream2, gain2_ref[...], unit2, rate2)
    middle_low = grad_middle.astype(BF)

    back_ref[...] = jnp.zeros_like(back_ref)
    part_ref[...] = jnp.zeros_like(part_ref)

    def attend_back(rank, carry):
        go_ref[...] = nt(middle_low, wout_ref[rank]).astype(BF)
        mix_grad_ref[rank, :, 3 * TILE:] = tn(middle_low, o_ref[rank]).astype(BF)
        go_pair = split_heads(go_ref[...])
        grad_probs = nt(go_pair, kv_ref[rank, :, TILE:])
        probs = probs_ref[rank].astype(F32)
        inner = jnp.sum(probs * grad_probs, axis=-1, keepdims=True)
        grad_scores = (probs * (grad_probs - inner) * (CHD ** -0.5)).astype(BF)
        q_pair = split_heads(q_ref[rank])
        gkv_ref[:, 0:TILE] = tn(grad_scores, q_pair).astype(BF)
        gkv_ref[:, TILE:] = tn(probs_ref[rank], go_pair).astype(BF)
        pair = jnp.concatenate([grad_scores[0:words], grad_scores[words:]], axis=1)
        gq_ref[...] = nn(pair, split_heads(kv_ref[rank, :, 0:TILE])).astype(BF)
        part_ref[...] += nt(gkv_ref[0:2 * words, :], wqkv_ref[rank, :, TILE:])
        back_ref[...] += nt(gkv_ref[2 * words:, :], wqkv_ref[rank, :, TILE:])
        back_ref[...] += nt(gq_ref[...], wqkv_ref[rank, :, 0:TILE])
        mix_grad_ref[rank, :, 0:TILE] = tn(n1_ref[2 * words:, :], gq_ref[...]).astype(BF)
        mix_grad_ref[rank, :, TILE:3 * TILE] = tn(n1_ref[...], gkv_ref[...]).astype(BF)
        return carry

    lax.fori_loop(0, RANKS, attend_back, 0)
    near_ref_low = got_ref.at[2]
    near_ref_low[...] = part_ref[...].astype(BF).reshape(2, words, wide)
    sends = []
    for slot, offset in ((0, RANKS - 2), (1, RANKS - 1)):
        sends.append(remote(got_ref.at[2, slot], got_ref.at[slot, 0], (send_sem.at[slot], recv_sem.at[slot]),
                            p.ring_device(offset)))
    for copy in sends:
        copy.start()
    for copy in sends:
        copy.wait()
    upstream1 = back_ref[...] + got_ref[0, 0].astype(F32) + got_ref[1, 0].astype(F32)
    dgain_ref[0:1, :] = jnp.sum(upstream1 * unit1, axis=0, keepdims=True)
    grad_vec = (grad_middle + norm_back(upstream1, gain1_ref[...], unit1, rate1)).astype(BF)
    dproj_ref[...] = tn(pooled_ref[...], grad_vec).astype(BF)
    gpl_ref[...] = nt(grad_vec, wproj_ref[...])


def word_layer(bits, vec, near, doc_ids, cotangent, wqkv, wout, wup, wdown, gain1, gain2, wproj, pooled):
    words, wide = vec.shape
    width = pooled.shape[1]
    window = 3 * words
    rank = lax.axis_index("tensor")
    padded = jnp.concatenate([jnp.full((2 * words,), -1, jnp.int32), doc_ids[0]])
    key_docs = lax.dynamic_slice_in_dim(padded, rank * words, window, 0)
    hidden = wup.shape[2]
    vm = pl.BlockSpec(memory_space=pltpu.VMEM)
    return pl.pallas_call(
        functools.partial(word_kernel, bits),
        in_specs=[vm] * 4 + [pl.BlockSpec(memory_space=pl.ANY)] + [vm] * 8,
        out_specs=[vm] * 7,
        out_shape=[
            jax.ShapeDtypeStruct((words, wide), BF),
            jax.ShapeDtypeStruct((words, width), F32),
            jax.ShapeDtypeStruct((width, wide), BF),
            jax.ShapeDtypeStruct((8, wide), F32),
        ] + [
            jax.ShapeDtypeStruct((RANKS, wide, wide), BF) for _ in range(3)
        ],
        scratch_shapes=[
            pltpu.VMEM((window, wide), BF),
            pltpu.VMEM((RANKS, words, TILE), BF),
            pltpu.VMEM((RANKS, window, 2 * TILE), BF),
            pltpu.VMEM((RANKS, 2 * words, window), BF),
            pltpu.VMEM((RANKS, words, TILE), BF),
            pltpu.VMEM((RANKS, words, hidden), BF),
            pltpu.VMEM((RANKS, words, hidden), BF),
            pltpu.VMEM((words, TILE), BF),
            pltpu.VMEM((words, TILE), BF),
            pltpu.VMEM((window, 2 * TILE), BF),
            pltpu.VMEM((words, wide), F32),
            pltpu.VMEM((words, wide), BF),
            pltpu.SemaphoreType.DMA,
            pltpu.VMEM((2 * words, wide), F32),
            pltpu.VMEM((3, 2, words, wide), BF),
            pltpu.SemaphoreType.DMA((2,)),
            pltpu.SemaphoreType.DMA((2,)),
        ],
        compiler_params=pltpu.CompilerParams(
            vmem_limit_bytes=62 << 20, collective_id=1, has_side_effects=True),
        name="word_layer",
    )(vec, near, key_docs[2 * words:, None], key_docs[None, :], cotangent, wqkv, wout, wup, wdown,
      gain1[None, :], gain2[None, :], wproj, pooled)


CHAINS = 6
PLAN = (
    (0, 1, 4, 7, 10, 12, 13),
    (0, 2, 7, 10, 13, 14, 15),
    (1, 5, 9, 12, 15, 16, 17),
    (2, 6, 8, 9, 11, 12, 14, 15),
    (8, 10, 12, 13, 15, 16, 17, 18),
    (16, 17, 19, 20, 23),
)


def char_backward_kernel(slots, bits, x_ref, cnt_col_ref, inv_ref, gain1_ref, wqkv_ref, wout_ref, gain2_ref,
                         wup_ref, wdown_ref, gpl_ref, act_pool_ref, dproj_ref, wgain_ref, qkv_ref, probs_ref,
                         mixed_ref, first_ref, slope_ref, up_grad_ref, down_grad_ref, mix_grad_ref,
                         dx_ref, up_out, down_out, mix_out, early_out, mid_out, late_out,
                         down_ref, gq_ref, gmix_ref, gup_ref, spread_ref, dgain_ref, dqkv_ref, dout_ref, dup_ref,
                         all_ref, early_ref, mid_ref, late_ref, *rest):
    step = pl.program_id(0)
    steps = pl.num_programs(0)
    half_steps = CHAR_STEPS
    rows, width = x_ref.shape
    words = rows // slots
    p = Place()
    send_sem, recv_sem, own_sem = rest[-3:]
    sources = (up_grad_ref, down_grad_ref, mix_grad_ref, early_ref, mid_ref, late_ref)
    results = (up_out, down_out, mix_out, early_out, mid_out, late_out)
    outs = rest[6 * CHAINS:7 * CHAINS]
    leave = [pltpu.make_async_copy(out, result, own_sem.at[CHAINS + index])
             for index, (out, result) in enumerate(zip(outs, results))]
    word_chains = 3
    chains, first_sem = [], 0
    for index in range(CHAINS):
        everywhere = index >= word_chains
        refs = tuple(rest[6 * index:6 * index + 6]) + (outs[index],)
        chains.append(Chain(p, bits, sources[index], refs, Sems(send_sem, recv_sem, first_sem), everywhere))
        first_sem += chain_copies(bits, everywhere)

    @pl.when(step == 0)
    def _():
        meet(p.mates(bits) + [p.ring_device(offset) for offset in (1, 2, 3)])
        for index in range(word_chains):
            chains[index].fetch(own_sem.at[index]).start()

    for at in range(3 * half_steps):
        todo = [(index, stages.index(at)) for index, stages in enumerate(PLAN) if at in stages]
        if todo:
            @pl.when(step == at)
            def _(todo=todo):
                for index, stage in todo:
                    if stage == 1 and index < word_chains:
                        chains[index].fetch(own_sem.at[index]).wait()
                    chains[index].step(stage)

    low = lambda value: value.astype(BF)

    @pl.when(step == 0)
    def _():
        dgain_ref[...] = jnp.zeros_like(dgain_ref)
        dqkv_ref[...] = jnp.zeros_like(dqkv_ref)
        dout_ref[...] = jnp.zeros_like(dout_ref)
        dup_ref[...] = jnp.zeros_like(dup_ref)
        grad_down = low(tn(act_pool_ref[...], low(gpl_ref[...])))
        quarter = early_ref.shape[1]
        for index in range(RANKS):
            early_ref[index, :, 0:width] = grad_down[index * quarter:(index + 1) * quarter]
            early_ref[index, :, width:] = grad_down[(RANKS + index) * quarter:(RANKS + index + 1) * quarter]
        scaled = gpl_ref[...] * inv_ref[...]
        down_ref[:, width:] = nt(scaled.astype(BF), wdown_ref[...])
        down_ref[:, :width] = scaled

    @pl.when(step < half_steps)
    def _():
        here = rows_at(step * rows, rows)
        for word in range(words):
            line = down_ref[pl.ds(step * words + word, 1), :width]
            at = slice(word * slots, (word + 1) * slots)
            gq_ref[at, :width] = jnp.broadcast_to(line, (slots, width))
            line = down_ref[pl.ds(step * words + word, 1), width:]
            gup_ref[at, :] = (jnp.broadcast_to(line, (slots, line.shape[1])) * slope_ref[at, :].astype(F32)).astype(BF)

        slot = jnp.bitwise_and(lax.broadcasted_iota(jnp.int32, (rows, 1), 0), slots - 1)
        valid_col = slot < cnt_col_ref[...]
        unit2, rate2 = norm_parts(first_ref[...])
        dup_ref[...] += tn((unit2 * gain2_ref[...]).astype(BF), gup_ref[...])
        upstream = nt(gup_ref[...], wup_ref[...])
        dgain_ref[1:2, :] += jnp.sum(upstream * unit2, axis=0, keepdims=True)
        grad_first = jnp.where(valid_col, gq_ref[:, :width], 0.0) + norm_back(upstream, gain2_ref[...], unit2, rate2)
        spread_ref[here, :] = grad_first
        grad_low = low(grad_first)
        dout_ref[...] += tn(mixed_ref[...], grad_low)
        gmix_ref[here, :] = low(nt(grad_low, wout_ref[...]))

    @pl.when(step == half_steps - 1)
    def _():
        mid_ref[0] = low(dup_ref[:, 0:2 * width])
        mid_ref[1] = low(dup_ref[:, 2 * width:])
        mid_ref[2] = dproj_ref[...]
        half = width // 2
        mid_ref[3, 0:half, 0:width] = low(dout_ref[0:half, :])
        mid_ref[3, 0:half, width:] = low(dout_ref[half:, :])
        mid_ref[3, half:, :] = jnp.zeros_like(mid_ref[3, half:, :])
        both = jnp.concatenate([dgain_ref[...], dgain_ref[...]], axis=1)
        mid_ref[3, half:half + 16, :] = low(jnp.concatenate([wgain_ref[...], both], axis=0))

    @pl.when((step >= half_steps) & (step < 2 * half_steps))
    def _():
        base = (step - half_steps) * rows
        for tile in range(rows // TILE):
            at = pl.ds(tile * TILE, TILE)
            here = rows_at(base + tile * TILE, TILE)
            for pair in range(CHEADS // 2):
                c0 = pair * TILE
                queries = split_heads(qkv_ref[at, c0:c0 + TILE])
                keys = split_heads(qkv_ref[at, width + c0:width + c0 + TILE])
                values = qkv_ref[at, 2 * width + c0:2 * width + c0 + TILE]
                grads = split_heads(gmix_ref[here, c0:c0 + TILE])
                probs_low = probs_ref[tile, pair]
                probs = probs_low.astype(F32)
                grad_probs = compact(nt(values, grads), slots)
                inner = jnp.sum(probs * grad_probs, axis=0, keepdims=True)
                grad_scores = (probs * (grad_probs - inner) * (CHD ** -0.5)).astype(BF)
                wide_scores = expand(grad_scores, slots)
                wide_probs = expand(probs_low, slots)
                all_ref[here, c0:c0 + TILE] = tn(stack_lanes(wide_scores), keys).astype(BF)
                all_ref[here, width + c0:width + c0 + TILE] = nn(wide_scores, queries).astype(BF)
                all_ref[here, 2 * width + c0:2 * width + c0 + TILE] = nn(wide_probs, grads).astype(BF)
        unit1, _ = norm_parts(x_ref[...].astype(F32))
        dqkv_ref[...] += tn((unit1 * gain1_ref[...]).astype(BF), all_ref[rows_at(base, rows), :])

    @pl.when(step == 2 * half_steps - 1)
    def _():
        half = width // 2
        for index in range(2):
            late_ref[index] = low(dqkv_ref[index * half:(index + 1) * half, 0:2 * width])
            late_ref[2, :, index * width:(index + 1) * width] = low(dqkv_ref[index * half:(index + 1) * half, 2 * width:])
        late_ref[3] = jnp.zeros_like(late_ref[3])

    @pl.when(step >= 2 * half_steps)
    def _():
        here = rows_at((step - 2 * half_steps) * rows, rows)
        unit1, rate1 = norm_parts(x_ref[...].astype(F32))
        upstream1 = nt(all_ref[here, :], wqkv_ref[...])
        dx_ref[...] = low(spread_ref[here, :] + norm_back(upstream1, gain1_ref[...], unit1, rate1))

    @pl.when(step == steps - 1)
    def _():
        done = [len(stages) for stages in PLAN]
        while any(done[index] <= len(chains[index].stages) for index in range(CHAINS)):
            for index in reversed(range(CHAINS)):
                if done[index] <= len(chains[index].stages):
                    chains[index].step(done[index])
                    done[index] += 1
                    if done[index] > len(chains[index].stages):
                        leave[index].start()
        for copy in leave:
            copy.wait()


def char_backward(bits, x, counts, gain1, wqkv, wout, gain2, wup, wdown, grad_pooled, saved, grad_proj,
                  word_gains, word_grads):
    qkv, probs, mixed, first, slope, act_pool = saved
    rows, width = x.shape
    words = counts.shape[0]
    slots = rows // words
    hidden = wup.shape[1]
    wide = word_gains.shape[1]
    step = rows // CHAR_STEPS
    spread = jnp.repeat(counts, slots)
    last = CHAR_STEPS - 1
    ahead = lambda i: i - ((i // CHAR_STEPS + 1) // 2) * (i - last)
    behind = lambda i: (i // CHAR_STEPS % 2) * (i - CHAR_STEPS) + (i // CHAR_STEPS // 2) * last
    inputs = lambda i: (i % CHAR_STEPS) * ((i // CHAR_STEPS + 1) // 2)
    final = lambda i: (i // CHAR_STEPS // 2) * (i - 2 * CHAR_STEPS)
    ahead_block = lambda cols: pl.BlockSpec((step, cols), lambda i: (ahead(i), 0))
    behind_block = lambda cols: pl.BlockSpec((step, cols), lambda i: (behind(i), 0))
    whole = lambda shape: pl.BlockSpec(shape, lambda i: (0,) * len(shape))
    tiles = step // TILE
    sum_shapes = [(wide, wide)] * 3 + [(RANKS, width // 2, wide), (RANKS, width, wide), (RANKS, width // 2, wide)]
    sources = [(RANKS,) + shape if len(shape) == 2 else shape for shape in sum_shapes]
    copies = sum(chain_copies(bits, index >= 3) for index in range(CHAINS))
    scratch = []
    for shape in sources:
        scratch += chain_scratch(bits, shape[1], wide)
    return pl.pallas_call(
        functools.partial(char_backward_kernel, slots, bits),
        grid=(3 * CHAR_STEPS,),
        in_specs=[
            pl.BlockSpec((step, width), lambda i: (inputs(i), 0)),
            ahead_block(1),
            whole((words, 1)),
            whole((1, width)),
            whole((width, 3 * width)),
            whole((width, width)),
            whole((1, width)),
            whole((width, hidden)),
            whole((hidden, width)),
            whole((words, width)),
            whole((words, hidden)),
            whole((width, wide)),
            whole((8, wide)),
            behind_block(3 * width),
            pl.BlockSpec((tiles, CHEADS // 2, slots, 2 * TILE), lambda i: (behind(i), 0, 0, 0)),
            ahead_block(width),
            ahead_block(width),
            ahead_block(hidden),
        ] + [pl.BlockSpec(memory_space=pl.ANY)] * 3,
        out_specs=[pl.BlockSpec((step, width), lambda i: (final(i), 0))] + [pl.BlockSpec(memory_space=pl.ANY)] * CHAINS,
        out_shape=[jax.ShapeDtypeStruct((rows, width), BF)]
        + [jax.ShapeDtypeStruct(shape, BF) for shape in sum_shapes],
        scratch_shapes=[
            pltpu.VMEM((words, width + hidden), F32),
            pltpu.VMEM((step, width), F32),
            pltpu.VMEM((rows, width), BF),
            pltpu.VMEM((step, hidden), BF),
            pltpu.VMEM((rows, width), F32),
            pltpu.VMEM((8, width), F32),
            pltpu.VMEM((width, 3 * width), F32),
            pltpu.VMEM((width, width), F32),
            pltpu.VMEM((width, hidden), F32),
            pltpu.VMEM((rows, 3 * width), BF),
        ] + [pltpu.VMEM(shape, BF) for shape in sources[3:]] + scratch
        + [pltpu.VMEM(shape, BF) for shape in sum_shapes] + [pltpu.SemaphoreType.DMA((copies,)), pltpu.SemaphoreType.DMA((copies,)), pltpu.SemaphoreType.DMA((2 * CHAINS,))],
        compiler_params=pltpu.CompilerParams(
            vmem_limit_bytes=63 << 20, collective_id=2, has_side_effects=True),
        name="char_backward",
    )(x, spread[:, None], (1.0 / counts.astype(F32))[:, None], gain1[None, :], wqkv, wout, gain2[None, :],
      wup, wdown, grad_pooled, act_pool, grad_proj, word_gains, qkv, probs, mixed, first, slope, *word_grads)


def unpack_kernel(out_in, dx_in, wqkv_in, gain1_in, up_in, down_in, mix_in, early_in, mid_in, late_in,
                  out_ref, dx_ref, gain1_ref, dq_ref, dk_ref, dv_ref, dout_ref, gain2_ref, dup_ref, ddown_ref, dproj_ref,
                  wgain1_ref, wq_ref, wk_ref, wv_ref, wout_ref, wgain2_ref, wup_ref, wdown_ref):
    dx_ref[...] = dx_in[...].astype(F32)
    out_ref[...] = out_in[...]
    width = dout_ref.shape[0]
    half = width // 2

    @pl.when(pl.program_id(0) == 0)
    def _():
        wup_ref[...] = up_in[...].astype(F32)
        wdown_ref[...] = down_in[...].astype(F32)
        wq_ref[...] = mix_in[:, 0:TILE].astype(F32)
        wk_ref[...] = mix_in[:, TILE:2 * TILE].astype(F32)
        wv_ref[...] = mix_in[:, 2 * TILE:3 * TILE].astype(F32)
        wout_ref[...] = mix_in[:, 3 * TILE:].astype(F32).T
        for index in range(RANKS):
            quarter = early_in.shape[1]
            ddown_ref[index * quarter:(index + 1) * quarter, :] = early_in[index, :, 0:width].astype(F32)
            ddown_ref[(RANKS + index) * quarter:(RANKS + index + 1) * quarter, :] = early_in[index, :, width:].astype(F32)
        dup_ref[:, 0:2 * width] = mid_in[0].astype(F32)
        dup_ref[:, 2 * width:] = mid_in[1].astype(F32)
        dproj_ref[...] = mid_in[2].astype(F32)
        gains = mid_in[3, half:half + 16, :].astype(F32)
        wgain1_ref[...] = gains[0:1]
        wgain2_ref[...] = gains[1:2]
        gain2_ref[...] = gains[9:10, 0:width]
        parts = []
        for index in range(2):
            at = slice(index * half, (index + 1) * half)
            cols = slice(index * width, (index + 1) * width)
            own = wqkv_in[at, 0:2 * width].astype(F32) * late_in[index].astype(F32)
            last = wqkv_in[at, 2 * width:].astype(F32) * late_in[2, :, cols].astype(F32)
            parts.append(jnp.sum(own, axis=1, keepdims=True) + jnp.sum(last, axis=1, keepdims=True))
        column = jnp.concatenate(parts, axis=0)
        diagonal = (lax.broadcasted_iota(jnp.int32, (width, width), 0)
                    == lax.broadcasted_iota(jnp.int32, (width, width), 1))
        gain1_ref[...] = jnp.sum(jnp.where(diagonal, column, 0.0), axis=0, keepdims=True) / gain1_in[...]
        for index in range(2):
            at = slice(index * half, (index + 1) * half)
            cols = slice(index * width, (index + 1) * width)
            dout_ref[at, :] = mid_in[3, 0:half, cols].astype(F32)
            dq_ref[at, :] = late_in[index, :, 0:width].astype(F32)
            dk_ref[at, :] = late_in[index, :, width:].astype(F32)
            dv_ref[at, :] = late_in[2, :, cols].astype(F32)


def unpack(word_output, grad_inputs, char_qkv, gain1, sums, width, hidden):
    steps = 8
    rows = grad_inputs.shape[0]
    words, wide = word_output.shape
    whole = lambda shape: pl.BlockSpec(shape, lambda i: (0,) * len(shape))
    split = lambda array: pl.BlockSpec((array.shape[0] // steps, array.shape[1]), lambda i: (i, 0))
    shapes = [(1, width), (width, width), (width, width), (width, width), (width, width), (1, width),
              (width, hidden), (hidden, width), (width, wide),
              (1, wide), (wide, TILE), (wide, TILE), (wide, TILE), (TILE, wide), (1, wide), (wide, wide), (wide, wide)]
    results = pl.pallas_call(
        unpack_kernel,
        grid=(steps,),
        in_specs=[split(word_output), split(grad_inputs), whole(char_qkv.shape), whole((1, width))] + [whole(array.shape) for array in sums],
        out_specs=[split(word_output), split(grad_inputs)] + [whole(shape) for shape in shapes],
        out_shape=[jax.ShapeDtypeStruct(word_output.shape, BF), jax.ShapeDtypeStruct(grad_inputs.shape, F32)]
        + [jax.ShapeDtypeStruct(shape, F32) for shape in shapes],
        compiler_params=pltpu.CompilerParams(vmem_limit_bytes=60 << 20),
        name="unpack",
    )(word_output, grad_inputs, char_qkv, gain1[None, :], *sums)
    return tuple(array[0] if array.shape[0] == 1 else array for array in results)


def per_device(
    bits,
    char_inputs,
    char_counts,
    doc_ids,
    cotangent,
    char_norm_one,
    char_query,
    char_key,
    char_value,
    char_out,
    char_norm_two,
    char_up,
    char_down,
    char_proj,
    word_norm_one,
    word_query,
    word_key,
    word_value,
    word_out_proj,
    word_norm_two,
    word_up,
    word_down,
):
    char_qkv = jnp.concatenate([char_query, char_key, char_value], axis=1)
    word_qkv = jnp.concatenate([word_query, word_key, word_value], axis=1)
    vec, pooled, *saved, near, qkv_all, out_all, up_all, down_all = char_forward(
        char_inputs, char_counts, char_norm_one, char_qkv, char_out, char_norm_two, char_up, char_down, char_proj,
        word_qkv, word_out_proj, word_up, word_down,
    )
    word_output, grad_pooled, grad_proj, word_gains, *word_grads = word_layer(
        bits, vec, near, doc_ids, cotangent, qkv_all, out_all, up_all, down_all,
        word_norm_one, word_norm_two, char_proj, pooled,
    )
    grad_inputs, *sums = char_backward(
        bits, char_inputs, char_counts, char_norm_one, char_qkv, char_out, char_norm_two, char_up, char_down,
        grad_pooled, saved, grad_proj, word_gains, word_grads,
    )
    return unpack(word_output, grad_inputs, char_qkv, char_norm_one, sums, char_out.shape[0], char_up.shape[1])


def solution(mesh):
    in_specs = (
        P(("dp", "tensor"), None),
        P(("dp", "tensor")),
        P("dp", None),
        P("dp", None),
        P(),
        P(),
        P(),
        P(),
        P(),
        P(),
        P(),
        P(),
        P(),
        P(),
        P(None, "tensor"),
        P(None, "tensor"),
        P(None, "tensor"),
        P("tensor", None),
        P(),
        P(None, "tensor"),
        P("tensor", None),
    )
    out_specs = (
        P(("dp", "tensor"), None),
        P(("dp", "tensor"), None),
        P(),
        P(),
        P(),
        P(),
        P(),
        P(),
        P(),
        P(),
        P(),
        P(),
        P(None, "tensor"),
        P(None, "tensor"),
        P(None, "tensor"),
        P("tensor", None),
        P(),
        P(None, "tensor"),
        P("tensor", None),
    )
    assert mesh.shape["tensor"] == RANKS
    bits = mesh.shape["dp"].bit_length() - 1
    assert bits >= 3 and mesh.shape["dp"] == 1 << bits
    return jax.shard_map(
        functools.partial(per_device, bits), mesh=mesh, in_specs=in_specs, out_specs=out_specs, check_vma=False
    )
```

```python
import functools

import jax
import jax.numpy as jnp
from jax import lax
from jax.experimental import pallas as pl
from jax.experimental.pallas import tpu as pltpu
from jax.sharding import PartitionSpec as P

BF = jnp.bfloat16
F32 = jnp.float32
EPSILON = 1e-05
NEG_LARGE = -1e30
RANKS = 4
CHEADS = 4
CHD = 64
TILE = 128
CHAR_STEPS = 8
GELU_C = 0.7978845608028654
GELU_A = 0.044715


def nn(left, right):
    return lax.dot_general(left, right, (((1,), (0,)), ((), ())), preferred_element_type=F32)


def nt(left, right):
    return lax.dot_general(left, right, (((1,), (1,)), ((), ())), preferred_element_type=F32)


def tn(left, right):
    return lax.dot_general(left, right, (((0,), (0,)), ((), ())), preferred_element_type=F32)


def norm_parts(values):
    centre = values - jnp.mean(values, axis=-1, keepdims=True)
    spread = jnp.mean(centre * centre, axis=-1, keepdims=True)
    rate = lax.rsqrt(spread + EPSILON)
    return centre * rate, rate


def norm_back(upstream, gain, unit, rate):
    scaled = upstream * gain
    first = jnp.mean(scaled, axis=-1, keepdims=True)
    second = jnp.mean(scaled * unit, axis=-1, keepdims=True)
    return rate * (scaled - first - unit * second)


def gelu_parts(values):
    square = values * values
    inner = values * (GELU_C + (GELU_C * GELU_A) * square)
    half = 0.5 + 0.5 * jnp.tanh(inner)
    active = values * half
    slope = half + (active * (1.0 - half)) * (2.0 * GELU_C + (6.0 * GELU_C * GELU_A) * square)
    return active, slope


def split_heads(pair):
    low_half = lax.broadcasted_iota(jnp.int32, pair.shape, 1) < CHD
    zero = jnp.zeros_like(pair)
    return jnp.concatenate([jnp.where(low_half, pair, zero), jnp.where(low_half, zero, pair)], axis=0)


def word_of_lane(shape, slots):
    lane = lax.broadcasted_iota(jnp.int32, shape, 1)
    return jnp.bitwise_and(lane, TILE - 1) // slots


def compact(scores, slots):
    words = word_of_lane((slots, scores.shape[1]), slots)
    result = scores[0:slots]
    for word in range(1, TILE // slots):
        result = jnp.where(words == word, scores[word * slots:(word + 1) * slots], result)
    return result


def expand(packed, slots):
    words = word_of_lane(packed.shape, slots)
    zero = jnp.zeros_like(packed)
    return jnp.concatenate(
        [jnp.where(words == word, packed, zero) for word in range(TILE // slots)], axis=0
    )


def stack_lanes(pair):
    return jnp.concatenate([pair[:, :TILE], pair[:, TILE:]], axis=0)


def split_counts(counts_ref, table_ref, words):
    for step in range(CHAR_STEPS):
        table_ref[step:step + 1, 0:words] = counts_ref[:, step * words:(step + 1) * words]


def valid_slots(rows, slots, mine):
    words = rows // slots
    row = lax.broadcasted_iota(jnp.int32, (rows, words), 0)
    word = lax.broadcasted_iota(jnp.int32, (rows, words), 1)
    return (row // slots == word) & (jnp.bitwise_and(row, slots - 1) < mine)


def join_lanes(parts, whole_ref):
    width = parts[0].shape[1]
    for index, part in enumerate(parts):
        whole_ref[:, index * width:(index + 1) * width] = part[...]


def any_lane(mask):
    return jnp.max(jnp.where(mask, 1.0, 0.0), axis=1, keepdims=True) > 0.0


def column(row):
    size = row.shape[1]
    diagonal = (lax.broadcasted_iota(jnp.int32, (size, size), 0)
                == lax.broadcasted_iota(jnp.int32, (size, size), 1))
    return jnp.sum(jnp.where(diagonal, row, 0.0), axis=1, keepdims=True)


MESH = pl.DeviceIdType.MESH
LANE_SPLIT = 256


class Place:
    def __init__(self):
        self.dp = lax.axis_index("dp")
        self.rank = lax.axis_index("tensor")
        self.core = lax.rem(self.dp, 2)
        self.x = lax.rem(self.dp // 2, 2)
        self.y = lax.rem(self.dp // 4, 2)
        self.core_mate = (self.dp + 1 - 2 * self.core, self.rank)
        self.x_mate = (self.dp + 2 - 4 * self.x, self.rank)
        self.y_mate = (self.dp + 4 - 8 * self.y, self.rank)

    def ring(self, offset):
        return lax.rem(self.rank + offset, RANKS)

    def ring_device(self, offset):
        return (self.dp, self.ring(offset))

    def bit_mate(self, bit):
        size = 1 << bit
        mine = lax.rem(self.dp // size, 2)
        return (self.dp + size - 2 * size * mine, self.rank)

    def mates(self, bits):
        extra = [self.bit_mate(bit) for bit in range(3, bits)]
        return [self.core_mate, self.x_mate, self.y_mate] + extra


def meet(devices):
    barrier = pltpu.get_barrier_semaphore()
    for device in devices:
        pl.semaphore_signal(barrier, inc=1, device_id=device, device_id_type=MESH)
    pl.semaphore_wait(barrier, len(devices))


def remote(source, target, sems, device):
    return pltpu.make_async_remote_copy(
        src_ref=source, dst_ref=target, send_sem=sems[0], recv_sem=sems[1],
        device_id=device, device_id_type=MESH,
    )


class Sems:
    def __init__(self, send, recv, start=0):
        self.send, self.recv, self.next = send, recv, start

    def take(self):
        at = self.next
        self.next += 1
        return self.send.at[at], self.recv.at[at]


def rows_at(start, size):
    return pl.ds(pl.multiple_of(start, 16), size)


def halves(width):
    return (slice(0, LANE_SPLIT), slice(LANE_SPLIT, width))


class Gather:
    def __init__(self, place, local, whole, sems):
        self.stages = [[], [], [], []]
        rows = local.shape[0]
        unit = rows // 8
        p = place
        left, right = halves(local.shape[1])
        left_at = p.core * 4 + p.x * 2 + p.y
        right_at = p.core * 4 + p.y * 2 + p.x
        for offset in range(1, RANKS):
            for lanes, at in ((left, left_at), (right, right_at)):
                at = rows_at(at * unit, unit)
                self.stages[0].append(remote(
                    local.at[at, lanes], whole.at[p.rank, at, lanes], sems.take(), p.ring_device(offset)))
        for offset in range(1, RANKS):
            rank = p.ring(offset)
            for lanes, at, first, second, mate_first, mate_second in (
                (left, left_at, p.x, None, p.y_mate, p.x_mate),
                (right, right_at, p.y, None, p.x_mate, p.y_mate),
            ):
                one = rows_at(at * unit, unit)
                two = rows_at((p.core * 4 + first * 2) * unit, 2 * unit)
                self.stages[1].append(remote(
                    whole.at[rank, one, lanes], whole.at[rank, one, lanes], sems.take(), mate_first))
                self.stages[2].append(remote(
                    whole.at[rank, two, lanes], whole.at[rank, two, lanes], sems.take(), mate_second))
            four = rows_at(p.core * 4 * unit, 4 * unit)
            self.stages[3].append(remote(
                whole.at[rank, four], whole.at[rank, four], sems.take(), p.core_mate))

    def start(self, stage):
        for copy in self.stages[stage]:
            copy.start()

    def wait(self, stage):
        for copy in self.stages[stage]:
            copy.wait()


def gather_copies():
    return 2 * (RANKS - 1) * 3 + (RANKS - 1)


class Chain:
    def __init__(self, place, bits, src, refs, sems, everywhere):
        p = place
        buf, got_core, got_one, got_two, got_more, got_rank, out = refs
        self.p, self.src, self.everywhere = p, src, everywhere
        self.buf, self.got_core, self.got_one, self.got_two = buf, got_core, got_one, got_two
        self.got_more, self.got_rank = got_more, got_rank
        self.mine = out.at[p.rank] if everywhere else out
        unit = src.shape[1] // 8
        lanes = left, right = halves(src.shape[2])
        self.lanes = lanes
        self.own = rows_at(p.core * 4 * unit, 4 * unit)
        stages = [("core", [remote(src.at[:, rows_at((1 - p.core) * 4 * unit, 4 * unit)], got_core,
                                   sems.take(), p.core_mate)])]
        first, second = (p.x, p.y), (p.y, p.x)
        first_mate, second_mate = (p.x_mate, p.y_mate), (p.y_mate, p.x_mate)
        one = lambda side, at: rows_at(at * 2 * unit, 2 * unit)
        two = lambda side, at: rows_at((first[side] * 2 + at) * unit, unit)
        self.one_rows = [one(side, first[side]) for side in (0, 1)]
        self.two_rows = [two(side, second[side]) for side in (0, 1)]
        stages.append(("one", [
            remote(buf.at[:, one(side, 1 - first[side]), lanes[side]], got_one.at[:, :, lanes[side]],
                   sems.take(), first_mate[side]) for side in (0, 1)]))
        stages.append(("two", [
            remote(buf.at[:, two(side, 1 - second[side]), lanes[side]], got_two.at[:, :, lanes[side]],
                   sems.take(), second_mate[side]) for side in (0, 1)]))
        for bit in range(3, bits):
            stages.append((bit - 3, [
                remote(buf.at[:, self.two_rows[side], lanes[side]], got_more.at[bit - 3, :, :, lanes[side]],
                       sems.take(), p.bit_mate(bit)) for side in (0, 1)]))
        stages.append(("rank", [
            remote(buf.at[p.ring(offset), self.two_rows[side], lanes[side]],
                   got_rank.at[offset - 1, :, lanes[side]], sems.take(), p.ring_device(offset))
            for offset in range(1, RANKS) for side in (0, 1)]))
        base = p.core * 4 * unit
        self.out_two = [rows_at(base + (first[side] * 2 + second[side]) * unit, unit) for side in (0, 1)]
        out_one = [rows_at(base + first[side] * 2 * unit, 2 * unit) for side in (0, 1)]
        if everywhere:
            stages.append(("rank_back", [
                remote(out.at[p.rank, self.out_two[side], lanes[side]], out.at[p.rank, self.out_two[side], lanes[side]],
                       sems.take(), p.ring_device(offset))
                for offset in range(1, RANKS) for side in (0, 1)]))

        def back(at, part_lanes, mate):
            part = out.at[:, at, part_lanes] if everywhere else out.at[at, part_lanes]
            return remote(part, part, sems.take(), mate)

        stages.append(("back_two", [back(self.out_two[side], lanes[side], second_mate[side]) for side in (0, 1)]))
        stages.append(("back_one", [back(out_one[side], lanes[side], first_mate[side]) for side in (0, 1)]))
        stages.append(("back_core", [back(self.own, slice(None), p.core_mate)]))
        self.stages = stages

    def fetch(self, sem):
        return pltpu.make_async_copy(self.src.at[:, self.own], self.buf, sem)

    def start(self, index):
        for copy in self.stages[index][1]:
            copy.start()

    def finish(self, index):
        name, copies = self.stages[index]
        for copy in copies:
            copy.wait()
        buf = self.buf
        if name == "core":
            own = self.src if self.everywhere else None
            for quarter in range(RANKS):
                mine = own[quarter, self.own, :] if self.everywhere else buf[quarter]
                buf[quarter] = mine + self.got_core[quarter]
        elif name == "one":
            for at, lanes in zip(self.one_rows, self.lanes):
                for quarter in range(RANKS):
                    buf[quarter, at, lanes] += self.got_one[quarter, :, lanes]
        elif name == "two":
            for at, lanes in zip(self.two_rows, self.lanes):
                for quarter in range(RANKS):
                    buf[quarter, at, lanes] += self.got_two[quarter, :, lanes]
        elif name == "rank":
            for side in (0, 1):
                at, lanes = self.two_rows[side], self.lanes[side]
                total = buf[self.p.rank, at, lanes].astype(F32)
                for k in range(RANKS - 1):
                    total = total + self.got_rank[k, :, lanes].astype(F32)
                self.mine[self.out_two[side], lanes] = total.astype(BF)
        elif isinstance(name, int):
            for at, lanes in zip(self.two_rows, self.lanes):
                for quarter in range(RANKS):
                    buf[quarter, at, lanes] += self.got_more[name, quarter, :, lanes]

    def step(self, index):
        if index:
            self.finish(index - 1)
        if index < len(self.stages):
            self.start(index)


def chain_copies(bits, everywhere):
    pairs = 2 * (RANKS - 1)
    return 1 + 2 + 2 + 2 * (bits - 3) + pairs + (pairs if everywhere else 0) + 2 + 2 + 1


def chain_scratch(bits, rows, lanes):
    unit = rows // 8
    return [
        pltpu.VMEM((RANKS, 4 * unit, lanes), BF),
        pltpu.VMEM((RANKS, 4 * unit, lanes), BF),
        pltpu.VMEM((RANKS, 2 * unit, lanes), BF),
        pltpu.VMEM((RANKS, unit, lanes), BF),
        pltpu.VMEM((max(bits - 3, 1), RANKS, unit, lanes), BF),
        pltpu.VMEM((RANKS - 1, unit, lanes), BF),
    ]


FORWARD_PLAN = {
    2: ((0, 1), (1, 1)),
    3: ((2, 1), (0, 2), (1, 2)),
    4: ((3, 1), (2, 2)),
    5: ((0, 3), (1, 3), (3, 2)),
    6: ((2, 3),),
    7: ((3, 3),),
}


def char_forward_kernel(slots, x_ref, counts_ref, gain1_ref, wq_ref, wk_ref, wv_ref, wout_ref,
                        gain2_ref, wup_ref, wdown_ref, wproj_ref,
                        lq_ref, lk_ref, lv_ref, lout_ref, lup_ref, ldown_ref,
                        vec_ref, pooled_ref, qkv_ref, probs_ref, mixed_ref, first_ref,
                        slope_ref, act_pool_ref, near_ref, wqkv_all, wout_all, wup_all, wdown_all,
                        wqkv_ref, lqkv_ref, table_ref, own_sem, send_sem, recv_sem):
    rows = x_ref.shape[0]
    width = x_ref.shape[1]
    step = pl.program_id(0)
    steps = pl.num_programs(0)
    words = rows // slots
    p = Place()
    pairs = ((lqkv_ref, wqkv_all), (lout_ref, wout_all), (lup_ref, wup_all), (ldown_ref, wdown_all))
    gathers = [Gather(p, mine, whole, Sems(send_sem, recv_sem, gather_copies() * index))
               for index, (mine, whole) in enumerate(pairs)]
    own_copies = [pltpu.make_async_copy(mine, whole.at[p.rank], own_sem.at[index])
                  for index, (mine, whole) in enumerate(pairs)]
    vec_base = gather_copies() * len(pairs)

    def vec_copies(at):
        copies = []
        for slot, offset in ((1, 1), (0, 2)):
            sem = vec_base + 2 * at + slot
            part = rows_at(at * words, words)
            copies.append(remote(vec_ref.at[part], near_ref.at[slot, part],
                                 (send_sem.at[sem], recv_sem.at[sem]), p.ring_device(offset)))
        return copies

    @pl.when(step == 0)
    def _():
        join_lanes((lq_ref, lk_ref, lv_ref), lqkv_ref)
        join_lanes((wq_ref, wk_ref, wv_ref), wqkv_ref)
        meet([p.ring_device(offset) for offset in (1, 2, 3)] + [p.core_mate, p.x_mate, p.y_mate])
        split_counts(counts_ref, table_ref, words)
        for copy in own_copies:
            copy.start()
        for gather in gathers:
            gather.start(0)

    base = x_ref[...].astype(F32)
    unit, _ = norm_parts(base)
    normed = (unit * gain1_ref[...]).astype(BF)
    qkv_ref[...] = nn(normed, wqkv_ref[...]).astype(BF)
    mine = table_ref[pl.ds(step, 1), 0:words]
    word_at = lax.broadcasted_iota(jnp.int32, (words, rows), 0)
    row_at = lax.broadcasted_iota(jnp.int32, (words, rows), 1)
    onto_rows = jnp.where(row_at // slots == word_at, 1.0, 0.0).astype(BF)
    row_counts = nn(jnp.broadcast_to(mine.astype(F32), (16, words)).astype(BF), onto_rows)[0:1]
    for tile in range(rows // TILE):
        at = pl.ds(tile * TILE, TILE)
        valid = (lax.broadcasted_iota(jnp.int32, (slots, TILE), 0).astype(F32)
                 < row_counts[:, tile * TILE:(tile + 1) * TILE])
        for pair in range(CHEADS // 2):
            c0 = pair * TILE
            queries = split_heads(qkv_ref[at, c0:c0 + TILE])
            keys = qkv_ref[at, width + c0:width + c0 + TILE]
            values = split_heads(qkv_ref[at, 2 * width + c0:2 * width + c0 + TILE])
            scores = compact(nt(keys, queries), slots)
            parts = []
            for head in range(2):
                own = jnp.where(valid, scores[:, head * TILE:(head + 1) * TILE], NEG_LARGE)
                top = jnp.max(own, axis=0, keepdims=True)
                weight = jnp.exp((own - top) * (CHD ** -0.5))
                parts.append(weight / jnp.sum(weight, axis=0, keepdims=True))
            probs = jnp.concatenate(parts, axis=1).astype(BF)
            probs_ref[tile, pair] = probs
            mixed_ref[at, c0:c0 + TILE] = tn(stack_lanes(expand(probs, slots)), values).astype(BF)

    for at, todo in FORWARD_PLAN.items():
        @pl.when(step == at)
        def _(todo=todo):
            for member, stage in todo:
                gathers[member].wait(stage - 1)
                gathers[member].start(stage)

    @pl.when(step > 0)
    def _():
        for copy in vec_copies(step - 1):
            copy.start()

    first = base + nn(mixed_ref[...], wout_ref[...])
    first_ref[...] = first
    unit2, _ = norm_parts(first)
    normed2 = (unit2 * gain2_ref[...]).astype(BF)
    members = valid_slots(rows, slots, mine)
    valid_col = any_lane(members)
    pool = jnp.where(members, 1.0 / mine.astype(F32), 0.0).astype(BF)
    chunk = 256
    for part in range(wup_ref.shape[1] // chunk):
        cols = slice(part * chunk, (part + 1) * chunk)
        active, slope = gelu_parts(nn(normed2, wup_ref[:, cols]))
        slope_ref[:, cols] = jnp.where(valid_col, slope, 0.0).astype(BF)
        act_pool_ref[:, cols] = tn(pool, active.astype(BF)).astype(BF)
    pooled = tn(pool, first.astype(BF)) + nn(act_pool_ref[...], wdown_ref[...])
    pooled = pooled.astype(BF)
    pooled_ref[...] = pooled
    vec_ref[rows_at(step * words, words), :] = nn(pooled, wproj_ref[...]).astype(BF)

    @pl.when(step == steps - 1)
    def _():
        for copy in vec_copies(step):
            copy.start()
        for copy in own_copies:
            copy.wait()
        for gather in gathers:
            gather.wait(3)
        for at in range(CHAR_STEPS):
            for copy in vec_copies(at):
                copy.wait()


def char_forward(x, counts, gain1, weights, wout, gain2, wup, wdown, wproj, local, lout, lup, ldown):
    rows, width = x.shape
    words = counts.shape[0]
    slots = rows // words
    hidden = wup.shape[1]
    wide = wproj.shape[1]
    step = rows // CHAR_STEPS
    step_words = step // slots
    row_block = lambda cols: pl.BlockSpec((step, cols), lambda i: (i, 0))
    word_block = lambda cols: pl.BlockSpec((step_words, cols), lambda i: (i, 0))
    whole = lambda shape: pl.BlockSpec(shape, lambda i: (0, 0))
    tiles = step // TILE
    return pl.pallas_call(
        functools.partial(char_forward_kernel, slots),
        grid=(rows // step,),
        in_specs=[
            row_block(width),
            whole((1, words)),
            whole((1, width)),
            whole((width, width)),
            whole((width, width)),
            whole((width, width)),
            whole((width, width)),
            whole((1, width)),
            whole((width, hidden)),
            whole((hidden, width)),
            whole((width, wide)),
            whole(local[0].shape),
            whole(local[0].shape),
            whole(local[0].shape),
            whole(lout.shape),
            whole(lup.shape),
            whole(ldown.shape),
        ],
        out_specs=[
            whole((words, wide)),
            word_block(width),
            row_block(3 * width),
            pl.BlockSpec((tiles, CHEADS // 2, slots, 2 * TILE), lambda i: (i, 0, 0, 0)),
            row_block(width),
            row_block(width),
            row_block(hidden),
            word_block(hidden),
        ] + [pl.BlockSpec(memory_space=pl.ANY)] * 5,
        out_shape=[
            jax.ShapeDtypeStruct((words, wide), BF),
            jax.ShapeDtypeStruct((words, width), BF),
            jax.ShapeDtypeStruct((rows, 3 * width), BF),
            jax.ShapeDtypeStruct((rows // TILE, CHEADS // 2, slots, 2 * TILE), BF),
            jax.ShapeDtypeStruct((rows, width), BF),
            jax.ShapeDtypeStruct((rows, width), F32),
            jax.ShapeDtypeStruct((rows, hidden), BF),
            jax.ShapeDtypeStruct((words, hidden), BF),
            jax.ShapeDtypeStruct((2, words, wide), BF),
            jax.ShapeDtypeStruct((RANKS, wide, 3 * TILE), BF),
            jax.ShapeDtypeStruct((RANKS,) + lout.shape, BF),
            jax.ShapeDtypeStruct((RANKS,) + lup.shape, BF),
            jax.ShapeDtypeStruct((RANKS,) + ldown.shape, BF),
        ],
        scratch_shapes=[
            pltpu.VMEM((width, 3 * width), BF),
            pltpu.VMEM((wide, 3 * TILE), BF),
            pltpu.VMEM((CHAR_STEPS, TILE), jnp.int32),
            pltpu.SemaphoreType.DMA((4,)),
            pltpu.SemaphoreType.DMA((gather_copies() * 4 + 2 * CHAR_STEPS,)),
            pltpu.SemaphoreType.DMA((gather_copies() * 4 + 2 * CHAR_STEPS,)),
        ],
        compiler_params=pltpu.CompilerParams(
            vmem_limit_bytes=60 << 20, collective_id=0, has_side_effects=True),
        name="char_forward",
    )(x, counts[None, :], gain1[None, :], *weights, wout, gain2[None, :], wup, wdown, wproj,
      *local, lout, lup, ldown)


def word_kernel(bits, vec_ref, near_ref, docs_ref, cot_ref, wqkv_ref, wout_ref, wup_ref,
                wdown_ref, gain1_ref, gain2_ref, wproj_ref, pooled_ref,
                out_ref, gpl_ref, dproj_ref, dgain_ref, up_grad_ref, down_grad_ref, mix_grad_ref,
                n1_ref, q_ref, kv_ref, probs_ref, o_ref, act_ref, slope_ref, go_ref, gq_ref, gkv_ref,
                back_ref, cot_own, cot_sem, part_ref, got_ref, table_ref, send_sem, recv_sem):
    p = Place()
    words, wide = vec_ref.shape
    window = 3 * words
    fetch = pltpu.make_async_copy(cot_ref.at[rows_at(p.rank * words, words)], cot_own, cot_sem)
    fetch.start()
    meet([p.ring_device(offset) for offset in (1, 2, 3)])

    table_ref[:, 0:2 * words] = jnp.full((1, 2 * words), -1, jnp.int32)
    table_ref[:, 2 * words:] = docs_ref[...]
    start = pl.multiple_of(p.rank * words, TILE)
    key_docs = table_ref[:, pl.ds(start, window)].astype(F32)
    row_docs = column(key_docs[:, 2 * words:])

    own = vec_ref[...].astype(F32)
    unit1, rate1 = norm_parts(own)
    n1_ref[2 * words:, :] = (unit1 * gain1_ref[...]).astype(BF)
    for slot in range(2):
        unit, _ = norm_parts(near_ref[slot].astype(F32))
        n1_ref[slot * words:(slot + 1) * words, :] = (unit * gain1_ref[...]).astype(BF)

    def project(rank, carry):
        q_ref[rank] = nn(n1_ref[2 * words:, :], wqkv_ref[rank, :, 0:TILE]).astype(BF)
        kv_ref[rank] = nn(n1_ref[...], wqkv_ref[rank, :, TILE:]).astype(BF)
        scores = nt(split_heads(q_ref[rank]), kv_ref[rank, :, 0:TILE]) * (CHD ** -0.5)
        row = lax.broadcasted_iota(jnp.int32, (words, window), 0)
        key = lax.broadcasted_iota(jnp.int32, (words, window), 1)
        allowed = (row_docs == key_docs) & (key <= row + 2 * words)
        for head in range(2):
            at = slice(head * words, (head + 1) * words)
            masked = jnp.where(allowed, scores[at], NEG_LARGE)
            top = jnp.max(masked, axis=-1, keepdims=True)
            weight = jnp.exp(masked - top)
            probs_ref[rank, at, :] = (weight * (1.0 / jnp.sum(weight, axis=-1, keepdims=True))).astype(BF)
        pair = jnp.concatenate([probs_ref[rank, 0:words, :], probs_ref[rank, words:, :]], axis=1)
        o_ref[rank] = nn(pair, split_heads(kv_ref[rank, :, TILE:])).astype(BF)
        back_ref[...] += nn(o_ref[rank], wout_ref[rank])
        return carry

    back_ref[...] = own
    lax.fori_loop(0, RANKS, project, 0)
    middle = back_ref[...]
    unit2, rate2 = norm_parts(middle)
    normed2 = (unit2 * gain2_ref[...]).astype(BF)

    def feed(rank, carry):
        active, slope = gelu_parts(nn(normed2, wup_ref[rank]))
        act_ref[rank] = active.astype(BF)
        slope_ref[rank] = slope.astype(BF)
        back_ref[...] += nn(act_ref[rank], wdown_ref[rank])
        return carry

    lax.fori_loop(0, RANKS, feed, 0)
    out_ref[...] = back_ref[...].astype(BF)
    fetch.wait()
    back_ref[...] = jnp.zeros_like(back_ref)

    def feed_back(rank, carry):
        upstream = (nt(cot_own[...], wdown_ref[rank]) * slope_ref[rank].astype(F32)).astype(BF)
        back_ref[...] += nt(upstream, wup_ref[rank])
        up_grad_ref[rank] = tn(normed2, upstream).astype(BF)
        down_grad_ref[rank] = tn(act_ref[rank], cot_own[...]).astype(BF)
        return carry

    lax.fori_loop(0, RANKS, feed_back, 0)
    upstream2 = back_ref[...]
    dgain_ref[...] = jnp.zeros_like(dgain_ref)
    dgain_ref[1:2, :] = jnp.sum(upstream2 * unit2, axis=0, keepdims=True)
    grad_middle = cot_own[...].astype(F32) + norm_back(upstream2, gain2_ref[...], unit2, rate2)
    middle_low = grad_middle.astype(BF)

    back_ref[...] = jnp.zeros_like(back_ref)
    part_ref[...] = jnp.zeros_like(part_ref)

    def attend_back(rank, carry):
        go_ref[...] = nt(middle_low, wout_ref[rank]).astype(BF)
        mix_grad_ref[rank, :, 3 * TILE:] = tn(middle_low, o_ref[rank]).astype(BF)
        go_pair = split_heads(go_ref[...])
        grad_probs = nt(go_pair, kv_ref[rank, :, TILE:])
        probs = probs_ref[rank].astype(F32)
        inner = jnp.sum(probs * grad_probs, axis=-1, keepdims=True)
        grad_scores = (probs * (grad_probs - inner) * (CHD ** -0.5)).astype(BF)
        q_pair = split_heads(q_ref[rank])
        gkv_ref[:, 0:TILE] = tn(grad_scores, q_pair).astype(BF)
        gkv_ref[:, TILE:] = tn(probs_ref[rank], go_pair).astype(BF)
        pair = jnp.concatenate([grad_scores[0:words], grad_scores[words:]], axis=1)
        gq_ref[...] = nn(pair, split_heads(kv_ref[rank, :, 0:TILE])).astype(BF)
        part_ref[...] += nt(gkv_ref[0:2 * words, :], wqkv_ref[rank, :, TILE:])
        back_ref[...] += nt(gkv_ref[2 * words:, :], wqkv_ref[rank, :, TILE:])
        back_ref[...] += nt(gq_ref[...], wqkv_ref[rank, :, 0:TILE])
        mix_grad_ref[rank, :, 0:TILE] = tn(n1_ref[2 * words:, :], gq_ref[...]).astype(BF)
        mix_grad_ref[rank, :, TILE:3 * TILE] = tn(n1_ref[...], gkv_ref[...]).astype(BF)
        return carry

    lax.fori_loop(0, RANKS, attend_back, 0)
    near_ref_low = got_ref.at[2]
    near_ref_low[...] = part_ref[...].astype(BF).reshape(2, words, wide)
    sends = []
    for slot, offset in ((0, RANKS - 2), (1, RANKS - 1)):
        sends.append(remote(got_ref.at[2, slot], got_ref.at[slot, 0], (send_sem.at[slot], recv_sem.at[slot]),
                            p.ring_device(offset)))
    for copy in sends:
        copy.start()
    for copy in sends:
        copy.wait()
    upstream1 = back_ref[...] + got_ref[0, 0].astype(F32) + got_ref[1, 0].astype(F32)
    dgain_ref[0:1, :] = jnp.sum(upstream1 * unit1, axis=0, keepdims=True)
    grad_vec = (grad_middle + norm_back(upstream1, gain1_ref[...], unit1, rate1)).astype(BF)
    dproj_ref[...] = tn(pooled_ref[...], grad_vec).astype(BF)
    gpl_ref[...] = nt(grad_vec, wproj_ref[...])


def word_layer(bits, vec, near, doc_ids, cotangent, wqkv, wout, wup, wdown, gain1, gain2, wproj, pooled):
    words, wide = vec.shape
    width = pooled.shape[1]
    window = 3 * words
    hidden = wup.shape[2]
    vm = pl.BlockSpec(memory_space=pltpu.VMEM)
    return pl.pallas_call(
        functools.partial(word_kernel, bits),
        in_specs=[vm] * 3 + [pl.BlockSpec(memory_space=pl.ANY)] + [vm] * 8,
        out_specs=[vm] * 7,
        out_shape=[
            jax.ShapeDtypeStruct((words, wide), BF),
            jax.ShapeDtypeStruct((words, width), F32),
            jax.ShapeDtypeStruct((width, wide), BF),
            jax.ShapeDtypeStruct((8, wide), F32),
        ] + [
            jax.ShapeDtypeStruct((RANKS, wide, wide), BF) for _ in range(3)
        ],
        scratch_shapes=[
            pltpu.VMEM((window, wide), BF),
            pltpu.VMEM((RANKS, words, TILE), BF),
            pltpu.VMEM((RANKS, window, 2 * TILE), BF),
            pltpu.VMEM((RANKS, 2 * words, window), BF),
            pltpu.VMEM((RANKS, words, TILE), BF),
            pltpu.VMEM((RANKS, words, hidden), BF),
            pltpu.VMEM((RANKS, words, hidden), BF),
            pltpu.VMEM((words, TILE), BF),
            pltpu.VMEM((words, TILE), BF),
            pltpu.VMEM((window, 2 * TILE), BF),
            pltpu.VMEM((words, wide), F32),
            pltpu.VMEM((words, wide), BF),
            pltpu.SemaphoreType.DMA,
            pltpu.VMEM((2 * words, wide), F32),
            pltpu.VMEM((3, 2, words, wide), BF),
            pltpu.VMEM((1, 2 * words + doc_ids.shape[1]), jnp.int32),
            pltpu.SemaphoreType.DMA((2,)),
            pltpu.SemaphoreType.DMA((2,)),
        ],
        compiler_params=pltpu.CompilerParams(
            vmem_limit_bytes=62 << 20, collective_id=1, has_side_effects=True),
        name="word_layer",
    )(vec, near, doc_ids, cotangent, wqkv, wout, wup, wdown,
      gain1[None, :], gain2[None, :], wproj, pooled)


CHAINS = 6
PLAN = (
    (0, 2, 7, 10, 14, 16, 20,),
    (1, 5, 10, 13, 18, 22,),
    (2, 11, 15, 19,),
    (1, 4, 9, 12, 15, 19,),
    (7, 9, 14, 16,),
    (15, 17, 22,),
)


def char_backward_kernel(slots, bits, x_ref, counts_ref, gain1_ref, wq_ref, wk_ref, wv_ref, wout_ref, gain2_ref,
                         wup_ref, wdown_ref, gpl_ref, act_pool_ref, dproj_ref, wgain_ref, qkv_ref, probs_ref,
                         mixed_ref, first_ref, slope_ref, up_grad_ref, down_grad_ref, mix_grad_ref,
                         dx_ref, up_out, down_out, mix_out, early_out, mid_out, late_out,
                         down_ref, gq_ref, gmix_ref, gup_ref, spread_ref, dgain_ref, dqkv_ref, dout_ref, dup_ref,
                         all_ref, wqkv_ref, table_ref, early_ref, mid_ref, late_ref, *rest):
    step = pl.program_id(0)
    steps = pl.num_programs(0)
    half_steps = CHAR_STEPS
    rows, width = x_ref.shape
    words = rows // slots
    p = Place()
    send_sem, recv_sem, own_sem = rest[-3:]
    sources = (up_grad_ref, down_grad_ref, mix_grad_ref, early_ref, mid_ref, late_ref)
    results = (up_out, down_out, mix_out, early_out, mid_out, late_out)
    outs = rest[6 * CHAINS:7 * CHAINS]
    leave = [pltpu.make_async_copy(out, result, own_sem.at[CHAINS + index])
             for index, (out, result) in enumerate(zip(outs, results))]
    word_chains = 3
    chains, first_sem = [], 0
    for index in range(CHAINS):
        everywhere = index >= word_chains
        refs = tuple(rest[6 * index:6 * index + 6]) + (outs[index],)
        chains.append(Chain(p, bits, sources[index], refs, Sems(send_sem, recv_sem, first_sem), everywhere))
        first_sem += chain_copies(bits, everywhere)

    @pl.when(step == 0)
    def _():
        meet(p.mates(bits) + [p.ring_device(offset) for offset in (1, 2, 3)])
        for index in range(word_chains):
            chains[index].fetch(own_sem.at[index]).start()

    low = lambda value: value.astype(BF)

    @pl.when(step == 0)
    def _():
        dgain_ref[...] = jnp.zeros_like(dgain_ref)
        dqkv_ref[...] = jnp.zeros_like(dqkv_ref)
        dout_ref[...] = jnp.zeros_like(dout_ref)
        dup_ref[...] = jnp.zeros_like(dup_ref)
        grad_down = low(tn(act_pool_ref[...], low(gpl_ref[...])))
        quarter = early_ref.shape[1]
        for index in range(RANKS):
            early_ref[index, :, 0:width] = grad_down[index * quarter:(index + 1) * quarter]
            early_ref[index, :, width:] = grad_down[(RANKS + index) * quarter:(RANKS + index + 1) * quarter]
        split_counts(counts_ref, table_ref, words)
        join_lanes((wq_ref, wk_ref, wv_ref), wqkv_ref)
        scaled = gpl_ref[...] * (1.0 / column(counts_ref[...].astype(F32)))
        down_ref[:, width:] = nt(scaled.astype(BF), wdown_ref[...])
        down_ref[:, :width] = scaled

    @pl.when(step < half_steps)
    def _():
        here = rows_at(step * rows, rows)
        for word in range(words):
            line = down_ref[pl.ds(step * words + word, 1), :width]
            at = slice(word * slots, (word + 1) * slots)
            gq_ref[at, :width] = jnp.broadcast_to(line, (slots, width))
            line = down_ref[pl.ds(step * words + word, 1), width:]
            gup_ref[at, :] = (jnp.broadcast_to(line, (slots, line.shape[1])) * slope_ref[at, :].astype(F32)).astype(BF)

        valid_col = any_lane(valid_slots(rows, slots, table_ref[pl.ds(step, 1), 0:words]))
        unit2, rate2 = norm_parts(first_ref[...])
        dup_ref[...] += tn((unit2 * gain2_ref[...]).astype(BF), gup_ref[...])
        upstream = nt(gup_ref[...], wup_ref[...])
        dgain_ref[1:2, :] += jnp.sum(upstream * unit2, axis=0, keepdims=True)
        grad_first = jnp.where(valid_col, gq_ref[:, :width], 0.0) + norm_back(upstream, gain2_ref[...], unit2, rate2)
        spread_ref[here, :] = grad_first
        grad_low = low(grad_first)
        dout_ref[...] += tn(mixed_ref[...], grad_low)
        gmix_ref[here, :] = low(nt(grad_low, wout_ref[...]))

    @pl.when(step == half_steps - 1)
    def _():
        mid_ref[0] = low(dup_ref[:, 0:2 * width])
        mid_ref[1] = low(dup_ref[:, 2 * width:])
        mid_ref[2] = dproj_ref[...]
        half = width // 2
        mid_ref[3, 0:half, 0:width] = low(dout_ref[0:half, :])
        mid_ref[3, 0:half, width:] = low(dout_ref[half:, :])
        mid_ref[3, half:, :] = jnp.zeros_like(mid_ref[3, half:, :])
        both = jnp.concatenate([dgain_ref[...], dgain_ref[...]], axis=1)
        mid_ref[3, half:half + 16, :] = low(jnp.concatenate([wgain_ref[...], both], axis=0))

    @pl.when((step >= half_steps) & (step < 2 * half_steps))
    def _():
        base = (step - half_steps) * rows
        for tile in range(rows // TILE):
            at = pl.ds(tile * TILE, TILE)
            here = rows_at(base + tile * TILE, TILE)
            for pair in range(CHEADS // 2):
                c0 = pair * TILE
                queries = split_heads(qkv_ref[at, c0:c0 + TILE])
                keys = split_heads(qkv_ref[at, width + c0:width + c0 + TILE])
                values = qkv_ref[at, 2 * width + c0:2 * width + c0 + TILE]
                grads = split_heads(gmix_ref[here, c0:c0 + TILE])
                probs_low = probs_ref[tile, pair]
                probs = probs_low.astype(F32)
                grad_probs = compact(nt(values, grads), slots)
                inner = jnp.sum(probs * grad_probs, axis=0, keepdims=True)
                grad_scores = (probs * (grad_probs - inner) * (CHD ** -0.5)).astype(BF)
                wide_scores = expand(grad_scores, slots)
                wide_probs = expand(probs_low, slots)
                all_ref[here, c0:c0 + TILE] = tn(stack_lanes(wide_scores), keys).astype(BF)
                all_ref[here, width + c0:width + c0 + TILE] = nn(wide_scores, queries).astype(BF)
                all_ref[here, 2 * width + c0:2 * width + c0 + TILE] = nn(wide_probs, grads).astype(BF)
        unit1, _ = norm_parts(x_ref[...].astype(F32))
        dqkv_ref[...] += tn((unit1 * gain1_ref[...]).astype(BF), all_ref[rows_at(base, rows), :])

    @pl.when(step == 2 * half_steps - 1)
    def _():
        half = width // 2
        for index in range(2):
            late_ref[index] = low(dqkv_ref[index * half:(index + 1) * half, 0:2 * width])
            late_ref[2, :, index * width:(index + 1) * width] = low(dqkv_ref[index * half:(index + 1) * half, 2 * width:])
        late_ref[3] = jnp.zeros_like(late_ref[3])

    @pl.when(step >= 2 * half_steps)
    def _():
        here = rows_at((step - 2 * half_steps) * rows, rows)
        unit1, rate1 = norm_parts(x_ref[...].astype(F32))
        upstream1 = nt(all_ref[here, :], wqkv_ref[...])
        dx_ref[...] = low(spread_ref[here, :] + norm_back(upstream1, gain1_ref[...], unit1, rate1))

    for at in range(3 * half_steps):
        todo = [(index, stages.index(at)) for index, stages in reversed(list(enumerate(PLAN))) if at in stages]
        if todo:
            @pl.when(step == at)
            def _(todo=todo):
                for index, stage in todo:
                    if stage == 1 and index < word_chains:
                        chains[index].fetch(own_sem.at[index]).wait()
                    chains[index].step(stage)

    @pl.when(step == steps - 1)
    def _():
        done = [len(stages) for stages in PLAN]
        while any(done[index] <= len(chains[index].stages) for index in range(CHAINS)):
            for index in reversed(range(CHAINS)):
                if done[index] <= len(chains[index].stages):
                    chains[index].step(done[index])
                    done[index] += 1
                    if done[index] > len(chains[index].stages):
                        leave[index].start()
        for copy in leave:
            copy.wait()


def char_backward(bits, x, counts, gain1, weights, wout, gain2, wup, wdown, grad_pooled, saved, grad_proj,
                  word_gains, word_grads):
    qkv, probs, mixed, first, slope, act_pool = saved
    rows, width = x.shape
    words = counts.shape[0]
    slots = rows // words
    hidden = wup.shape[1]
    wide = word_gains.shape[1]
    step = rows // CHAR_STEPS
    last = CHAR_STEPS - 1
    ahead = lambda i: i - ((i // CHAR_STEPS + 1) // 2) * (i - last)
    behind = lambda i: (i // CHAR_STEPS % 2) * (i - CHAR_STEPS) + (i // CHAR_STEPS // 2) * last
    inputs = lambda i: (i % CHAR_STEPS) * ((i // CHAR_STEPS + 1) // 2)
    final = lambda i: (i // CHAR_STEPS // 2) * (i - 2 * CHAR_STEPS)
    ahead_block = lambda cols: pl.BlockSpec((step, cols), lambda i: (ahead(i), 0))
    behind_block = lambda cols: pl.BlockSpec((step, cols), lambda i: (behind(i), 0))
    whole = lambda shape: pl.BlockSpec(shape, lambda i: (0,) * len(shape))
    tiles = step // TILE
    sum_shapes = [(wide, wide)] * 3 + [(RANKS, width // 2, wide), (RANKS, width, wide), (RANKS, width // 2, wide)]
    sources = [(RANKS,) + shape if len(shape) == 2 else shape for shape in sum_shapes]
    copies = sum(chain_copies(bits, index >= 3) for index in range(CHAINS))
    scratch = []
    for shape in sources:
        scratch += chain_scratch(bits, shape[1], wide)
    return pl.pallas_call(
        functools.partial(char_backward_kernel, slots, bits),
        grid=(3 * CHAR_STEPS,),
        in_specs=[
            pl.BlockSpec((step, width), lambda i: (inputs(i), 0)),
            whole((1, words)),
            whole((1, width)),
            whole((width, width)),
            whole((width, width)),
            whole((width, width)),
            whole((width, width)),
            whole((1, width)),
            whole((width, hidden)),
            whole((hidden, width)),
            whole((words, width)),
            whole((words, hidden)),
            whole((width, wide)),
            whole((8, wide)),
            behind_block(3 * width),
            pl.BlockSpec((tiles, CHEADS // 2, slots, 2 * TILE), lambda i: (behind(i), 0, 0, 0)),
            ahead_block(width),
            ahead_block(width),
            ahead_block(hidden),
        ] + [pl.BlockSpec(memory_space=pl.ANY)] * 3,
        out_specs=[pl.BlockSpec((step, width), lambda i: (final(i), 0))] + [pl.BlockSpec(memory_space=pl.ANY)] * CHAINS,
        out_shape=[jax.ShapeDtypeStruct((rows, width), BF)]
        + [jax.ShapeDtypeStruct(shape, BF) for shape in sum_shapes],
        scratch_shapes=[
            pltpu.VMEM((words, width + hidden), F32),
            pltpu.VMEM((step, width), F32),
            pltpu.VMEM((rows, width), BF),
            pltpu.VMEM((step, hidden), BF),
            pltpu.VMEM((rows, width), F32),
            pltpu.VMEM((8, width), F32),
            pltpu.VMEM((width, 3 * width), F32),
            pltpu.VMEM((width, width), F32),
            pltpu.VMEM((width, hidden), F32),
            pltpu.VMEM((rows, 3 * width), BF),
            pltpu.VMEM((width, 3 * width), BF),
            pltpu.VMEM((CHAR_STEPS, TILE), jnp.int32),
        ] + [pltpu.VMEM(shape, BF) for shape in sources[3:]] + scratch
        + [pltpu.VMEM(shape, BF) for shape in sum_shapes] + [pltpu.SemaphoreType.DMA((copies,)), pltpu.SemaphoreType.DMA((copies,)), pltpu.SemaphoreType.DMA((2 * CHAINS,))],
        compiler_params=pltpu.CompilerParams(
            vmem_limit_bytes=63 << 20, collective_id=2, has_side_effects=True),
        name="char_backward",
    )(x, counts[None, :], gain1[None, :], *weights, wout, gain2[None, :],
      wup, wdown, grad_pooled, act_pool, grad_proj, word_gains, qkv, probs, mixed, first, slope, *word_grads)


def unpack_kernel(out_in, dx_in, wq_in, wk_in, wv_in, gain1_in, up_in, down_in, mix_in, early_in, mid_in, late_in,
                  out_ref, dx_ref, gain1_ref, dq_ref, dk_ref, dv_ref, dout_ref, gain2_ref, dup_ref, ddown_ref, dproj_ref,
                  wgain1_ref, wq_ref, wk_ref, wv_ref, wout_ref, wgain2_ref, wup_ref, wdown_ref):
    dx_ref[...] = dx_in[...].astype(F32)
    out_ref[...] = out_in[...]
    width = dout_ref.shape[0]
    half = width // 2

    @pl.when(pl.program_id(0) == 0)
    def _():
        wup_ref[...] = up_in[...].astype(F32)
        wdown_ref[...] = down_in[...].astype(F32)
        wq_ref[...] = mix_in[:, 0:TILE].astype(F32)
        wk_ref[...] = mix_in[:, TILE:2 * TILE].astype(F32)
        wv_ref[...] = mix_in[:, 2 * TILE:3 * TILE].astype(F32)
        wout_ref[...] = mix_in[:, 3 * TILE:].astype(F32).T
        for index in range(RANKS):
            quarter = early_in.shape[1]
            ddown_ref[index * quarter:(index + 1) * quarter, :] = early_in[index, :, 0:width].astype(F32)
            ddown_ref[(RANKS + index) * quarter:(RANKS + index + 1) * quarter, :] = early_in[index, :, width:].astype(F32)
        dup_ref[:, 0:2 * width] = mid_in[0].astype(F32)
        dup_ref[:, 2 * width:] = mid_in[1].astype(F32)
        dproj_ref[...] = mid_in[2].astype(F32)
        gains = mid_in[3, half:half + 16, :].astype(F32)
        wgain1_ref[...] = gains[0:1]
        wgain2_ref[...] = gains[1:2]
        gain2_ref[...] = gains[9:10, 0:width]
        parts = []
        for index in range(2):
            at = slice(index * half, (index + 1) * half)
            cols = slice(index * width, (index + 1) * width)
            total = wq_in[at].astype(F32) * late_in[index, :, 0:width].astype(F32)
            total += wk_in[at].astype(F32) * late_in[index, :, width:].astype(F32)
            total += wv_in[at].astype(F32) * late_in[2, :, cols].astype(F32)
            parts.append(jnp.sum(total, axis=1, keepdims=True))
        sums = jnp.concatenate(parts, axis=0)
        diagonal = (lax.broadcasted_iota(jnp.int32, (width, width), 0)
                    == lax.broadcasted_iota(jnp.int32, (width, width), 1))
        gain1_ref[...] = jnp.sum(jnp.where(diagonal, sums, 0.0), axis=0, keepdims=True) / gain1_in[...]
        for index in range(2):
            at = slice(index * half, (index + 1) * half)
            cols = slice(index * width, (index + 1) * width)
            dout_ref[at, :] = mid_in[3, 0:half, cols].astype(F32)
            dq_ref[at, :] = late_in[index, :, 0:width].astype(F32)
            dk_ref[at, :] = late_in[index, :, width:].astype(F32)
            dv_ref[at, :] = late_in[2, :, cols].astype(F32)


def unpack(word_output, grad_inputs, weights, gain1, sums, width, hidden):
    steps = 8
    rows = grad_inputs.shape[0]
    words, wide = word_output.shape
    whole = lambda shape: pl.BlockSpec(shape, lambda i: (0,) * len(shape))
    split = lambda array: pl.BlockSpec((array.shape[0] // steps, array.shape[1]), lambda i: (i, 0))
    shapes = [(1, width), (width, width), (width, width), (width, width), (width, width), (1, width),
              (width, hidden), (hidden, width), (width, wide),
              (1, wide), (wide, TILE), (wide, TILE), (wide, TILE), (TILE, wide), (1, wide), (wide, wide), (wide, wide)]
    results = pl.pallas_call(
        unpack_kernel,
        grid=(steps,),
        in_specs=[split(word_output), split(grad_inputs)] + [whole((width, width))] * 3 + [whole((1, width))] + [whole(array.shape) for array in sums],
        out_specs=[split(word_output), split(grad_inputs)] + [whole(shape) for shape in shapes],
        out_shape=[jax.ShapeDtypeStruct(word_output.shape, BF), jax.ShapeDtypeStruct(grad_inputs.shape, F32)]
        + [jax.ShapeDtypeStruct(shape, F32) for shape in shapes],
        compiler_params=pltpu.CompilerParams(vmem_limit_bytes=60 << 20),
        name="unpack",
    )(word_output, grad_inputs, *weights, gain1[None, :], *sums)
    return tuple(array[0] if array.shape[0] == 1 else array for array in results)


def per_device(
    bits,
    char_inputs,
    char_counts,
    doc_ids,
    cotangent,
    char_norm_one,
    char_query,
    char_key,
    char_value,
    char_out,
    char_norm_two,
    char_up,
    char_down,
    char_proj,
    word_norm_one,
    word_query,
    word_key,
    word_value,
    word_out_proj,
    word_norm_two,
    word_up,
    word_down,
):
    char_qkv = (char_query, char_key, char_value)
    word_qkv = (word_query, word_key, word_value)
    vec, pooled, *saved, near, qkv_all, out_all, up_all, down_all = char_forward(
        char_inputs, char_counts, char_norm_one, char_qkv, char_out, char_norm_two, char_up, char_down, char_proj,
        word_qkv, word_out_proj, word_up, word_down,
    )
    word_output, grad_pooled, grad_proj, word_gains, *word_grads = word_layer(
        bits, vec, near, doc_ids, cotangent, qkv_all, out_all, up_all, down_all,
        word_norm_one, word_norm_two, char_proj, pooled,
    )
    grad_inputs, *sums = char_backward(
        bits, char_inputs, char_counts, char_norm_one, char_qkv, char_out, char_norm_two, char_up, char_down,
        grad_pooled, saved, grad_proj, word_gains, word_grads,
    )
    return unpack(word_output, grad_inputs, char_qkv, char_norm_one, sums, char_out.shape[0], char_up.shape[1])


def solution(mesh):
    in_specs = (
        P(("dp", "tensor"), None),
        P(("dp", "tensor")),
        P("dp", None),
        P("dp", None),
        P(),
        P(),
        P(),
        P(),
        P(),
        P(),
        P(),
        P(),
        P(),
        P(),
        P(None, "tensor"),
        P(None, "tensor"),
        P(None, "tensor"),
        P("tensor", None),
        P(),
        P(None, "tensor"),
        P("tensor", None),
    )
    out_specs = (
        P(("dp", "tensor"), None),
        P(("dp", "tensor"), None),
        P(),
        P(),
        P(),
        P(),
        P(),
        P(),
        P(),
        P(),
        P(),
        P(),
        P(None, "tensor"),
        P(None, "tensor"),
        P(None, "tensor"),
        P("tensor", None),
        P(),
        P(None, "tensor"),
        P("tensor", None),
    )
    assert mesh.shape["tensor"] == RANKS
    bits = mesh.shape["dp"].bit_length() - 1
    assert bits >= 3 and mesh.shape["dp"] == 1 << bits
    return jax.shard_map(
        functools.partial(per_device, bits), mesh=mesh, in_specs=in_specs, out_specs=out_specs, check_vma=False
    )
```

```python
import functools

import jax
import jax.numpy as jnp
from jax import lax
from jax.experimental import pallas as pl
from jax.experimental.pallas import tpu as pltpu
from jax.sharding import PartitionSpec as P

BF = jnp.bfloat16
F32 = jnp.float32
EPSILON = 1e-05
NEG_LARGE = -1e30
RANKS = 4
CHEADS = 4
CHD = 64
TILE = 128
CHAR_STEPS = 8
GELU_C = 0.7978845608028654
GELU_A = 0.044715


def nn(left, right):
    return lax.dot_general(left, right, (((1,), (0,)), ((), ())), preferred_element_type=F32)


def nt(left, right):
    return lax.dot_general(left, right, (((1,), (1,)), ((), ())), preferred_element_type=F32)


def tn(left, right):
    return lax.dot_general(left, right, (((0,), (0,)), ((), ())), preferred_element_type=F32)


def norm_parts(values):
    centre = values - jnp.mean(values, axis=-1, keepdims=True)
    spread = jnp.mean(centre * centre, axis=-1, keepdims=True)
    rate = lax.rsqrt(spread + EPSILON)
    return centre * rate, rate


def norm_back(upstream, gain, unit, rate):
    scaled = upstream * gain
    first = jnp.mean(scaled, axis=-1, keepdims=True)
    second = jnp.mean(scaled * unit, axis=-1, keepdims=True)
    return rate * (scaled - first - unit * second)


def gelu_parts(values):
    square = values * values
    inner = values * (GELU_C + (GELU_C * GELU_A) * square)
    half = 0.5 + 0.5 * jnp.tanh(inner)
    active = values * half
    slope = half + (active * (1.0 - half)) * (2.0 * GELU_C + (6.0 * GELU_C * GELU_A) * square)
    return active, slope


def split_heads(pair):
    low_half = lax.broadcasted_iota(jnp.int32, pair.shape, 1) < CHD
    zero = jnp.zeros_like(pair)
    return jnp.concatenate([jnp.where(low_half, pair, zero), jnp.where(low_half, zero, pair)], axis=0)


def word_of_lane(shape, slots):
    lane = lax.broadcasted_iota(jnp.int32, shape, 1)
    return jnp.bitwise_and(lane, TILE - 1) // slots


def compact(scores, slots):
    words = word_of_lane((slots, scores.shape[1]), slots)
    result = scores[0:slots]
    for word in range(1, TILE // slots):
        result = jnp.where(words == word, scores[word * slots:(word + 1) * slots], result)
    return result


def expand(packed, slots):
    words = word_of_lane(packed.shape, slots)
    zero = jnp.zeros_like(packed)
    return jnp.concatenate(
        [jnp.where(words == word, packed, zero) for word in range(TILE // slots)], axis=0
    )


def stack_lanes(pair):
    return jnp.concatenate([pair[:, :TILE], pair[:, TILE:]], axis=0)


def split_counts(counts_ref, table_ref, words):
    for step in range(CHAR_STEPS):
        table_ref[step:step + 1, 0:words] = counts_ref[:, step * words:(step + 1) * words]


def valid_slots(rows, slots, mine):
    words = rows // slots
    row = lax.broadcasted_iota(jnp.int32, (rows, words), 0)
    word = lax.broadcasted_iota(jnp.int32, (rows, words), 1)
    return (row // slots == word) & (jnp.bitwise_and(row, slots - 1) < mine)


def join_lanes(parts, whole_ref):
    width = parts[0].shape[1]
    for index, part in enumerate(parts):
        whole_ref[:, index * width:(index + 1) * width] = part[...]


def any_lane(mask):
    return jnp.max(jnp.where(mask, 1.0, 0.0), axis=1, keepdims=True) > 0.0


def column(row):
    size = row.shape[1]
    diagonal = (lax.broadcasted_iota(jnp.int32, (size, size), 0)
                == lax.broadcasted_iota(jnp.int32, (size, size), 1))
    return jnp.sum(jnp.where(diagonal, row, 0.0), axis=1, keepdims=True)


MESH = pl.DeviceIdType.MESH
LANE_SPLIT = 256


class Place:
    def __init__(self):
        self.dp = lax.axis_index("dp")
        self.rank = lax.axis_index("tensor")
        self.core = lax.rem(self.dp, 2)
        self.x = lax.rem(self.dp // 2, 2)
        self.y = lax.rem(self.dp // 4, 2)
        self.core_mate = (self.dp + 1 - 2 * self.core, self.rank)
        self.x_mate = (self.dp + 2 - 4 * self.x, self.rank)
        self.y_mate = (self.dp + 4 - 8 * self.y, self.rank)

    def ring(self, offset):
        return lax.rem(self.rank + offset, RANKS)

    def ring_device(self, offset):
        return (self.dp, self.ring(offset))

    def bit_mate(self, bit):
        size = 1 << bit
        mine = lax.rem(self.dp // size, 2)
        return (self.dp + size - 2 * size * mine, self.rank)

    def mates(self, bits):
        extra = [self.bit_mate(bit) for bit in range(3, bits)]
        return [self.core_mate, self.x_mate, self.y_mate] + extra


def meet(devices):
    barrier = pltpu.get_barrier_semaphore()
    for device in devices:
        pl.semaphore_signal(barrier, inc=1, device_id=device, device_id_type=MESH)
    pl.semaphore_wait(barrier, len(devices))


def remote(source, target, sems, device):
    return pltpu.make_async_remote_copy(
        src_ref=source, dst_ref=target, send_sem=sems[0], recv_sem=sems[1],
        device_id=device, device_id_type=MESH,
    )


class Sems:
    def __init__(self, send, recv, start=0):
        self.send, self.recv, self.next = send, recv, start

    def take(self):
        at = self.next
        self.next += 1
        return self.send.at[at], self.recv.at[at]


def rows_at(start, size):
    return pl.ds(pl.multiple_of(start, 16), size)


def halves(width):
    return (slice(0, LANE_SPLIT), slice(LANE_SPLIT, width))


class Gather:
    def __init__(self, place, local, whole, sems):
        self.stages = [[], [], [], []]
        rows = local.shape[0]
        unit = rows // 8
        p = place
        left, right = halves(local.shape[1])
        left_at = p.core * 4 + p.x * 2 + p.y
        right_at = p.core * 4 + p.y * 2 + p.x
        for offset in range(1, RANKS):
            for lanes, at in ((left, left_at), (right, right_at)):
                at = rows_at(at * unit, unit)
                self.stages[0].append(remote(
                    local.at[at, lanes], whole.at[p.rank, at, lanes], sems.take(), p.ring_device(offset)))
        for offset in range(1, RANKS):
            rank = p.ring(offset)
            for lanes, at, first, second, mate_first, mate_second in (
                (left, left_at, p.x, None, p.y_mate, p.x_mate),
                (right, right_at, p.y, None, p.x_mate, p.y_mate),
            ):
                one = rows_at(at * unit, unit)
                two = rows_at((p.core * 4 + first * 2) * unit, 2 * unit)
                self.stages[1].append(remote(
                    whole.at[rank, one, lanes], whole.at[rank, one, lanes], sems.take(), mate_first))
                self.stages[2].append(remote(
                    whole.at[rank, two, lanes], whole.at[rank, two, lanes], sems.take(), mate_second))
            four = rows_at(p.core * 4 * unit, 4 * unit)
            self.stages[3].append(remote(
                whole.at[rank, four], whole.at[rank, four], sems.take(), p.core_mate))

    def start(self, stage):
        for copy in self.stages[stage]:
            copy.start()

    def wait(self, stage):
        for copy in self.stages[stage]:
            copy.wait()


def gather_copies():
    return 2 * (RANKS - 1) * 3 + (RANKS - 1)


class Chain:
    def __init__(self, place, bits, src, refs, sems, everywhere):
        p = place
        buf, got_core, got_one, got_two, got_more, got_rank, out = refs
        self.p, self.src, self.everywhere = p, src, everywhere
        self.buf, self.got_core, self.got_one, self.got_two = buf, got_core, got_one, got_two
        self.got_more, self.got_rank = got_more, got_rank
        self.mine = out.at[p.rank] if everywhere else out
        unit = src.shape[1] // 8
        lanes = left, right = halves(src.shape[2])
        self.lanes = lanes
        self.own = rows_at(p.core * 4 * unit, 4 * unit)
        stages = [("core", [remote(src.at[:, rows_at((1 - p.core) * 4 * unit, 4 * unit)], got_core,
                                   sems.take(), p.core_mate)])]
        first, second = (p.x, p.y), (p.y, p.x)
        first_mate, second_mate = (p.x_mate, p.y_mate), (p.y_mate, p.x_mate)
        one = lambda side, at: rows_at(at * 2 * unit, 2 * unit)
        two = lambda side, at: rows_at((first[side] * 2 + at) * unit, unit)
        self.one_rows = [one(side, first[side]) for side in (0, 1)]
        self.two_rows = [two(side, second[side]) for side in (0, 1)]
        stages.append(("one", [
            remote(buf.at[:, one(side, 1 - first[side]), lanes[side]], got_one.at[:, :, lanes[side]],
                   sems.take(), first_mate[side]) for side in (0, 1)]))
        stages.append(("two", [
            remote(buf.at[:, two(side, 1 - second[side]), lanes[side]], got_two.at[:, :, lanes[side]],
                   sems.take(), second_mate[side]) for side in (0, 1)]))
        for bit in range(3, bits):
            stages.append((bit - 3, [
                remote(buf.at[:, self.two_rows[side], lanes[side]], got_more.at[bit - 3, :, :, lanes[side]],
                       sems.take(), p.bit_mate(bit)) for side in (0, 1)]))
        stages.append(("rank", [
            remote(buf.at[p.ring(offset), self.two_rows[side], lanes[side]],
                   got_rank.at[offset - 1, :, lanes[side]], sems.take(), p.ring_device(offset))
            for offset in range(1, RANKS) for side in (0, 1)]))
        base = p.core * 4 * unit
        self.out_two = [rows_at(base + (first[side] * 2 + second[side]) * unit, unit) for side in (0, 1)]
        out_one = [rows_at(base + first[side] * 2 * unit, 2 * unit) for side in (0, 1)]
        if everywhere:
            stages.append(("rank_back", [
                remote(out.at[p.rank, self.out_two[side], lanes[side]], out.at[p.rank, self.out_two[side], lanes[side]],
                       sems.take(), p.ring_device(offset))
                for offset in range(1, RANKS) for side in (0, 1)]))

        def back(at, part_lanes, mate):
            part = out.at[:, at, part_lanes] if everywhere else out.at[at, part_lanes]
            return remote(part, part, sems.take(), mate)

        stages.append(("back_two", [back(self.out_two[side], lanes[side], second_mate[side]) for side in (0, 1)]))
        stages.append(("back_one", [back(out_one[side], lanes[side], first_mate[side]) for side in (0, 1)]))
        stages.append(("back_core", [back(self.own, slice(None), p.core_mate)]))
        self.stages = stages

    def fetch(self, sem):
        return pltpu.make_async_copy(self.src.at[:, self.own], self.buf, sem)

    def start(self, index):
        for copy in self.stages[index][1]:
            copy.start()

    def finish(self, index):
        name, copies = self.stages[index]
        for copy in copies:
            copy.wait()
        buf = self.buf
        if name == "core":
            own = self.src if self.everywhere else None
            for quarter in range(RANKS):
                mine = own[quarter, self.own, :] if self.everywhere else buf[quarter]
                buf[quarter] = mine + self.got_core[quarter]
        elif name == "one":
            for at, lanes in zip(self.one_rows, self.lanes):
                for quarter in range(RANKS):
                    buf[quarter, at, lanes] += self.got_one[quarter, :, lanes]
        elif name == "two":
            for at, lanes in zip(self.two_rows, self.lanes):
                for quarter in range(RANKS):
                    buf[quarter, at, lanes] += self.got_two[quarter, :, lanes]
        elif name == "rank":
            for side in (0, 1):
                at, lanes = self.two_rows[side], self.lanes[side]
                total = buf[self.p.rank, at, lanes].astype(F32)
                for k in range(RANKS - 1):
                    total = total + self.got_rank[k, :, lanes].astype(F32)
                self.mine[self.out_two[side], lanes] = total.astype(BF)
        elif isinstance(name, int):
            for at, lanes in zip(self.two_rows, self.lanes):
                for quarter in range(RANKS):
                    buf[quarter, at, lanes] += self.got_more[name, quarter, :, lanes]

    def step(self, index):
        if index:
            self.finish(index - 1)
        if index < len(self.stages):
            self.start(index)


def chain_copies(bits, everywhere):
    pairs = 2 * (RANKS - 1)
    return 1 + 2 + 2 + 2 * (bits - 3) + pairs + (pairs if everywhere else 0) + 2 + 2 + 1


def chain_scratch(bits, rows, lanes):
    unit = rows // 8
    return [
        pltpu.VMEM((RANKS, 4 * unit, lanes), BF),
        pltpu.VMEM((RANKS, 4 * unit, lanes), BF),
        pltpu.VMEM((RANKS, 2 * unit, lanes), BF),
        pltpu.VMEM((RANKS, unit, lanes), BF),
        pltpu.VMEM((max(bits - 3, 1), RANKS, unit, lanes), BF),
        pltpu.VMEM((RANKS - 1, unit, lanes), BF),
    ]


FORWARD_PLAN = {
    2: ((0, 1), (1, 1)),
    3: ((2, 1), (0, 2), (1, 2)),
    4: ((3, 1), (2, 2)),
    5: ((0, 3), (1, 3), (3, 2)),
    6: ((2, 3),),
    7: ((3, 3),),
}


def char_forward_kernel(slots, x_ref, counts_ref, gain1_ref, wq_ref, wk_ref, wv_ref, wout_ref,
                        gain2_ref, wup_ref, wdown_ref, wproj_ref,
                        lq_ref, lk_ref, lv_ref, lout_ref, lup_ref, ldown_ref,
                        vec_ref, pooled_ref, qkv_ref, probs_ref, mixed_ref, first_ref,
                        slope_ref, act_pool_ref, near_ref, wqkv_all, wout_all, wup_all, wdown_all,
                        wqkv_ref, lqkv_ref, table_ref, own_sem, send_sem, recv_sem):
    rows = x_ref.shape[0]
    width = x_ref.shape[1]
    step = pl.program_id(0)
    steps = pl.num_programs(0)
    words = rows // slots
    p = Place()
    pairs = ((lqkv_ref, wqkv_all), (lout_ref, wout_all), (lup_ref, wup_all), (ldown_ref, wdown_all))
    gathers = [Gather(p, mine, whole, Sems(send_sem, recv_sem, gather_copies() * index))
               for index, (mine, whole) in enumerate(pairs)]
    own_copies = [pltpu.make_async_copy(mine, whole.at[p.rank], own_sem.at[index])
                  for index, (mine, whole) in enumerate(pairs)]
    vec_base = gather_copies() * len(pairs)

    def vec_copies(at):
        copies = []
        for slot, offset in ((1, 1), (0, 2)):
            sem = vec_base + 2 * at + slot
            part = rows_at(at * words, words)
            copies.append(remote(vec_ref.at[part], near_ref.at[slot, part],
                                 (send_sem.at[sem], recv_sem.at[sem]), p.ring_device(offset)))
        return copies

    def send_vec(at):
        for offset, copy in zip((1, 2), vec_copies(at)):
            @pl.when(p.rank + offset < RANKS)
            def _(copy=copy):
                copy.start()

    def wait_vec(at):
        for offset, copy in zip((1, 2), vec_copies(at)):
            @pl.when(p.rank + offset < RANKS)
            def _(copy=copy):
                copy.wait_send()

            @pl.when(p.rank >= offset)
            def _(copy=copy):
                copy.wait_recv()

    @pl.when(step == 0)
    def _():
        join_lanes((lq_ref, lk_ref, lv_ref), lqkv_ref)
        join_lanes((wq_ref, wk_ref, wv_ref), wqkv_ref)
        meet([p.ring_device(offset) for offset in (1, 2, 3)] + [p.core_mate, p.x_mate, p.y_mate])
        split_counts(counts_ref, table_ref, words)
        for copy in own_copies:
            copy.start()
        for gather in gathers:
            gather.start(0)

    base = x_ref[...].astype(F32)
    unit, _ = norm_parts(base)
    normed = (unit * gain1_ref[...]).astype(BF)
    qkv_ref[...] = nn(normed, wqkv_ref[...]).astype(BF)
    mine = table_ref[pl.ds(step, 1), 0:words]
    word_at = lax.broadcasted_iota(jnp.int32, (words, rows), 0)
    row_at = lax.broadcasted_iota(jnp.int32, (words, rows), 1)
    onto_rows = jnp.where(row_at // slots == word_at, 1.0, 0.0).astype(BF)
    row_counts = nn(jnp.broadcast_to(mine.astype(F32), (16, words)).astype(BF), onto_rows)[0:1]
    for tile in range(rows // TILE):
        at = pl.ds(tile * TILE, TILE)
        valid = (lax.broadcasted_iota(jnp.int32, (slots, TILE), 0).astype(F32)
                 < row_counts[:, tile * TILE:(tile + 1) * TILE])
        for pair in range(CHEADS // 2):
            c0 = pair * TILE
            queries = split_heads(qkv_ref[at, c0:c0 + TILE])
            keys = qkv_ref[at, width + c0:width + c0 + TILE]
            values = split_heads(qkv_ref[at, 2 * width + c0:2 * width + c0 + TILE])
            scores = compact(nt(keys, queries), slots)
            parts = []
            for head in range(2):
                own = jnp.where(valid, scores[:, head * TILE:(head + 1) * TILE], NEG_LARGE)
                top = jnp.max(own, axis=0, keepdims=True)
                weight = jnp.exp((own - top) * (CHD ** -0.5))
                parts.append(weight / jnp.sum(weight, axis=0, keepdims=True))
            probs = jnp.concatenate(parts, axis=1).astype(BF)
            probs_ref[tile, pair] = probs
            mixed_ref[at, c0:c0 + TILE] = tn(stack_lanes(expand(probs, slots)), values).astype(BF)

    for at, todo in FORWARD_PLAN.items():
        @pl.when(step == at)
        def _(todo=todo):
            for member, stage in todo:
                gathers[member].wait(stage - 1)
                gathers[member].start(stage)

    @pl.when(step > 0)
    def _():
        send_vec(step - 1)

    first = base + nn(mixed_ref[...], wout_ref[...])
    first_ref[...] = first
    unit2, _ = norm_parts(first)
    normed2 = (unit2 * gain2_ref[...]).astype(BF)
    members = valid_slots(rows, slots, mine)
    valid_col = any_lane(members)
    pool = jnp.where(members, 1.0 / mine.astype(F32), 0.0).astype(BF)
    chunk = 256
    for part in range(wup_ref.shape[1] // chunk):
        cols = slice(part * chunk, (part + 1) * chunk)
        active, slope = gelu_parts(nn(normed2, wup_ref[:, cols]))
        slope_ref[:, cols] = jnp.where(valid_col, slope, 0.0).astype(BF)
        act_pool_ref[:, cols] = tn(pool, active.astype(BF)).astype(BF)
    pooled = tn(pool, first.astype(BF)) + nn(act_pool_ref[...], wdown_ref[...])
    pooled = pooled.astype(BF)
    pooled_ref[...] = pooled
    vec_ref[rows_at(step * words, words), :] = nn(pooled, wproj_ref[...]).astype(BF)

    @pl.when(step == steps - 1)
    def _():
        send_vec(step)
        for copy in own_copies:
            copy.wait()
        for gather in gathers:
            gather.wait(3)
        for at in range(CHAR_STEPS):
            wait_vec(at)


def char_forward(x, counts, gain1, weights, wout, gain2, wup, wdown, wproj, local, lout, lup, ldown):
    rows, width = x.shape
    words = counts.shape[0]
    slots = rows // words
    hidden = wup.shape[1]
    wide = wproj.shape[1]
    step = rows // CHAR_STEPS
    step_words = step // slots
    row_block = lambda cols: pl.BlockSpec((step, cols), lambda i: (i, 0))
    word_block = lambda cols: pl.BlockSpec((step_words, cols), lambda i: (i, 0))
    whole = lambda shape: pl.BlockSpec(shape, lambda i: (0, 0))
    tiles = step // TILE
    return pl.pallas_call(
        functools.partial(char_forward_kernel, slots),
        grid=(rows // step,),
        in_specs=[
            row_block(width),
            whole((1, words)),
            whole((1, width)),
            whole((width, width)),
            whole((width, width)),
            whole((width, width)),
            whole((width, width)),
            whole((1, width)),
            whole((width, hidden)),
            whole((hidden, width)),
            whole((width, wide)),
            whole(local[0].shape),
            whole(local[0].shape),
            whole(local[0].shape),
            whole(lout.shape),
            whole(lup.shape),
            whole(ldown.shape),
        ],
        out_specs=[
            whole((words, wide)),
            word_block(width),
            row_block(3 * width),
            pl.BlockSpec((tiles, CHEADS // 2, slots, 2 * TILE), lambda i: (i, 0, 0, 0)),
            row_block(width),
            row_block(width),
            row_block(hidden),
            word_block(hidden),
        ] + [pl.BlockSpec(memory_space=pl.ANY)] * 5,
        out_shape=[
            jax.ShapeDtypeStruct((words, wide), BF),
            jax.ShapeDtypeStruct((words, width), BF),
            jax.ShapeDtypeStruct((rows, 3 * width), BF),
            jax.ShapeDtypeStruct((rows // TILE, CHEADS // 2, slots, 2 * TILE), BF),
            jax.ShapeDtypeStruct((rows, width), BF),
            jax.ShapeDtypeStruct((rows, width), F32),
            jax.ShapeDtypeStruct((rows, hidden), BF),
            jax.ShapeDtypeStruct((words, hidden), BF),
            jax.ShapeDtypeStruct((2, words, wide), BF),
            jax.ShapeDtypeStruct((RANKS, wide, 3 * TILE), BF),
            jax.ShapeDtypeStruct((RANKS,) + lout.shape, BF),
            jax.ShapeDtypeStruct((RANKS,) + lup.shape, BF),
            jax.ShapeDtypeStruct((RANKS,) + ldown.shape, BF),
        ],
        scratch_shapes=[
            pltpu.VMEM((width, 3 * width), BF),
            pltpu.VMEM((wide, 3 * TILE), BF),
            pltpu.VMEM((CHAR_STEPS, TILE), jnp.int32),
            pltpu.SemaphoreType.DMA((4,)),
            pltpu.SemaphoreType.DMA((gather_copies() * 4 + 2 * CHAR_STEPS,)),
            pltpu.SemaphoreType.DMA((gather_copies() * 4 + 2 * CHAR_STEPS,)),
        ],
        compiler_params=pltpu.CompilerParams(
            vmem_limit_bytes=60 << 20, collective_id=0, has_side_effects=True),
        name="char_forward",
    )(x, counts[None, :], gain1[None, :], *weights, wout, gain2[None, :], wup, wdown, wproj,
      *local, lout, lup, ldown)


def word_kernel(bits, vec_ref, near_ref, docs_ref, cot_ref, wqkv_in, wout_in, wup_in,
                wdown_in, gain1_ref, gain2_ref, wproj_ref, pooled_ref,
                out_ref, gpl_ref, dproj_ref, dgain_ref, up_grad_out, down_grad_out, mix_grad_out,
                n1_ref, q_ref, kv_ref, probs_ref, o_ref, act_ref, slope_ref, go_ref, gq_ref, gkv_ref,
                back_ref, cot_own, cot_sem, part_ref, got_ref, table_ref, wqkv_ref, wout_ref, wup_ref, wdown_ref,
                up_grad_ref, down_grad_ref, mix_grad_ref, io_sem, send_sem, recv_sem):
    p = Place()
    words, wide = vec_ref.shape
    window = 3 * words
    fetch = pltpu.make_async_copy(cot_ref.at[rows_at(p.rank * words, words)], cot_own, cot_sem)
    loads = [pltpu.make_async_copy(source, target, io_sem.at[index]) for index, (source, target) in enumerate((
        (wqkv_in, wqkv_ref), (wout_in, wout_ref), (wup_in, wup_ref), (wdown_in, wdown_ref)))]
    stores = [pltpu.make_async_copy(source, target, io_sem.at[4 + index]) for index, (source, target) in enumerate((
        (up_grad_ref, up_grad_out), (down_grad_ref, down_grad_out)))]

    def store_mix(rank):
        return pltpu.make_async_copy(mix_grad_ref.at[rank], mix_grad_out.at[rank], io_sem.at[6 + rank])

    for copy in loads:
        copy.start()
    fetch.start()
    meet([p.ring_device(offset) for offset in (1, 2, 3)])

    table_ref[:, 0:2 * words] = jnp.full((1, 2 * words), -1, jnp.int32)
    table_ref[:, 2 * words:] = docs_ref[...]
    start = pl.multiple_of(p.rank * words, TILE)
    key_docs = table_ref[:, pl.ds(start, window)].astype(F32)
    row_docs = column(key_docs[:, 2 * words:])

    own = vec_ref[...].astype(F32)
    unit1, rate1 = norm_parts(own)
    n1_ref[2 * words:, :] = (unit1 * gain1_ref[...]).astype(BF)
    for slot in range(2):
        near = jnp.where(p.rank + slot >= 2, near_ref[slot].astype(F32), 0.0)
        unit, _ = norm_parts(near)
        n1_ref[slot * words:(slot + 1) * words, :] = (unit * gain1_ref[...]).astype(BF)

    def project(rank, carry):
        q_ref[rank] = nn(n1_ref[2 * words:, :], wqkv_ref[rank, :, 0:TILE]).astype(BF)
        kv_ref[rank] = nn(n1_ref[...], wqkv_ref[rank, :, TILE:]).astype(BF)
        scores = nt(split_heads(q_ref[rank]), kv_ref[rank, :, 0:TILE]) * (CHD ** -0.5)
        row = lax.broadcasted_iota(jnp.int32, (words, window), 0)
        key = lax.broadcasted_iota(jnp.int32, (words, window), 1)
        allowed = (row_docs == key_docs) & (key <= row + 2 * words)
        for head in range(2):
            at = slice(head * words, (head + 1) * words)
            masked = jnp.where(allowed, scores[at], NEG_LARGE)
            top = jnp.max(masked, axis=-1, keepdims=True)
            weight = jnp.exp(masked - top)
            probs_ref[rank, at, :] = (weight * (1.0 / jnp.sum(weight, axis=-1, keepdims=True))).astype(BF)
        pair = jnp.concatenate([probs_ref[rank, 0:words, :], probs_ref[rank, words:, :]], axis=1)
        o_ref[rank] = nn(pair, split_heads(kv_ref[rank, :, TILE:])).astype(BF)
        back_ref[...] += nn(o_ref[rank], wout_ref[rank])
        return carry

    back_ref[...] = own
    loads[0].wait()
    loads[1].wait()
    lax.fori_loop(0, RANKS, project, 0)
    middle = back_ref[...]
    unit2, rate2 = norm_parts(middle)
    normed2 = (unit2 * gain2_ref[...]).astype(BF)

    def feed(rank, carry):
        active, slope = gelu_parts(nn(normed2, wup_ref[rank]))
        act_ref[rank] = active.astype(BF)
        slope_ref[rank] = slope.astype(BF)
        back_ref[...] += nn(act_ref[rank], wdown_ref[rank])
        return carry

    loads[2].wait()
    loads[3].wait()
    lax.fori_loop(0, RANKS, feed, 0)
    out_ref[...] = back_ref[...].astype(BF)
    fetch.wait()
    back_ref[...] = jnp.zeros_like(back_ref)

    def feed_back(rank, carry):
        upstream = (nt(cot_own[...], wdown_ref[rank]) * slope_ref[rank].astype(F32)).astype(BF)
        back_ref[...] += nt(upstream, wup_ref[rank])
        up_grad_ref[rank] = tn(normed2, upstream).astype(BF)
        down_grad_ref[rank] = tn(act_ref[rank], cot_own[...]).astype(BF)
        return carry

    lax.fori_loop(0, RANKS, feed_back, 0)
    for copy in stores:
        copy.start()
    upstream2 = back_ref[...]
    dgain_ref[...] = jnp.zeros_like(dgain_ref)
    dgain_ref[1:2, :] = jnp.sum(upstream2 * unit2, axis=0, keepdims=True)
    grad_middle = cot_own[...].astype(F32) + norm_back(upstream2, gain2_ref[...], unit2, rate2)
    middle_low = grad_middle.astype(BF)

    back_ref[...] = jnp.zeros_like(back_ref)
    part_ref[...] = jnp.zeros_like(part_ref)

    def attend_back(rank, carry):
        go_ref[...] = nt(middle_low, wout_ref[rank]).astype(BF)
        mix_grad_ref[rank, :, 3 * TILE:] = tn(middle_low, o_ref[rank]).astype(BF)
        go_pair = split_heads(go_ref[...])
        grad_probs = nt(go_pair, kv_ref[rank, :, TILE:])
        probs = probs_ref[rank].astype(F32)
        inner = jnp.sum(probs * grad_probs, axis=-1, keepdims=True)
        grad_scores = (probs * (grad_probs - inner) * (CHD ** -0.5)).astype(BF)
        q_pair = split_heads(q_ref[rank])
        gkv_ref[:, 0:TILE] = tn(grad_scores, q_pair).astype(BF)
        gkv_ref[:, TILE:] = tn(probs_ref[rank], go_pair).astype(BF)
        pair = jnp.concatenate([grad_scores[0:words], grad_scores[words:]], axis=1)
        gq_ref[...] = nn(pair, split_heads(kv_ref[rank, :, 0:TILE])).astype(BF)
        part_ref[...] += nt(gkv_ref[0:2 * words, :], wqkv_ref[rank, :, TILE:])
        back_ref[...] += nt(gkv_ref[2 * words:, :], wqkv_ref[rank, :, TILE:])
        back_ref[...] += nt(gq_ref[...], wqkv_ref[rank, :, 0:TILE])
        mix_grad_ref[rank, :, 0:TILE] = tn(n1_ref[2 * words:, :], gq_ref[...]).astype(BF)
        mix_grad_ref[rank, :, TILE:3 * TILE] = tn(n1_ref[...], gkv_ref[...]).astype(BF)
        store_mix(rank).start()
        return carry

    lax.fori_loop(0, RANKS, attend_back, 0)
    near_ref_low = got_ref.at[2]
    near_ref_low[...] = part_ref[...].astype(BF).reshape(2, words, wide)
    sends = []
    for slot, offset in ((0, RANKS - 2), (1, RANKS - 1)):
        sends.append(remote(got_ref.at[2, slot], got_ref.at[slot, 0], (send_sem.at[slot], recv_sem.at[slot]),
                            p.ring_device(offset)))
    for copy in sends:
        copy.start()
    for copy in sends:
        copy.wait()
    upstream1 = back_ref[...] + got_ref[0, 0].astype(F32) + got_ref[1, 0].astype(F32)
    dgain_ref[0:1, :] = jnp.sum(upstream1 * unit1, axis=0, keepdims=True)
    grad_vec = (grad_middle + norm_back(upstream1, gain1_ref[...], unit1, rate1)).astype(BF)
    dproj_ref[...] = tn(pooled_ref[...], grad_vec).astype(BF)
    gpl_ref[...] = nt(grad_vec, wproj_ref[...])
    for copy in stores + [store_mix(rank) for rank in range(RANKS)]:
        copy.wait()


def word_layer(bits, vec, near, doc_ids, cotangent, wqkv, wout, wup, wdown, gain1, gain2, wproj, pooled):
    words, wide = vec.shape
    width = pooled.shape[1]
    window = 3 * words
    hidden = wup.shape[2]
    vm = pl.BlockSpec(memory_space=pltpu.VMEM)
    return pl.pallas_call(
        functools.partial(word_kernel, bits),
        in_specs=[vm] * 3 + [pl.BlockSpec(memory_space=pl.ANY)] * 5 + [vm] * 4,
        out_specs=[vm] * 4 + [pl.BlockSpec(memory_space=pl.ANY)] * 3,
        out_shape=[
            jax.ShapeDtypeStruct((words, wide), BF),
            jax.ShapeDtypeStruct((words, width), F32),
            jax.ShapeDtypeStruct((width, wide), BF),
            jax.ShapeDtypeStruct((8, wide), F32),
        ] + [
            jax.ShapeDtypeStruct((RANKS, wide, wide), BF) for _ in range(3)
        ],
        scratch_shapes=[
            pltpu.VMEM((window, wide), BF),
            pltpu.VMEM((RANKS, words, TILE), BF),
            pltpu.VMEM((RANKS, window, 2 * TILE), BF),
            pltpu.VMEM((RANKS, 2 * words, window), BF),
            pltpu.VMEM((RANKS, words, TILE), BF),
            pltpu.VMEM((RANKS, words, hidden), BF),
            pltpu.VMEM((RANKS, words, hidden), BF),
            pltpu.VMEM((words, TILE), BF),
            pltpu.VMEM((words, TILE), BF),
            pltpu.VMEM((window, 2 * TILE), BF),
            pltpu.VMEM((words, wide), F32),
            pltpu.VMEM((words, wide), BF),
            pltpu.SemaphoreType.DMA,
            pltpu.VMEM((2 * words, wide), F32),
            pltpu.VMEM((3, 2, words, wide), BF),
            pltpu.VMEM((1, 2 * words + doc_ids.shape[1]), jnp.int32),
        ] + [pltpu.VMEM(array.shape, BF) for array in (wqkv, wout, wup, wdown)] + [
            pltpu.VMEM((RANKS, wide, wide), BF),
            pltpu.VMEM((RANKS, wide, wide), BF),
            pltpu.VMEM((RANKS, wide, wide), BF),
            pltpu.SemaphoreType.DMA((6 + RANKS,)),
            pltpu.SemaphoreType.DMA((2,)),
            pltpu.SemaphoreType.DMA((2,)),
        ],
        compiler_params=pltpu.CompilerParams(
            vmem_limit_bytes=62 << 20, collective_id=1, has_side_effects=True),
        name="word_layer",
    )(vec, near, doc_ids, cotangent, wqkv, wout, wup, wdown,
      gain1[None, :], gain2[None, :], wproj, pooled)


CHAINS = 6
PLAN = (
    (0, 2, 7, 10, 14, 16, 20,),
    (1, 5, 10, 13, 18, 22,),
    (2, 11, 15, 19,),
    (1, 4, 9, 12, 15, 19,),
    (7, 9, 14, 16,),
    (15, 17, 22,),
)


def char_backward_kernel(slots, bits, x_ref, counts_ref, gain1_ref, wq_ref, wk_ref, wv_ref, wout_ref, gain2_ref,
                         wup_ref, wdown_ref, gpl_ref, act_pool_ref, dproj_ref, wgain_ref, qkv_ref, probs_ref,
                         mixed_ref, first_ref, slope_ref, up_grad_ref, down_grad_ref, mix_grad_ref,
                         dx_ref, up_out, down_out, mix_out, early_out, mid_out, late_out,
                         down_ref, gq_ref, gmix_ref, gup_ref, spread_ref, dgain_ref, dqkv_ref, dout_ref, dup_ref,
                         all_ref, wqkv_ref, table_ref, early_ref, mid_ref, late_ref, *rest):
    step = pl.program_id(0)
    steps = pl.num_programs(0)
    half_steps = CHAR_STEPS
    rows, width = x_ref.shape
    words = rows // slots
    p = Place()
    send_sem, recv_sem, own_sem = rest[-3:]
    sources = (up_grad_ref, down_grad_ref, mix_grad_ref, early_ref, mid_ref, late_ref)
    results = (up_out, down_out, mix_out, early_out, mid_out, late_out)
    outs = rest[6 * CHAINS:7 * CHAINS]
    leave = [pltpu.make_async_copy(out, result, own_sem.at[CHAINS + index])
             for index, (out, result) in enumerate(zip(outs, results))]
    word_chains = 3
    chains, first_sem = [], 0
    for index in range(CHAINS):
        everywhere = index >= word_chains
        refs = tuple(rest[6 * index:6 * index + 6]) + (outs[index],)
        chains.append(Chain(p, bits, sources[index], refs, Sems(send_sem, recv_sem, first_sem), everywhere))
        first_sem += chain_copies(bits, everywhere)

    @pl.when(step == 0)
    def _():
        meet(p.mates(bits) + [p.ring_device(offset) for offset in (1, 2, 3)])
        for index in range(word_chains):
            chains[index].fetch(own_sem.at[index]).start()

    low = lambda value: value.astype(BF)

    @pl.when(step == 0)
    def _():
        dgain_ref[...] = jnp.zeros_like(dgain_ref)
        dqkv_ref[...] = jnp.zeros_like(dqkv_ref)
        dout_ref[...] = jnp.zeros_like(dout_ref)
        dup_ref[...] = jnp.zeros_like(dup_ref)
        grad_down = low(tn(act_pool_ref[...], low(gpl_ref[...])))
        quarter = early_ref.shape[1]
        for index in range(RANKS):
            early_ref[index, :, 0:width] = grad_down[index * quarter:(index + 1) * quarter]
            early_ref[index, :, width:] = grad_down[(RANKS + index) * quarter:(RANKS + index + 1) * quarter]
        split_counts(counts_ref, table_ref, words)
        join_lanes((wq_ref, wk_ref, wv_ref), wqkv_ref)
        scaled = gpl_ref[...] * (1.0 / column(counts_ref[...].astype(F32)))
        down_ref[:, width:] = nt(scaled.astype(BF), wdown_ref[...])
        down_ref[:, :width] = scaled

    @pl.when(step < half_steps)
    def _():
        here = rows_at(step * rows, rows)
        for word in range(words):
            line = down_ref[pl.ds(step * words + word, 1), :width]
            at = slice(word * slots, (word + 1) * slots)
            gq_ref[at, :width] = jnp.broadcast_to(line, (slots, width))
            line = down_ref[pl.ds(step * words + word, 1), width:]
            gup_ref[at, :] = (jnp.broadcast_to(line, (slots, line.shape[1])) * slope_ref[at, :].astype(F32)).astype(BF)

        valid_col = any_lane(valid_slots(rows, slots, table_ref[pl.ds(step, 1), 0:words]))
        unit2, rate2 = norm_parts(first_ref[...])
        dup_ref[...] += tn((unit2 * gain2_ref[...]).astype(BF), gup_ref[...])
        upstream = nt(gup_ref[...], wup_ref[...])
        dgain_ref[1:2, :] += jnp.sum(upstream * unit2, axis=0, keepdims=True)
        grad_first = jnp.where(valid_col, gq_ref[:, :width], 0.0) + norm_back(upstream, gain2_ref[...], unit2, rate2)
        spread_ref[here, :] = grad_first
        grad_low = low(grad_first)
        dout_ref[...] += tn(mixed_ref[...], grad_low)
        gmix_ref[here, :] = low(nt(grad_low, wout_ref[...]))

    @pl.when(step == half_steps - 1)
    def _():
        mid_ref[0] = low(dup_ref[:, 0:2 * width])
        mid_ref[1] = low(dup_ref[:, 2 * width:])
        mid_ref[2] = dproj_ref[...]
        half = width // 2
        mid_ref[3, 0:half, 0:width] = low(dout_ref[0:half, :])
        mid_ref[3, 0:half, width:] = low(dout_ref[half:, :])
        mid_ref[3, half:, :] = jnp.zeros_like(mid_ref[3, half:, :])
        both = jnp.concatenate([dgain_ref[...], dgain_ref[...]], axis=1)
        mid_ref[3, half:half + 16, :] = low(jnp.concatenate([wgain_ref[...], both], axis=0))

    @pl.when((step >= half_steps) & (step < 2 * half_steps))
    def _():
        base = (step - half_steps) * rows
        for tile in range(rows // TILE):
            at = pl.ds(tile * TILE, TILE)
            here = rows_at(base + tile * TILE, TILE)
            for pair in range(CHEADS // 2):
                c0 = pair * TILE
                queries = split_heads(qkv_ref[at, c0:c0 + TILE])
                keys = split_heads(qkv_ref[at, width + c0:width + c0 + TILE])
                values = qkv_ref[at, 2 * width + c0:2 * width + c0 + TILE]
                grads = split_heads(gmix_ref[here, c0:c0 + TILE])
                probs_low = probs_ref[tile, pair]
                probs = probs_low.astype(F32)
                grad_probs = compact(nt(values, grads), slots)
                inner = jnp.sum(probs * grad_probs, axis=0, keepdims=True)
                grad_scores = (probs * (grad_probs - inner) * (CHD ** -0.5)).astype(BF)
                wide_scores = expand(grad_scores, slots)
                wide_probs = expand(probs_low, slots)
                all_ref[here, c0:c0 + TILE] = tn(stack_lanes(wide_scores), keys).astype(BF)
                all_ref[here, width + c0:width + c0 + TILE] = nn(wide_scores, queries).astype(BF)
                all_ref[here, 2 * width + c0:2 * width + c0 + TILE] = nn(wide_probs, grads).astype(BF)
        unit1, _ = norm_parts(x_ref[...].astype(F32))
        dqkv_ref[...] += tn((unit1 * gain1_ref[...]).astype(BF), all_ref[rows_at(base, rows), :])

    @pl.when(step == 2 * half_steps - 1)
    def _():
        half = width // 2
        for index in range(2):
            late_ref[index] = low(dqkv_ref[index * half:(index + 1) * half, 0:2 * width])
            late_ref[2, :, index * width:(index + 1) * width] = low(dqkv_ref[index * half:(index + 1) * half, 2 * width:])
        late_ref[3] = jnp.zeros_like(late_ref[3])

    @pl.when(step >= 2 * half_steps)
    def _():
        here = rows_at((step - 2 * half_steps) * rows, rows)
        unit1, rate1 = norm_parts(x_ref[...].astype(F32))
        upstream1 = nt(all_ref[here, :], wqkv_ref[...])
        dx_ref[...] = low(spread_ref[here, :] + norm_back(upstream1, gain1_ref[...], unit1, rate1))

    for at in range(3 * half_steps):
        todo = [(index, stages.index(at)) for index, stages in reversed(list(enumerate(PLAN))) if at in stages]
        if todo:
            @pl.when(step == at)
            def _(todo=todo):
                for index, stage in todo:
                    if stage == 1 and index < word_chains:
                        chains[index].fetch(own_sem.at[index]).wait()
                    chains[index].step(stage)

    @pl.when(step == steps - 1)
    def _():
        done = [len(stages) for stages in PLAN]
        while any(done[index] <= len(chains[index].stages) for index in range(CHAINS)):
            for index in reversed(range(CHAINS)):
                if done[index] <= len(chains[index].stages):
                    chains[index].step(done[index])
                    done[index] += 1
                    if done[index] > len(chains[index].stages):
                        leave[index].start()
        for copy in leave:
            copy.wait()


def char_backward(bits, x, counts, gain1, weights, wout, gain2, wup, wdown, grad_pooled, saved, grad_proj,
                  word_gains, word_grads):
    qkv, probs, mixed, first, slope, act_pool = saved
    rows, width = x.shape
    words = counts.shape[0]
    slots = rows // words
    hidden = wup.shape[1]
    wide = word_gains.shape[1]
    step = rows // CHAR_STEPS
    last = CHAR_STEPS - 1
    ahead = lambda i: i - ((i // CHAR_STEPS + 1) // 2) * (i - last)
    behind = lambda i: (i // CHAR_STEPS % 2) * (i - CHAR_STEPS) + (i // CHAR_STEPS // 2) * last
    inputs = lambda i: (i % CHAR_STEPS) * ((i // CHAR_STEPS + 1) // 2)
    final = lambda i: (i // CHAR_STEPS // 2) * (i - 2 * CHAR_STEPS)
    ahead_block = lambda cols: pl.BlockSpec((step, cols), lambda i: (ahead(i), 0))
    behind_block = lambda cols: pl.BlockSpec((step, cols), lambda i: (behind(i), 0))
    whole = lambda shape: pl.BlockSpec(shape, lambda i: (0,) * len(shape))
    tiles = step // TILE
    sum_shapes = [(wide, wide)] * 3 + [(RANKS, width // 2, wide), (RANKS, width, wide), (RANKS, width // 2, wide)]
    sources = [(RANKS,) + shape if len(shape) == 2 else shape for shape in sum_shapes]
    copies = sum(chain_copies(bits, index >= 3) for index in range(CHAINS))
    scratch = []
    for shape in sources:
        scratch += chain_scratch(bits, shape[1], wide)
    return pl.pallas_call(
        functools.partial(char_backward_kernel, slots, bits),
        grid=(3 * CHAR_STEPS,),
        in_specs=[
            pl.BlockSpec((step, width), lambda i: (inputs(i), 0)),
            whole((1, words)),
            whole((1, width)),
            whole((width, width)),
            whole((width, width)),
            whole((width, width)),
            whole((width, width)),
            whole((1, width)),
            whole((width, hidden)),
            whole((hidden, width)),
            whole((words, width)),
            whole((words, hidden)),
            whole((width, wide)),
            whole((8, wide)),
            behind_block(3 * width),
            pl.BlockSpec((tiles, CHEADS // 2, slots, 2 * TILE), lambda i: (behind(i), 0, 0, 0)),
            ahead_block(width),
            ahead_block(width),
            ahead_block(hidden),
        ] + [pl.BlockSpec(memory_space=pl.ANY)] * 3,
        out_specs=[pl.BlockSpec((step, width), lambda i: (final(i), 0))] + [pl.BlockSpec(memory_space=pl.ANY)] * CHAINS,
        out_shape=[jax.ShapeDtypeStruct((rows, width), BF)]
        + [jax.ShapeDtypeStruct(shape, BF) for shape in sum_shapes],
        scratch_shapes=[
            pltpu.VMEM((words, width + hidden), F32),
            pltpu.VMEM((step, width), F32),
            pltpu.VMEM((rows, width), BF),
            pltpu.VMEM((step, hidden), BF),
            pltpu.VMEM((rows, width), F32),
            pltpu.VMEM((8, width), F32),
            pltpu.VMEM((width, 3 * width), F32),
            pltpu.VMEM((width, width), F32),
            pltpu.VMEM((width, hidden), F32),
            pltpu.VMEM((rows, 3 * width), BF),
            pltpu.VMEM((width, 3 * width), BF),
            pltpu.VMEM((CHAR_STEPS, TILE), jnp.int32),
        ] + [pltpu.VMEM(shape, BF) for shape in sources[3:]] + scratch
        + [pltpu.VMEM(shape, BF) for shape in sum_shapes] + [pltpu.SemaphoreType.DMA((copies,)), pltpu.SemaphoreType.DMA((copies,)), pltpu.SemaphoreType.DMA((2 * CHAINS,))],
        compiler_params=pltpu.CompilerParams(
            vmem_limit_bytes=63 << 20, collective_id=2, has_side_effects=True),
        name="char_backward",
    )(x, counts[None, :], gain1[None, :], *weights, wout, gain2[None, :],
      wup, wdown, grad_pooled, act_pool, grad_proj, word_gains, qkv, probs, mixed, first, slope, *word_grads)


def unpack_kernel(out_in, dx_in, wq_in, wk_in, wv_in, gain1_in, up_in, down_in, mix_in, turn_in, early_in, mid_in, late_in,
                  out_ref, dx_ref, gain1_ref, dq_ref, dk_ref, dv_ref, dout_ref, gain2_ref, dup_ref, ddown_ref, dproj_ref,
                  wgain1_ref, wq_ref, wk_ref, wv_ref, wout_ref, wgain2_ref, wup_ref, wdown_ref):
    step = pl.program_id(0)
    dx_ref[...] = dx_in[...].astype(F32)
    out_ref[...] = out_in[...]
    width = dq_ref.shape[0]
    half = width // 2
    wup_ref[...] = up_in[...].astype(F32)
    wdown_ref[...] = down_in[...].astype(F32)
    wq_ref[...] = mix_in[:, 0:TILE].astype(F32)
    wk_ref[...] = mix_in[:, TILE:2 * TILE].astype(F32)
    wv_ref[...] = mix_in[:, 2 * TILE:3 * TILE].astype(F32)
    for side in range(2):
        cols = slice(side * width, (side + 1) * width)
        ddown_ref[side] = early_in[0, :, cols].astype(F32)
        dup_ref[:, side * 2 * width:(side + 1) * 2 * width] = mid_in[side].astype(F32)
    dproj_ref[...] = mid_in[2].astype(F32)

    @pl.when(step < UNPACK_STEPS // 2)
    def _():
        for side in range(2):
            dout_ref[side] = mid_in[3, :, side * width:(side + 1) * width].astype(F32)

    @pl.when(step == UNPACK_STEPS // 2)
    def _():
        gains = mid_in[3, 0:16, :].astype(F32)
        wgain1_ref[...] = gains[0:1]
        wgain2_ref[...] = gains[1:2]
        gain2_ref[...] = gains[9:10, 0:width]

    @pl.when(step == 0)
    def _():
        wout_ref[...] = turn_in[...].astype(F32).T
        parts = []
        for index in range(2):
            at = slice(index * half, (index + 1) * half)
            cols = slice(index * width, (index + 1) * width)
            grads = (late_in[index, :, 0:width].astype(F32), late_in[index, :, width:].astype(F32),
                     late_in[2, :, cols].astype(F32))
            total = 0.0
            for grad, weight, target in zip(grads, (wq_in, wk_in, wv_in), (dq_ref, dk_ref, dv_ref)):
                target[at, :] = grad
                total += weight[at].astype(F32) * grad
            parts.append(jnp.sum(total, axis=1, keepdims=True))
        sums = jnp.concatenate(parts, axis=0)
        diagonal = (lax.broadcasted_iota(jnp.int32, (width, width), 0)
                    == lax.broadcasted_iota(jnp.int32, (width, width), 1))
        gain1_ref[...] = jnp.sum(jnp.where(diagonal, sums, 0.0), axis=0, keepdims=True) / gain1_in[...]


UNPACK_STEPS = 8


def unpack(word_output, grad_inputs, weights, gain1, sums, width, hidden):
    steps = UNPACK_STEPS
    up, down, mix, early, mid, late = sums
    wide = word_output.shape[1]
    whole = lambda shape: pl.BlockSpec(shape, lambda i: (0,) * len(shape))
    split = lambda shape: pl.BlockSpec((shape[0] // steps, shape[1]), lambda i: (i, 0))
    middle = lambda shape: pl.BlockSpec((shape[0], shape[1] // steps, shape[2]), lambda i: (0, i, 0))
    per = early.shape[1] * RANKS // steps
    blocks = early.shape[1] // per
    pinned = lambda i: i - (i // (steps // 2)) * (i - (steps // 2 - 1))
    outs = [
        (whole, (1, width)), (whole, (width, width)), (whole, (width, width)), (whole, (width, width)),
        (lambda shape: pl.BlockSpec((2, shape[1] * 2 // steps, width), lambda i: (0, pinned(i), 0)), (2, width // 2, width)),
        (whole, (1, width)), (split, (width, hidden)), (middle, (2, hidden // 2, width)), (split, (width, wide)),
        (whole, (1, wide)), (split, (wide, TILE)), (split, (wide, TILE)), (split, (wide, TILE)),
        (whole, (TILE, wide)), (whole, (1, wide)), (split, (wide, wide)), (split, (wide, wide)),
    ]
    results = pl.pallas_call(
        unpack_kernel,
        grid=(steps,),
        in_specs=[split(word_output.shape), split(grad_inputs.shape)] + [whole((width, width))] * 3 + [whole((1, width))]
        + [split(up.shape), split(down.shape), split(mix.shape), pl.BlockSpec((wide, TILE), lambda i: (0, 3)),
           pl.BlockSpec((1, per, wide), lambda i: (i // blocks, i % blocks, 0)), middle(mid.shape), whole(late.shape)],
        out_specs=[split(word_output.shape), split(grad_inputs.shape)] + [spec(shape) for spec, shape in outs],
        out_shape=[jax.ShapeDtypeStruct(word_output.shape, BF), jax.ShapeDtypeStruct(grad_inputs.shape, F32)]
        + [jax.ShapeDtypeStruct(shape, F32) for _, shape in outs],
        compiler_params=pltpu.CompilerParams(vmem_limit_bytes=60 << 20),
        name="unpack",
    )(word_output, grad_inputs, *weights, gain1[None, :], up, down, mix, mix, early, mid, late)

    def shaped(array):
        if array.ndim == 3:
            return array.reshape(-1, array.shape[2])
        return array[0] if array.shape[0] == 1 else array

    return tuple(shaped(array) for array in results)


def per_device(
    bits,
    char_inputs,
    char_counts,
    doc_ids,
    cotangent,
    char_norm_one,
    char_query,
    char_key,
    char_value,
    char_out,
    char_norm_two,
    char_up,
    char_down,
    char_proj,
    word_norm_one,
    word_query,
    word_key,
    word_value,
    word_out_proj,
    word_norm_two,
    word_up,
    word_down,
):
    char_qkv = (char_query, char_key, char_value)
    word_qkv = (word_query, word_key, word_value)
    vec, pooled, *saved, near, qkv_all, out_all, up_all, down_all = char_forward(
        char_inputs, char_counts, char_norm_one, char_qkv, char_out, char_norm_two, char_up, char_down, char_proj,
        word_qkv, word_out_proj, word_up, word_down,
    )
    word_output, grad_pooled, grad_proj, word_gains, *word_grads = word_layer(
        bits, vec, near, doc_ids, cotangent, qkv_all, out_all, up_all, down_all,
        word_norm_one, word_norm_two, char_proj, pooled,
    )
    grad_inputs, *sums = char_backward(
        bits, char_inputs, char_counts, char_norm_one, char_qkv, char_out, char_norm_two, char_up, char_down,
        grad_pooled, saved, grad_proj, word_gains, word_grads,
    )
    return unpack(word_output, grad_inputs, char_qkv, char_norm_one, sums, char_out.shape[0], char_up.shape[1])


def solution(mesh):
    in_specs = (
        P(("dp", "tensor"), None),
        P(("dp", "tensor")),
        P("dp", None),
        P("dp", None),
        P(),
        P(),
        P(),
        P(),
        P(),
        P(),
        P(),
        P(),
        P(),
        P(),
        P(None, "tensor"),
        P(None, "tensor"),
        P(None, "tensor"),
        P("tensor", None),
        P(),
        P(None, "tensor"),
        P("tensor", None),
    )
    out_specs = (
        P(("dp", "tensor"), None),
        P(("dp", "tensor"), None),
        P(),
        P(),
        P(),
        P(),
        P(),
        P(),
        P(),
        P(),
        P(),
        P(),
        P(None, "tensor"),
        P(None, "tensor"),
        P(None, "tensor"),
        P("tensor", None),
        P(),
        P(None, "tensor"),
        P("tensor", None),
    )
    assert mesh.shape["tensor"] == RANKS
    bits = mesh.shape["dp"].bit_length() - 1
    assert bits >= 3 and mesh.shape["dp"] == 1 << bits
    return jax.shard_map(
        functools.partial(per_device, bits), mesh=mesh, in_specs=in_specs, out_specs=out_specs, check_vma=False
    )
```

```python
import functools

import jax
import jax.numpy as jnp
from jax import lax
from jax.experimental import pallas as pl
from jax.experimental.pallas import tpu as pltpu
from jax.sharding import PartitionSpec as P

BF = jnp.bfloat16
F32 = jnp.float32
EPSILON = 1e-05
NEG_LARGE = -1e30
RANKS = 4
CHEADS = 4
CHD = 64
TILE = 128
CHAR_STEPS = 8
GELU_C = 0.7978845608028654
GELU_A = 0.044715


def nn(left, right):
    return lax.dot_general(left, right, (((1,), (0,)), ((), ())), preferred_element_type=F32)


def nt(left, right):
    return lax.dot_general(left, right, (((1,), (1,)), ((), ())), preferred_element_type=F32)


def tn(left, right):
    return lax.dot_general(left, right, (((0,), (0,)), ((), ())), preferred_element_type=F32)


def norm_parts(values):
    centre = values - jnp.mean(values, axis=-1, keepdims=True)
    spread = jnp.mean(centre * centre, axis=-1, keepdims=True)
    rate = lax.rsqrt(spread + EPSILON)
    return centre * rate, rate


def norm_back(upstream, gain, unit, rate):
    scaled = upstream * gain
    first = jnp.mean(scaled, axis=-1, keepdims=True)
    second = jnp.mean(scaled * unit, axis=-1, keepdims=True)
    return rate * (scaled - first - unit * second)


def gelu_parts(values):
    square = values * values
    inner = values * (GELU_C + (GELU_C * GELU_A) * square)
    half = 0.5 + 0.5 * jnp.tanh(inner)
    active = values * half
    slope = half + (active * (1.0 - half)) * (2.0 * GELU_C + (6.0 * GELU_C * GELU_A) * square)
    return active, slope


def split_heads(pair):
    low_half = lax.broadcasted_iota(jnp.int32, pair.shape, 1) < CHD
    zero = jnp.zeros_like(pair)
    return jnp.concatenate([jnp.where(low_half, pair, zero), jnp.where(low_half, zero, pair)], axis=0)


def word_of_lane(shape, slots):
    lane = lax.broadcasted_iota(jnp.int32, shape, 1)
    return jnp.bitwise_and(lane, TILE - 1) // slots


def compact(scores, slots):
    words = word_of_lane((slots, scores.shape[1]), slots)
    result = scores[0:slots]
    for word in range(1, TILE // slots):
        result = jnp.where(words == word, scores[word * slots:(word + 1) * slots], result)
    return result


def expand(packed, slots):
    words = word_of_lane(packed.shape, slots)
    zero = jnp.zeros_like(packed)
    return jnp.concatenate(
        [jnp.where(words == word, packed, zero) for word in range(TILE // slots)], axis=0
    )


def stack_lanes(pair):
    return jnp.concatenate([pair[:, :TILE], pair[:, TILE:]], axis=0)


def split_counts(counts_ref, table_ref, words):
    for step in range(CHAR_STEPS):
        table_ref[step:step + 1, 0:words] = counts_ref[:, step * words:(step + 1) * words]


def valid_slots(rows, slots, mine):
    words = rows // slots
    row = lax.broadcasted_iota(jnp.int32, (rows, words), 0)
    word = lax.broadcasted_iota(jnp.int32, (rows, words), 1)
    return (row // slots == word) & (jnp.bitwise_and(row, slots - 1) < mine)


def join_lanes(parts, whole_ref):
    width = parts[0].shape[1]
    for index, part in enumerate(parts):
        whole_ref[:, index * width:(index + 1) * width] = part[...]


def any_lane(mask):
    return jnp.max(jnp.where(mask, 1.0, 0.0), axis=1, keepdims=True) > 0.0


def column(row):
    size = row.shape[1]
    diagonal = (lax.broadcasted_iota(jnp.int32, (size, size), 0)
                == lax.broadcasted_iota(jnp.int32, (size, size), 1))
    return jnp.sum(jnp.where(diagonal, row, 0.0), axis=1, keepdims=True)


MESH = pl.DeviceIdType.MESH
LANE_SPLIT = 256


class Place:
    def __init__(self):
        self.dp = lax.axis_index("dp")
        self.rank = lax.axis_index("tensor")
        self.core = lax.rem(self.dp, 2)
        self.x = lax.rem(self.dp // 2, 2)
        self.y = lax.rem(self.dp // 4, 2)
        self.core_mate = (self.dp + 1 - 2 * self.core, self.rank)
        self.x_mate = (self.dp + 2 - 4 * self.x, self.rank)
        self.y_mate = (self.dp + 4 - 8 * self.y, self.rank)

    def ring(self, offset):
        return lax.rem(self.rank + offset, RANKS)

    def ring_device(self, offset):
        return (self.dp, self.ring(offset))

    def bit_mate(self, bit):
        size = 1 << bit
        mine = lax.rem(self.dp // size, 2)
        return (self.dp + size - 2 * size * mine, self.rank)

    def mates(self, bits):
        extra = [self.bit_mate(bit) for bit in range(3, bits)]
        return [self.core_mate, self.x_mate, self.y_mate] + extra


def meet(devices):
    barrier = pltpu.get_barrier_semaphore()
    for device in devices:
        pl.semaphore_signal(barrier, inc=1, device_id=device, device_id_type=MESH)
    pl.semaphore_wait(barrier, len(devices))


def remote(source, target, sems, device):
    return pltpu.make_async_remote_copy(
        src_ref=source, dst_ref=target, send_sem=sems[0], recv_sem=sems[1],
        device_id=device, device_id_type=MESH,
    )


class Sems:
    def __init__(self, send, recv, start=0):
        self.send, self.recv, self.next = send, recv, start

    def take(self):
        at = self.next
        self.next += 1
        return self.send.at[at], self.recv.at[at]


def rows_at(start, size):
    return pl.ds(pl.multiple_of(start, 16), size)


def halves(width):
    return (slice(0, LANE_SPLIT), slice(LANE_SPLIT, width))


class Gather:
    def __init__(self, place, local, whole, sems):
        self.stages = [[], [], [], []]
        rows = local.shape[0]
        unit = rows // 8
        p = place
        left, right = halves(local.shape[1])
        left_at = p.core * 4 + p.x * 2 + p.y
        right_at = p.core * 4 + p.y * 2 + p.x
        for offset in range(1, RANKS):
            for lanes, at in ((left, left_at), (right, right_at)):
                at = rows_at(at * unit, unit)
                self.stages[0].append(remote(
                    local.at[at, lanes], whole.at[p.rank, at, lanes], sems.take(), p.ring_device(offset)))
        for offset in range(1, RANKS):
            rank = p.ring(offset)
            for lanes, at, first, second, mate_first, mate_second in (
                (left, left_at, p.x, None, p.y_mate, p.x_mate),
                (right, right_at, p.y, None, p.x_mate, p.y_mate),
            ):
                one = rows_at(at * unit, unit)
                two = rows_at((p.core * 4 + first * 2) * unit, 2 * unit)
                self.stages[1].append(remote(
                    whole.at[rank, one, lanes], whole.at[rank, one, lanes], sems.take(), mate_first))
                self.stages[2].append(remote(
                    whole.at[rank, two, lanes], whole.at[rank, two, lanes], sems.take(), mate_second))
            four = rows_at(p.core * 4 * unit, 4 * unit)
            self.stages[3].append(remote(
                whole.at[rank, four], whole.at[rank, four], sems.take(), p.core_mate))

    def start(self, stage):
        for copy in self.stages[stage]:
            copy.start()

    def wait(self, stage):
        for copy in self.stages[stage]:
            copy.wait()


def gather_copies():
    return 2 * (RANKS - 1) * 3 + (RANKS - 1)


class Chain:
    def __init__(self, place, bits, src, refs, sems, everywhere, begin=0):
        p = place
        buf, got_core, got_one, got_two, got_more, got_rank, out = refs
        self.p, self.src, self.everywhere, self.begin = p, src, everywhere, begin
        self.buf, self.got_core, self.got_one, self.got_two = buf, got_core, got_one, got_two
        self.got_more, self.got_rank, self.out = got_more, got_rank, out
        unit = buf.shape[1] // 4
        lanes = halves(buf.shape[2])
        self.lanes = lanes
        base = p.core * 4 * unit
        self.own = rows_at(base, 4 * unit)
        first, second = (p.x, p.y), (p.y, p.x)
        first_mate, second_mate = (p.x_mate, p.y_mate), (p.y_mate, p.x_mate)
        one = lambda side, at: rows_at(at * 2 * unit, 2 * unit)
        two = lambda side, at: rows_at((first[side] * 2 + at) * unit, unit)
        self.one_rows = [one(side, first[side]) for side in (0, 1)]
        self.two_rows = [two(side, second[side]) for side in (0, 1)]
        self.out_two = [rows_at(base + (first[side] * 2 + second[side]) * unit, unit) for side in (0, 1)]
        out_one = [rows_at(base + first[side] * 2 * unit, 2 * unit) for side in (0, 1)]
        sides = (0, 1)

        def mine(side):
            return out.at[p.rank, self.out_two[side], lanes[side]]

        def back(at, part_lanes, mate, sem):
            part = out.at[:, at, part_lanes] if everywhere else out.at[at, part_lanes]
            return remote(part, part, sem.take(), mate)

        stages = [
            ("core", 1, lambda sem: [remote(
                src.at[:, rows_at((1 - p.core) * 4 * unit, 4 * unit)], got_core, sem.take(), p.core_mate)]),
            ("one", 2, lambda sem: [remote(
                buf.at[:, one(side, 1 - first[side]), lanes[side]], got_one.at[:, :, lanes[side]],
                sem.take(), first_mate[side]) for side in sides]),
            ("two", 2, lambda sem: [remote(
                buf.at[:, two(side, 1 - second[side]), lanes[side]], got_two.at[:, :, lanes[side]],
                sem.take(), second_mate[side]) for side in sides]),
        ]
        for bit in range(3, bits):
            stages.append((bit - 3, 2, lambda sem, bit=bit: [remote(
                buf.at[:, self.two_rows[side], lanes[side]], got_more.at[bit - 3, :, :, lanes[side]],
                sem.take(), p.bit_mate(bit)) for side in sides]))
        pairs = 2 * (RANKS - 1)
        stages.append(("rank", pairs, lambda sem: [remote(
            buf.at[p.ring(offset), self.two_rows[side], lanes[side]], got_rank.at[offset - 1, :, lanes[side]],
            sem.take(), p.ring_device(offset)) for offset in range(1, RANKS) for side in sides]))
        if everywhere:
            stages.append(("rank_back", pairs, lambda sem: [
                remote(mine(side), mine(side), sem.take(), p.ring_device(offset))
                for offset in range(1, RANKS) for side in sides]))
        stages.append(("back_two", 2, lambda sem: [
            back(self.out_two[side], lanes[side], second_mate[side], sem) for side in sides]))
        stages.append(("back_one", 2, lambda sem: [
            back(out_one[side], lanes[side], first_mate[side], sem) for side in sides]))
        stages.append(("back_core", 1, lambda sem: [back(self.own, slice(None), p.core_mate, sem)]))
        self.stages = stages
        self.sems, self.first_sem, at = sems, [], sems.next
        for _, count, _ in stages:
            self.first_sem.append(at)
            at += count

    def copies(self, index):
        return self.stages[index][2](Sems(self.sems.send, self.sems.recv, self.first_sem[index]))

    def fetch(self, sem):
        source = self.src if self.begin else self.src.at[:, self.own]
        return pltpu.make_async_copy(source, self.buf, sem)

    def start(self, index):
        for copy in self.copies(index):
            copy.start()

    def finish(self, index, staged=False):
        name = self.stages[index][0]
        for copy in self.copies(index):
            copy.wait()
        buf = self.buf
        if name == "core":
            for quarter in range(RANKS):
                own = self.src[quarter, self.own, :] if staged or self.everywhere else buf[quarter]
                buf[quarter] = own + self.got_core[quarter]
        elif name == "one":
            for at, lanes in zip(self.one_rows, self.lanes):
                for quarter in range(RANKS):
                    buf[quarter, at, lanes] += self.got_one[quarter, :, lanes]
        elif name == "two":
            for at, lanes in zip(self.two_rows, self.lanes):
                for quarter in range(RANKS):
                    buf[quarter, at, lanes] += self.got_two[quarter, :, lanes]
        elif name == "rank":
            target = self.out.at[self.p.rank] if self.everywhere else self.out
            for side in (0, 1):
                at, lanes = self.two_rows[side], self.lanes[side]
                total = buf[self.p.rank, at, lanes].astype(F32)
                for k in range(RANKS - 1):
                    total = total + self.got_rank[k, :, lanes].astype(F32)
                target[self.out_two[side], lanes] = total.astype(BF)
        elif isinstance(name, int):
            for at, lanes in zip(self.two_rows, self.lanes):
                for quarter in range(RANKS):
                    buf[quarter, at, lanes] += self.got_more[name, quarter, :, lanes]

    def step(self, index):
        if index > self.begin:
            self.finish(index - 1)
        if index < len(self.stages):
            self.start(index)


def chain_copies(bits, everywhere):
    pairs = 2 * (RANKS - 1)
    return 1 + 2 + 2 + 2 * (bits - 3) + pairs + (pairs if everywhere else 0) + 2 + 2 + 1


def chain_scratch(bits, rows, lanes, begin=0):
    unit = rows // 8
    early = 16 if begin else 4 * unit
    return [
        pltpu.VMEM((RANKS, 4 * unit, lanes), BF),
        pltpu.VMEM((RANKS, early, lanes), BF),
        pltpu.VMEM((RANKS, early // 2 if not begin else 16, lanes), BF),
        pltpu.VMEM((RANKS, unit, lanes), BF),
        pltpu.VMEM((max(bits - 3, 1), RANKS, unit, lanes), BF),
        pltpu.VMEM((RANKS - 1, unit, lanes), BF),
    ]


FORWARD_PLAN = {
    2: ((0, 1), (1, 1)),
    3: ((2, 1), (0, 2), (1, 2)),
    4: ((3, 1), (2, 2)),
    5: ((0, 3), (1, 3), (3, 2)),
    6: ((2, 3),),
    7: ((3, 3),),
}


def char_forward_kernel(slots, x_ref, counts_ref, gain1_ref, wq_ref, wk_ref, wv_ref, wout_ref,
                        gain2_ref, wup_ref, wdown_ref, wproj_ref,
                        lq_ref, lk_ref, lv_ref, lout_ref, lup_ref, ldown_ref,
                        vec_ref, pooled_ref, qkv_ref, probs_ref, mixed_ref, first_ref,
                        slope_ref, act_pool_ref, near_ref, wqkv_all, wout_all, wup_all, wdown_all,
                        wqkv_ref, lqkv_ref, table_ref, own_sem, send_sem, recv_sem):
    rows = x_ref.shape[0]
    width = x_ref.shape[1]
    step = pl.program_id(0)
    steps = pl.num_programs(0)
    words = rows // slots
    p = Place()
    pairs = ((lqkv_ref, wqkv_all), (lout_ref, wout_all), (lup_ref, wup_all), (ldown_ref, wdown_all))
    gathers = [Gather(p, mine, whole, Sems(send_sem, recv_sem, gather_copies() * index))
               for index, (mine, whole) in enumerate(pairs)]
    own_copies = [pltpu.make_async_copy(mine, whole.at[p.rank], own_sem.at[index])
                  for index, (mine, whole) in enumerate(pairs)]
    vec_base = gather_copies() * len(pairs)

    def vec_copies(at):
        copies = []
        for slot, offset in ((1, 1), (0, 2)):
            sem = vec_base + 2 * at + slot
            part = rows_at(at * words, words)
            copies.append(remote(vec_ref.at[part], near_ref.at[slot, part],
                                 (send_sem.at[sem], recv_sem.at[sem]), p.ring_device(offset)))
        return copies

    def send_vec(at):
        for offset, copy in zip((1, 2), vec_copies(at)):
            @pl.when(p.rank + offset < RANKS)
            def _(copy=copy):
                copy.start()

    def wait_vec(at):
        for offset, copy in zip((1, 2), vec_copies(at)):
            @pl.when(p.rank + offset < RANKS)
            def _(copy=copy):
                copy.wait_send()

            @pl.when(p.rank >= offset)
            def _(copy=copy):
                copy.wait_recv()

    @pl.when(step == 0)
    def _():
        join_lanes((lq_ref, lk_ref, lv_ref), lqkv_ref)
        join_lanes((wq_ref, wk_ref, wv_ref), wqkv_ref)
        meet([p.ring_device(offset) for offset in (1, 2, 3)] + [p.core_mate, p.x_mate, p.y_mate])
        split_counts(counts_ref, table_ref, words)
        for copy in own_copies:
            copy.start()
        for gather in gathers:
            gather.start(0)

    base = x_ref[...].astype(F32)
    unit, _ = norm_parts(base)
    normed = (unit * gain1_ref[...]).astype(BF)
    qkv_ref[...] = nn(normed, wqkv_ref[...]).astype(BF)
    mine = table_ref[pl.ds(step, 1), 0:words]
    word_at = lax.broadcasted_iota(jnp.int32, (words, rows), 0)
    row_at = lax.broadcasted_iota(jnp.int32, (words, rows), 1)
    onto_rows = jnp.where(row_at // slots == word_at, 1.0, 0.0).astype(BF)
    row_counts = nn(jnp.broadcast_to(mine.astype(F32), (16, words)).astype(BF), onto_rows)[0:1]
    for tile in range(rows // TILE):
        at = pl.ds(tile * TILE, TILE)
        valid = (lax.broadcasted_iota(jnp.int32, (slots, TILE), 0).astype(F32)
                 < row_counts[:, tile * TILE:(tile + 1) * TILE])
        for pair in range(CHEADS // 2):
            c0 = pair * TILE
            queries = split_heads(qkv_ref[at, c0:c0 + TILE])
            keys = qkv_ref[at, width + c0:width + c0 + TILE]
            values = split_heads(qkv_ref[at, 2 * width + c0:2 * width + c0 + TILE])
            scores = compact(nt(keys, queries), slots)
            parts = []
            for head in range(2):
                own = jnp.where(valid, scores[:, head * TILE:(head + 1) * TILE], NEG_LARGE)
                top = jnp.max(own, axis=0, keepdims=True)
                weight = jnp.exp((own - top) * (CHD ** -0.5))
                parts.append(weight / jnp.sum(weight, axis=0, keepdims=True))
            probs = jnp.concatenate(parts, axis=1).astype(BF)
            probs_ref[tile, pair] = probs
            mixed_ref[at, c0:c0 + TILE] = tn(stack_lanes(expand(probs, slots)), values).astype(BF)

    for at, todo in FORWARD_PLAN.items():
        @pl.when(step == at)
        def _(todo=todo):
            for member, stage in todo:
                gathers[member].wait(stage - 1)
                gathers[member].start(stage)

    @pl.when(step > 0)
    def _():
        send_vec(step - 1)

    first = base + nn(mixed_ref[...], wout_ref[...])
    first_ref[...] = first
    unit2, _ = norm_parts(first)
    normed2 = (unit2 * gain2_ref[...]).astype(BF)
    members = valid_slots(rows, slots, mine)
    valid_col = any_lane(members)
    pool = jnp.where(members, 1.0 / mine.astype(F32), 0.0).astype(BF)
    chunk = 256
    for part in range(wup_ref.shape[1] // chunk):
        cols = slice(part * chunk, (part + 1) * chunk)
        active, slope = gelu_parts(nn(normed2, wup_ref[:, cols]))
        slope_ref[:, cols] = jnp.where(valid_col, slope, 0.0).astype(BF)
        act_pool_ref[:, cols] = tn(pool, active.astype(BF)).astype(BF)
    pooled = tn(pool, first.astype(BF)) + nn(act_pool_ref[...], wdown_ref[...])
    pooled = pooled.astype(BF)
    pooled_ref[...] = pooled
    vec_ref[rows_at(step * words, words), :] = nn(pooled, wproj_ref[...]).astype(BF)

    @pl.when(step == steps - 1)
    def _():
        send_vec(step)
        for copy in own_copies:
            copy.wait()
        for gather in gathers:
            gather.wait(3)
        for at in range(CHAR_STEPS):
            wait_vec(at)


def char_forward(x, counts, gain1, weights, wout, gain2, wup, wdown, wproj, local, lout, lup, ldown):
    rows, width = x.shape
    words = counts.shape[0]
    slots = rows // words
    hidden = wup.shape[1]
    wide = wproj.shape[1]
    step = rows // CHAR_STEPS
    step_words = step // slots
    row_block = lambda cols: pl.BlockSpec((step, cols), lambda i: (i, 0))
    word_block = lambda cols: pl.BlockSpec((step_words, cols), lambda i: (i, 0))
    whole = lambda shape: pl.BlockSpec(shape, lambda i: (0, 0))
    tiles = step // TILE
    return pl.pallas_call(
        functools.partial(char_forward_kernel, slots),
        grid=(rows // step,),
        in_specs=[
            row_block(width),
            whole((1, words)),
            whole((1, width)),
            whole((width, width)),
            whole((width, width)),
            whole((width, width)),
            whole((width, width)),
            whole((1, width)),
            whole((width, hidden)),
            whole((hidden, width)),
            whole((width, wide)),
            whole(local[0].shape),
            whole(local[0].shape),
            whole(local[0].shape),
            whole(lout.shape),
            whole(lup.shape),
            whole(ldown.shape),
        ],
        out_specs=[
            whole((words, wide)),
            word_block(width),
            row_block(3 * width),
            pl.BlockSpec((tiles, CHEADS // 2, slots, 2 * TILE), lambda i: (i, 0, 0, 0)),
            row_block(width),
            row_block(width),
            row_block(hidden),
            word_block(hidden),
        ] + [pl.BlockSpec(memory_space=pl.ANY)] * 5,
        out_shape=[
            jax.ShapeDtypeStruct((words, wide), BF),
            jax.ShapeDtypeStruct((words, width), BF),
            jax.ShapeDtypeStruct((rows, 3 * width), BF),
            jax.ShapeDtypeStruct((rows // TILE, CHEADS // 2, slots, 2 * TILE), BF),
            jax.ShapeDtypeStruct((rows, width), BF),
            jax.ShapeDtypeStruct((rows, width), F32),
            jax.ShapeDtypeStruct((rows, hidden), BF),
            jax.ShapeDtypeStruct((words, hidden), BF),
            jax.ShapeDtypeStruct((2, words, wide), BF),
            jax.ShapeDtypeStruct((RANKS, wide, 3 * TILE), BF),
            jax.ShapeDtypeStruct((RANKS,) + lout.shape, BF),
            jax.ShapeDtypeStruct((RANKS,) + lup.shape, BF),
            jax.ShapeDtypeStruct((RANKS,) + ldown.shape, BF),
        ],
        scratch_shapes=[
            pltpu.VMEM((width, 3 * width), BF),
            pltpu.VMEM((wide, 3 * TILE), BF),
            pltpu.VMEM((CHAR_STEPS, TILE), jnp.int32),
            pltpu.SemaphoreType.DMA((4,)),
            pltpu.SemaphoreType.DMA((gather_copies() * 4 + 2 * CHAR_STEPS,)),
            pltpu.SemaphoreType.DMA((gather_copies() * 4 + 2 * CHAR_STEPS,)),
        ],
        compiler_params=pltpu.CompilerParams(
            vmem_limit_bytes=60 << 20, collective_id=0, has_side_effects=True),
        name="char_forward",
    )(x, counts[None, :], gain1[None, :], *weights, wout, gain2[None, :], wup, wdown, wproj,
      *local, lout, lup, ldown)


def word_kernel(bits, vec_ref, near_ref, docs_ref, cot_ref, wqkv_in, wout_in, wup_in,
                wdown_in, gain1_ref, gain2_ref, wproj_ref, pooled_ref,
                out_ref, gpl_ref, dproj_ref, dgain_ref, up_grad_out, down_grad_out, mix_grad_out,
                n1_ref, q_ref, kv_ref, probs_ref, o_ref, act_ref, slope_ref, go_ref, gq_ref, gkv_ref,
                back_ref, cot_own, cot_sem, part_ref, got_ref, table_ref, wqkv_ref, wout_ref, wup_ref, wdown_ref,
                up_grad_ref, down_grad_ref, mix_grad_ref, up_buf, up_core, up_one, down_buf, down_core, down_one,
                io_sem, send_sem, recv_sem):
    p = Place()
    words, wide = vec_ref.shape
    window = 3 * words
    fetch = pltpu.make_async_copy(cot_ref.at[rows_at(p.rank * words, words)], cot_own, cot_sem)
    loads = [pltpu.make_async_copy(source, target, io_sem.at[index]) for index, (source, target) in enumerate((
        (wqkv_in, wqkv_ref), (wout_in, wout_ref), (wup_in, wup_ref), (wdown_in, wdown_ref)))]
    stores = [pltpu.make_async_copy(source, target, io_sem.at[4 + index]) for index, (source, target) in enumerate((
        (up_buf, up_grad_out), (down_buf, down_grad_out)))]

    def store_mix(rank):
        return pltpu.make_async_copy(mix_grad_ref.at[rank], mix_grad_out.at[rank], io_sem.at[6 + rank])

    up_chain = Chain(p, bits, up_grad_ref, (up_buf, up_core, up_one, None, None, None, None),
                     Sems(send_sem, recv_sem, 2), False)
    down_chain = Chain(p, bits, down_grad_ref, (down_buf, down_core, down_one, None, None, None, None),
                       Sems(send_sem, recv_sem, 5), False)
    for copy in loads:
        copy.start()
    fetch.start()
    meet(p.mates(3) + [p.ring_device(offset) for offset in (1, 2, 3)])

    table_ref[:, 0:2 * words] = jnp.full((1, 2 * words), -1, jnp.int32)
    table_ref[:, 2 * words:] = docs_ref[...]
    start = pl.multiple_of(p.rank * words, TILE)
    key_docs = table_ref[:, pl.ds(start, window)].astype(F32)
    row_docs = column(key_docs[:, 2 * words:])

    own = vec_ref[...].astype(F32)
    unit1, rate1 = norm_parts(own)
    n1_ref[2 * words:, :] = (unit1 * gain1_ref[...]).astype(BF)
    for slot in range(2):
        near = jnp.where(p.rank + slot >= 2, near_ref[slot].astype(F32), 0.0)
        unit, _ = norm_parts(near)
        n1_ref[slot * words:(slot + 1) * words, :] = (unit * gain1_ref[...]).astype(BF)

    def project(rank, carry):
        q_ref[rank] = nn(n1_ref[2 * words:, :], wqkv_ref[rank, :, 0:TILE]).astype(BF)
        kv_ref[rank] = nn(n1_ref[...], wqkv_ref[rank, :, TILE:]).astype(BF)
        scores = nt(split_heads(q_ref[rank]), kv_ref[rank, :, 0:TILE]) * (CHD ** -0.5)
        row = lax.broadcasted_iota(jnp.int32, (words, window), 0)
        key = lax.broadcasted_iota(jnp.int32, (words, window), 1)
        allowed = (row_docs == key_docs) & (key <= row + 2 * words)
        for head in range(2):
            at = slice(head * words, (head + 1) * words)
            masked = jnp.where(allowed, scores[at], NEG_LARGE)
            top = jnp.max(masked, axis=-1, keepdims=True)
            weight = jnp.exp(masked - top)
            probs_ref[rank, at, :] = (weight * (1.0 / jnp.sum(weight, axis=-1, keepdims=True))).astype(BF)
        pair = jnp.concatenate([probs_ref[rank, 0:words, :], probs_ref[rank, words:, :]], axis=1)
        o_ref[rank] = nn(pair, split_heads(kv_ref[rank, :, TILE:])).astype(BF)
        back_ref[...] += nn(o_ref[rank], wout_ref[rank])
        return carry

    back_ref[...] = own
    loads[0].wait()
    loads[1].wait()
    lax.fori_loop(0, RANKS, project, 0)
    middle = back_ref[...]
    unit2, rate2 = norm_parts(middle)
    normed2 = (unit2 * gain2_ref[...]).astype(BF)

    def feed(rank, carry):
        active, slope = gelu_parts(nn(normed2, wup_ref[rank]))
        act_ref[rank] = active.astype(BF)
        slope_ref[rank] = slope.astype(BF)
        back_ref[...] += nn(act_ref[rank], wdown_ref[rank])
        down_grad_ref[rank] = tn(act_ref[rank], cot_own[...]).astype(BF)
        return carry

    loads[2].wait()
    loads[3].wait()
    fetch.wait()
    lax.fori_loop(0, RANKS, feed, 0)
    out_ref[...] = back_ref[...].astype(BF)
    back_ref[...] = jnp.zeros_like(back_ref)

    def feed_back(rank, carry):
        upstream = (nt(cot_own[...], wdown_ref[rank]) * slope_ref[rank].astype(F32)).astype(BF)
        back_ref[...] += nt(upstream, wup_ref[rank])
        up_grad_ref[rank] = tn(normed2, upstream).astype(BF)
        return carry

    down_chain.start(0)
    lax.fori_loop(0, RANKS, feed_back, 0)
    up_chain.start(0)
    down_chain.finish(0, True)
    down_chain.start(1)
    upstream2 = back_ref[...]
    dgain_ref[...] = jnp.zeros_like(dgain_ref)
    dgain_ref[1:2, :] = jnp.sum(upstream2 * unit2, axis=0, keepdims=True)
    grad_middle = cot_own[...].astype(F32) + norm_back(upstream2, gain2_ref[...], unit2, rate2)
    middle_low = grad_middle.astype(BF)

    back_ref[...] = jnp.zeros_like(back_ref)
    part_ref[...] = jnp.zeros_like(part_ref)

    def attend_back(rank, carry):
        @pl.when(rank == 2)
        def _():
            up_chain.finish(0, True)
            up_chain.start(1)

        go_ref[...] = nt(middle_low, wout_ref[rank]).astype(BF)
        mix_grad_ref[rank, :, 3 * TILE:] = tn(middle_low, o_ref[rank]).astype(BF)
        go_pair = split_heads(go_ref[...])
        grad_probs = nt(go_pair, kv_ref[rank, :, TILE:])
        probs = probs_ref[rank].astype(F32)
        inner = jnp.sum(probs * grad_probs, axis=-1, keepdims=True)
        grad_scores = (probs * (grad_probs - inner) * (CHD ** -0.5)).astype(BF)
        q_pair = split_heads(q_ref[rank])
        gkv_ref[:, 0:TILE] = tn(grad_scores, q_pair).astype(BF)
        gkv_ref[:, TILE:] = tn(probs_ref[rank], go_pair).astype(BF)
        pair = jnp.concatenate([grad_scores[0:words], grad_scores[words:]], axis=1)
        gq_ref[...] = nn(pair, split_heads(kv_ref[rank, :, 0:TILE])).astype(BF)
        part_ref[...] += nt(gkv_ref[0:2 * words, :], wqkv_ref[rank, :, TILE:])
        back_ref[...] += nt(gkv_ref[2 * words:, :], wqkv_ref[rank, :, TILE:])
        back_ref[...] += nt(gq_ref[...], wqkv_ref[rank, :, 0:TILE])
        mix_grad_ref[rank, :, 0:TILE] = tn(n1_ref[2 * words:, :], gq_ref[...]).astype(BF)
        mix_grad_ref[rank, :, TILE:3 * TILE] = tn(n1_ref[...], gkv_ref[...]).astype(BF)
        store_mix(rank).start()
        return carry

    lax.fori_loop(0, RANKS, attend_back, 0)
    near_ref_low = got_ref.at[2]
    near_ref_low[...] = part_ref[...].astype(BF).reshape(2, words, wide)
    sends = []
    for slot, offset in ((0, RANKS - 2), (1, RANKS - 1)):
        sends.append(remote(got_ref.at[2, slot], got_ref.at[slot, 0], (send_sem.at[slot], recv_sem.at[slot]),
                            p.ring_device(offset)))
    for copy in sends:
        copy.start()
    for copy in sends:
        copy.wait()
    down_chain.finish(1)
    stores[1].start()
    upstream1 = back_ref[...] + got_ref[0, 0].astype(F32) + got_ref[1, 0].astype(F32)
    dgain_ref[0:1, :] = jnp.sum(upstream1 * unit1, axis=0, keepdims=True)
    grad_vec = (grad_middle + norm_back(upstream1, gain1_ref[...], unit1, rate1)).astype(BF)
    dproj_ref[...] = tn(pooled_ref[...], grad_vec).astype(BF)
    gpl_ref[...] = nt(grad_vec, wproj_ref[...])
    up_chain.finish(1)
    stores[0].start()
    for copy in stores + [store_mix(rank) for rank in range(RANKS)]:
        copy.wait()


def word_layer(bits, vec, near, doc_ids, cotangent, wqkv, wout, wup, wdown, gain1, gain2, wproj, pooled):
    words, wide = vec.shape
    width = pooled.shape[1]
    window = 3 * words
    hidden = wup.shape[2]
    vm = pl.BlockSpec(memory_space=pltpu.VMEM)
    return pl.pallas_call(
        functools.partial(word_kernel, bits),
        in_specs=[vm] * 3 + [pl.BlockSpec(memory_space=pl.ANY)] * 5 + [vm] * 4,
        out_specs=[vm] * 4 + [pl.BlockSpec(memory_space=pl.ANY)] * 3,
        out_shape=[
            jax.ShapeDtypeStruct((words, wide), BF),
            jax.ShapeDtypeStruct((words, width), F32),
            jax.ShapeDtypeStruct((width, wide), BF),
            jax.ShapeDtypeStruct((8, wide), F32),
        ] + [
            jax.ShapeDtypeStruct((RANKS, rows, wide), BF) for rows in (wide // 2, wide // 2, wide)
        ],
        scratch_shapes=[
            pltpu.VMEM((window, wide), BF),
            pltpu.VMEM((RANKS, words, TILE), BF),
            pltpu.VMEM((RANKS, window, 2 * TILE), BF),
            pltpu.VMEM((RANKS, 2 * words, window), BF),
            pltpu.VMEM((RANKS, words, TILE), BF),
            pltpu.VMEM((RANKS, words, hidden), BF),
            pltpu.VMEM((RANKS, words, hidden), BF),
            pltpu.VMEM((words, TILE), BF),
            pltpu.VMEM((words, TILE), BF),
            pltpu.VMEM((window, 2 * TILE), BF),
            pltpu.VMEM((words, wide), F32),
            pltpu.VMEM((words, wide), BF),
            pltpu.SemaphoreType.DMA,
            pltpu.VMEM((2 * words, wide), F32),
            pltpu.VMEM((3, 2, words, wide), BF),
            pltpu.VMEM((1, 2 * words + doc_ids.shape[1]), jnp.int32),
        ] + [pltpu.VMEM(array.shape, BF) for array in (wqkv, wout, wup, wdown)] + [
            pltpu.VMEM((RANKS, wide, wide), BF),
            pltpu.VMEM((RANKS, wide, wide), BF),
            pltpu.VMEM((RANKS, wide, wide), BF),
        ] + [pltpu.VMEM((RANKS, rows, wide), BF) for rows in (wide // 2, wide // 2, wide // 4) * 2] + [
            pltpu.SemaphoreType.DMA((6 + RANKS,)),
            pltpu.SemaphoreType.DMA((8,)),
            pltpu.SemaphoreType.DMA((8,)),
        ],
        compiler_params=pltpu.CompilerParams(
            vmem_limit_bytes=62 << 20, collective_id=1, has_side_effects=True),
        name="word_layer",
    )(vec, near, doc_ids, cotangent, wqkv, wout, wup, wdown,
      gain1[None, :], gain2[None, :], wproj, pooled)


CHAINS = 6
BEGIN = (2, 2, 0, 0, 0, 0)
PLAN = (
    (0, 3, 8, 10, 12),
    (0, 4, 10, 13, 15),
    (0, 2, 7, 10, 14, 16, 20),
    (0, 3, 7, 10, 15, 19, 22),
    (7, 9, 12, 14, 18),
    (15, 17, 21),
)


def char_backward_kernel(slots, bits, x_ref, counts_ref, gain1_ref, wq_ref, wk_ref, wv_ref, wout_ref, gain2_ref,
                         wup_ref, wdown_ref, gpl_ref, act_pool_ref, dproj_ref, wgain_ref, qkv_ref, probs_ref,
                         mixed_ref, first_ref, slope_ref, up_grad_ref, down_grad_ref, mix_grad_ref,
                         dx_ref, up_out, down_out, mix_out, early_out, mid_out, late_out,
                         down_ref, gq_ref, gmix_ref, gup_ref, spread_ref, dgain_ref, dqkv_ref, dout_ref, dup_ref,
                         all_ref, wqkv_ref, table_ref, early_ref, mid_ref, late_ref, *rest):
    step = pl.program_id(0)
    steps = pl.num_programs(0)
    half_steps = CHAR_STEPS
    rows, width = x_ref.shape
    words = rows // slots
    p = Place()
    send_sem, recv_sem, own_sem = rest[-3:]
    sources = (up_grad_ref, down_grad_ref, mix_grad_ref, early_ref, mid_ref, late_ref)
    results = (up_out, down_out, mix_out, early_out, mid_out, late_out)
    outs = rest[6 * CHAINS:7 * CHAINS]
    leave = [pltpu.make_async_copy(out, result, own_sem.at[CHAINS + index])
             for index, (out, result) in enumerate(zip(outs, results))]
    word_chains = 3
    chains, first_sem = [], 0
    for index in range(CHAINS):
        everywhere = index >= word_chains
        refs = tuple(rest[6 * index:6 * index + 6]) + (outs[index],)
        chains.append(Chain(p, bits, sources[index], refs, Sems(send_sem, recv_sem, first_sem), everywhere,
                            BEGIN[index]))
        first_sem += chain_copies(bits, everywhere)

    @pl.when(step == 0)
    def _():
        meet(p.mates(bits) + [p.ring_device(offset) for offset in (1, 2, 3)])
        for index in range(word_chains):
            chains[index].fetch(own_sem.at[index]).start()

    low = lambda value: value.astype(BF)

    @pl.when(step == 0)
    def _():
        dgain_ref[...] = jnp.zeros_like(dgain_ref)
        dqkv_ref[...] = jnp.zeros_like(dqkv_ref)
        dout_ref[...] = jnp.zeros_like(dout_ref)
        dup_ref[...] = jnp.zeros_like(dup_ref)
        grad_down = low(tn(act_pool_ref[...], low(gpl_ref[...])))
        quarter = early_ref.shape[1]
        for index in range(RANKS):
            early_ref[index, :, 0:width] = grad_down[index * quarter:(index + 1) * quarter]
            early_ref[index, :, width:] = grad_down[(RANKS + index) * quarter:(RANKS + index + 1) * quarter]
        split_counts(counts_ref, table_ref, words)
        join_lanes((wq_ref, wk_ref, wv_ref), wqkv_ref)
        scaled = gpl_ref[...] * (1.0 / column(counts_ref[...].astype(F32)))
        down_ref[:, width:] = nt(scaled.astype(BF), wdown_ref[...])
        down_ref[:, :width] = scaled

    @pl.when(step < half_steps)
    def _():
        here = rows_at(step * rows, rows)
        for word in range(words):
            line = down_ref[pl.ds(step * words + word, 1), :width]
            at = slice(word * slots, (word + 1) * slots)
            gq_ref[at, :width] = jnp.broadcast_to(line, (slots, width))
            line = down_ref[pl.ds(step * words + word, 1), width:]
            gup_ref[at, :] = (jnp.broadcast_to(line, (slots, line.shape[1])) * slope_ref[at, :].astype(F32)).astype(BF)

        valid_col = any_lane(valid_slots(rows, slots, table_ref[pl.ds(step, 1), 0:words]))
        unit2, rate2 = norm_parts(first_ref[...])
        dup_ref[...] += tn((unit2 * gain2_ref[...]).astype(BF), gup_ref[...])
        upstream = nt(gup_ref[...], wup_ref[...])
        dgain_ref[1:2, :] += jnp.sum(upstream * unit2, axis=0, keepdims=True)
        grad_first = jnp.where(valid_col, gq_ref[:, :width], 0.0) + norm_back(upstream, gain2_ref[...], unit2, rate2)
        spread_ref[here, :] = grad_first
        grad_low = low(grad_first)
        dout_ref[...] += tn(mixed_ref[...], grad_low)
        gmix_ref[here, :] = low(nt(grad_low, wout_ref[...]))

    @pl.when(step == half_steps - 1)
    def _():
        mid_ref[0] = low(dup_ref[:, 0:2 * width])
        mid_ref[1] = low(dup_ref[:, 2 * width:])
        mid_ref[2] = dproj_ref[...]
        half = width // 2
        mid_ref[3, 0:half, 0:width] = low(dout_ref[0:half, :])
        mid_ref[3, 0:half, width:] = low(dout_ref[half:, :])
        mid_ref[3, half:, :] = jnp.zeros_like(mid_ref[3, half:, :])
        both = jnp.concatenate([dgain_ref[...], dgain_ref[...]], axis=1)
        mid_ref[3, half:half + 16, :] = low(jnp.concatenate([wgain_ref[...], both], axis=0))

    @pl.when((step >= half_steps) & (step < 2 * half_steps))
    def _():
        base = (step - half_steps) * rows
        for tile in range(rows // TILE):
            at = pl.ds(tile * TILE, TILE)
            here = rows_at(base + tile * TILE, TILE)
            for pair in range(CHEADS // 2):
                c0 = pair * TILE
                queries = split_heads(qkv_ref[at, c0:c0 + TILE])
                keys = split_heads(qkv_ref[at, width + c0:width + c0 + TILE])
                values = qkv_ref[at, 2 * width + c0:2 * width + c0 + TILE]
                grads = split_heads(gmix_ref[here, c0:c0 + TILE])
                probs_low = probs_ref[tile, pair]
                probs = probs_low.astype(F32)
                grad_probs = compact(nt(values, grads), slots)
                inner = jnp.sum(probs * grad_probs, axis=0, keepdims=True)
                grad_scores = (probs * (grad_probs - inner) * (CHD ** -0.5)).astype(BF)
                wide_scores = expand(grad_scores, slots)
                wide_probs = expand(probs_low, slots)
                all_ref[here, c0:c0 + TILE] = tn(stack_lanes(wide_scores), keys).astype(BF)
                all_ref[here, width + c0:width + c0 + TILE] = nn(wide_scores, queries).astype(BF)
                all_ref[here, 2 * width + c0:2 * width + c0 + TILE] = nn(wide_probs, grads).astype(BF)
        unit1, _ = norm_parts(x_ref[...].astype(F32))
        dqkv_ref[...] += tn((unit1 * gain1_ref[...]).astype(BF), all_ref[rows_at(base, rows), :])

    @pl.when(step == 2 * half_steps - 1)
    def _():
        half = width // 2
        for index in range(2):
            late_ref[index] = low(dqkv_ref[index * half:(index + 1) * half, 0:2 * width])
            late_ref[2, :, index * width:(index + 1) * width] = low(dqkv_ref[index * half:(index + 1) * half, 2 * width:])
        late_ref[3] = jnp.zeros_like(late_ref[3])

    @pl.when(step >= 2 * half_steps)
    def _():
        here = rows_at((step - 2 * half_steps) * rows, rows)
        unit1, rate1 = norm_parts(x_ref[...].astype(F32))
        upstream1 = nt(all_ref[here, :], wqkv_ref[...])
        dx_ref[...] = low(spread_ref[here, :] + norm_back(upstream1, gain1_ref[...], unit1, rate1))

    for at in range(3 * half_steps):
        todo = [(index, stages.index(at) + BEGIN[index]) for index, stages in reversed(list(enumerate(PLAN))) if at in stages]
        if todo:
            @pl.when(step == at)
            def _(todo=todo):
                for index, stage in todo:
                    if index < word_chains and stage == max(BEGIN[index], 1):
                        chains[index].fetch(own_sem.at[index]).wait()
                    chains[index].step(stage)

    @pl.when(step == steps - 1)
    def _():
        done = [begin + len(stages) for begin, stages in zip(BEGIN, PLAN)]
        while any(done[index] <= len(chains[index].stages) for index in range(CHAINS)):
            for index in reversed(range(CHAINS)):
                if done[index] <= len(chains[index].stages):
                    chains[index].step(done[index])
                    done[index] += 1
                    if done[index] > len(chains[index].stages):
                        leave[index].start()
        for copy in leave:
            copy.wait()


def char_backward(bits, x, counts, gain1, weights, wout, gain2, wup, wdown, grad_pooled, saved, grad_proj,
                  word_gains, word_grads):
    qkv, probs, mixed, first, slope, act_pool = saved
    rows, width = x.shape
    words = counts.shape[0]
    slots = rows // words
    hidden = wup.shape[1]
    wide = word_gains.shape[1]
    step = rows // CHAR_STEPS
    last = CHAR_STEPS - 1
    ahead = lambda i: i - ((i // CHAR_STEPS + 1) // 2) * (i - last)
    behind = lambda i: (i // CHAR_STEPS % 2) * (i - CHAR_STEPS) + (i // CHAR_STEPS // 2) * last
    inputs = lambda i: (i % CHAR_STEPS) * ((i // CHAR_STEPS + 1) // 2)
    final = lambda i: (i // CHAR_STEPS // 2) * (i - 2 * CHAR_STEPS)
    ahead_block = lambda cols: pl.BlockSpec((step, cols), lambda i: (ahead(i), 0))
    behind_block = lambda cols: pl.BlockSpec((step, cols), lambda i: (behind(i), 0))
    whole = lambda shape: pl.BlockSpec(shape, lambda i: (0,) * len(shape))
    tiles = step // TILE
    sum_shapes = [(wide, wide)] * 3 + [(RANKS, width // 2, wide), (RANKS, width, wide), (RANKS, width // 2, wide)]
    sources = [(RANKS,) + shape if len(shape) == 2 else shape for shape in sum_shapes]
    copies = sum(chain_copies(bits, index >= 3) for index in range(CHAINS))
    scratch = []
    for begin, shape in zip(BEGIN, sources):
        scratch += chain_scratch(bits, shape[1], wide, begin)
    return pl.pallas_call(
        functools.partial(char_backward_kernel, slots, bits),
        grid=(3 * CHAR_STEPS,),
        in_specs=[
            pl.BlockSpec((step, width), lambda i: (inputs(i), 0)),
            whole((1, words)),
            whole((1, width)),
            whole((width, width)),
            whole((width, width)),
            whole((width, width)),
            whole((width, width)),
            whole((1, width)),
            whole((width, hidden)),
            whole((hidden, width)),
            whole((words, width)),
            whole((words, hidden)),
            whole((width, wide)),
            whole((8, wide)),
            behind_block(3 * width),
            pl.BlockSpec((tiles, CHEADS // 2, slots, 2 * TILE), lambda i: (behind(i), 0, 0, 0)),
            ahead_block(width),
            ahead_block(width),
            ahead_block(hidden),
        ] + [pl.BlockSpec(memory_space=pl.ANY)] * 3,
        out_specs=[pl.BlockSpec((step, width), lambda i: (final(i), 0))] + [pl.BlockSpec(memory_space=pl.ANY)] * CHAINS,
        out_shape=[jax.ShapeDtypeStruct((rows, width), BF)]
        + [jax.ShapeDtypeStruct(shape, BF) for shape in sum_shapes],
        scratch_shapes=[
            pltpu.VMEM((words, width + hidden), F32),
            pltpu.VMEM((step, width), F32),
            pltpu.VMEM((rows, width), BF),
            pltpu.VMEM((step, hidden), BF),
            pltpu.VMEM((rows, width), F32),
            pltpu.VMEM((8, width), F32),
            pltpu.VMEM((width, 3 * width), F32),
            pltpu.VMEM((width, width), F32),
            pltpu.VMEM((width, hidden), F32),
            pltpu.VMEM((rows, 3 * width), BF),
            pltpu.VMEM((width, 3 * width), BF),
            pltpu.VMEM((CHAR_STEPS, TILE), jnp.int32),
        ] + [pltpu.VMEM(shape, BF) for shape in sources[3:]] + scratch
        + [pltpu.VMEM(shape, BF) for shape in sum_shapes] + [pltpu.SemaphoreType.DMA((copies,)), pltpu.SemaphoreType.DMA((copies,)), pltpu.SemaphoreType.DMA((2 * CHAINS,))],
        compiler_params=pltpu.CompilerParams(
            vmem_limit_bytes=63 << 20, collective_id=2, has_side_effects=True),
        name="char_backward",
    )(x, counts[None, :], gain1[None, :], *weights, wout, gain2[None, :],
      wup, wdown, grad_pooled, act_pool, grad_proj, word_gains, qkv, probs, mixed, first, slope, *word_grads)


def unpack_kernel(out_in, dx_in, wq_in, wk_in, wv_in, gain1_in, up_in, down_in, mix_in, turn_in, early_in, mid_in, late_in,
                  out_ref, dx_ref, gain1_ref, dq_ref, dk_ref, dv_ref, dout_ref, gain2_ref, dup_ref, ddown_ref, dproj_ref,
                  wgain1_ref, wq_ref, wk_ref, wv_ref, wout_ref, wgain2_ref, wup_ref, wdown_ref):
    step = pl.program_id(0)
    dx_ref[...] = dx_in[...].astype(F32)
    out_ref[...] = out_in[...]
    width = dq_ref.shape[0]
    half = width // 2
    wup_ref[...] = up_in[...].astype(F32)
    wdown_ref[...] = down_in[...].astype(F32)
    wq_ref[...] = mix_in[:, 0:TILE].astype(F32)
    wk_ref[...] = mix_in[:, TILE:2 * TILE].astype(F32)
    wv_ref[...] = mix_in[:, 2 * TILE:3 * TILE].astype(F32)
    for side in range(2):
        cols = slice(side * width, (side + 1) * width)
        ddown_ref[side] = early_in[0, :, cols].astype(F32)
        dup_ref[:, side * 2 * width:(side + 1) * 2 * width] = mid_in[side].astype(F32)
    dproj_ref[...] = mid_in[2].astype(F32)

    @pl.when(step < UNPACK_STEPS // 2)
    def _():
        for side in range(2):
            dout_ref[side] = mid_in[3, :, side * width:(side + 1) * width].astype(F32)

    @pl.when(step == UNPACK_STEPS // 2)
    def _():
        gains = mid_in[3, 0:16, :].astype(F32)
        wgain1_ref[...] = gains[0:1]
        wgain2_ref[...] = gains[1:2]
        gain2_ref[...] = gains[9:10, 0:width]

    @pl.when(step == 0)
    def _():
        wout_ref[...] = turn_in[...].astype(F32).T
        parts = []
        for index in range(2):
            at = slice(index * half, (index + 1) * half)
            cols = slice(index * width, (index + 1) * width)
            grads = (late_in[index, :, 0:width].astype(F32), late_in[index, :, width:].astype(F32),
                     late_in[2, :, cols].astype(F32))
            total = 0.0
            for grad, weight, target in zip(grads, (wq_in, wk_in, wv_in), (dq_ref, dk_ref, dv_ref)):
                target[at, :] = grad
                total += weight[at].astype(F32) * grad
            parts.append(jnp.sum(total, axis=1, keepdims=True))
        sums = jnp.concatenate(parts, axis=0)
        diagonal = (lax.broadcasted_iota(jnp.int32, (width, width), 0)
                    == lax.broadcasted_iota(jnp.int32, (width, width), 1))
        gain1_ref[...] = jnp.sum(jnp.where(diagonal, sums, 0.0), axis=0, keepdims=True) / gain1_in[...]


UNPACK_STEPS = 8


def unpack(word_output, grad_inputs, weights, gain1, sums, width, hidden):
    steps = UNPACK_STEPS
    up, down, mix, early, mid, late = sums
    wide = word_output.shape[1]
    whole = lambda shape: pl.BlockSpec(shape, lambda i: (0,) * len(shape))
    split = lambda shape: pl.BlockSpec((shape[0] // steps, shape[1]), lambda i: (i, 0))
    middle = lambda shape: pl.BlockSpec((shape[0], shape[1] // steps, shape[2]), lambda i: (0, i, 0))
    per = early.shape[1] * RANKS // steps
    blocks = early.shape[1] // per
    pinned = lambda i: i - (i // (steps // 2)) * (i - (steps // 2 - 1))
    outs = [
        (whole, (1, width)), (whole, (width, width)), (whole, (width, width)), (whole, (width, width)),
        (lambda shape: pl.BlockSpec((2, shape[1] * 2 // steps, width), lambda i: (0, pinned(i), 0)), (2, width // 2, width)),
        (whole, (1, width)), (split, (width, hidden)), (middle, (2, hidden // 2, width)), (split, (width, wide)),
        (whole, (1, wide)), (split, (wide, TILE)), (split, (wide, TILE)), (split, (wide, TILE)),
        (whole, (TILE, wide)), (whole, (1, wide)), (split, (wide, wide)), (split, (wide, wide)),
    ]
    results = pl.pallas_call(
        unpack_kernel,
        grid=(steps,),
        in_specs=[split(word_output.shape), split(grad_inputs.shape)] + [whole((width, width))] * 3 + [whole((1, width))]
        + [split(up.shape), split(down.shape), split(mix.shape), pl.BlockSpec((wide, TILE), lambda i: (0, 3)),
           pl.BlockSpec((1, per, wide), lambda i: (i // blocks, i % blocks, 0)), middle(mid.shape), whole(late.shape)],
        out_specs=[split(word_output.shape), split(grad_inputs.shape)] + [spec(shape) for spec, shape in outs],
        out_shape=[jax.ShapeDtypeStruct(word_output.shape, BF), jax.ShapeDtypeStruct(grad_inputs.shape, F32)]
        + [jax.ShapeDtypeStruct(shape, F32) for _, shape in outs],
        compiler_params=pltpu.CompilerParams(vmem_limit_bytes=60 << 20),
        name="unpack",
    )(word_output, grad_inputs, *weights, gain1[None, :], up, down, mix, mix, early, mid, late)

    def shaped(array):
        if array.ndim == 3:
            return array.reshape(-1, array.shape[2])
        return array[0] if array.shape[0] == 1 else array

    return tuple(shaped(array) for array in results)


def per_device(
    bits,
    char_inputs,
    char_counts,
    doc_ids,
    cotangent,
    char_norm_one,
    char_query,
    char_key,
    char_value,
    char_out,
    char_norm_two,
    char_up,
    char_down,
    char_proj,
    word_norm_one,
    word_query,
    word_key,
    word_value,
    word_out_proj,
    word_norm_two,
    word_up,
    word_down,
):
    char_qkv = (char_query, char_key, char_value)
    word_qkv = (word_query, word_key, word_value)
    vec, pooled, *saved, near, qkv_all, out_all, up_all, down_all = char_forward(
        char_inputs, char_counts, char_norm_one, char_qkv, char_out, char_norm_two, char_up, char_down, char_proj,
        word_qkv, word_out_proj, word_up, word_down,
    )
    word_output, grad_pooled, grad_proj, word_gains, *word_grads = word_layer(
        bits, vec, near, doc_ids, cotangent, qkv_all, out_all, up_all, down_all,
        word_norm_one, word_norm_two, char_proj, pooled,
    )
    grad_inputs, *sums = char_backward(
        bits, char_inputs, char_counts, char_norm_one, char_qkv, char_out, char_norm_two, char_up, char_down,
        grad_pooled, saved, grad_proj, word_gains, word_grads,
    )
    return unpack(word_output, grad_inputs, char_qkv, char_norm_one, sums, char_out.shape[0], char_up.shape[1])


def solution(mesh):
    in_specs = (
        P(("dp", "tensor"), None),
        P(("dp", "tensor")),
        P("dp", None),
        P("dp", None),
        P(),
        P(),
        P(),
        P(),
        P(),
        P(),
        P(),
        P(),
        P(),
        P(),
        P(None, "tensor"),
        P(None, "tensor"),
        P(None, "tensor"),
        P("tensor", None),
        P(),
        P(None, "tensor"),
        P("tensor", None),
    )
    out_specs = (
        P(("dp", "tensor"), None),
        P(("dp", "tensor"), None),
        P(),
        P(),
        P(),
        P(),
        P(),
        P(),
        P(),
        P(),
        P(),
        P(),
        P(None, "tensor"),
        P(None, "tensor"),
        P(None, "tensor"),
        P("tensor", None),
        P(),
        P(None, "tensor"),
        P("tensor", None),
    )
    assert mesh.shape["tensor"] == RANKS
    bits = mesh.shape["dp"].bit_length() - 1
    assert bits >= 3 and mesh.shape["dp"] == 1 << bits
    return jax.shard_map(
        functools.partial(per_device, bits), mesh=mesh, in_specs=in_specs, out_specs=out_specs, check_vma=False
    )
```

```python
import functools

import jax
import jax.numpy as jnp
from jax import lax
from jax.experimental import pallas as pl
from jax.experimental.pallas import tpu as pltpu
from jax.sharding import PartitionSpec as P

BF = jnp.bfloat16
F32 = jnp.float32
EPSILON = 1e-05
NEG_LARGE = -1e30
RANKS = 4
CHEADS = 4
CHD = 64
TILE = 128
CHAR_STEPS = 8
GELU_C = 0.7978845608028654
GELU_A = 0.044715


def nn(left, right):
    return lax.dot_general(left, right, (((1,), (0,)), ((), ())), preferred_element_type=F32)


def nt(left, right):
    return lax.dot_general(left, right, (((1,), (1,)), ((), ())), preferred_element_type=F32)


def tn(left, right):
    return lax.dot_general(left, right, (((0,), (0,)), ((), ())), preferred_element_type=F32)


def norm_parts(values):
    centre = values - jnp.mean(values, axis=-1, keepdims=True)
    spread = jnp.mean(centre * centre, axis=-1, keepdims=True)
    rate = lax.rsqrt(spread + EPSILON)
    return centre * rate, rate


def norm_back(upstream, gain, unit, rate):
    scaled = upstream * gain
    first = jnp.mean(scaled, axis=-1, keepdims=True)
    second = jnp.mean(scaled * unit, axis=-1, keepdims=True)
    return rate * (scaled - first - unit * second)


def gelu_parts(values):
    square = values * values
    inner = values * (GELU_C + (GELU_C * GELU_A) * square)
    half = 0.5 + 0.5 * jnp.tanh(inner)
    active = values * half
    slope = half + (active * (1.0 - half)) * (2.0 * GELU_C + (6.0 * GELU_C * GELU_A) * square)
    return active, slope


def split_heads(pair):
    low_half = lax.broadcasted_iota(jnp.int32, pair.shape, 1) < CHD
    zero = jnp.zeros_like(pair)
    return jnp.concatenate([jnp.where(low_half, pair, zero), jnp.where(low_half, zero, pair)], axis=0)


def word_of_lane(shape, slots):
    lane = lax.broadcasted_iota(jnp.int32, shape, 1)
    return jnp.bitwise_and(lane, TILE - 1) // slots


def compact(scores, slots):
    words = word_of_lane((slots, scores.shape[1]), slots)
    result = scores[0:slots]
    for word in range(1, TILE // slots):
        result = jnp.where(words == word, scores[word * slots:(word + 1) * slots], result)
    return result


def expand(packed, slots):
    words = word_of_lane(packed.shape, slots)
    zero = jnp.zeros_like(packed)
    return jnp.concatenate(
        [jnp.where(words == word, packed, zero) for word in range(TILE // slots)], axis=0
    )


def stack_lanes(pair):
    return jnp.concatenate([pair[:, :TILE], pair[:, TILE:]], axis=0)


def split_counts(counts_ref, table_ref, words):
    for step in range(CHAR_STEPS):
        table_ref[step:step + 1, 0:words] = counts_ref[:, step * words:(step + 1) * words]


def valid_slots(rows, slots, mine):
    words = rows // slots
    row = lax.broadcasted_iota(jnp.int32, (rows, words), 0)
    word = lax.broadcasted_iota(jnp.int32, (rows, words), 1)
    return (row // slots == word) & (jnp.bitwise_and(row, slots - 1) < mine)


def join_lanes(parts, whole_ref):
    width = parts[0].shape[1]
    for index, part in enumerate(parts):
        whole_ref[:, index * width:(index + 1) * width] = part[...]


def any_lane(mask):
    return jnp.max(jnp.where(mask, 1.0, 0.0), axis=1, keepdims=True) > 0.0


def column(row):
    size = row.shape[1]
    diagonal = (lax.broadcasted_iota(jnp.int32, (size, size), 0)
                == lax.broadcasted_iota(jnp.int32, (size, size), 1))
    return jnp.sum(jnp.where(diagonal, row, 0.0), axis=1, keepdims=True)


MESH = pl.DeviceIdType.MESH
LANE_SPLIT = 256


class Place:
    def __init__(self):
        self.dp = lax.axis_index("dp")
        self.rank = lax.axis_index("tensor")
        self.core = lax.rem(self.dp, 2)
        self.x = lax.rem(self.dp // 2, 2)
        self.y = lax.rem(self.dp // 4, 2)
        self.core_mate = (self.dp + 1 - 2 * self.core, self.rank)
        self.x_mate = (self.dp + 2 - 4 * self.x, self.rank)
        self.y_mate = (self.dp + 4 - 8 * self.y, self.rank)

    def ring(self, offset):
        return lax.rem(self.rank + offset, RANKS)

    def ring_device(self, offset):
        return (self.dp, self.ring(offset))

    def bit_mate(self, bit):
        size = 1 << bit
        mine = lax.rem(self.dp // size, 2)
        return (self.dp + size - 2 * size * mine, self.rank)

    def mates(self, bits):
        extra = [self.bit_mate(bit) for bit in range(3, bits)]
        return [self.core_mate, self.x_mate, self.y_mate] + extra


def meet(devices):
    barrier = pltpu.get_barrier_semaphore()
    for device in devices:
        pl.semaphore_signal(barrier, inc=1, device_id=device, device_id_type=MESH)
    pl.semaphore_wait(barrier, len(devices))


def remote(source, target, sems, device):
    return pltpu.make_async_remote_copy(
        src_ref=source, dst_ref=target, send_sem=sems[0], recv_sem=sems[1],
        device_id=device, device_id_type=MESH,
    )


class Sems:
    def __init__(self, send, recv, start=0):
        self.send, self.recv, self.next = send, recv, start

    def take(self):
        at = self.next
        self.next += 1
        return self.send.at[at], self.recv.at[at]


def rows_at(start, size):
    return pl.ds(pl.multiple_of(start, 16), size)


def halves(width):
    return (slice(0, LANE_SPLIT), slice(LANE_SPLIT, width))


class Gather:
    def __init__(self, place, local, whole, sems):
        self.stages = [[], [], [], []]
        rows = local.shape[0]
        unit = rows // 8
        p = place
        left, right = halves(local.shape[1])
        left_at = p.core * 4 + p.x * 2 + p.y
        right_at = p.core * 4 + p.y * 2 + p.x
        for offset in range(1, RANKS):
            for lanes, at in ((left, left_at), (right, right_at)):
                at = rows_at(at * unit, unit)
                self.stages[0].append(remote(
                    local.at[at, lanes], whole.at[p.rank, at, lanes], sems.take(), p.ring_device(offset)))
        for offset in range(1, RANKS):
            rank = p.ring(offset)
            for lanes, at, first, second, mate_first, mate_second in (
                (left, left_at, p.x, None, p.y_mate, p.x_mate),
                (right, right_at, p.y, None, p.x_mate, p.y_mate),
            ):
                one = rows_at(at * unit, unit)
                two = rows_at((p.core * 4 + first * 2) * unit, 2 * unit)
                self.stages[1].append(remote(
                    whole.at[rank, one, lanes], whole.at[rank, one, lanes], sems.take(), mate_first))
                self.stages[2].append(remote(
                    whole.at[rank, two, lanes], whole.at[rank, two, lanes], sems.take(), mate_second))
            four = rows_at(p.core * 4 * unit, 4 * unit)
            self.stages[3].append(remote(
                whole.at[rank, four], whole.at[rank, four], sems.take(), p.core_mate))

    def start(self, stage):
        for copy in self.stages[stage]:
            copy.start()

    def wait(self, stage):
        for copy in self.stages[stage]:
            copy.wait()


def gather_copies():
    return 2 * (RANKS - 1) * 3 + (RANKS - 1)


class Chain:
    def __init__(self, place, bits, src, refs, sems, everywhere):
        p = place
        buf, got_core, got_one, got_two, got_more, got_rank, out = refs
        self.p, self.src, self.everywhere = p, src, everywhere
        self.buf, self.got_core, self.got_one, self.got_two = buf, got_core, got_one, got_two
        self.got_more, self.got_rank = got_more, got_rank
        self.mine = out.at[p.rank] if everywhere else out
        unit = src.shape[1] // 8
        lanes = left, right = halves(src.shape[2])
        self.lanes = lanes
        self.own = rows_at(p.core * 4 * unit, 4 * unit)
        stages = [("core", [remote(src.at[:, rows_at((1 - p.core) * 4 * unit, 4 * unit)], got_core,
                                   sems.take(), p.core_mate)])]
        first, second = (p.x, p.y), (p.y, p.x)
        first_mate, second_mate = (p.x_mate, p.y_mate), (p.y_mate, p.x_mate)
        one = lambda side, at: rows_at(at * 2 * unit, 2 * unit)
        two = lambda side, at: rows_at((first[side] * 2 + at) * unit, unit)
        self.one_rows = [one(side, first[side]) for side in (0, 1)]
        self.two_rows = [two(side, second[side]) for side in (0, 1)]
        stages.append(("one", [
            remote(buf.at[:, one(side, 1 - first[side]), lanes[side]], got_one.at[:, :, lanes[side]],
                   sems.take(), first_mate[side]) for side in (0, 1)]))
        stages.append(("two", [
            remote(buf.at[:, two(side, 1 - second[side]), lanes[side]], got_two.at[:, :, lanes[side]],
                   sems.take(), second_mate[side]) for side in (0, 1)]))
        for bit in range(3, bits):
            stages.append((bit - 3, [
                remote(buf.at[:, self.two_rows[side], lanes[side]], got_more.at[bit - 3, :, :, lanes[side]],
                       sems.take(), p.bit_mate(bit)) for side in (0, 1)]))
        stages.append(("rank", [
            remote(buf.at[p.ring(offset), self.two_rows[side], lanes[side]],
                   got_rank.at[offset - 1, :, lanes[side]], sems.take(), p.ring_device(offset))
            for offset in range(1, RANKS) for side in (0, 1)]))
        base = p.core * 4 * unit
        self.out_two = [rows_at(base + (first[side] * 2 + second[side]) * unit, unit) for side in (0, 1)]
        out_one = [rows_at(base + first[side] * 2 * unit, 2 * unit) for side in (0, 1)]
        if everywhere:
            stages.append(("rank_back", [
                remote(out.at[p.rank, self.out_two[side], lanes[side]], out.at[p.rank, self.out_two[side], lanes[side]],
                       sems.take(), p.ring_device(offset))
                for offset in range(1, RANKS) for side in (0, 1)]))

        def back(at, part_lanes, mate):
            part = out.at[:, at, part_lanes] if everywhere else out.at[at, part_lanes]
            return remote(part, part, sems.take(), mate)

        stages.append(("back_two", [back(self.out_two[side], lanes[side], second_mate[side]) for side in (0, 1)]))
        stages.append(("back_one", [back(out_one[side], lanes[side], first_mate[side]) for side in (0, 1)]))
        stages.append(("back_core", [back(self.own, slice(None), p.core_mate)]))
        self.stages = stages

    def fetch(self, sem):
        return pltpu.make_async_copy(self.src.at[:, self.own], self.buf, sem)

    def start(self, index):
        for copy in self.stages[index][1]:
            copy.start()

    def finish(self, index):
        name, copies = self.stages[index]
        for copy in copies:
            copy.wait()
        buf = self.buf
        if name == "core":
            own = self.src if self.everywhere else None
            for quarter in range(RANKS):
                mine = own[quarter, self.own, :] if self.everywhere else buf[quarter]
                buf[quarter] = mine + self.got_core[quarter]
        elif name == "one":
            for at, lanes in zip(self.one_rows, self.lanes):
                for quarter in range(RANKS):
                    buf[quarter, at, lanes] += self.got_one[quarter, :, lanes]
        elif name == "two":
            for at, lanes in zip(self.two_rows, self.lanes):
                for quarter in range(RANKS):
                    buf[quarter, at, lanes] += self.got_two[quarter, :, lanes]
        elif name == "rank":
            for side in (0, 1):
                at, lanes = self.two_rows[side], self.lanes[side]
                total = buf[self.p.rank, at, lanes].astype(F32)
                for k in range(RANKS - 1):
                    total = total + self.got_rank[k, :, lanes].astype(F32)
                self.mine[self.out_two[side], lanes] = total.astype(BF)
        elif isinstance(name, int):
            for at, lanes in zip(self.two_rows, self.lanes):
                for quarter in range(RANKS):
                    buf[quarter, at, lanes] += self.got_more[name, quarter, :, lanes]

    def step(self, index):
        if index:
            self.finish(index - 1)
        if index < len(self.stages):
            self.start(index)


def chain_copies(bits, everywhere):
    pairs = 2 * (RANKS - 1)
    return 1 + 2 + 2 + 2 * (bits - 3) + pairs + (pairs if everywhere else 0) + 2 + 2 + 1


def chain_scratch(bits, rows, lanes):
    unit = rows // 8
    return [
        pltpu.VMEM((RANKS, 4 * unit, lanes), BF),
        pltpu.VMEM((RANKS, 4 * unit, lanes), BF),
        pltpu.VMEM((RANKS, 2 * unit, lanes), BF),
        pltpu.VMEM((RANKS, unit, lanes), BF),
        pltpu.VMEM((max(bits - 3, 1), RANKS, unit, lanes), BF),
        pltpu.VMEM((RANKS - 1, unit, lanes), BF),
    ]


FORWARD_PLAN = {
    2: ((0, 1), (1, 1)),
    3: ((2, 1), (0, 2), (1, 2)),
    4: ((3, 1), (2, 2)),
    5: ((0, 3), (1, 3), (3, 2)),
    6: ((2, 3),),
    7: ((3, 3),),
}


def char_forward_kernel(slots, x_ref, counts_ref, gain1_ref, wq_ref, wk_ref, wv_ref, wout_ref,
                        gain2_ref, wup_ref, wdown_ref, wproj_ref,
                        lq_ref, lk_ref, lv_ref, lout_ref, lup_ref, ldown_ref,
                        vec_ref, pooled_ref, qkv_ref, probs_ref, mixed_ref, first_ref,
                        slope_ref, act_pool_ref, normed_ref, near_ref, wqkv_all, wout_all, wup_all, wdown_all,
                        wqkv_ref, lqkv_ref, table_ref, own_sem, send_sem, recv_sem):
    rows = x_ref.shape[0]
    width = x_ref.shape[1]
    step = pl.program_id(0)
    steps = pl.num_programs(0)
    words = rows // slots
    p = Place()
    pairs = ((lqkv_ref, wqkv_all), (lout_ref, wout_all), (lup_ref, wup_all), (ldown_ref, wdown_all))
    gathers = [Gather(p, mine, whole, Sems(send_sem, recv_sem, gather_copies() * index))
               for index, (mine, whole) in enumerate(pairs)]
    own_copies = [pltpu.make_async_copy(mine, whole.at[p.rank], own_sem.at[index])
                  for index, (mine, whole) in enumerate(pairs)]
    vec_base = gather_copies() * len(pairs)

    def vec_copies(at):
        copies = []
        for slot, offset in ((1, 1), (0, 2)):
            sem = vec_base + 2 * at + slot
            part = rows_at(at * words, words)
            copies.append(remote(vec_ref.at[part], near_ref.at[slot, part],
                                 (send_sem.at[sem], recv_sem.at[sem]), p.ring_device(offset)))
        return copies

    def send_vec(at):
        for offset, copy in zip((1, 2), vec_copies(at)):
            @pl.when(p.rank + offset < RANKS)
            def _(copy=copy):
                copy.start()

    def wait_vec(at):
        for offset, copy in zip((1, 2), vec_copies(at)):
            @pl.when(p.rank + offset < RANKS)
            def _(copy=copy):
                copy.wait_send()

            @pl.when(p.rank >= offset)
            def _(copy=copy):
                copy.wait_recv()

    @pl.when(step == 0)
    def _():
        join_lanes((lq_ref, lk_ref, lv_ref), lqkv_ref)
        join_lanes((wq_ref, wk_ref, wv_ref), wqkv_ref)
        meet([p.ring_device(offset) for offset in (1, 2, 3)] + [p.core_mate, p.x_mate, p.y_mate])
        split_counts(counts_ref, table_ref, words)
        for copy in own_copies:
            copy.start()
        for gather in gathers:
            gather.start(0)

    base = x_ref[...].astype(F32)
    unit, _ = norm_parts(base)
    normed = (unit * gain1_ref[...]).astype(BF)
    normed_ref[...] = normed
    qkv_ref[...] = nn(normed, wqkv_ref[...]).astype(BF)
    mine = table_ref[pl.ds(step, 1), 0:words]
    word_at = lax.broadcasted_iota(jnp.int32, (words, rows), 0)
    row_at = lax.broadcasted_iota(jnp.int32, (words, rows), 1)
    onto_rows = jnp.where(row_at // slots == word_at, 1.0, 0.0).astype(BF)
    row_counts = nn(jnp.broadcast_to(mine.astype(F32), (16, words)).astype(BF), onto_rows)[0:1]
    for tile in range(rows // TILE):
        at = pl.ds(tile * TILE, TILE)
        valid = (lax.broadcasted_iota(jnp.int32, (slots, TILE), 0).astype(F32)
                 < row_counts[:, tile * TILE:(tile + 1) * TILE])
        for pair in range(CHEADS // 2):
            c0 = pair * TILE
            queries = split_heads(qkv_ref[at, c0:c0 + TILE])
            keys = qkv_ref[at, width + c0:width + c0 + TILE]
            values = split_heads(qkv_ref[at, 2 * width + c0:2 * width + c0 + TILE])
            scores = compact(nt(keys, queries), slots)
            parts = []
            for head in range(2):
                own = jnp.where(valid, scores[:, head * TILE:(head + 1) * TILE], NEG_LARGE)
                top = jnp.max(own, axis=0, keepdims=True)
                weight = jnp.exp((own - top) * (CHD ** -0.5))
                parts.append(weight / jnp.sum(weight, axis=0, keepdims=True))
            probs = jnp.concatenate(parts, axis=1).astype(BF)
            probs_ref[tile, pair] = probs
            mixed_ref[at, c0:c0 + TILE] = tn(stack_lanes(expand(probs, slots)), values).astype(BF)

    for at, todo in FORWARD_PLAN.items():
        @pl.when(step == at)
        def _(todo=todo):
            for member, stage in todo:
                gathers[member].wait(stage - 1)
                gathers[member].start(stage)

    @pl.when(step > 0)
    def _():
        send_vec(step - 1)

    first = base + nn(mixed_ref[...], wout_ref[...])
    first_ref[...] = first
    unit2, _ = norm_parts(first)
    normed2 = (unit2 * gain2_ref[...]).astype(BF)
    members = valid_slots(rows, slots, mine)
    valid_col = any_lane(members)
    pool = jnp.where(members, 1.0 / mine.astype(F32), 0.0).astype(BF)
    chunk = 256
    for part in range(wup_ref.shape[1] // chunk):
        cols = slice(part * chunk, (part + 1) * chunk)
        active, slope = gelu_parts(nn(normed2, wup_ref[:, cols]))
        slope_ref[:, cols] = jnp.where(valid_col, slope, 0.0).astype(BF)
        act_pool_ref[:, cols] = tn(pool, active.astype(BF)).astype(BF)
    pooled = tn(pool, first.astype(BF)) + nn(act_pool_ref[...], wdown_ref[...])
    pooled = pooled.astype(BF)
    pooled_ref[...] = pooled
    vec_ref[rows_at(step * words, words), :] = nn(pooled, wproj_ref[...]).astype(BF)

    @pl.when(step == steps - 1)
    def _():
        send_vec(step)
        for copy in own_copies:
            copy.wait()
        for gather in gathers:
            gather.wait(3)
        for at in range(CHAR_STEPS):
            wait_vec(at)


def char_forward(x, counts, gain1, weights, wout, gain2, wup, wdown, wproj, local, lout, lup, ldown):
    rows, width = x.shape
    words = counts.shape[0]
    slots = rows // words
    hidden = wup.shape[1]
    wide = wproj.shape[1]
    step = rows // CHAR_STEPS
    step_words = step // slots
    row_block = lambda cols: pl.BlockSpec((step, cols), lambda i: (i, 0))
    word_block = lambda cols: pl.BlockSpec((step_words, cols), lambda i: (i, 0))
    whole = lambda shape: pl.BlockSpec(shape, lambda i: (0, 0))
    tiles = step // TILE
    return pl.pallas_call(
        functools.partial(char_forward_kernel, slots),
        grid=(rows // step,),
        in_specs=[
            row_block(width),
            whole((1, words)),
            whole((1, width)),
            whole((width, width)),
            whole((width, width)),
            whole((width, width)),
            whole((width, width)),
            whole((1, width)),
            whole((width, hidden)),
            whole((hidden, width)),
            whole((width, wide)),
            whole(local[0].shape),
            whole(local[0].shape),
            whole(local[0].shape),
            whole(lout.shape),
            whole(lup.shape),
            whole(ldown.shape),
        ],
        out_specs=[
            whole((words, wide)),
            word_block(width),
            row_block(3 * width),
            pl.BlockSpec((tiles, CHEADS // 2, slots, 2 * TILE), lambda i: (i, 0, 0, 0)),
            row_block(width),
            row_block(width),
            row_block(hidden),
            word_block(hidden),
            row_block(width),
        ] + [pl.BlockSpec(memory_space=pl.ANY)] * 5,
        out_shape=[
            jax.ShapeDtypeStruct((words, wide), BF),
            jax.ShapeDtypeStruct((words, width), BF),
            jax.ShapeDtypeStruct((rows, 3 * width), BF),
            jax.ShapeDtypeStruct((rows // TILE, CHEADS // 2, slots, 2 * TILE), BF),
            jax.ShapeDtypeStruct((rows, width), BF),
            jax.ShapeDtypeStruct((rows, width), F32),
            jax.ShapeDtypeStruct((rows, hidden), BF),
            jax.ShapeDtypeStruct((words, hidden), BF),
            jax.ShapeDtypeStruct((rows, width), BF),
            jax.ShapeDtypeStruct((2, words, wide), BF),
            jax.ShapeDtypeStruct((RANKS, wide, 3 * TILE), BF),
            jax.ShapeDtypeStruct((RANKS,) + lout.shape, BF),
            jax.ShapeDtypeStruct((RANKS,) + lup.shape, BF),
            jax.ShapeDtypeStruct((RANKS,) + ldown.shape, BF),
        ],
        scratch_shapes=[
            pltpu.VMEM((width, 3 * width), BF),
            pltpu.VMEM((wide, 3 * TILE), BF),
            pltpu.VMEM((CHAR_STEPS, TILE), jnp.int32),
            pltpu.SemaphoreType.DMA((4,)),
            pltpu.SemaphoreType.DMA((gather_copies() * 4 + 2 * CHAR_STEPS,)),
            pltpu.SemaphoreType.DMA((gather_copies() * 4 + 2 * CHAR_STEPS,)),
        ],
        compiler_params=pltpu.CompilerParams(
            vmem_limit_bytes=60 << 20, collective_id=0, has_side_effects=True),
        name="char_forward",
    )(x, counts[None, :], gain1[None, :], *weights, wout, gain2[None, :], wup, wdown, wproj,
      *local, lout, lup, ldown)


def word_kernel(bits, vec_ref, near_ref, docs_ref, cot_ref, wqkv_in, wout_in, wup_in,
                wdown_in, gain1_ref, gain2_ref, wproj_ref, pooled_ref,
                out_ref, gpl_ref, dproj_ref, dgain_ref, up_grad_out, down_grad_out, mix_grad_out,
                n1_ref, q_ref, kv_ref, probs_ref, o_ref, act_ref, slope_ref, go_ref, gq_ref, gkv_ref,
                back_ref, cot_own, cot_sem, part_ref, got_ref, table_ref, wqkv_ref, wout_ref, wup_ref, wdown_ref,
                up_grad_ref, down_grad_ref, mix_grad_ref, io_sem, send_sem, recv_sem):
    p = Place()
    words, wide = vec_ref.shape
    window = 3 * words
    fetch = pltpu.make_async_copy(cot_ref.at[rows_at(p.rank * words, words)], cot_own, cot_sem)
    loads = [pltpu.make_async_copy(source, target, io_sem.at[index]) for index, (source, target) in enumerate((
        (wqkv_in, wqkv_ref), (wout_in, wout_ref), (wup_in, wup_ref), (wdown_in, wdown_ref)))]
    stores = [pltpu.make_async_copy(source, target, io_sem.at[4 + index]) for index, (source, target) in enumerate((
        (up_grad_ref, up_grad_out), (down_grad_ref, down_grad_out)))]

    def store_mix(rank):
        return pltpu.make_async_copy(mix_grad_ref.at[rank], mix_grad_out.at[rank], io_sem.at[6 + rank])

    for copy in loads:
        copy.start()
    fetch.start()
    meet([p.ring_device(offset) for offset in (1, 2, 3)])

    table_ref[:, 0:2 * words] = jnp.full((1, 2 * words), -1, jnp.int32)
    table_ref[:, 2 * words:] = docs_ref[...]
    start = pl.multiple_of(p.rank * words, TILE)
    key_docs = table_ref[:, pl.ds(start, window)].astype(F32)
    row_docs = column(key_docs[:, 2 * words:])

    own = vec_ref[...].astype(F32)
    unit1, rate1 = norm_parts(own)
    n1_ref[2 * words:, :] = (unit1 * gain1_ref[...]).astype(BF)
    for slot in range(2):
        near = jnp.where(p.rank + slot >= 2, near_ref[slot].astype(F32), 0.0)
        unit, _ = norm_parts(near)
        n1_ref[slot * words:(slot + 1) * words, :] = (unit * gain1_ref[...]).astype(BF)

    def project(rank, carry):
        q_ref[rank] = nn(n1_ref[2 * words:, :], wqkv_ref[rank, :, 0:TILE]).astype(BF)
        kv_ref[rank] = nn(n1_ref[...], wqkv_ref[rank, :, TILE:]).astype(BF)
        scores = nt(split_heads(q_ref[rank]), kv_ref[rank, :, 0:TILE]) * (CHD ** -0.5)
        row = lax.broadcasted_iota(jnp.int32, (words, window), 0)
        key = lax.broadcasted_iota(jnp.int32, (words, window), 1)
        allowed = (row_docs == key_docs) & (key <= row + 2 * words)
        for head in range(2):
            at = slice(head * words, (head + 1) * words)
            masked = jnp.where(allowed, scores[at], NEG_LARGE)
            top = jnp.max(masked, axis=-1, keepdims=True)
            weight = jnp.exp(masked - top)
            probs_ref[rank, at, :] = (weight * (1.0 / jnp.sum(weight, axis=-1, keepdims=True))).astype(BF)
        pair = jnp.concatenate([probs_ref[rank, 0:words, :], probs_ref[rank, words:, :]], axis=1)
        o_ref[rank] = nn(pair, split_heads(kv_ref[rank, :, TILE:])).astype(BF)
        back_ref[...] += nn(o_ref[rank], wout_ref[rank])
        return carry

    back_ref[...] = own
    loads[0].wait()
    loads[1].wait()
    lax.fori_loop(0, RANKS, project, 0)
    middle = back_ref[...]
    unit2, rate2 = norm_parts(middle)
    normed2 = (unit2 * gain2_ref[...]).astype(BF)

    def feed(rank, carry):
        active, slope = gelu_parts(nn(normed2, wup_ref[rank]))
        act_ref[rank] = active.astype(BF)
        slope_ref[rank] = slope.astype(BF)
        back_ref[...] += nn(act_ref[rank], wdown_ref[rank])
        return carry

    loads[2].wait()
    loads[3].wait()
    lax.fori_loop(0, RANKS, feed, 0)
    out_ref[...] = back_ref[...].astype(BF)
    fetch.wait()
    back_ref[...] = jnp.zeros_like(back_ref)

    def feed_back(rank, carry):
        upstream = (nt(cot_own[...], wdown_ref[rank]) * slope_ref[rank].astype(F32)).astype(BF)
        back_ref[...] += nt(upstream, wup_ref[rank])
        up_grad_ref[rank] = tn(normed2, upstream).astype(BF)
        down_grad_ref[rank] = tn(act_ref[rank], cot_own[...]).astype(BF)
        return carry

    lax.fori_loop(0, RANKS, feed_back, 0)
    for copy in stores:
        copy.start()
    upstream2 = back_ref[...]
    dgain_ref[...] = jnp.zeros_like(dgain_ref)
    dgain_ref[1:2, :] = jnp.sum(upstream2 * unit2, axis=0, keepdims=True)
    grad_middle = cot_own[...].astype(F32) + norm_back(upstream2, gain2_ref[...], unit2, rate2)
    middle_low = grad_middle.astype(BF)

    back_ref[...] = jnp.zeros_like(back_ref)
    part_ref[...] = jnp.zeros_like(part_ref)

    def attend_back(rank, carry):
        go_ref[...] = nt(middle_low, wout_ref[rank]).astype(BF)
        mix_grad_ref[rank, :, 3 * TILE:] = tn(middle_low, o_ref[rank]).astype(BF)
        go_pair = split_heads(go_ref[...])
        grad_probs = nt(go_pair, kv_ref[rank, :, TILE:])
        probs = probs_ref[rank].astype(F32)
        inner = jnp.sum(probs * grad_probs, axis=-1, keepdims=True)
        grad_scores = (probs * (grad_probs - inner) * (CHD ** -0.5)).astype(BF)
        q_pair = split_heads(q_ref[rank])
        gkv_ref[:, 0:TILE] = tn(grad_scores, q_pair).astype(BF)
        gkv_ref[:, TILE:] = tn(probs_ref[rank], go_pair).astype(BF)
        pair = jnp.concatenate([grad_scores[0:words], grad_scores[words:]], axis=1)
        gq_ref[...] = nn(pair, split_heads(kv_ref[rank, :, 0:TILE])).astype(BF)
        part_ref[...] += nt(gkv_ref[0:2 * words, :], wqkv_ref[rank, :, TILE:])
        back_ref[...] += nt(gkv_ref[2 * words:, :], wqkv_ref[rank, :, TILE:])
        back_ref[...] += nt(gq_ref[...], wqkv_ref[rank, :, 0:TILE])
        mix_grad_ref[rank, :, 0:TILE] = tn(n1_ref[2 * words:, :], gq_ref[...]).astype(BF)
        mix_grad_ref[rank, :, TILE:3 * TILE] = tn(n1_ref[...], gkv_ref[...]).astype(BF)
        store_mix(rank).start()
        return carry

    lax.fori_loop(0, RANKS, attend_back, 0)
    near_ref_low = got_ref.at[2]
    near_ref_low[...] = part_ref[...].astype(BF).reshape(2, words, wide)
    sends = []
    for slot, offset in ((0, RANKS - 2), (1, RANKS - 1)):
        sends.append(remote(got_ref.at[2, slot], got_ref.at[slot, 0], (send_sem.at[slot], recv_sem.at[slot]),
                            p.ring_device(offset)))
    for copy in sends:
        copy.start()
    for copy in sends:
        copy.wait()
    upstream1 = back_ref[...] + got_ref[0, 0].astype(F32) + got_ref[1, 0].astype(F32)
    dgain_ref[0:1, :] = jnp.sum(upstream1 * unit1, axis=0, keepdims=True)
    grad_vec = (grad_middle + norm_back(upstream1, gain1_ref[...], unit1, rate1)).astype(BF)
    dproj_ref[...] = tn(pooled_ref[...], grad_vec).astype(BF)
    gpl_ref[...] = nt(grad_vec, wproj_ref[...])
    for copy in stores + [store_mix(rank) for rank in range(RANKS)]:
        copy.wait()


def word_layer(bits, vec, near, doc_ids, cotangent, wqkv, wout, wup, wdown, gain1, gain2, wproj, pooled):
    words, wide = vec.shape
    width = pooled.shape[1]
    window = 3 * words
    hidden = wup.shape[2]
    vm = pl.BlockSpec(memory_space=pltpu.VMEM)
    return pl.pallas_call(
        functools.partial(word_kernel, bits),
        in_specs=[vm] * 3 + [pl.BlockSpec(memory_space=pl.ANY)] * 5 + [vm] * 4,
        out_specs=[vm] * 4 + [pl.BlockSpec(memory_space=pl.ANY)] * 3,
        out_shape=[
            jax.ShapeDtypeStruct((words, wide), BF),
            jax.ShapeDtypeStruct((words, width), F32),
            jax.ShapeDtypeStruct((width, wide), BF),
            jax.ShapeDtypeStruct((8, wide), F32),
        ] + [
            jax.ShapeDtypeStruct((RANKS, wide, wide), BF) for _ in range(3)
        ],
        scratch_shapes=[
            pltpu.VMEM((window, wide), BF),
            pltpu.VMEM((RANKS, words, TILE), BF),
            pltpu.VMEM((RANKS, window, 2 * TILE), BF),
            pltpu.VMEM((RANKS, 2 * words, window), BF),
            pltpu.VMEM((RANKS, words, TILE), BF),
            pltpu.VMEM((RANKS, words, hidden), BF),
            pltpu.VMEM((RANKS, words, hidden), BF),
            pltpu.VMEM((words, TILE), BF),
            pltpu.VMEM((words, TILE), BF),
            pltpu.VMEM((window, 2 * TILE), BF),
            pltpu.VMEM((words, wide), F32),
            pltpu.VMEM((words, wide), BF),
            pltpu.SemaphoreType.DMA,
            pltpu.VMEM((2 * words, wide), F32),
            pltpu.VMEM((3, 2, words, wide), BF),
            pltpu.VMEM((1, 2 * words + doc_ids.shape[1]), jnp.int32),
        ] + [pltpu.VMEM(array.shape, BF) for array in (wqkv, wout, wup, wdown)] + [
            pltpu.VMEM((RANKS, wide, wide), BF),
            pltpu.VMEM((RANKS, wide, wide), BF),
            pltpu.VMEM((RANKS, wide, wide), BF),
            pltpu.SemaphoreType.DMA((6 + RANKS,)),
            pltpu.SemaphoreType.DMA((2,)),
            pltpu.SemaphoreType.DMA((2,)),
        ],
        compiler_params=pltpu.CompilerParams(
            vmem_limit_bytes=62 << 20, collective_id=1, has_side_effects=True),
        name="word_layer",
    )(vec, near, doc_ids, cotangent, wqkv, wout, wup, wdown,
      gain1[None, :], gain2[None, :], wproj, pooled)


CHAINS = 6
PLAN = (
    (0, 2, 7, 10, 14, 16, 20,),
    (1, 5, 10, 13, 18, 22,),
    (2, 11, 15, 19,),
    (1, 4, 9, 12, 15, 19,),
    (7, 9, 14, 16,),
    (15, 17, 22,),
)


def char_backward_kernel(slots, bits, x_ref, counts_ref, gain1_ref, wq_ref, wk_ref, wv_ref, wout_ref, gain2_ref,
                         wup_ref, wdown_ref, gpl_ref, act_pool_ref, dproj_ref, wgain_ref, normed_ref, qkv_ref, probs_ref,
                         mixed_ref, first_ref, slope_ref, up_grad_ref, down_grad_ref, mix_grad_ref,
                         dx_ref, up_out, down_out, mix_out, early_out, mid_out, late_out,
                         down_ref, gq_ref, gmix_ref, gup_ref, spread_ref, dgain_ref, dqkv_ref, dout_ref, dup_ref,
                         all_ref, wqkv_ref, table_ref, early_ref, mid_ref, late_ref, *rest):
    step = pl.program_id(0)
    steps = pl.num_programs(0)
    half_steps = CHAR_STEPS
    rows, width = x_ref.shape
    words = rows // slots
    p = Place()
    send_sem, recv_sem, own_sem = rest[-3:]
    sources = (up_grad_ref, down_grad_ref, mix_grad_ref, early_ref, mid_ref, late_ref)
    results = (up_out, down_out, mix_out, early_out, mid_out, late_out)
    outs = rest[6 * CHAINS:7 * CHAINS]
    leave = [pltpu.make_async_copy(out, result, own_sem.at[CHAINS + index])
             for index, (out, result) in enumerate(zip(outs, results))]
    word_chains = 3
    chains, first_sem = [], 0
    for index in range(CHAINS):
        everywhere = index >= word_chains
        refs = tuple(rest[6 * index:6 * index + 6]) + (outs[index],)
        chains.append(Chain(p, bits, sources[index], refs, Sems(send_sem, recv_sem, first_sem), everywhere))
        first_sem += chain_copies(bits, everywhere)

    @pl.when(step == 0)
    def _():
        meet(p.mates(bits) + [p.ring_device(offset) for offset in (1, 2, 3)])
        for index in range(word_chains):
            chains[index].fetch(own_sem.at[index]).start()

    low = lambda value: value.astype(BF)

    @pl.when(step == 0)
    def _():
        dgain_ref[...] = jnp.zeros_like(dgain_ref)
        dqkv_ref[...] = jnp.zeros_like(dqkv_ref)
        dout_ref[...] = jnp.zeros_like(dout_ref)
        dup_ref[...] = jnp.zeros_like(dup_ref)
        grad_down = low(tn(act_pool_ref[...], low(gpl_ref[...])))
        quarter = early_ref.shape[1]
        for index in range(RANKS):
            early_ref[index, :, 0:width] = grad_down[index * quarter:(index + 1) * quarter]
            early_ref[index, :, width:] = grad_down[(RANKS + index) * quarter:(RANKS + index + 1) * quarter]
        split_counts(counts_ref, table_ref, words)
        join_lanes((wq_ref, wk_ref, wv_ref), wqkv_ref)
        scaled = gpl_ref[...] * (1.0 / column(counts_ref[...].astype(F32)))
        down_ref[:, width:] = nt(scaled.astype(BF), wdown_ref[...])
        down_ref[:, :width] = scaled

    @pl.when(step < half_steps)
    def _():
        here = rows_at(step * rows, rows)
        for word in range(words):
            line = down_ref[pl.ds(step * words + word, 1), :width]
            at = slice(word * slots, (word + 1) * slots)
            gq_ref[at, :width] = jnp.broadcast_to(line, (slots, width))
            line = down_ref[pl.ds(step * words + word, 1), width:]
            gup_ref[at, :] = (jnp.broadcast_to(line, (slots, line.shape[1])) * slope_ref[at, :].astype(F32)).astype(BF)

        valid_col = any_lane(valid_slots(rows, slots, table_ref[pl.ds(step, 1), 0:words]))
        unit2, rate2 = norm_parts(first_ref[...])
        dup_ref[...] += tn((unit2 * gain2_ref[...]).astype(BF), gup_ref[...])
        upstream = nt(gup_ref[...], wup_ref[...])
        dgain_ref[1:2, :] += jnp.sum(upstream * unit2, axis=0, keepdims=True)
        grad_first = jnp.where(valid_col, gq_ref[:, :width], 0.0) + norm_back(upstream, gain2_ref[...], unit2, rate2)
        spread_ref[here, :] = grad_first
        grad_low = low(grad_first)
        dout_ref[...] += tn(mixed_ref[...], grad_low)
        gmix_ref[here, :] = low(nt(grad_low, wout_ref[...]))

    @pl.when(step == half_steps - 1)
    def _():
        mid_ref[0] = low(dup_ref[:, 0:2 * width])
        mid_ref[1] = low(dup_ref[:, 2 * width:])
        mid_ref[2] = dproj_ref[...]
        half = width // 2
        mid_ref[3, 0:half, 0:width] = low(dout_ref[0:half, :])
        mid_ref[3, 0:half, width:] = low(dout_ref[half:, :])
        mid_ref[3, half:, :] = jnp.zeros_like(mid_ref[3, half:, :])
        both = jnp.concatenate([dgain_ref[...], dgain_ref[...]], axis=1)
        mid_ref[3, half:half + 16, :] = low(jnp.concatenate([wgain_ref[...], both], axis=0))

    @pl.when((step >= half_steps) & (step < 2 * half_steps))
    def _():
        base = (step - half_steps) * rows
        for tile in range(rows // TILE):
            at = pl.ds(tile * TILE, TILE)
            here = rows_at(base + tile * TILE, TILE)
            for pair in range(CHEADS // 2):
                c0 = pair * TILE
                queries = split_heads(qkv_ref[at, c0:c0 + TILE])
                keys = split_heads(qkv_ref[at, width + c0:width + c0 + TILE])
                values = qkv_ref[at, 2 * width + c0:2 * width + c0 + TILE]
                grads = split_heads(gmix_ref[here, c0:c0 + TILE])
                probs_low = probs_ref[tile, pair]
                probs = probs_low.astype(F32)
                grad_probs = compact(nt(values, grads), slots)
                inner = jnp.sum(probs * grad_probs, axis=0, keepdims=True)
                grad_scores = (probs * (grad_probs - inner) * (CHD ** -0.5)).astype(BF)
                wide_scores = expand(grad_scores, slots)
                wide_probs = expand(probs_low, slots)
                all_ref[here, c0:c0 + TILE] = tn(stack_lanes(wide_scores), keys).astype(BF)
                all_ref[here, width + c0:width + c0 + TILE] = nn(wide_scores, queries).astype(BF)
                all_ref[here, 2 * width + c0:2 * width + c0 + TILE] = nn(wide_probs, grads).astype(BF)
        dqkv_ref[...] += tn(normed_ref[...], all_ref[rows_at(base, rows), :])

    @pl.when(step == 2 * half_steps - 1)
    def _():
        half = width // 2
        for index in range(2):
            late_ref[index] = low(dqkv_ref[index * half:(index + 1) * half, 0:2 * width])
            late_ref[2, :, index * width:(index + 1) * width] = low(dqkv_ref[index * half:(index + 1) * half, 2 * width:])
        late_ref[3] = jnp.zeros_like(late_ref[3])

    @pl.when(step >= 2 * half_steps)
    def _():
        here = rows_at((step - 2 * half_steps) * rows, rows)
        unit1, rate1 = norm_parts(x_ref[...].astype(F32))
        upstream1 = nt(all_ref[here, :], wqkv_ref[...])
        dx_ref[...] = low(spread_ref[here, :] + norm_back(upstream1, gain1_ref[...], unit1, rate1))

    for at in range(3 * half_steps):
        todo = [(index, stages.index(at)) for index, stages in reversed(list(enumerate(PLAN))) if at in stages]
        if todo:
            @pl.when(step == at)
            def _(todo=todo):
                for index, stage in todo:
                    if stage == 1 and index < word_chains:
                        chains[index].fetch(own_sem.at[index]).wait()
                    chains[index].step(stage)

    @pl.when(step == steps - 1)
    def _():
        done = [len(stages) for stages in PLAN]
        while any(done[index] <= len(chains[index].stages) for index in range(CHAINS)):
            for index in reversed(range(CHAINS)):
                if done[index] <= len(chains[index].stages):
                    chains[index].step(done[index])
                    done[index] += 1
                    if done[index] > len(chains[index].stages):
                        leave[index].start()
        for copy in leave:
            copy.wait()


def char_backward(bits, x, counts, gain1, weights, wout, gain2, wup, wdown, grad_pooled, saved, grad_proj,
                  word_gains, word_grads):
    qkv, probs, mixed, first, slope, act_pool, normed = saved
    rows, width = x.shape
    words = counts.shape[0]
    slots = rows // words
    hidden = wup.shape[1]
    wide = word_gains.shape[1]
    step = rows // CHAR_STEPS
    last = CHAR_STEPS - 1
    ahead = lambda i: i - ((i // CHAR_STEPS + 1) // 2) * (i - last)
    behind = lambda i: (i // CHAR_STEPS % 2) * (i - CHAR_STEPS) + (i // CHAR_STEPS // 2) * last
    final = lambda i: (i // CHAR_STEPS // 2) * (i - 2 * CHAR_STEPS)
    ahead_block = lambda cols: pl.BlockSpec((step, cols), lambda i: (ahead(i), 0))
    behind_block = lambda cols: pl.BlockSpec((step, cols), lambda i: (behind(i), 0))
    whole = lambda shape: pl.BlockSpec(shape, lambda i: (0,) * len(shape))
    tiles = step // TILE
    sum_shapes = [(wide, wide)] * 3 + [(RANKS, width // 2, wide), (RANKS, width, wide), (RANKS, width // 2, wide)]
    sources = [(RANKS,) + shape if len(shape) == 2 else shape for shape in sum_shapes]
    copies = sum(chain_copies(bits, index >= 3) for index in range(CHAINS))
    scratch = []
    for shape in sources:
        scratch += chain_scratch(bits, shape[1], wide)
    return pl.pallas_call(
        functools.partial(char_backward_kernel, slots, bits),
        grid=(3 * CHAR_STEPS,),
        in_specs=[
            pl.BlockSpec((step, width), lambda i: (final(i), 0)),
            whole((1, words)),
            whole((1, width)),
            whole((width, width)),
            whole((width, width)),
            whole((width, width)),
            whole((width, width)),
            whole((1, width)),
            whole((width, hidden)),
            whole((hidden, width)),
            whole((words, width)),
            whole((words, hidden)),
            whole((width, wide)),
            whole((8, wide)),
            behind_block(width),
            behind_block(3 * width),
            pl.BlockSpec((tiles, CHEADS // 2, slots, 2 * TILE), lambda i: (behind(i), 0, 0, 0)),
            ahead_block(width),
            ahead_block(width),
            ahead_block(hidden),
        ] + [pl.BlockSpec(memory_space=pl.ANY)] * 3,
        out_specs=[pl.BlockSpec((step, width), lambda i: (final(i), 0))] + [pl.BlockSpec(memory_space=pl.ANY)] * CHAINS,
        out_shape=[jax.ShapeDtypeStruct((rows, width), BF)]
        + [jax.ShapeDtypeStruct(shape, BF) for shape in sum_shapes],
        scratch_shapes=[
            pltpu.VMEM((words, width + hidden), F32),
            pltpu.VMEM((step, width), F32),
            pltpu.VMEM((rows, width), BF),
            pltpu.VMEM((step, hidden), BF),
            pltpu.VMEM((rows, width), F32),
            pltpu.VMEM((8, width), F32),
            pltpu.VMEM((width, 3 * width), F32),
            pltpu.VMEM((width, width), F32),
            pltpu.VMEM((width, hidden), F32),
            pltpu.VMEM((rows, 3 * width), BF),
            pltpu.VMEM((width, 3 * width), BF),
            pltpu.VMEM((CHAR_STEPS, TILE), jnp.int32),
        ] + [pltpu.VMEM(shape, BF) for shape in sources[3:]] + scratch
        + [pltpu.VMEM(shape, BF) for shape in sum_shapes] + [pltpu.SemaphoreType.DMA((copies,)), pltpu.SemaphoreType.DMA((copies,)), pltpu.SemaphoreType.DMA((2 * CHAINS,))],
        compiler_params=pltpu.CompilerParams(
            vmem_limit_bytes=63 << 20, collective_id=2, has_side_effects=True),
        name="char_backward",
    )(x, counts[None, :], gain1[None, :], *weights, wout, gain2[None, :],
      wup, wdown, grad_pooled, act_pool, grad_proj, word_gains, normed, qkv, probs, mixed, first, slope, *word_grads)


def unpack_kernel(out_in, dx_in, wq_in, wk_in, wv_in, gain1_in, up_in, down_in, mix_in, turn_in, early_in, mid_in, late_in,
                  out_ref, dx_ref, gain1_ref, dq_ref, dk_ref, dv_ref, dout_ref, gain2_ref, dup_ref, ddown_ref, dproj_ref,
                  wgain1_ref, wq_ref, wk_ref, wv_ref, wout_ref, wgain2_ref, wup_ref, wdown_ref):
    step = pl.program_id(0)
    dx_ref[...] = dx_in[...].astype(F32)
    out_ref[...] = out_in[...]
    width = dq_ref.shape[0]
    half = width // 2
    wup_ref[...] = up_in[...].astype(F32)
    wdown_ref[...] = down_in[...].astype(F32)
    wq_ref[...] = mix_in[:, 0:TILE].astype(F32)
    wk_ref[...] = mix_in[:, TILE:2 * TILE].astype(F32)
    wv_ref[...] = mix_in[:, 2 * TILE:3 * TILE].astype(F32)
    for side in range(2):
        cols = slice(side * width, (side + 1) * width)
        ddown_ref[side] = early_in[0, :, cols].astype(F32)
        dup_ref[:, side * 2 * width:(side + 1) * 2 * width] = mid_in[side].astype(F32)
    dproj_ref[...] = mid_in[2].astype(F32)

    @pl.when(step < UNPACK_STEPS // 2)
    def _():
        for side in range(2):
            dout_ref[side] = mid_in[3, :, side * width:(side + 1) * width].astype(F32)

    @pl.when(step == UNPACK_STEPS // 2)
    def _():
        gains = mid_in[3, 0:16, :].astype(F32)
        wgain1_ref[...] = gains[0:1]
        wgain2_ref[...] = gains[1:2]
        gain2_ref[...] = gains[9:10, 0:width]

    @pl.when(step == 0)
    def _():
        wout_ref[...] = turn_in[...].astype(F32).T
        parts = []
        for index in range(2):
            at = slice(index * half, (index + 1) * half)
            cols = slice(index * width, (index + 1) * width)
            grads = (late_in[index, :, 0:width].astype(F32), late_in[index, :, width:].astype(F32),
                     late_in[2, :, cols].astype(F32))
            total = 0.0
            for grad, weight, target in zip(grads, (wq_in, wk_in, wv_in), (dq_ref, dk_ref, dv_ref)):
                target[at, :] = grad
                total += weight[at].astype(F32) * grad
            parts.append(jnp.sum(total, axis=1, keepdims=True))
        sums = jnp.concatenate(parts, axis=0)
        diagonal = (lax.broadcasted_iota(jnp.int32, (width, width), 0)
                    == lax.broadcasted_iota(jnp.int32, (width, width), 1))
        gain1_ref[...] = jnp.sum(jnp.where(diagonal, sums, 0.0), axis=0, keepdims=True) / gain1_in[...]


UNPACK_STEPS = 8


def unpack(word_output, grad_inputs, weights, gain1, sums, width, hidden):
    steps = UNPACK_STEPS
    up, down, mix, early, mid, late = sums
    wide = word_output.shape[1]
    whole = lambda shape: pl.BlockSpec(shape, lambda i: (0,) * len(shape))
    split = lambda shape: pl.BlockSpec((shape[0] // steps, shape[1]), lambda i: (i, 0))
    middle = lambda shape: pl.BlockSpec((shape[0], shape[1] // steps, shape[2]), lambda i: (0, i, 0))
    per = early.shape[1] * RANKS // steps
    blocks = early.shape[1] // per
    pinned = lambda i: i - (i // (steps // 2)) * (i - (steps // 2 - 1))
    outs = [
        (whole, (1, width)), (whole, (width, width)), (whole, (width, width)), (whole, (width, width)),
        (lambda shape: pl.BlockSpec((2, shape[1] * 2 // steps, width), lambda i: (0, pinned(i), 0)), (2, width // 2, width)),
        (whole, (1, width)), (split, (width, hidden)), (middle, (2, hidden // 2, width)), (split, (width, wide)),
        (whole, (1, wide)), (split, (wide, TILE)), (split, (wide, TILE)), (split, (wide, TILE)),
        (whole, (TILE, wide)), (whole, (1, wide)), (split, (wide, wide)), (split, (wide, wide)),
    ]
    results = pl.pallas_call(
        unpack_kernel,
        grid=(steps,),
        in_specs=[split(word_output.shape), split(grad_inputs.shape)] + [whole((width, width))] * 3 + [whole((1, width))]
        + [split(up.shape), split(down.shape), split(mix.shape), pl.BlockSpec((wide, TILE), lambda i: (0, 3)),
           pl.BlockSpec((1, per, wide), lambda i: (i // blocks, i % blocks, 0)), middle(mid.shape), whole(late.shape)],
        out_specs=[split(word_output.shape), split(grad_inputs.shape)] + [spec(shape) for spec, shape in outs],
        out_shape=[jax.ShapeDtypeStruct(word_output.shape, BF), jax.ShapeDtypeStruct(grad_inputs.shape, F32)]
        + [jax.ShapeDtypeStruct(shape, F32) for _, shape in outs],
        compiler_params=pltpu.CompilerParams(vmem_limit_bytes=60 << 20),
        name="unpack",
    )(word_output, grad_inputs, *weights, gain1[None, :], up, down, mix, mix, early, mid, late)

    def shaped(array):
        if array.ndim == 3:
            return array.reshape(-1, array.shape[2])
        return array[0] if array.shape[0] == 1 else array

    return tuple(shaped(array) for array in results)


def per_device(
    bits,
    char_inputs,
    char_counts,
    doc_ids,
    cotangent,
    char_norm_one,
    char_query,
    char_key,
    char_value,
    char_out,
    char_norm_two,
    char_up,
    char_down,
    char_proj,
    word_norm_one,
    word_query,
    word_key,
    word_value,
    word_out_proj,
    word_norm_two,
    word_up,
    word_down,
):
    char_qkv = (char_query, char_key, char_value)
    word_qkv = (word_query, word_key, word_value)
    vec, pooled, *saved, near, qkv_all, out_all, up_all, down_all = char_forward(
        char_inputs, char_counts, char_norm_one, char_qkv, char_out, char_norm_two, char_up, char_down, char_proj,
        word_qkv, word_out_proj, word_up, word_down,
    )
    word_output, grad_pooled, grad_proj, word_gains, *word_grads = word_layer(
        bits, vec, near, doc_ids, cotangent, qkv_all, out_all, up_all, down_all,
        word_norm_one, word_norm_two, char_proj, pooled,
    )
    grad_inputs, *sums = char_backward(
        bits, char_inputs, char_counts, char_norm_one, char_qkv, char_out, char_norm_two, char_up, char_down,
        grad_pooled, saved, grad_proj, word_gains, word_grads,
    )
    return unpack(word_output, grad_inputs, char_qkv, char_norm_one, sums, char_out.shape[0], char_up.shape[1])


def solution(mesh):
    in_specs = (
        P(("dp", "tensor"), None),
        P(("dp", "tensor")),
        P("dp", None),
        P("dp", None),
        P(),
        P(),
        P(),
        P(),
        P(),
        P(),
        P(),
        P(),
        P(),
        P(),
        P(None, "tensor"),
        P(None, "tensor"),
        P(None, "tensor"),
        P("tensor", None),
        P(),
        P(None, "tensor"),
        P("tensor", None),
    )
    out_specs = (
        P(("dp", "tensor"), None),
        P(("dp", "tensor"), None),
        P(),
        P(),
        P(),
        P(),
        P(),
        P(),
        P(),
        P(),
        P(),
        P(),
        P(None, "tensor"),
        P(None, "tensor"),
        P(None, "tensor"),
        P("tensor", None),
        P(),
        P(None, "tensor"),
        P("tensor", None),
    )
    assert mesh.shape["tensor"] == RANKS
    bits = mesh.shape["dp"].bit_length() - 1
    assert bits >= 3 and mesh.shape["dp"] == 1 << bits
    return jax.shard_map(
        functools.partial(per_device, bits), mesh=mesh, in_specs=in_specs, out_specs=out_specs, check_vma=False
    )
```

```python
import functools

import jax
import jax.numpy as jnp
from jax import lax
from jax.experimental import pallas as pl
from jax.experimental.pallas import tpu as pltpu
from jax.sharding import PartitionSpec as P

BF = jnp.bfloat16
F32 = jnp.float32
EPSILON = 1e-05
NEG_LARGE = -1e30
RANKS = 4
CHEADS = 4
CHD = 64
TILE = 128
CHAR_STEPS = 8
GELU_C = 0.7978845608028654
GELU_A = 0.044715


def nn(left, right):
    return lax.dot_general(left, right, (((1,), (0,)), ((), ())), preferred_element_type=F32)


def nt(left, right):
    return lax.dot_general(left, right, (((1,), (1,)), ((), ())), preferred_element_type=F32)


def tn(left, right):
    return lax.dot_general(left, right, (((0,), (0,)), ((), ())), preferred_element_type=F32)


def norm_parts(values):
    centre = values - jnp.mean(values, axis=-1, keepdims=True)
    spread = jnp.mean(centre * centre, axis=-1, keepdims=True)
    rate = lax.rsqrt(spread + EPSILON)
    return centre * rate, rate


def norm_back(upstream, gain, unit, rate):
    scaled = upstream * gain
    first = jnp.mean(scaled, axis=-1, keepdims=True)
    second = jnp.mean(scaled * unit, axis=-1, keepdims=True)
    return rate * (scaled - first - unit * second)


def gelu_parts(values):
    square = values * values
    inner = values * (GELU_C + (GELU_C * GELU_A) * square)
    half = 0.5 + 0.5 * jnp.tanh(inner)
    active = values * half
    slope = half + (active * (1.0 - half)) * (2.0 * GELU_C + (6.0 * GELU_C * GELU_A) * square)
    return active, slope


def split_heads(pair):
    low_half = lax.broadcasted_iota(jnp.int32, pair.shape, 1) < CHD
    zero = jnp.zeros_like(pair)
    return jnp.concatenate([jnp.where(low_half, pair, zero), jnp.where(low_half, zero, pair)], axis=0)


def word_of_lane(shape, slots):
    lane = lax.broadcasted_iota(jnp.int32, shape, 1)
    return jnp.bitwise_and(lane, TILE - 1) // slots


def compact(scores, slots):
    words = word_of_lane((slots, scores.shape[1]), slots)
    result = scores[0:slots]
    for word in range(1, TILE // slots):
        result = jnp.where(words == word, scores[word * slots:(word + 1) * slots], result)
    return result


def expand(packed, slots):
    words = word_of_lane(packed.shape, slots)
    zero = jnp.zeros_like(packed)
    return jnp.concatenate(
        [jnp.where(words == word, packed, zero) for word in range(TILE // slots)], axis=0
    )


def stack_lanes(pair):
    return jnp.concatenate([pair[:, :TILE], pair[:, TILE:]], axis=0)


def split_counts(counts_ref, table_ref, words):
    for step in range(CHAR_STEPS):
        table_ref[step:step + 1, 0:words] = counts_ref[:, step * words:(step + 1) * words]


def valid_slots(rows, slots, mine):
    words = rows // slots
    row = lax.broadcasted_iota(jnp.int32, (rows, words), 0)
    word = lax.broadcasted_iota(jnp.int32, (rows, words), 1)
    return (row // slots == word) & (jnp.bitwise_and(row, slots - 1) < mine)


def join_lanes(parts, whole_ref):
    width = parts[0].shape[1]
    for index, part in enumerate(parts):
        whole_ref[:, index * width:(index + 1) * width] = part[...]


def any_lane(mask):
    return jnp.max(jnp.where(mask, 1.0, 0.0), axis=1, keepdims=True) > 0.0


def column(row):
    size = row.shape[1]
    diagonal = (lax.broadcasted_iota(jnp.int32, (size, size), 0)
                == lax.broadcasted_iota(jnp.int32, (size, size), 1))
    return jnp.sum(jnp.where(diagonal, row, 0.0), axis=1, keepdims=True)


MESH = pl.DeviceIdType.MESH
LANE_SPLIT = 256


class Place:
    def __init__(self):
        self.dp = lax.axis_index("dp")
        self.rank = lax.axis_index("tensor")
        self.core = lax.rem(self.dp, 2)
        self.x = lax.rem(self.dp // 2, 2)
        self.y = lax.rem(self.dp // 4, 2)
        self.core_mate = (self.dp + 1 - 2 * self.core, self.rank)
        self.x_mate = (self.dp + 2 - 4 * self.x, self.rank)
        self.y_mate = (self.dp + 4 - 8 * self.y, self.rank)

    def ring(self, offset):
        return lax.rem(self.rank + offset, RANKS)

    def ring_device(self, offset):
        return (self.dp, self.ring(offset))

    def bit_mate(self, bit):
        size = 1 << bit
        mine = lax.rem(self.dp // size, 2)
        return (self.dp + size - 2 * size * mine, self.rank)

    def mates(self, bits):
        extra = [self.bit_mate(bit) for bit in range(3, bits)]
        return [self.core_mate, self.x_mate, self.y_mate] + extra


def meet(devices):
    barrier = pltpu.get_barrier_semaphore()
    for device in devices:
        pl.semaphore_signal(barrier, inc=1, device_id=device, device_id_type=MESH)
    pl.semaphore_wait(barrier, len(devices))


def remote(source, target, sems, device):
    return pltpu.make_async_remote_copy(
        src_ref=source, dst_ref=target, send_sem=sems[0], recv_sem=sems[1],
        device_id=device, device_id_type=MESH,
    )


class Sems:
    def __init__(self, send, recv, start=0):
        self.send, self.recv, self.next = send, recv, start

    def take(self):
        at = self.next
        self.next += 1
        return self.send.at[at], self.recv.at[at]


def rows_at(start, size):
    return pl.ds(pl.multiple_of(start, 16), size)


def halves(width):
    return (slice(0, LANE_SPLIT), slice(LANE_SPLIT, width))


class Gather:
    def __init__(self, place, local, whole, sems):
        self.stages = [[], [], [], []]
        rows = local.shape[0]
        unit = rows // 8
        p = place
        left, right = halves(local.shape[1])
        left_at = p.core * 4 + p.x * 2 + p.y
        right_at = p.core * 4 + p.y * 2 + p.x
        for offset in range(1, RANKS):
            for lanes, at in ((left, left_at), (right, right_at)):
                at = rows_at(at * unit, unit)
                self.stages[0].append(remote(
                    local.at[at, lanes], whole.at[p.rank, at, lanes], sems.take(), p.ring_device(offset)))
        for offset in range(1, RANKS):
            rank = p.ring(offset)
            for lanes, at, first, second, mate_first, mate_second in (
                (left, left_at, p.x, None, p.y_mate, p.x_mate),
                (right, right_at, p.y, None, p.x_mate, p.y_mate),
            ):
                one = rows_at(at * unit, unit)
                two = rows_at((p.core * 4 + first * 2) * unit, 2 * unit)
                self.stages[1].append(remote(
                    whole.at[rank, one, lanes], whole.at[rank, one, lanes], sems.take(), mate_first))
                self.stages[2].append(remote(
                    whole.at[rank, two, lanes], whole.at[rank, two, lanes], sems.take(), mate_second))
            four = rows_at(p.core * 4 * unit, 4 * unit)
            self.stages[3].append(remote(
                whole.at[rank, four], whole.at[rank, four], sems.take(), p.core_mate))

    def start(self, stage):
        for copy in self.stages[stage]:
            copy.start()

    def wait(self, stage):
        for copy in self.stages[stage]:
            copy.wait()


def gather_copies():
    return 2 * (RANKS - 1) * 3 + (RANKS - 1)


class Chain:
    def __init__(self, place, bits, src, refs, sems, everywhere):
        p = place
        buf, got_core, got_one, got_two, got_more, got_rank, out = refs
        self.p, self.src, self.everywhere = p, src, everywhere
        self.buf, self.got_core, self.got_one, self.got_two = buf, got_core, got_one, got_two
        self.got_more, self.got_rank = got_more, got_rank
        self.mine = out.at[p.rank] if everywhere else out
        unit = src.shape[1] // 8
        lanes = left, right = halves(src.shape[2])
        self.lanes = lanes
        self.own = rows_at(p.core * 4 * unit, 4 * unit)
        stages = [("core", [remote(src.at[:, rows_at((1 - p.core) * 4 * unit, 4 * unit)], got_core,
                                   sems.take(), p.core_mate)])]
        first, second = (p.x, p.y), (p.y, p.x)
        first_mate, second_mate = (p.x_mate, p.y_mate), (p.y_mate, p.x_mate)
        one = lambda side, at: rows_at(at * 2 * unit, 2 * unit)
        two = lambda side, at: rows_at((first[side] * 2 + at) * unit, unit)
        self.one_rows = [one(side, first[side]) for side in (0, 1)]
        self.two_rows = [two(side, second[side]) for side in (0, 1)]
        stages.append(("one", [
            remote(buf.at[:, one(side, 1 - first[side]), lanes[side]], got_one.at[:, :, lanes[side]],
                   sems.take(), first_mate[side]) for side in (0, 1)]))
        stages.append(("two", [
            remote(buf.at[:, two(side, 1 - second[side]), lanes[side]], got_two.at[:, :, lanes[side]],
                   sems.take(), second_mate[side]) for side in (0, 1)]))
        for bit in range(3, bits):
            stages.append((bit - 3, [
                remote(buf.at[:, self.two_rows[side], lanes[side]], got_more.at[bit - 3, :, :, lanes[side]],
                       sems.take(), p.bit_mate(bit)) for side in (0, 1)]))
        stages.append(("rank", [
            remote(buf.at[p.ring(offset), self.two_rows[side], lanes[side]],
                   got_rank.at[offset - 1, :, lanes[side]], sems.take(), p.ring_device(offset))
            for offset in range(1, RANKS) for side in (0, 1)]))
        base = p.core * 4 * unit
        self.out_two = [rows_at(base + (first[side] * 2 + second[side]) * unit, unit) for side in (0, 1)]
        out_one = [rows_at(base + first[side] * 2 * unit, 2 * unit) for side in (0, 1)]
        if everywhere:
            stages.append(("rank_back", [
                remote(out.at[p.rank, self.out_two[side], lanes[side]], out.at[p.rank, self.out_two[side], lanes[side]],
                       sems.take(), p.ring_device(offset))
                for offset in range(1, RANKS) for side in (0, 1)]))

        def back(at, part_lanes, mate):
            part = out.at[:, at, part_lanes] if everywhere else out.at[at, part_lanes]
            return remote(part, part, sems.take(), mate)

        stages.append(("back_two", [back(self.out_two[side], lanes[side], second_mate[side]) for side in (0, 1)]))
        stages.append(("back_one", [back(out_one[side], lanes[side], first_mate[side]) for side in (0, 1)]))
        stages.append(("back_core", [back(self.own, slice(None), p.core_mate)]))
        self.stages = stages

    def fetch(self, sem):
        return pltpu.make_async_copy(self.src.at[:, self.own], self.buf, sem)

    def start(self, index):
        for copy in self.stages[index][1]:
            copy.start()

    def finish(self, index):
        name, copies = self.stages[index]
        for copy in copies:
            copy.wait()
        buf = self.buf
        if name == "core":
            own = self.src if self.everywhere else None
            for quarter in range(RANKS):
                mine = own[quarter, self.own, :] if self.everywhere else buf[quarter]
                buf[quarter] = mine + self.got_core[quarter]
        elif name == "one":
            for at, lanes in zip(self.one_rows, self.lanes):
                for quarter in range(RANKS):
                    buf[quarter, at, lanes] += self.got_one[quarter, :, lanes]
        elif name == "two":
            for at, lanes in zip(self.two_rows, self.lanes):
                for quarter in range(RANKS):
                    buf[quarter, at, lanes] += self.got_two[quarter, :, lanes]
        elif name == "rank":
            for side in (0, 1):
                at, lanes = self.two_rows[side], self.lanes[side]
                total = buf[self.p.rank, at, lanes].astype(F32)
                for k in range(RANKS - 1):
                    total = total + self.got_rank[k, :, lanes].astype(F32)
                self.mine[self.out_two[side], lanes] = total.astype(BF)
        elif isinstance(name, int):
            for at, lanes in zip(self.two_rows, self.lanes):
                for quarter in range(RANKS):
                    buf[quarter, at, lanes] += self.got_more[name, quarter, :, lanes]

    def step(self, index):
        if index:
            self.finish(index - 1)
        if index < len(self.stages):
            self.start(index)


def chain_copies(bits, everywhere):
    pairs = 2 * (RANKS - 1)
    return 1 + 2 + 2 + 2 * (bits - 3) + pairs + (pairs if everywhere else 0) + 2 + 2 + 1


def chain_scratch(bits, rows, lanes):
    unit = rows // 8
    return [
        pltpu.VMEM((RANKS, 4 * unit, lanes), BF),
        pltpu.VMEM((RANKS, 4 * unit, lanes), BF),
        pltpu.VMEM((RANKS, 2 * unit, lanes), BF),
        pltpu.VMEM((RANKS, unit, lanes), BF),
        pltpu.VMEM((max(bits - 3, 1), RANKS, unit, lanes), BF),
        pltpu.VMEM((RANKS - 1, unit, lanes), BF),
    ]


FORWARD_PLAN = {
    2: ((0, 1), (1, 1)),
    3: ((2, 1), (0, 2), (1, 2)),
    4: ((3, 1), (2, 2)),
    5: ((0, 3), (1, 3), (3, 2)),
    6: ((2, 3),),
    7: ((3, 3),),
}


def char_forward_kernel(slots, x_ref, counts_ref, gain1_ref, wq_ref, wk_ref, wv_ref, wout_ref,
                        gain2_ref, wup_ref, wdown_ref, wproj_ref,
                        lq_ref, lk_ref, lv_ref, lout_ref, lup_ref, ldown_ref,
                        vec_ref, pooled_ref, qkv_ref, probs_ref, mixed_ref, first_ref,
                        slope_ref, act_pool_ref, normed_ref, near_ref, wqkv_all, wout_all, wup_all, wdown_all,
                        wqkv_ref, lqkv_ref, table_ref, own_sem, send_sem, recv_sem):
    rows = x_ref.shape[0]
    width = x_ref.shape[1]
    step = pl.program_id(0)
    steps = pl.num_programs(0)
    words = rows // slots
    p = Place()
    pairs = ((lqkv_ref, wqkv_all), (lout_ref, wout_all), (lup_ref, wup_all), (ldown_ref, wdown_all))
    gathers = [Gather(p, mine, whole, Sems(send_sem, recv_sem, gather_copies() * index))
               for index, (mine, whole) in enumerate(pairs)]
    own_copies = [pltpu.make_async_copy(mine, whole.at[p.rank], own_sem.at[index])
                  for index, (mine, whole) in enumerate(pairs)]
    vec_base = gather_copies() * len(pairs)

    def vec_copies(at):
        copies = []
        for slot, offset in ((1, 1), (0, 2)):
            sem = vec_base + 2 * at + slot
            part = rows_at(at * words, words)
            copies.append(remote(vec_ref.at[part], near_ref.at[slot, part],
                                 (send_sem.at[sem], recv_sem.at[sem]), p.ring_device(offset)))
        return copies

    def send_vec(at):
        for offset, copy in zip((1, 2), vec_copies(at)):
            @pl.when(p.rank + offset < RANKS)
            def _(copy=copy):
                copy.start()

    def wait_vec(at):
        for offset, copy in zip((1, 2), vec_copies(at)):
            @pl.when(p.rank + offset < RANKS)
            def _(copy=copy):
                copy.wait_send()

            @pl.when(p.rank >= offset)
            def _(copy=copy):
                copy.wait_recv()

    @pl.when(step == 0)
    def _():
        join_lanes((lq_ref, lk_ref, lv_ref), lqkv_ref)
        join_lanes((wq_ref, wk_ref, wv_ref), wqkv_ref)
        meet([p.ring_device(offset) for offset in (1, 2, 3)] + [p.core_mate, p.x_mate, p.y_mate])
        split_counts(counts_ref, table_ref, words)
        for copy in own_copies:
            copy.start()
        for gather in gathers:
            gather.start(0)

    base = x_ref[...].astype(F32)
    unit, _ = norm_parts(base)
    normed = (unit * gain1_ref[...]).astype(BF)
    normed_ref[...] = normed
    qkv_ref[...] = nn(normed, wqkv_ref[...]).astype(BF)
    mine = table_ref[pl.ds(step, 1), 0:words]
    word_at = lax.broadcasted_iota(jnp.int32, (words, rows), 0)
    row_at = lax.broadcasted_iota(jnp.int32, (words, rows), 1)
    onto_rows = jnp.where(row_at // slots == word_at, 1.0, 0.0).astype(BF)
    row_counts = nn(jnp.broadcast_to(mine.astype(F32), (16, words)).astype(BF), onto_rows)[0:1]
    for tile in range(rows // TILE):
        at = pl.ds(tile * TILE, TILE)
        valid = (lax.broadcasted_iota(jnp.int32, (slots, TILE), 0).astype(F32)
                 < row_counts[:, tile * TILE:(tile + 1) * TILE])
        for pair in range(CHEADS // 2):
            c0 = pair * TILE
            queries = split_heads(qkv_ref[at, c0:c0 + TILE])
            keys = qkv_ref[at, width + c0:width + c0 + TILE]
            values = split_heads(qkv_ref[at, 2 * width + c0:2 * width + c0 + TILE])
            scores = compact(nt(keys, queries), slots)
            parts = []
            for head in range(2):
                own = jnp.where(valid, scores[:, head * TILE:(head + 1) * TILE], NEG_LARGE)
                top = jnp.max(own, axis=0, keepdims=True)
                weight = jnp.exp((own - top) * (CHD ** -0.5))
                parts.append(weight / jnp.sum(weight, axis=0, keepdims=True))
            probs = jnp.concatenate(parts, axis=1).astype(BF)
            probs_ref[tile, pair] = probs
            mixed_ref[at, c0:c0 + TILE] = tn(stack_lanes(expand(probs, slots)), values).astype(BF)

    for at, todo in FORWARD_PLAN.items():
        @pl.when(step == at)
        def _(todo=todo):
            for member, stage in todo:
                gathers[member].wait(stage - 1)
                gathers[member].start(stage)

    @pl.when(step > 0)
    def _():
        send_vec(step - 1)

    first = base + nn(mixed_ref[...], wout_ref[...])
    first_ref[...] = first
    unit2, _ = norm_parts(first)
    normed2 = (unit2 * gain2_ref[...]).astype(BF)
    members = valid_slots(rows, slots, mine)
    valid_col = any_lane(members)
    pool = jnp.where(members, 1.0 / mine.astype(F32), 0.0).astype(BF)
    chunk = 256
    for part in range(wup_ref.shape[1] // chunk):
        cols = slice(part * chunk, (part + 1) * chunk)
        active, slope = gelu_parts(nn(normed2, wup_ref[:, cols]))
        slope_ref[:, cols] = jnp.where(valid_col, slope, 0.0).astype(BF)
        act_pool_ref[:, cols] = tn(pool, active.astype(BF)).astype(BF)
    pooled = tn(pool, first.astype(BF)) + nn(act_pool_ref[...], wdown_ref[...])
    pooled = pooled.astype(BF)
    pooled_ref[...] = pooled
    vec_ref[rows_at(step * words, words), :] = nn(pooled, wproj_ref[...]).astype(BF)

    @pl.when(step == steps - 1)
    def _():
        send_vec(step)
        for copy in own_copies:
            copy.wait()
        for gather in gathers:
            gather.wait(3)
        for at in range(CHAR_STEPS):
            wait_vec(at)


def char_forward(x, counts, gain1, weights, wout, gain2, wup, wdown, wproj, local, lout, lup, ldown):
    rows, width = x.shape
    words = counts.shape[0]
    slots = rows // words
    hidden = wup.shape[1]
    wide = wproj.shape[1]
    step = rows // CHAR_STEPS
    step_words = step // slots
    row_block = lambda cols: pl.BlockSpec((step, cols), lambda i: (i, 0))
    word_block = lambda cols: pl.BlockSpec((step_words, cols), lambda i: (i, 0))
    whole = lambda shape: pl.BlockSpec(shape, lambda i: (0, 0))
    tiles = step // TILE
    return pl.pallas_call(
        functools.partial(char_forward_kernel, slots),
        grid=(rows // step,),
        in_specs=[
            row_block(width),
            whole((1, words)),
            whole((1, width)),
            whole((width, width)),
            whole((width, width)),
            whole((width, width)),
            whole((width, width)),
            whole((1, width)),
            whole((width, hidden)),
            whole((hidden, width)),
            whole((width, wide)),
            whole(local[0].shape),
            whole(local[0].shape),
            whole(local[0].shape),
            whole(lout.shape),
            whole(lup.shape),
            whole(ldown.shape),
        ],
        out_specs=[
            whole((words, wide)),
            word_block(width),
            row_block(3 * width),
            pl.BlockSpec((tiles, CHEADS // 2, slots, 2 * TILE), lambda i: (i, 0, 0, 0)),
            row_block(width),
            row_block(width),
            row_block(hidden),
            word_block(hidden),
            row_block(width),
        ] + [pl.BlockSpec(memory_space=pl.ANY)] * 5,
        out_shape=[
            jax.ShapeDtypeStruct((words, wide), BF),
            jax.ShapeDtypeStruct((words, width), BF),
            jax.ShapeDtypeStruct((rows, 3 * width), BF),
            jax.ShapeDtypeStruct((rows // TILE, CHEADS // 2, slots, 2 * TILE), BF),
            jax.ShapeDtypeStruct((rows, width), BF),
            jax.ShapeDtypeStruct((rows, width), F32),
            jax.ShapeDtypeStruct((rows, hidden), BF),
            jax.ShapeDtypeStruct((words, hidden), BF),
            jax.ShapeDtypeStruct((rows, width), BF),
            jax.ShapeDtypeStruct((2, words, wide), BF),
            jax.ShapeDtypeStruct((RANKS, wide, 3 * TILE), BF),
            jax.ShapeDtypeStruct((RANKS,) + lout.shape, BF),
            jax.ShapeDtypeStruct((RANKS,) + lup.shape, BF),
            jax.ShapeDtypeStruct((RANKS,) + ldown.shape, BF),
        ],
        scratch_shapes=[
            pltpu.VMEM((width, 3 * width), BF),
            pltpu.VMEM((wide, 3 * TILE), BF),
            pltpu.VMEM((CHAR_STEPS, TILE), jnp.int32),
            pltpu.SemaphoreType.DMA((4,)),
            pltpu.SemaphoreType.DMA((gather_copies() * 4 + 2 * CHAR_STEPS,)),
            pltpu.SemaphoreType.DMA((gather_copies() * 4 + 2 * CHAR_STEPS,)),
        ],
        compiler_params=pltpu.CompilerParams(
            vmem_limit_bytes=60 << 20, collective_id=0, has_side_effects=True),
        name="char_forward",
    )(x, counts[None, :], gain1[None, :], *weights, wout, gain2[None, :], wup, wdown, wproj,
      *local, lout, lup, ldown)


def word_kernel(bits, vec_ref, near_ref, docs_ref, cot_ref, wqkv_in, wout_in, wup_in,
                wdown_in, gain1_ref, gain2_ref, wproj_ref, pooled_ref,
                out_ref, gpl_ref, dproj_ref, dgain_ref, up_grad_out, down_grad_out, mix_grad_out,
                n1_ref, q_ref, kv_ref, probs_ref, o_ref, act_ref, slope_ref, go_ref, gq_ref, gkv_ref,
                back_ref, cot_own, cot_sem, part_ref, got_ref, table_ref, wqkv_ref, wout_ref, wup_ref, wdown_ref,
                up_grad_ref, down_grad_ref, mix_grad_ref, io_sem, send_sem, recv_sem):
    p = Place()
    words, wide = vec_ref.shape
    window = 3 * words
    fetch = pltpu.make_async_copy(cot_ref.at[rows_at(p.rank * words, words)], cot_own, cot_sem)
    loads = [pltpu.make_async_copy(source, target, io_sem.at[index]) for index, (source, target) in enumerate((
        (wqkv_in, wqkv_ref), (wout_in, wout_ref), (wup_in, wup_ref), (wdown_in, wdown_ref)))]
    stores = [pltpu.make_async_copy(source, target, io_sem.at[4 + index]) for index, (source, target) in enumerate((
        (up_grad_ref, up_grad_out), (down_grad_ref, down_grad_out)))]

    def store_mix(rank):
        return pltpu.make_async_copy(mix_grad_ref.at[rank], mix_grad_out.at[rank], io_sem.at[6 + rank])

    for copy in loads:
        copy.start()
    fetch.start()
    meet([p.ring_device(offset) for offset in (1, 2, 3)])

    table_ref[:, 0:2 * words] = jnp.full((1, 2 * words), -1, jnp.int32)
    table_ref[:, 2 * words:] = docs_ref[...]
    start = pl.multiple_of(p.rank * words, TILE)
    key_docs = table_ref[:, pl.ds(start, window)].astype(F32)
    row_docs = column(key_docs[:, 2 * words:])

    own = vec_ref[...].astype(F32)
    unit1, rate1 = norm_parts(own)
    n1_ref[2 * words:, :] = (unit1 * gain1_ref[...]).astype(BF)
    for slot in range(2):
        near = jnp.where(p.rank + slot >= 2, near_ref[slot].astype(F32), 0.0)
        unit, _ = norm_parts(near)
        n1_ref[slot * words:(slot + 1) * words, :] = (unit * gain1_ref[...]).astype(BF)

    def project(rank, carry):
        q_ref[rank] = nn(n1_ref[2 * words:, :], wqkv_ref[rank, :, 0:TILE]).astype(BF)
        kv_ref[rank] = nn(n1_ref[...], wqkv_ref[rank, :, TILE:]).astype(BF)
        scores = nt(split_heads(q_ref[rank]), kv_ref[rank, :, 0:TILE]) * (CHD ** -0.5)
        row = lax.broadcasted_iota(jnp.int32, (words, window), 0)
        key = lax.broadcasted_iota(jnp.int32, (words, window), 1)
        allowed = (row_docs == key_docs) & (key <= row + 2 * words)
        for head in range(2):
            at = slice(head * words, (head + 1) * words)
            masked = jnp.where(allowed, scores[at], NEG_LARGE)
            top = jnp.max(masked, axis=-1, keepdims=True)
            weight = jnp.exp(masked - top)
            probs_ref[rank, at, :] = (weight * (1.0 / jnp.sum(weight, axis=-1, keepdims=True))).astype(BF)
        pair = jnp.concatenate([probs_ref[rank, 0:words, :], probs_ref[rank, words:, :]], axis=1)
        o_ref[rank] = nn(pair, split_heads(kv_ref[rank, :, TILE:])).astype(BF)
        back_ref[...] += nn(o_ref[rank], wout_ref[rank])
        return carry

    back_ref[...] = own
    loads[0].wait()
    loads[1].wait()
    lax.fori_loop(0, RANKS, project, 0)
    middle = back_ref[...]
    unit2, rate2 = norm_parts(middle)
    normed2 = (unit2 * gain2_ref[...]).astype(BF)

    def feed(rank, carry):
        active, slope = gelu_parts(nn(normed2, wup_ref[rank]))
        act_ref[rank] = active.astype(BF)
        slope_ref[rank] = slope.astype(BF)
        back_ref[...] += nn(act_ref[rank], wdown_ref[rank])
        return carry

    loads[2].wait()
    loads[3].wait()
    lax.fori_loop(0, RANKS, feed, 0)
    out_ref[...] = back_ref[...].astype(BF)
    fetch.wait()
    back_ref[...] = jnp.zeros_like(back_ref)

    def feed_back(rank, carry):
        upstream = (nt(cot_own[...], wdown_ref[rank]) * slope_ref[rank].astype(F32)).astype(BF)
        back_ref[...] += nt(upstream, wup_ref[rank])
        up_grad_ref[rank] = tn(normed2, upstream).astype(BF)
        down_grad_ref[rank] = tn(act_ref[rank], cot_own[...]).astype(BF)
        return carry

    lax.fori_loop(0, RANKS, feed_back, 0)
    for copy in stores:
        copy.start()
    upstream2 = back_ref[...]
    dgain_ref[...] = jnp.zeros_like(dgain_ref)
    dgain_ref[1:2, :] = jnp.sum(upstream2 * unit2, axis=0, keepdims=True)
    grad_middle = cot_own[...].astype(F32) + norm_back(upstream2, gain2_ref[...], unit2, rate2)
    middle_low = grad_middle.astype(BF)

    back_ref[...] = jnp.zeros_like(back_ref)
    part_ref[...] = jnp.zeros_like(part_ref)

    def attend_back(rank, carry):
        go_ref[...] = nt(middle_low, wout_ref[rank]).astype(BF)
        mix_grad_ref[rank, :, 3 * TILE:] = tn(middle_low, o_ref[rank]).astype(BF)
        go_pair = split_heads(go_ref[...])
        grad_probs = nt(go_pair, kv_ref[rank, :, TILE:])
        probs = probs_ref[rank].astype(F32)
        inner = jnp.sum(probs * grad_probs, axis=-1, keepdims=True)
        grad_scores = (probs * (grad_probs - inner) * (CHD ** -0.5)).astype(BF)
        q_pair = split_heads(q_ref[rank])
        gkv_ref[:, 0:TILE] = tn(grad_scores, q_pair).astype(BF)
        gkv_ref[:, TILE:] = tn(probs_ref[rank], go_pair).astype(BF)
        pair = jnp.concatenate([grad_scores[0:words], grad_scores[words:]], axis=1)
        gq_ref[...] = nn(pair, split_heads(kv_ref[rank, :, 0:TILE])).astype(BF)
        part_ref[...] += nt(gkv_ref[0:2 * words, :], wqkv_ref[rank, :, TILE:])
        back_ref[...] += nt(gkv_ref[2 * words:, :], wqkv_ref[rank, :, TILE:])
        back_ref[...] += nt(gq_ref[...], wqkv_ref[rank, :, 0:TILE])
        mix_grad_ref[rank, :, 0:TILE] = tn(n1_ref[2 * words:, :], gq_ref[...]).astype(BF)
        mix_grad_ref[rank, :, TILE:3 * TILE] = tn(n1_ref[...], gkv_ref[...]).astype(BF)
        store_mix(rank).start()
        return carry

    lax.fori_loop(0, RANKS, attend_back, 0)
    near_ref_low = got_ref.at[2]
    near_ref_low[...] = part_ref[...].astype(BF).reshape(2, words, wide)
    sends = []
    for slot, offset in ((0, RANKS - 2), (1, RANKS - 1)):
        sends.append(remote(got_ref.at[2, slot], got_ref.at[slot, 0], (send_sem.at[slot], recv_sem.at[slot]),
                            p.ring_device(offset)))
    for copy in sends:
        copy.start()
    for copy in sends:
        copy.wait()
    upstream1 = back_ref[...] + got_ref[0, 0].astype(F32) + got_ref[1, 0].astype(F32)
    dgain_ref[0:1, :] = jnp.sum(upstream1 * unit1, axis=0, keepdims=True)
    grad_vec = (grad_middle + norm_back(upstream1, gain1_ref[...], unit1, rate1)).astype(BF)
    dproj_ref[...] = tn(pooled_ref[...], grad_vec).astype(BF)
    gpl_ref[...] = nt(grad_vec, wproj_ref[...])
    for copy in stores + [store_mix(rank) for rank in range(RANKS)]:
        copy.wait()


def word_layer(bits, vec, near, doc_ids, cotangent, wqkv, wout, wup, wdown, gain1, gain2, wproj, pooled):
    words, wide = vec.shape
    width = pooled.shape[1]
    window = 3 * words
    hidden = wup.shape[2]
    vm = pl.BlockSpec(memory_space=pltpu.VMEM)
    return pl.pallas_call(
        functools.partial(word_kernel, bits),
        in_specs=[vm] * 3 + [pl.BlockSpec(memory_space=pl.ANY)] * 5 + [vm] * 4,
        out_specs=[vm] * 4 + [pl.BlockSpec(memory_space=pl.ANY)] * 3,
        out_shape=[
            jax.ShapeDtypeStruct((words, wide), BF),
            jax.ShapeDtypeStruct((words, width), F32),
            jax.ShapeDtypeStruct((width, wide), BF),
            jax.ShapeDtypeStruct((8, wide), F32),
        ] + [
            jax.ShapeDtypeStruct((RANKS, wide, wide), BF) for _ in range(3)
        ],
        scratch_shapes=[
            pltpu.VMEM((window, wide), BF),
            pltpu.VMEM((RANKS, words, TILE), BF),
            pltpu.VMEM((RANKS, window, 2 * TILE), BF),
            pltpu.VMEM((RANKS, 2 * words, window), BF),
            pltpu.VMEM((RANKS, words, TILE), BF),
            pltpu.VMEM((RANKS, words, hidden), BF),
            pltpu.VMEM((RANKS, words, hidden), BF),
            pltpu.VMEM((words, TILE), BF),
            pltpu.VMEM((words, TILE), BF),
            pltpu.VMEM((window, 2 * TILE), BF),
            pltpu.VMEM((words, wide), F32),
            pltpu.VMEM((words, wide), BF),
            pltpu.SemaphoreType.DMA,
            pltpu.VMEM((2 * words, wide), F32),
            pltpu.VMEM((3, 2, words, wide), BF),
            pltpu.VMEM((1, 2 * words + doc_ids.shape[1]), jnp.int32),
        ] + [pltpu.VMEM(array.shape, BF) for array in (wqkv, wout, wup, wdown)] + [
            pltpu.VMEM((RANKS, wide, wide), BF),
            pltpu.VMEM((RANKS, wide, wide), BF),
            pltpu.VMEM((RANKS, wide, wide), BF),
            pltpu.SemaphoreType.DMA((6 + RANKS,)),
            pltpu.SemaphoreType.DMA((2,)),
            pltpu.SemaphoreType.DMA((2,)),
        ],
        compiler_params=pltpu.CompilerParams(
            vmem_limit_bytes=62 << 20, collective_id=1, has_side_effects=True),
        name="word_layer",
    )(vec, near, doc_ids, cotangent, wqkv, wout, wup, wdown,
      gain1[None, :], gain2[None, :], wproj, pooled)


CHAINS = 6
PLAN = (
    (0, 2, 7, 10, 14, 16, 20,),
    (1, 5, 10, 13, 18, 22,),
    (2, 11, 15, 19,),
    (1, 4, 9, 12, 15, 19,),
    (7, 9, 14, 16,),
    (15, 17, 22,),
)


def char_backward_kernel(slots, bits, x_ref, counts_ref, gain1_ref, wq_ref, wk_ref, wv_ref, wout_ref, gain2_ref,
                         wup_ref, wdown_ref, gpl_ref, act_pool_ref, dproj_ref, wgain_ref, normed_ref, qkv_ref, probs_ref,
                         mixed_ref, first_ref, slope_ref, up_grad_ref, down_grad_ref, mix_grad_ref,
                         dx_ref, up_out, down_out, mix_out, early_out, mid_out, late_out,
                         down_ref, gq_ref, gmix_ref, gup_ref, spread_ref, dgain_ref, dqkv_ref, dout_ref, dup_ref,
                         all_ref, wqkv_ref, table_ref, early_ref, mid_ref, late_ref, *rest):
    step = pl.program_id(0)
    steps = pl.num_programs(0)
    half_steps = CHAR_STEPS
    rows, width = x_ref.shape
    words = rows // slots
    p = Place()
    send_sem, recv_sem, own_sem = rest[-3:]
    sources = (up_grad_ref, down_grad_ref, mix_grad_ref, early_ref, mid_ref, late_ref)
    results = (up_out, down_out, mix_out, early_out, mid_out, late_out)
    outs = rest[6 * CHAINS:7 * CHAINS]
    leave = [pltpu.make_async_copy(out, result, own_sem.at[CHAINS + index])
             for index, (out, result) in enumerate(zip(outs, results))]
    word_chains = 3
    chains, first_sem = [], 0
    for index in range(CHAINS):
        everywhere = index >= word_chains
        refs = tuple(rest[6 * index:6 * index + 6]) + (outs[index],)
        chains.append(Chain(p, bits, sources[index], refs, Sems(send_sem, recv_sem, first_sem), everywhere))
        first_sem += chain_copies(bits, everywhere)

    @pl.when(step == 0)
    def _():
        meet(p.mates(bits) + [p.ring_device(offset) for offset in (1, 2, 3)])
        for index in range(word_chains):
            chains[index].fetch(own_sem.at[index]).start()

    low = lambda value: value.astype(BF)

    @pl.when(step == 0)
    def _():
        dgain_ref[...] = jnp.zeros_like(dgain_ref)
        dqkv_ref[...] = jnp.zeros_like(dqkv_ref)
        dout_ref[...] = jnp.zeros_like(dout_ref)
        dup_ref[...] = jnp.zeros_like(dup_ref)
        grad_down = low(tn(act_pool_ref[...], low(gpl_ref[...])))
        quarter = early_ref.shape[1]
        for index in range(RANKS):
            early_ref[index, :, 0:width] = grad_down[index * quarter:(index + 1) * quarter]
            early_ref[index, :, width:] = grad_down[(RANKS + index) * quarter:(RANKS + index + 1) * quarter]
        split_counts(counts_ref, table_ref, words)
        join_lanes((wq_ref, wk_ref, wv_ref), wqkv_ref)
        scaled = gpl_ref[...] * (1.0 / column(counts_ref[...].astype(F32)))
        down_ref[:, width:] = nt(scaled.astype(BF), wdown_ref[...])
        down_ref[:, :width] = scaled

    @pl.when(step < half_steps)
    def _():
        here = rows_at(step * rows, rows)
        for word in range(words):
            line = down_ref[pl.ds(step * words + word, 1), :width]
            at = slice(word * slots, (word + 1) * slots)
            gq_ref[at, :width] = jnp.broadcast_to(line, (slots, width))
            line = down_ref[pl.ds(step * words + word, 1), width:]
            gup_ref[at, :] = (jnp.broadcast_to(line, (slots, line.shape[1])) * slope_ref[at, :].astype(F32)).astype(BF)

        valid_col = any_lane(valid_slots(rows, slots, table_ref[pl.ds(step, 1), 0:words]))
        unit2, rate2 = norm_parts(first_ref[...])
        dup_ref[...] += tn((unit2 * gain2_ref[...]).astype(BF), gup_ref[...])
        upstream = nt(gup_ref[...], wup_ref[...])
        dgain_ref[1:2, :] += jnp.sum(upstream * unit2, axis=0, keepdims=True)
        grad_first = jnp.where(valid_col, gq_ref[:, :width], 0.0) + norm_back(upstream, gain2_ref[...], unit2, rate2)
        spread_ref[here, :] = grad_first
        grad_low = low(grad_first)
        dout_ref[...] += tn(mixed_ref[...], grad_low)
        gmix_ref[here, :] = low(nt(grad_low, wout_ref[...]))

    @pl.when(step == half_steps - 1)
    def _():
        mid_ref[0] = low(dup_ref[:, 0:2 * width])
        mid_ref[1] = low(dup_ref[:, 2 * width:])
        mid_ref[2] = dproj_ref[...]
        half = width // 2
        mid_ref[3, 0:half, 0:width] = low(dout_ref[0:half, :])
        mid_ref[3, 0:half, width:] = low(dout_ref[half:, :])
        mid_ref[3, half:, :] = jnp.zeros_like(mid_ref[3, half:, :])
        both = jnp.concatenate([dgain_ref[...], dgain_ref[...]], axis=1)
        mid_ref[3, half:half + 16, :] = low(jnp.concatenate([wgain_ref[...], both], axis=0))

    @pl.when((step >= half_steps) & (step < 2 * half_steps))
    def _():
        base = (step - half_steps) * rows
        for tile in range(rows // TILE):
            at = pl.ds(tile * TILE, TILE)
            here = rows_at(base + tile * TILE, TILE)
            for pair in range(CHEADS // 2):
                c0 = pair * TILE
                queries = split_heads(qkv_ref[at, c0:c0 + TILE])
                keys = split_heads(qkv_ref[at, width + c0:width + c0 + TILE])
                values = qkv_ref[at, 2 * width + c0:2 * width + c0 + TILE]
                grads = split_heads(gmix_ref[here, c0:c0 + TILE])
                probs_low = probs_ref[tile, pair]
                probs = probs_low.astype(F32)
                grad_probs = compact(nt(values, grads), slots)
                inner = jnp.sum(probs * grad_probs, axis=0, keepdims=True)
                grad_scores = (probs * (grad_probs - inner) * (CHD ** -0.5)).astype(BF)
                wide_scores = expand(grad_scores, slots)
                wide_probs = expand(probs_low, slots)
                all_ref[here, c0:c0 + TILE] = tn(stack_lanes(wide_scores), keys).astype(BF)
                all_ref[here, width + c0:width + c0 + TILE] = nn(wide_scores, queries).astype(BF)
                all_ref[here, 2 * width + c0:2 * width + c0 + TILE] = nn(wide_probs, grads).astype(BF)
        dqkv_ref[...] += tn(normed_ref[...], all_ref[rows_at(base, rows), :])

    @pl.when(step == 2 * half_steps - 1)
    def _():
        rows_half, lanes_half = width // 2, 3 * width // 2
        for index in range(RANKS):
            rows_from, lanes_from = index % 2 * rows_half, index // 2 * lanes_half
            late_ref[index] = low(dqkv_ref[rows_from:rows_from + rows_half, lanes_from:lanes_from + lanes_half])

    @pl.when(step >= 2 * half_steps)
    def _():
        here = rows_at((step - 2 * half_steps) * rows, rows)
        unit1, rate1 = norm_parts(x_ref[...].astype(F32))
        upstream1 = nt(all_ref[here, :], wqkv_ref[...])
        dx_ref[...] = low(spread_ref[here, :] + norm_back(upstream1, gain1_ref[...], unit1, rate1))

    for at in range(3 * half_steps):
        todo = [(index, stages.index(at)) for index, stages in reversed(list(enumerate(PLAN))) if at in stages]
        if todo:
            @pl.when(step == at)
            def _(todo=todo):
                for index, stage in todo:
                    if stage == 1 and index < word_chains:
                        chains[index].fetch(own_sem.at[index]).wait()
                    chains[index].step(stage)

    @pl.when(step == steps - 1)
    def _():
        done = [len(stages) for stages in PLAN]
        while any(done[index] <= len(chains[index].stages) for index in range(CHAINS)):
            for index in reversed(range(CHAINS)):
                if done[index] <= len(chains[index].stages):
                    chains[index].step(done[index])
                    done[index] += 1
                    if done[index] > len(chains[index].stages):
                        leave[index].start()
        for copy in leave:
            copy.wait()


def char_backward(bits, x, counts, gain1, weights, wout, gain2, wup, wdown, grad_pooled, saved, grad_proj,
                  word_gains, word_grads):
    qkv, probs, mixed, first, slope, act_pool, normed = saved
    rows, width = x.shape
    words = counts.shape[0]
    slots = rows // words
    hidden = wup.shape[1]
    wide = word_gains.shape[1]
    step = rows // CHAR_STEPS
    last = CHAR_STEPS - 1
    ahead = lambda i: i - ((i // CHAR_STEPS + 1) // 2) * (i - last)
    behind = lambda i: (i // CHAR_STEPS % 2) * (i - CHAR_STEPS) + (i // CHAR_STEPS // 2) * last
    final = lambda i: (i // CHAR_STEPS // 2) * (i - 2 * CHAR_STEPS)
    ahead_block = lambda cols: pl.BlockSpec((step, cols), lambda i: (ahead(i), 0))
    behind_block = lambda cols: pl.BlockSpec((step, cols), lambda i: (behind(i), 0))
    whole = lambda shape: pl.BlockSpec(shape, lambda i: (0,) * len(shape))
    tiles = step // TILE
    sum_shapes = [(wide, wide)] * 3 + [(RANKS, width // 2, wide), (RANKS, width, wide), (RANKS, width // 2, 3 * width // 2)]
    sources = [(RANKS,) + shape if len(shape) == 2 else shape for shape in sum_shapes]
    copies = sum(chain_copies(bits, index >= 3) for index in range(CHAINS))
    scratch = []
    for shape in sources:
        scratch += chain_scratch(bits, shape[1], shape[2])
    return pl.pallas_call(
        functools.partial(char_backward_kernel, slots, bits),
        grid=(3 * CHAR_STEPS,),
        in_specs=[
            pl.BlockSpec((step, width), lambda i: (final(i), 0)),
            whole((1, words)),
            whole((1, width)),
            whole((width, width)),
            whole((width, width)),
            whole((width, width)),
            whole((width, width)),
            whole((1, width)),
            whole((width, hidden)),
            whole((hidden, width)),
            whole((words, width)),
            whole((words, hidden)),
            whole((width, wide)),
            whole((8, wide)),
            behind_block(width),
            behind_block(3 * width),
            pl.BlockSpec((tiles, CHEADS // 2, slots, 2 * TILE), lambda i: (behind(i), 0, 0, 0)),
            ahead_block(width),
            ahead_block(width),
            ahead_block(hidden),
        ] + [pl.BlockSpec(memory_space=pl.ANY)] * 3,
        out_specs=[pl.BlockSpec((step, width), lambda i: (final(i), 0))] + [pl.BlockSpec(memory_space=pl.ANY)] * CHAINS,
        out_shape=[jax.ShapeDtypeStruct((rows, width), BF)]
        + [jax.ShapeDtypeStruct(shape, BF) for shape in sum_shapes],
        scratch_shapes=[
            pltpu.VMEM((words, width + hidden), F32),
            pltpu.VMEM((step, width), F32),
            pltpu.VMEM((rows, width), BF),
            pltpu.VMEM((step, hidden), BF),
            pltpu.VMEM((rows, width), F32),
            pltpu.VMEM((8, width), F32),
            pltpu.VMEM((width, 3 * width), F32),
            pltpu.VMEM((width, width), F32),
            pltpu.VMEM((width, hidden), F32),
            pltpu.VMEM((rows, 3 * width), BF),
            pltpu.VMEM((width, 3 * width), BF),
            pltpu.VMEM((CHAR_STEPS, TILE), jnp.int32),
        ] + [pltpu.VMEM(shape, BF) for shape in sources[3:]] + scratch
        + [pltpu.VMEM(shape, BF) for shape in sum_shapes] + [pltpu.SemaphoreType.DMA((copies,)), pltpu.SemaphoreType.DMA((copies,)), pltpu.SemaphoreType.DMA((2 * CHAINS,))],
        compiler_params=pltpu.CompilerParams(
            vmem_limit_bytes=63 << 20, collective_id=2, has_side_effects=True),
        name="char_backward",
    )(x, counts[None, :], gain1[None, :], *weights, wout, gain2[None, :],
      wup, wdown, grad_pooled, act_pool, grad_proj, word_gains, normed, qkv, probs, mixed, first, slope, *word_grads)


def unpack_kernel(out_in, dx_in, wq_in, wk_in, wv_in, gain1_in, up_in, down_in, mix_in, turn_in, early_in, mid_in, late_in,
                  out_ref, dx_ref, gain1_ref, dq_ref, dk_ref, dv_ref, dout_ref, gain2_ref, dup_ref, ddown_ref, dproj_ref,
                  wgain1_ref, wq_ref, wk_ref, wv_ref, wout_ref, wgain2_ref, wup_ref, wdown_ref):
    step = pl.program_id(0)
    dx_ref[...] = dx_in[...].astype(F32)
    out_ref[...] = out_in[...]
    width = dq_ref.shape[0]
    half = width // 2
    wup_ref[...] = up_in[...].astype(F32)
    wdown_ref[...] = down_in[...].astype(F32)
    wq_ref[...] = mix_in[:, 0:TILE].astype(F32)
    wk_ref[...] = mix_in[:, TILE:2 * TILE].astype(F32)
    wv_ref[...] = mix_in[:, 2 * TILE:3 * TILE].astype(F32)
    for side in range(2):
        cols = slice(side * width, (side + 1) * width)
        ddown_ref[side] = early_in[0, :, cols].astype(F32)
        dup_ref[:, side * 2 * width:(side + 1) * 2 * width] = mid_in[side].astype(F32)
    dproj_ref[...] = mid_in[2].astype(F32)

    @pl.when(step < UNPACK_STEPS // 2)
    def _():
        for side in range(2):
            dout_ref[side] = mid_in[3, :, side * width:(side + 1) * width].astype(F32)

    @pl.when(step == UNPACK_STEPS // 2)
    def _():
        gains = mid_in[3, 0:16, :].astype(F32)
        wgain1_ref[...] = gains[0:1]
        wgain2_ref[...] = gains[1:2]
        gain2_ref[...] = gains[9:10, 0:width]

    @pl.when(step == 0)
    def _():
        wout_ref[...] = turn_in[...].astype(F32).T
        parts = []
        for index in range(2):
            at = slice(index * half, (index + 1) * half)
            joined = jnp.concatenate([late_in[index], late_in[2 + index]], axis=1).astype(F32)
            grads = [joined[:, part * width:(part + 1) * width] for part in range(3)]
            total = 0.0
            for grad, weight, target in zip(grads, (wq_in, wk_in, wv_in), (dq_ref, dk_ref, dv_ref)):
                target[at, :] = grad
                total += weight[at].astype(F32) * grad
            parts.append(jnp.sum(total, axis=1, keepdims=True))
        sums = jnp.concatenate(parts, axis=0)
        diagonal = (lax.broadcasted_iota(jnp.int32, (width, width), 0)
                    == lax.broadcasted_iota(jnp.int32, (width, width), 1))
        gain1_ref[...] = jnp.sum(jnp.where(diagonal, sums, 0.0), axis=0, keepdims=True) / gain1_in[...]


UNPACK_STEPS = 8


def unpack(word_output, grad_inputs, weights, gain1, sums, width, hidden):
    steps = UNPACK_STEPS
    up, down, mix, early, mid, late = sums
    wide = word_output.shape[1]
    whole = lambda shape: pl.BlockSpec(shape, lambda i: (0,) * len(shape))
    split = lambda shape: pl.BlockSpec((shape[0] // steps, shape[1]), lambda i: (i, 0))
    middle = lambda shape: pl.BlockSpec((shape[0], shape[1] // steps, shape[2]), lambda i: (0, i, 0))
    per = early.shape[1] * RANKS // steps
    blocks = early.shape[1] // per
    pinned = lambda i: i - (i // (steps // 2)) * (i - (steps // 2 - 1))
    outs = [
        (whole, (1, width)), (whole, (width, width)), (whole, (width, width)), (whole, (width, width)),
        (lambda shape: pl.BlockSpec((2, shape[1] * 2 // steps, width), lambda i: (0, pinned(i), 0)), (2, width // 2, width)),
        (whole, (1, width)), (split, (width, hidden)), (middle, (2, hidden // 2, width)), (split, (width, wide)),
        (whole, (1, wide)), (split, (wide, TILE)), (split, (wide, TILE)), (split, (wide, TILE)),
        (whole, (TILE, wide)), (whole, (1, wide)), (split, (wide, wide)), (split, (wide, wide)),
    ]
    results = pl.pallas_call(
        unpack_kernel,
        grid=(steps,),
        in_specs=[split(word_output.shape), split(grad_inputs.shape)] + [whole((width, width))] * 3 + [whole((1, width))]
        + [split(up.shape), split(down.shape), split(mix.shape), pl.BlockSpec((wide, TILE), lambda i: (0, 3)),
           pl.BlockSpec((1, per, wide), lambda i: (i // blocks, i % blocks, 0)), middle(mid.shape), whole(late.shape)],
        out_specs=[split(word_output.shape), split(grad_inputs.shape)] + [spec(shape) for spec, shape in outs],
        out_shape=[jax.ShapeDtypeStruct(word_output.shape, BF), jax.ShapeDtypeStruct(grad_inputs.shape, F32)]
        + [jax.ShapeDtypeStruct(shape, F32) for _, shape in outs],
        compiler_params=pltpu.CompilerParams(vmem_limit_bytes=60 << 20),
        name="unpack",
    )(word_output, grad_inputs, *weights, gain1[None, :], up, down, mix, mix, early, mid, late)

    def shaped(array):
        if array.ndim == 3:
            return array.reshape(-1, array.shape[2])
        return array[0] if array.shape[0] == 1 else array

    return tuple(shaped(array) for array in results)


def per_device(
    bits,
    char_inputs,
    char_counts,
    doc_ids,
    cotangent,
    char_norm_one,
    char_query,
    char_key,
    char_value,
    char_out,
    char_norm_two,
    char_up,
    char_down,
    char_proj,
    word_norm_one,
    word_query,
    word_key,
    word_value,
    word_out_proj,
    word_norm_two,
    word_up,
    word_down,
):
    char_qkv = (char_query, char_key, char_value)
    word_qkv = (word_query, word_key, word_value)
    vec, pooled, *saved, near, qkv_all, out_all, up_all, down_all = char_forward(
        char_inputs, char_counts, char_norm_one, char_qkv, char_out, char_norm_two, char_up, char_down, char_proj,
        word_qkv, word_out_proj, word_up, word_down,
    )
    word_output, grad_pooled, grad_proj, word_gains, *word_grads = word_layer(
        bits, vec, near, doc_ids, cotangent, qkv_all, out_all, up_all, down_all,
        word_norm_one, word_norm_two, char_proj, pooled,
    )
    grad_inputs, *sums = char_backward(
        bits, char_inputs, char_counts, char_norm_one, char_qkv, char_out, char_norm_two, char_up, char_down,
        grad_pooled, saved, grad_proj, word_gains, word_grads,
    )
    return unpack(word_output, grad_inputs, char_qkv, char_norm_one, sums, char_out.shape[0], char_up.shape[1])


def solution(mesh):
    in_specs = (
        P(("dp", "tensor"), None),
        P(("dp", "tensor")),
        P("dp", None),
        P("dp", None),
        P(),
        P(),
        P(),
        P(),
        P(),
        P(),
        P(),
        P(),
        P(),
        P(),
        P(None, "tensor"),
        P(None, "tensor"),
        P(None, "tensor"),
        P("tensor", None),
        P(),
        P(None, "tensor"),
        P("tensor", None),
    )
    out_specs = (
        P(("dp", "tensor"), None),
        P(("dp", "tensor"), None),
        P(),
        P(),
        P(),
        P(),
        P(),
        P(),
        P(),
        P(),
        P(),
        P(),
        P(None, "tensor"),
        P(None, "tensor"),
        P(None, "tensor"),
        P("tensor", None),
        P(),
        P(None, "tensor"),
        P("tensor", None),
    )
    assert mesh.shape["tensor"] == RANKS
    bits = mesh.shape["dp"].bit_length() - 1
    assert bits >= 3 and mesh.shape["dp"] == 1 << bits
    return jax.shard_map(
        functools.partial(per_device, bits), mesh=mesh, in_specs=in_specs, out_specs=out_specs, check_vma=False
    )
```

```python
import functools

import jax
import jax.numpy as jnp
from jax import lax
from jax.experimental import pallas as pl
from jax.experimental.pallas import tpu as pltpu
from jax.sharding import PartitionSpec as P

BF = jnp.bfloat16
F32 = jnp.float32
EPSILON = 1e-05
NEG_LARGE = -1e30
RANKS = 4
CHEADS = 4
CHD = 64
TILE = 128
CHAR_STEPS = 8
GELU_C = 0.7978845608028654
GELU_A = 0.044715


def nn(left, right):
    return lax.dot_general(left, right, (((1,), (0,)), ((), ())), preferred_element_type=F32)


def nt(left, right):
    return lax.dot_general(left, right, (((1,), (1,)), ((), ())), preferred_element_type=F32)


def tn(left, right):
    return lax.dot_general(left, right, (((0,), (0,)), ((), ())), preferred_element_type=F32)


def norm_parts(values):
    centre = values - jnp.mean(values, axis=-1, keepdims=True)
    spread = jnp.mean(centre * centre, axis=-1, keepdims=True)
    rate = lax.rsqrt(spread + EPSILON)
    return centre * rate, rate


def norm_back(upstream, gain, unit, rate):
    scaled = upstream * gain
    first = jnp.mean(scaled, axis=-1, keepdims=True)
    second = jnp.mean(scaled * unit, axis=-1, keepdims=True)
    return rate * (scaled - first - unit * second)


def gelu_parts(values):
    square = values * values
    inner = values * (GELU_C + (GELU_C * GELU_A) * square)
    half = 0.5 + 0.5 * jnp.tanh(inner)
    active = values * half
    slope = half + (active * (1.0 - half)) * (2.0 * GELU_C + (6.0 * GELU_C * GELU_A) * square)
    return active, slope


def split_heads(pair):
    low_half = lax.broadcasted_iota(jnp.int32, pair.shape, 1) < CHD
    zero = jnp.zeros_like(pair)
    return jnp.concatenate([jnp.where(low_half, pair, zero), jnp.where(low_half, zero, pair)], axis=0)


def word_of_lane(shape, slots):
    lane = lax.broadcasted_iota(jnp.int32, shape, 1)
    return jnp.bitwise_and(lane, TILE - 1) // slots


def compact(scores, slots):
    words = word_of_lane((slots, scores.shape[1]), slots)
    result = scores[0:slots]
    for word in range(1, TILE // slots):
        result = jnp.where(words == word, scores[word * slots:(word + 1) * slots], result)
    return result


def expand(packed, slots):
    words = word_of_lane(packed.shape, slots)
    zero = jnp.zeros_like(packed)
    return jnp.concatenate(
        [jnp.where(words == word, packed, zero) for word in range(TILE // slots)], axis=0
    )


def stack_lanes(pair):
    return jnp.concatenate([pair[:, :TILE], pair[:, TILE:]], axis=0)


def split_counts(counts_ref, table_ref, words):
    for step in range(CHAR_STEPS):
        table_ref[step:step + 1, 0:words] = counts_ref[:, step * words:(step + 1) * words]


def valid_slots(rows, slots, mine):
    words = rows // slots
    row = lax.broadcasted_iota(jnp.int32, (rows, words), 0)
    word = lax.broadcasted_iota(jnp.int32, (rows, words), 1)
    return (row // slots == word) & (jnp.bitwise_and(row, slots - 1) < mine)


def join_lanes(parts, whole_ref):
    width = parts[0].shape[1]
    for index, part in enumerate(parts):
        whole_ref[:, index * width:(index + 1) * width] = part[...]


def any_lane(mask):
    return jnp.max(jnp.where(mask, 1.0, 0.0), axis=1, keepdims=True) > 0.0


def column(row):
    size = row.shape[1]
    diagonal = (lax.broadcasted_iota(jnp.int32, (size, size), 0)
                == lax.broadcasted_iota(jnp.int32, (size, size), 1))
    return jnp.sum(jnp.where(diagonal, row, 0.0), axis=1, keepdims=True)


MESH = pl.DeviceIdType.MESH
LANE_SPLIT = 256


class Place:
    def __init__(self):
        self.dp = lax.axis_index("dp")
        self.rank = lax.axis_index("tensor")
        self.core = lax.rem(self.dp, 2)
        self.x = lax.rem(self.dp // 2, 2)
        self.y = lax.rem(self.dp // 4, 2)
        self.core_mate = (self.dp + 1 - 2 * self.core, self.rank)
        self.x_mate = (self.dp + 2 - 4 * self.x, self.rank)
        self.y_mate = (self.dp + 4 - 8 * self.y, self.rank)

    def ring(self, offset):
        return lax.rem(self.rank + offset, RANKS)

    def ring_device(self, offset):
        return (self.dp, self.ring(offset))

    def bit_mate(self, bit):
        size = 1 << bit
        mine = lax.rem(self.dp // size, 2)
        return (self.dp + size - 2 * size * mine, self.rank)

    def mates(self, bits):
        extra = [self.bit_mate(bit) for bit in range(3, bits)]
        return [self.core_mate, self.x_mate, self.y_mate] + extra


def meet(devices):
    barrier = pltpu.get_barrier_semaphore()
    for device in devices:
        pl.semaphore_signal(barrier, inc=1, device_id=device, device_id_type=MESH)
    pl.semaphore_wait(barrier, len(devices))


def remote(source, target, sems, device):
    return pltpu.make_async_remote_copy(
        src_ref=source, dst_ref=target, send_sem=sems[0], recv_sem=sems[1],
        device_id=device, device_id_type=MESH,
    )


class Sems:
    def __init__(self, send, recv, start=0):
        self.send, self.recv, self.next = send, recv, start

    def take(self):
        at = self.next
        self.next += 1
        return self.send.at[at], self.recv.at[at]


def rows_at(start, size):
    return pl.ds(pl.multiple_of(start, 16), size)


def halves(width):
    return (slice(0, LANE_SPLIT), slice(LANE_SPLIT, width))


class Gather:
    def __init__(self, place, local, whole, sems):
        self.stages = [[], [], [], []]
        rows = local.shape[0]
        unit = rows // 8
        p = place
        left, right = halves(local.shape[1])
        left_at = p.core * 4 + p.x * 2 + p.y
        right_at = p.core * 4 + p.y * 2 + p.x
        for offset in range(1, RANKS):
            for lanes, at in ((left, left_at), (right, right_at)):
                at = rows_at(at * unit, unit)
                self.stages[0].append(remote(
                    local.at[at, lanes], whole.at[p.rank, at, lanes], sems.take(), p.ring_device(offset)))
        for offset in range(1, RANKS):
            rank = p.ring(offset)
            for lanes, at, first, second, mate_first, mate_second in (
                (left, left_at, p.x, None, p.y_mate, p.x_mate),
                (right, right_at, p.y, None, p.x_mate, p.y_mate),
            ):
                one = rows_at(at * unit, unit)
                two = rows_at((p.core * 4 + first * 2) * unit, 2 * unit)
                self.stages[1].append(remote(
                    whole.at[rank, one, lanes], whole.at[rank, one, lanes], sems.take(), mate_first))
                self.stages[2].append(remote(
                    whole.at[rank, two, lanes], whole.at[rank, two, lanes], sems.take(), mate_second))
            four = rows_at(p.core * 4 * unit, 4 * unit)
            self.stages[3].append(remote(
                whole.at[rank, four], whole.at[rank, four], sems.take(), p.core_mate))

    def start(self, stage):
        for copy in self.stages[stage]:
            copy.start()

    def wait(self, stage):
        for copy in self.stages[stage]:
            copy.wait()


def gather_copies():
    return 2 * (RANKS - 1) * 3 + (RANKS - 1)


class Chain:
    def __init__(self, place, bits, src, refs, sems, everywhere):
        p = place
        buf, got_core, got_one, got_two, got_more, got_rank, out = refs
        self.p, self.src, self.everywhere = p, src, everywhere
        self.buf, self.got_core, self.got_one, self.got_two = buf, got_core, got_one, got_two
        self.got_more, self.got_rank = got_more, got_rank
        self.mine = out.at[p.rank] if everywhere else out
        unit = src.shape[1] // 8
        lanes = left, right = halves(src.shape[2])
        self.lanes = lanes
        self.own = rows_at(p.core * 4 * unit, 4 * unit)
        stages = [("core", [remote(src.at[:, rows_at((1 - p.core) * 4 * unit, 4 * unit)], got_core,
                                   sems.take(), p.core_mate)])]
        first, second = (p.x, p.y), (p.y, p.x)
        first_mate, second_mate = (p.x_mate, p.y_mate), (p.y_mate, p.x_mate)
        one = lambda side, at: rows_at(at * 2 * unit, 2 * unit)
        two = lambda side, at: rows_at((first[side] * 2 + at) * unit, unit)
        self.one_rows = [one(side, first[side]) for side in (0, 1)]
        self.two_rows = [two(side, second[side]) for side in (0, 1)]
        stages.append(("one", [
            remote(buf.at[:, one(side, 1 - first[side]), lanes[side]], got_one.at[:, :, lanes[side]],
                   sems.take(), first_mate[side]) for side in (0, 1)]))
        stages.append(("two", [
            remote(buf.at[:, two(side, 1 - second[side]), lanes[side]], got_two.at[:, :, lanes[side]],
                   sems.take(), second_mate[side]) for side in (0, 1)]))
        for bit in range(3, bits):
            stages.append((bit - 3, [
                remote(buf.at[:, self.two_rows[side], lanes[side]], got_more.at[bit - 3, :, :, lanes[side]],
                       sems.take(), p.bit_mate(bit)) for side in (0, 1)]))
        stages.append(("rank", [
            remote(buf.at[p.ring(offset), self.two_rows[side], lanes[side]],
                   got_rank.at[offset - 1, :, lanes[side]], sems.take(), p.ring_device(offset))
            for offset in range(1, RANKS) for side in (0, 1)]))
        base = p.core * 4 * unit
        self.out_two = [rows_at(base + (first[side] * 2 + second[side]) * unit, unit) for side in (0, 1)]
        out_one = [rows_at(base + first[side] * 2 * unit, 2 * unit) for side in (0, 1)]
        if everywhere:
            stages.append(("rank_back", [
                remote(out.at[p.rank, self.out_two[side], lanes[side]], out.at[p.rank, self.out_two[side], lanes[side]],
                       sems.take(), p.ring_device(offset))
                for offset in range(1, RANKS) for side in (0, 1)]))

        def back(at, part_lanes, mate):
            part = out.at[:, at, part_lanes] if everywhere else out.at[at, part_lanes]
            return remote(part, part, sems.take(), mate)

        stages.append(("back_two", [back(self.out_two[side], lanes[side], second_mate[side]) for side in (0, 1)]))
        stages.append(("back_one", [back(out_one[side], lanes[side], first_mate[side]) for side in (0, 1)]))
        stages.append(("back_core", [back(self.own, slice(None), p.core_mate)]))
        self.stages = stages

    def fetch(self, sem):
        return pltpu.make_async_copy(self.src.at[:, self.own], self.buf, sem)

    def start(self, index):
        for copy in self.stages[index][1]:
            copy.start()

    def finish(self, index):
        name, copies = self.stages[index]
        for copy in copies:
            copy.wait()
        buf = self.buf
        if name == "core":
            own = self.src if self.everywhere else None
            for quarter in range(RANKS):
                mine = own[quarter, self.own, :] if self.everywhere else buf[quarter]
                buf[quarter] = mine + self.got_core[quarter]
        elif name == "one":
            for at, lanes in zip(self.one_rows, self.lanes):
                for quarter in range(RANKS):
                    buf[quarter, at, lanes] += self.got_one[quarter, :, lanes]
        elif name == "two":
            for at, lanes in zip(self.two_rows, self.lanes):
                for quarter in range(RANKS):
                    buf[quarter, at, lanes] += self.got_two[quarter, :, lanes]
        elif name == "rank":
            for side in (0, 1):
                at, lanes = self.two_rows[side], self.lanes[side]
                total = buf[self.p.rank, at, lanes].astype(F32)
                for k in range(RANKS - 1):
                    total = total + self.got_rank[k, :, lanes].astype(F32)
                self.mine[self.out_two[side], lanes] = total.astype(BF)
        elif isinstance(name, int):
            for at, lanes in zip(self.two_rows, self.lanes):
                for quarter in range(RANKS):
                    buf[quarter, at, lanes] += self.got_more[name, quarter, :, lanes]

    def step(self, index):
        if index:
            self.finish(index - 1)
        if index < len(self.stages):
            self.start(index)


def chain_copies(bits, everywhere):
    pairs = 2 * (RANKS - 1)
    return 1 + 2 + 2 + 2 * (bits - 3) + pairs + (pairs if everywhere else 0) + 2 + 2 + 1


def chain_scratch(bits, rows, lanes):
    unit = rows // 8
    return [
        pltpu.VMEM((RANKS, 4 * unit, lanes), BF),
        pltpu.VMEM((RANKS, 4 * unit, lanes), BF),
        pltpu.VMEM((RANKS, 2 * unit, lanes), BF),
        pltpu.VMEM((RANKS, unit, lanes), BF),
        pltpu.VMEM((max(bits - 3, 1), RANKS, unit, lanes), BF),
        pltpu.VMEM((RANKS - 1, unit, lanes), BF),
    ]


FORWARD_PLAN = {
    2: ((0, 1), (1, 1)),
    3: ((2, 1), (0, 2), (1, 2)),
    4: ((3, 1), (2, 2)),
    5: ((0, 3), (1, 3), (3, 2)),
    6: ((2, 3),),
    7: ((3, 3),),
}


def char_forward_kernel(slots, x_ref, counts_ref, gain1_ref, wq_ref, wk_ref, wv_ref, wout_ref,
                        gain2_ref, wup_ref, wdown_ref, wproj_ref,
                        lq_ref, lk_ref, lv_ref, lout_ref, lup_ref, ldown_ref,
                        vec_ref, pooled_ref, qkv_ref, probs_ref, mixed_ref, first_ref,
                        slope_ref, act_pool_ref, normed_ref, near_ref, wqkv_all, wout_all, wup_all, wdown_all,
                        wqkv_ref, lqkv_ref, table_ref, own_sem, send_sem, recv_sem):
    rows = x_ref.shape[0]
    width = x_ref.shape[1]
    step = pl.program_id(0)
    steps = pl.num_programs(0)
    words = rows // slots
    p = Place()
    pairs = ((lqkv_ref, wqkv_all), (lout_ref, wout_all), (lup_ref, wup_all), (ldown_ref, wdown_all))
    gathers = [Gather(p, mine, whole, Sems(send_sem, recv_sem, gather_copies() * index))
               for index, (mine, whole) in enumerate(pairs)]
    own_copies = [pltpu.make_async_copy(mine, whole.at[p.rank], own_sem.at[index])
                  for index, (mine, whole) in enumerate(pairs)]
    vec_base = gather_copies() * len(pairs)

    def vec_copies(at):
        copies = []
        for slot, offset in ((1, 1), (0, 2)):
            sem = vec_base + 2 * at + slot
            part = rows_at(at * words, words)
            copies.append(remote(vec_ref.at[part], near_ref.at[slot, part],
                                 (send_sem.at[sem], recv_sem.at[sem]), p.ring_device(offset)))
        return copies

    def send_vec(at):
        for offset, copy in zip((1, 2), vec_copies(at)):
            @pl.when(p.rank + offset < RANKS)
            def _(copy=copy):
                copy.start()

    def wait_vec(at):
        for offset, copy in zip((1, 2), vec_copies(at)):
            @pl.when(p.rank + offset < RANKS)
            def _(copy=copy):
                copy.wait_send()

            @pl.when(p.rank >= offset)
            def _(copy=copy):
                copy.wait_recv()

    @pl.when(step == 0)
    def _():
        join_lanes((lq_ref, lk_ref, lv_ref), lqkv_ref)
        join_lanes((wq_ref, wk_ref, wv_ref), wqkv_ref)
        meet([p.ring_device(offset) for offset in (1, 2, 3)] + [p.core_mate, p.x_mate, p.y_mate])
        split_counts(counts_ref, table_ref, words)
        for copy in own_copies:
            copy.start()
        for gather in gathers:
            gather.start(0)

    base = x_ref[...].astype(F32)
    unit, _ = norm_parts(base)
    normed = (unit * gain1_ref[...]).astype(BF)
    normed_ref[...] = normed
    qkv_ref[...] = nn(normed, wqkv_ref[...]).astype(BF)
    mine = table_ref[pl.ds(step, 1), 0:words]
    word_at = lax.broadcasted_iota(jnp.int32, (words, rows), 0)
    row_at = lax.broadcasted_iota(jnp.int32, (words, rows), 1)
    onto_rows = jnp.where(row_at // slots == word_at, 1.0, 0.0).astype(BF)
    row_counts = nn(jnp.broadcast_to(mine.astype(F32), (16, words)).astype(BF), onto_rows)[0:1]
    for tile in range(rows // TILE):
        at = pl.ds(tile * TILE, TILE)
        valid = (lax.broadcasted_iota(jnp.int32, (slots, TILE), 0).astype(F32)
                 < row_counts[:, tile * TILE:(tile + 1) * TILE])
        for pair in range(CHEADS // 2):
            c0 = pair * TILE
            queries = split_heads(qkv_ref[at, c0:c0 + TILE])
            keys = qkv_ref[at, width + c0:width + c0 + TILE]
            values = split_heads(qkv_ref[at, 2 * width + c0:2 * width + c0 + TILE])
            scores = compact(nt(keys, queries), slots)
            parts = []
            for head in range(2):
                own = jnp.where(valid, scores[:, head * TILE:(head + 1) * TILE], NEG_LARGE)
                top = jnp.max(own, axis=0, keepdims=True)
                weight = jnp.exp((own - top) * (CHD ** -0.5))
                parts.append(weight / jnp.sum(weight, axis=0, keepdims=True))
            probs = jnp.concatenate(parts, axis=1).astype(BF)
            probs_ref[tile, pair] = probs
            mixed_ref[at, c0:c0 + TILE] = tn(stack_lanes(expand(probs, slots)), values).astype(BF)

    for at, todo in FORWARD_PLAN.items():
        @pl.when(step == at)
        def _(todo=todo):
            for member, stage in todo:
                gathers[member].wait(stage - 1)
                gathers[member].start(stage)

    @pl.when(step > 0)
    def _():
        send_vec(step - 1)

    first = base + nn(mixed_ref[...], wout_ref[...])
    first_ref[...] = first
    unit2, _ = norm_parts(first)
    normed2 = (unit2 * gain2_ref[...]).astype(BF)
    members = valid_slots(rows, slots, mine)
    valid_col = any_lane(members)
    pool = jnp.where(members, 1.0 / mine.astype(F32), 0.0).astype(BF)
    chunk = 256
    for part in range(wup_ref.shape[1] // chunk):
        cols = slice(part * chunk, (part + 1) * chunk)
        active, slope = gelu_parts(nn(normed2, wup_ref[:, cols]))
        slope_ref[:, cols] = jnp.where(valid_col, slope, 0.0).astype(BF)
        act_pool_ref[:, cols] = tn(pool, active.astype(BF)).astype(BF)
    pooled = tn(pool, first.astype(BF)) + nn(act_pool_ref[...], wdown_ref[...])
    pooled = pooled.astype(BF)
    pooled_ref[...] = pooled
    vec_ref[rows_at(step * words, words), :] = nn(pooled, wproj_ref[...]).astype(BF)

    @pl.when(step == steps - 1)
    def _():
        send_vec(step)
        for copy in own_copies:
            copy.wait()
        for gather in gathers:
            gather.wait(3)
        for at in range(CHAR_STEPS):
            wait_vec(at)


def char_forward(x, counts, gain1, weights, wout, gain2, wup, wdown, wproj, local, lout, lup, ldown):
    rows, width = x.shape
    words = counts.shape[0]
    slots = rows // words
    hidden = wup.shape[1]
    wide = wproj.shape[1]
    step = rows // CHAR_STEPS
    step_words = step // slots
    row_block = lambda cols: pl.BlockSpec((step, cols), lambda i: (i, 0))
    word_block = lambda cols: pl.BlockSpec((step_words, cols), lambda i: (i, 0))
    whole = lambda shape: pl.BlockSpec(shape, lambda i: (0, 0))
    tiles = step // TILE
    return pl.pallas_call(
        functools.partial(char_forward_kernel, slots),
        grid=(rows // step,),
        in_specs=[
            row_block(width),
            whole((1, words)),
            whole((1, width)),
            whole((width, width)),
            whole((width, width)),
            whole((width, width)),
            whole((width, width)),
            whole((1, width)),
            whole((width, hidden)),
            whole((hidden, width)),
            whole((width, wide)),
            whole(local[0].shape),
            whole(local[0].shape),
            whole(local[0].shape),
            whole(lout.shape),
            whole(lup.shape),
            whole(ldown.shape),
        ],
        out_specs=[
            whole((words, wide)),
            word_block(width),
            row_block(3 * width),
            pl.BlockSpec((tiles, CHEADS // 2, slots, 2 * TILE), lambda i: (i, 0, 0, 0)),
            row_block(width),
            row_block(width),
            row_block(hidden),
            word_block(hidden),
            row_block(width),
        ] + [pl.BlockSpec(memory_space=pl.ANY)] * 5,
        out_shape=[
            jax.ShapeDtypeStruct((words, wide), BF),
            jax.ShapeDtypeStruct((words, width), BF),
            jax.ShapeDtypeStruct((rows, 3 * width), BF),
            jax.ShapeDtypeStruct((rows // TILE, CHEADS // 2, slots, 2 * TILE), BF),
            jax.ShapeDtypeStruct((rows, width), BF),
            jax.ShapeDtypeStruct((rows, width), F32),
            jax.ShapeDtypeStruct((rows, hidden), BF),
            jax.ShapeDtypeStruct((words, hidden), BF),
            jax.ShapeDtypeStruct((rows, width), BF),
            jax.ShapeDtypeStruct((2, words, wide), BF),
            jax.ShapeDtypeStruct((RANKS, wide, 3 * TILE), BF),
            jax.ShapeDtypeStruct((RANKS,) + lout.shape, BF),
            jax.ShapeDtypeStruct((RANKS,) + lup.shape, BF),
            jax.ShapeDtypeStruct((RANKS,) + ldown.shape, BF),
        ],
        scratch_shapes=[
            pltpu.VMEM((width, 3 * width), BF),
            pltpu.VMEM((wide, 3 * TILE), BF),
            pltpu.VMEM((CHAR_STEPS, TILE), jnp.int32),
            pltpu.SemaphoreType.DMA((4,)),
            pltpu.SemaphoreType.DMA((gather_copies() * 4 + 2 * CHAR_STEPS,)),
            pltpu.SemaphoreType.DMA((gather_copies() * 4 + 2 * CHAR_STEPS,)),
        ],
        compiler_params=pltpu.CompilerParams(
            vmem_limit_bytes=60 << 20, collective_id=0, has_side_effects=True),
        name="char_forward",
    )(x, counts[None, :], gain1[None, :], *weights, wout, gain2[None, :], wup, wdown, wproj,
      *local, lout, lup, ldown)


def word_kernel(bits, vec_ref, near_ref, docs_ref, cot_ref, wqkv_in, wout_in, wup_in,
                wdown_in, gain1_ref, gain2_ref, wproj_ref, pooled_ref,
                out_ref, gpl_ref, dproj_ref, dgain_ref, up_grad_out, down_grad_out, mix_grad_out,
                n1_ref, q_ref, kv_ref, probs_ref, o_ref, act_ref, slope_ref, go_ref, gq_ref, gkv_ref,
                back_ref, cot_own, cot_sem, part_ref, got_ref, table_ref, wqkv_ref, wout_ref, wup_ref, wdown_ref,
                up_grad_ref, down_grad_ref, mix_grad_ref, io_sem, send_sem, recv_sem):
    p = Place()
    words, wide = vec_ref.shape
    window = 3 * words
    fetch = pltpu.make_async_copy(cot_ref.at[rows_at(p.rank * words, words)], cot_own, cot_sem)
    loads = [pltpu.make_async_copy(source, target, io_sem.at[index]) for index, (source, target) in enumerate((
        (wqkv_in, wqkv_ref), (wout_in, wout_ref), (wup_in, wup_ref), (wdown_in, wdown_ref)))]
    stores = [pltpu.make_async_copy(source, target, io_sem.at[4 + index]) for index, (source, target) in enumerate((
        (up_grad_ref, up_grad_out), (down_grad_ref, down_grad_out)))]

    def store_mix(rank):
        return pltpu.make_async_copy(mix_grad_ref.at[rank], mix_grad_out.at[rank], io_sem.at[6 + rank])

    for copy in loads:
        copy.start()
    fetch.start()
    meet([p.ring_device(offset) for offset in (1, 2, 3)])

    table_ref[:, 0:2 * words] = jnp.full((1, 2 * words), -1, jnp.int32)
    table_ref[:, 2 * words:] = docs_ref[...]
    start = pl.multiple_of(p.rank * words, TILE)
    key_docs = table_ref[:, pl.ds(start, window)].astype(F32)
    row_docs = column(key_docs[:, 2 * words:])

    own = vec_ref[...].astype(F32)
    unit1, rate1 = norm_parts(own)
    n1_ref[2 * words:, :] = (unit1 * gain1_ref[...]).astype(BF)
    for slot in range(2):
        near = jnp.where(p.rank + slot >= 2, near_ref[slot].astype(F32), 0.0)
        unit, _ = norm_parts(near)
        n1_ref[slot * words:(slot + 1) * words, :] = (unit * gain1_ref[...]).astype(BF)

    def project(rank, carry):
        q_ref[rank] = nn(n1_ref[2 * words:, :], wqkv_ref[rank, :, 0:TILE]).astype(BF)
        kv_ref[rank] = nn(n1_ref[...], wqkv_ref[rank, :, TILE:]).astype(BF)
        scores = nt(split_heads(q_ref[rank]), kv_ref[rank, :, 0:TILE]) * (CHD ** -0.5)
        row = lax.broadcasted_iota(jnp.int32, (words, window), 0)
        key = lax.broadcasted_iota(jnp.int32, (words, window), 1)
        allowed = (row_docs == key_docs) & (key <= row + 2 * words)
        for head in range(2):
            at = slice(head * words, (head + 1) * words)
            masked = jnp.where(allowed, scores[at], NEG_LARGE)
            top = jnp.max(masked, axis=-1, keepdims=True)
            weight = jnp.exp(masked - top)
            probs_ref[rank, at, :] = (weight * (1.0 / jnp.sum(weight, axis=-1, keepdims=True))).astype(BF)
        pair = jnp.concatenate([probs_ref[rank, 0:words, :], probs_ref[rank, words:, :]], axis=1)
        o_ref[rank] = nn(pair, split_heads(kv_ref[rank, :, TILE:])).astype(BF)
        back_ref[...] += nn(o_ref[rank], wout_ref[rank])
        return carry

    back_ref[...] = own
    loads[0].wait()
    loads[1].wait()
    lax.fori_loop(0, RANKS, project, 0)
    middle = back_ref[...]
    unit2, rate2 = norm_parts(middle)
    normed2 = (unit2 * gain2_ref[...]).astype(BF)

    def feed(rank, carry):
        active, slope = gelu_parts(nn(normed2, wup_ref[rank]))
        act_ref[rank] = active.astype(BF)
        slope_ref[rank] = slope.astype(BF)
        back_ref[...] += nn(act_ref[rank], wdown_ref[rank])
        return carry

    loads[2].wait()
    loads[3].wait()
    lax.fori_loop(0, RANKS, feed, 0)
    out_ref[...] = back_ref[...].astype(BF)
    fetch.wait()
    back_ref[...] = jnp.zeros_like(back_ref)

    def feed_back(rank, carry):
        upstream = (nt(cot_own[...], wdown_ref[rank]) * slope_ref[rank].astype(F32)).astype(BF)
        back_ref[...] += nt(upstream, wup_ref[rank])
        up_grad_ref[rank] = tn(normed2, upstream).astype(BF)
        down_grad_ref[rank] = tn(act_ref[rank], cot_own[...]).astype(BF)
        return carry

    lax.fori_loop(0, RANKS, feed_back, 0)
    for copy in stores:
        copy.start()
    upstream2 = back_ref[...]
    dgain_ref[...] = jnp.zeros_like(dgain_ref)
    dgain_ref[1:2, :] = jnp.sum(upstream2 * unit2, axis=0, keepdims=True)
    grad_middle = cot_own[...].astype(F32) + norm_back(upstream2, gain2_ref[...], unit2, rate2)
    middle_low = grad_middle.astype(BF)

    back_ref[...] = jnp.zeros_like(back_ref)
    part_ref[...] = jnp.zeros_like(part_ref)

    def attend_back(rank, carry):
        go_ref[...] = nt(middle_low, wout_ref[rank]).astype(BF)
        mix_grad_ref[rank, :, 3 * TILE:] = tn(middle_low, o_ref[rank]).astype(BF)
        go_pair = split_heads(go_ref[...])
        grad_probs = nt(go_pair, kv_ref[rank, :, TILE:])
        probs = probs_ref[rank].astype(F32)
        inner = jnp.sum(probs * grad_probs, axis=-1, keepdims=True)
        grad_scores = (probs * (grad_probs - inner) * (CHD ** -0.5)).astype(BF)
        q_pair = split_heads(q_ref[rank])
        gkv_ref[rank, :, 0:TILE] = tn(grad_scores, q_pair).astype(BF)
        gkv_ref[rank, :, TILE:] = tn(probs_ref[rank], go_pair).astype(BF)
        pair = jnp.concatenate([grad_scores[0:words], grad_scores[words:]], axis=1)
        gq_ref[rank] = nn(pair, split_heads(kv_ref[rank, :, 0:TILE])).astype(BF)
        part_ref[...] += nt(gkv_ref[rank, 0:2 * words, :], wqkv_ref[rank, :, TILE:])
        back_ref[...] += nt(gkv_ref[rank, 2 * words:, :], wqkv_ref[rank, :, TILE:])
        back_ref[...] += nt(gq_ref[rank], wqkv_ref[rank, :, 0:TILE])
        return carry

    lax.fori_loop(0, RANKS, attend_back, 0)
    near_ref_low = got_ref.at[2]
    near_ref_low[...] = part_ref[...].astype(BF).reshape(2, words, wide)
    sends = []
    for slot, offset in ((0, RANKS - 2), (1, RANKS - 1)):
        sends.append(remote(got_ref.at[2, slot], got_ref.at[slot, 0], (send_sem.at[slot], recv_sem.at[slot]),
                            p.ring_device(offset)))
    for copy in sends:
        copy.start()

    def weigh(rank, carry):
        mix_grad_ref[rank, :, 0:TILE] = tn(n1_ref[2 * words:, :], gq_ref[rank]).astype(BF)
        mix_grad_ref[rank, :, TILE:3 * TILE] = tn(n1_ref[...], gkv_ref[rank]).astype(BF)
        store_mix(rank).start()
        return carry

    lax.fori_loop(0, RANKS, weigh, 0)
    for copy in sends:
        copy.wait()
    upstream1 = back_ref[...] + got_ref[0, 0].astype(F32) + got_ref[1, 0].astype(F32)
    dgain_ref[0:1, :] = jnp.sum(upstream1 * unit1, axis=0, keepdims=True)
    grad_vec = (grad_middle + norm_back(upstream1, gain1_ref[...], unit1, rate1)).astype(BF)
    dproj_ref[...] = tn(pooled_ref[...], grad_vec).astype(BF)
    gpl_ref[...] = nt(grad_vec, wproj_ref[...])
    for copy in stores + [store_mix(rank) for rank in range(RANKS)]:
        copy.wait()


def word_layer(bits, vec, near, doc_ids, cotangent, wqkv, wout, wup, wdown, gain1, gain2, wproj, pooled):
    words, wide = vec.shape
    width = pooled.shape[1]
    window = 3 * words
    hidden = wup.shape[2]
    vm = pl.BlockSpec(memory_space=pltpu.VMEM)
    return pl.pallas_call(
        functools.partial(word_kernel, bits),
        in_specs=[vm] * 3 + [pl.BlockSpec(memory_space=pl.ANY)] * 5 + [vm] * 4,
        out_specs=[vm] * 4 + [pl.BlockSpec(memory_space=pl.ANY)] * 3,
        out_shape=[
            jax.ShapeDtypeStruct((words, wide), BF),
            jax.ShapeDtypeStruct((words, width), F32),
            jax.ShapeDtypeStruct((width, wide), BF),
            jax.ShapeDtypeStruct((8, wide), F32),
        ] + [
            jax.ShapeDtypeStruct((RANKS, wide, wide), BF) for _ in range(3)
        ],
        scratch_shapes=[
            pltpu.VMEM((window, wide), BF),
            pltpu.VMEM((RANKS, words, TILE), BF),
            pltpu.VMEM((RANKS, window, 2 * TILE), BF),
            pltpu.VMEM((RANKS, 2 * words, window), BF),
            pltpu.VMEM((RANKS, words, TILE), BF),
            pltpu.VMEM((RANKS, words, hidden), BF),
            pltpu.VMEM((RANKS, words, hidden), BF),
            pltpu.VMEM((words, TILE), BF),
            pltpu.VMEM((RANKS, words, TILE), BF),
            pltpu.VMEM((RANKS, window, 2 * TILE), BF),
            pltpu.VMEM((words, wide), F32),
            pltpu.VMEM((words, wide), BF),
            pltpu.SemaphoreType.DMA,
            pltpu.VMEM((2 * words, wide), F32),
            pltpu.VMEM((3, 2, words, wide), BF),
            pltpu.VMEM((1, 2 * words + doc_ids.shape[1]), jnp.int32),
        ] + [pltpu.VMEM(array.shape, BF) for array in (wqkv, wout, wup, wdown)] + [
            pltpu.VMEM((RANKS, wide, wide), BF),
            pltpu.VMEM((RANKS, wide, wide), BF),
            pltpu.VMEM((RANKS, wide, wide), BF),
            pltpu.SemaphoreType.DMA((6 + RANKS,)),
            pltpu.SemaphoreType.DMA((2,)),
            pltpu.SemaphoreType.DMA((2,)),
        ],
        compiler_params=pltpu.CompilerParams(
            vmem_limit_bytes=62 << 20, collective_id=1, has_side_effects=True),
        name="word_layer",
    )(vec, near, doc_ids, cotangent, wqkv, wout, wup, wdown,
      gain1[None, :], gain2[None, :], wproj, pooled)


CHAINS = 6
PLAN = (
    (0, 2, 7, 10, 14, 16, 20,),
    (1, 5, 10, 13, 18, 22,),
    (2, 11, 15, 19,),
    (1, 4, 9, 12, 15, 19,),
    (7, 9, 14, 16,),
    (15, 17, 22,),
)


def char_backward_kernel(slots, bits, x_ref, counts_ref, gain1_ref, wq_ref, wk_ref, wv_ref, wout_ref, gain2_ref,
                         wup_ref, wdown_ref, gpl_ref, act_pool_ref, dproj_ref, wgain_ref, normed_ref, qkv_ref, probs_ref,
                         mixed_ref, first_ref, slope_ref, up_grad_ref, down_grad_ref, mix_grad_ref,
                         dx_ref, up_out, down_out, mix_out, early_out, mid_out, late_out,
                         down_ref, gq_ref, gmix_ref, gup_ref, spread_ref, dgain_ref, dqkv_ref, dout_ref, dup_ref,
                         all_ref, wqkv_ref, table_ref, early_ref, mid_ref, late_ref, *rest):
    step = pl.program_id(0)
    steps = pl.num_programs(0)
    half_steps = CHAR_STEPS
    rows, width = x_ref.shape
    words = rows // slots
    p = Place()
    send_sem, recv_sem, own_sem = rest[-3:]
    sources = (up_grad_ref, down_grad_ref, mix_grad_ref, early_ref, mid_ref, late_ref)
    results = (up_out, down_out, mix_out, early_out, mid_out, late_out)
    outs = rest[6 * CHAINS:7 * CHAINS]
    leave = [pltpu.make_async_copy(out, result, own_sem.at[CHAINS + index])
             for index, (out, result) in enumerate(zip(outs, results))]
    word_chains = 3
    chains, first_sem = [], 0
    for index in range(CHAINS):
        everywhere = index >= word_chains
        refs = tuple(rest[6 * index:6 * index + 6]) + (outs[index],)
        chains.append(Chain(p, bits, sources[index], refs, Sems(send_sem, recv_sem, first_sem), everywhere))
        first_sem += chain_copies(bits, everywhere)

    @pl.when(step == 0)
    def _():
        meet(p.mates(bits) + [p.ring_device(offset) for offset in (1, 2, 3)])
        for index in range(word_chains):
            chains[index].fetch(own_sem.at[index]).start()

    low = lambda value: value.astype(BF)

    @pl.when(step == 0)
    def _():
        dgain_ref[...] = jnp.zeros_like(dgain_ref)
        dqkv_ref[...] = jnp.zeros_like(dqkv_ref)
        dout_ref[...] = jnp.zeros_like(dout_ref)
        dup_ref[...] = jnp.zeros_like(dup_ref)
        grad_down = low(tn(act_pool_ref[...], low(gpl_ref[...])))
        quarter = early_ref.shape[1]
        for index in range(RANKS):
            early_ref[index, :, 0:width] = grad_down[index * quarter:(index + 1) * quarter]
            early_ref[index, :, width:] = grad_down[(RANKS + index) * quarter:(RANKS + index + 1) * quarter]
        split_counts(counts_ref, table_ref, words)
        join_lanes((wq_ref, wk_ref, wv_ref), wqkv_ref)
        scaled = gpl_ref[...] * (1.0 / column(counts_ref[...].astype(F32)))
        down_ref[:, width:] = nt(scaled.astype(BF), wdown_ref[...])
        down_ref[:, :width] = scaled

    @pl.when(step < half_steps)
    def _():
        here = rows_at(step * rows, rows)
        for word in range(words):
            line = down_ref[pl.ds(step * words + word, 1), :width]
            at = slice(word * slots, (word + 1) * slots)
            gq_ref[at, :width] = jnp.broadcast_to(line, (slots, width))
            line = down_ref[pl.ds(step * words + word, 1), width:]
            gup_ref[at, :] = (jnp.broadcast_to(line, (slots, line.shape[1])) * slope_ref[at, :].astype(F32)).astype(BF)

        valid_col = any_lane(valid_slots(rows, slots, table_ref[pl.ds(step, 1), 0:words]))
        unit2, rate2 = norm_parts(first_ref[...])
        dup_ref[...] += tn((unit2 * gain2_ref[...]).astype(BF), gup_ref[...])
        upstream = nt(gup_ref[...], wup_ref[...])
        dgain_ref[1:2, :] += jnp.sum(upstream * unit2, axis=0, keepdims=True)
        grad_first = jnp.where(valid_col, gq_ref[:, :width], 0.0) + norm_back(upstream, gain2_ref[...], unit2, rate2)
        spread_ref[here, :] = grad_first
        grad_low = low(grad_first)
        dout_ref[...] += tn(mixed_ref[...], grad_low)
        gmix_ref[here, :] = low(nt(grad_low, wout_ref[...]))

    @pl.when(step == half_steps - 1)
    def _():
        mid_ref[0] = low(dup_ref[:, 0:2 * width])
        mid_ref[1] = low(dup_ref[:, 2 * width:])
        mid_ref[2] = dproj_ref[...]
        half = width // 2
        mid_ref[3, 0:half, 0:width] = low(dout_ref[0:half, :])
        mid_ref[3, 0:half, width:] = low(dout_ref[half:, :])
        mid_ref[3, half:, :] = jnp.zeros_like(mid_ref[3, half:, :])
        both = jnp.concatenate([dgain_ref[...], dgain_ref[...]], axis=1)
        mid_ref[3, half:half + 16, :] = low(jnp.concatenate([wgain_ref[...], both], axis=0))

    @pl.when((step >= half_steps) & (step < 2 * half_steps))
    def _():
        base = (step - half_steps) * rows
        for tile in range(rows // TILE):
            at = pl.ds(tile * TILE, TILE)
            here = rows_at(base + tile * TILE, TILE)
            for pair in range(CHEADS // 2):
                c0 = pair * TILE
                queries = split_heads(qkv_ref[at, c0:c0 + TILE])
                keys = split_heads(qkv_ref[at, width + c0:width + c0 + TILE])
                values = qkv_ref[at, 2 * width + c0:2 * width + c0 + TILE]
                grads = split_heads(gmix_ref[here, c0:c0 + TILE])
                probs_low = probs_ref[tile, pair]
                probs = probs_low.astype(F32)
                grad_probs = compact(nt(values, grads), slots)
                inner = jnp.sum(probs * grad_probs, axis=0, keepdims=True)
                grad_scores = (probs * (grad_probs - inner) * (CHD ** -0.5)).astype(BF)
                wide_scores = expand(grad_scores, slots)
                wide_probs = expand(probs_low, slots)
                all_ref[here, c0:c0 + TILE] = tn(stack_lanes(wide_scores), keys).astype(BF)
                all_ref[here, width + c0:width + c0 + TILE] = nn(wide_scores, queries).astype(BF)
                all_ref[here, 2 * width + c0:2 * width + c0 + TILE] = nn(wide_probs, grads).astype(BF)
        dqkv_ref[...] += tn(normed_ref[...], all_ref[rows_at(base, rows), :])

    @pl.when(step == 2 * half_steps - 1)
    def _():
        rows_half, lanes_half = width // 2, 3 * width // 2
        for index in range(RANKS):
            rows_from, lanes_from = index % 2 * rows_half, index // 2 * lanes_half
            late_ref[index] = low(dqkv_ref[rows_from:rows_from + rows_half, lanes_from:lanes_from + lanes_half])

    @pl.when(step >= 2 * half_steps)
    def _():
        here = rows_at((step - 2 * half_steps) * rows, rows)
        unit1, rate1 = norm_parts(x_ref[...].astype(F32))
        upstream1 = nt(all_ref[here, :], wqkv_ref[...])
        dx_ref[...] = low(spread_ref[here, :] + norm_back(upstream1, gain1_ref[...], unit1, rate1))

    for at in range(3 * half_steps):
        todo = [(index, stages.index(at)) for index, stages in reversed(list(enumerate(PLAN))) if at in stages]
        if todo:
            @pl.when(step == at)
            def _(todo=todo):
                for index, stage in todo:
                    if stage == 1 and index < word_chains:
                        chains[index].fetch(own_sem.at[index]).wait()
                    chains[index].step(stage)

    @pl.when(step == steps - 1)
    def _():
        done = [len(stages) for stages in PLAN]
        while any(done[index] <= len(chains[index].stages) for index in range(CHAINS)):
            for index in reversed(range(CHAINS)):
                if done[index] <= len(chains[index].stages):
                    chains[index].step(done[index])
                    done[index] += 1
                    if done[index] > len(chains[index].stages):
                        leave[index].start()
        for copy in leave:
            copy.wait()


def char_backward(bits, x, counts, gain1, weights, wout, gain2, wup, wdown, grad_pooled, saved, grad_proj,
                  word_gains, word_grads):
    qkv, probs, mixed, first, slope, act_pool, normed = saved
    rows, width = x.shape
    words = counts.shape[0]
    slots = rows // words
    hidden = wup.shape[1]
    wide = word_gains.shape[1]
    step = rows // CHAR_STEPS
    last = CHAR_STEPS - 1
    ahead = lambda i: i - ((i // CHAR_STEPS + 1) // 2) * (i - last)
    behind = lambda i: (i // CHAR_STEPS % 2) * (i - CHAR_STEPS) + (i // CHAR_STEPS // 2) * last
    final = lambda i: (i // CHAR_STEPS // 2) * (i - 2 * CHAR_STEPS)
    ahead_block = lambda cols: pl.BlockSpec((step, cols), lambda i: (ahead(i), 0))
    behind_block = lambda cols: pl.BlockSpec((step, cols), lambda i: (behind(i), 0))
    whole = lambda shape: pl.BlockSpec(shape, lambda i: (0,) * len(shape))
    tiles = step // TILE
    sum_shapes = [(wide, wide)] * 3 + [(RANKS, width // 2, wide), (RANKS, width, wide), (RANKS, width // 2, 3 * width // 2)]
    sources = [(RANKS,) + shape if len(shape) == 2 else shape for shape in sum_shapes]
    copies = sum(chain_copies(bits, index >= 3) for index in range(CHAINS))
    scratch = []
    for shape in sources:
        scratch += chain_scratch(bits, shape[1], shape[2])
    return pl.pallas_call(
        functools.partial(char_backward_kernel, slots, bits),
        grid=(3 * CHAR_STEPS,),
        in_specs=[
            pl.BlockSpec((step, width), lambda i: (final(i), 0)),
            whole((1, words)),
            whole((1, width)),
            whole((width, width)),
            whole((width, width)),
            whole((width, width)),
            whole((width, width)),
            whole((1, width)),
            whole((width, hidden)),
            whole((hidden, width)),
            whole((words, width)),
            whole((words, hidden)),
            whole((width, wide)),
            whole((8, wide)),
            behind_block(width),
            behind_block(3 * width),
            pl.BlockSpec((tiles, CHEADS // 2, slots, 2 * TILE), lambda i: (behind(i), 0, 0, 0)),
            ahead_block(width),
            ahead_block(width),
            ahead_block(hidden),
        ] + [pl.BlockSpec(memory_space=pl.ANY)] * 3,
        out_specs=[pl.BlockSpec((step, width), lambda i: (final(i), 0))] + [pl.BlockSpec(memory_space=pl.ANY)] * CHAINS,
        out_shape=[jax.ShapeDtypeStruct((rows, width), BF)]
        + [jax.ShapeDtypeStruct(shape, BF) for shape in sum_shapes],
        scratch_shapes=[
            pltpu.VMEM((words, width + hidden), F32),
            pltpu.VMEM((step, width), F32),
            pltpu.VMEM((rows, width), BF),
            pltpu.VMEM((step, hidden), BF),
            pltpu.VMEM((rows, width), F32),
            pltpu.VMEM((8, width), F32),
            pltpu.VMEM((width, 3 * width), F32),
            pltpu.VMEM((width, width), F32),
            pltpu.VMEM((width, hidden), F32),
            pltpu.VMEM((rows, 3 * width), BF),
            pltpu.VMEM((width, 3 * width), BF),
            pltpu.VMEM((CHAR_STEPS, TILE), jnp.int32),
        ] + [pltpu.VMEM(shape, BF) for shape in sources[3:]] + scratch
        + [pltpu.VMEM(shape, BF) for shape in sum_shapes] + [pltpu.SemaphoreType.DMA((copies,)), pltpu.SemaphoreType.DMA((copies,)), pltpu.SemaphoreType.DMA((2 * CHAINS,))],
        compiler_params=pltpu.CompilerParams(
            vmem_limit_bytes=63 << 20, collective_id=2, has_side_effects=True),
        name="char_backward",
    )(x, counts[None, :], gain1[None, :], *weights, wout, gain2[None, :],
      wup, wdown, grad_pooled, act_pool, grad_proj, word_gains, normed, qkv, probs, mixed, first, slope, *word_grads)


def unpack_kernel(out_in, dx_in, wq_in, wk_in, wv_in, gain1_in, up_in, down_in, mix_in, turn_in, early_in, mid_in, late_in,
                  out_ref, dx_ref, gain1_ref, dq_ref, dk_ref, dv_ref, dout_ref, gain2_ref, dup_ref, ddown_ref, dproj_ref,
                  wgain1_ref, wq_ref, wk_ref, wv_ref, wout_ref, wgain2_ref, wup_ref, wdown_ref):
    step = pl.program_id(0)
    dx_ref[...] = dx_in[...].astype(F32)
    out_ref[...] = out_in[...]
    width = dq_ref.shape[0]
    half = width // 2
    wup_ref[...] = up_in[...].astype(F32)
    wdown_ref[...] = down_in[...].astype(F32)
    wq_ref[...] = mix_in[:, 0:TILE].astype(F32)
    wk_ref[...] = mix_in[:, TILE:2 * TILE].astype(F32)
    wv_ref[...] = mix_in[:, 2 * TILE:3 * TILE].astype(F32)
    for side in range(2):
        cols = slice(side * width, (side + 1) * width)
        ddown_ref[side] = early_in[0, :, cols].astype(F32)
        dup_ref[:, side * 2 * width:(side + 1) * 2 * width] = mid_in[side].astype(F32)
    dproj_ref[...] = mid_in[2].astype(F32)

    @pl.when(step < UNPACK_STEPS // 2)
    def _():
        for side in range(2):
            dout_ref[side] = mid_in[3, :, side * width:(side + 1) * width].astype(F32)

    @pl.when(step == UNPACK_STEPS // 2)
    def _():
        gains = mid_in[3, 0:16, :].astype(F32)
        wgain1_ref[...] = gains[0:1]
        wgain2_ref[...] = gains[1:2]
        gain2_ref[...] = gains[9:10, 0:width]

    @pl.when(step == 0)
    def _():
        wout_ref[...] = turn_in[...].astype(F32).T
        parts = []
        for index in range(2):
            at = slice(index * half, (index + 1) * half)
            joined = jnp.concatenate([late_in[index], late_in[2 + index]], axis=1).astype(F32)
            grads = [joined[:, part * width:(part + 1) * width] for part in range(3)]
            total = 0.0
            for grad, weight, target in zip(grads, (wq_in, wk_in, wv_in), (dq_ref, dk_ref, dv_ref)):
                target[at, :] = grad
                total += weight[at].astype(F32) * grad
            parts.append(jnp.sum(total, axis=1, keepdims=True))
        sums = jnp.concatenate(parts, axis=0)
        diagonal = (lax.broadcasted_iota(jnp.int32, (width, width), 0)
                    == lax.broadcasted_iota(jnp.int32, (width, width), 1))
        gain1_ref[...] = jnp.sum(jnp.where(diagonal, sums, 0.0), axis=0, keepdims=True) / gain1_in[...]


UNPACK_STEPS = 8


def unpack(word_output, grad_inputs, weights, gain1, sums, width, hidden):
    steps = UNPACK_STEPS
    up, down, mix, early, mid, late = sums
    wide = word_output.shape[1]
    whole = lambda shape: pl.BlockSpec(shape, lambda i: (0,) * len(shape))
    split = lambda shape: pl.BlockSpec((shape[0] // steps, shape[1]), lambda i: (i, 0))
    middle = lambda shape: pl.BlockSpec((shape[0], shape[1] // steps, shape[2]), lambda i: (0, i, 0))
    per = early.shape[1] * RANKS // steps
    blocks = early.shape[1] // per
    pinned = lambda i: i - (i // (steps // 2)) * (i - (steps // 2 - 1))
    outs = [
        (whole, (1, width)), (whole, (width, width)), (whole, (width, width)), (whole, (width, width)),
        (lambda shape: pl.BlockSpec((2, shape[1] * 2 // steps, width), lambda i: (0, pinned(i), 0)), (2, width // 2, width)),
        (whole, (1, width)), (split, (width, hidden)), (middle, (2, hidden // 2, width)), (split, (width, wide)),
        (whole, (1, wide)), (split, (wide, TILE)), (split, (wide, TILE)), (split, (wide, TILE)),
        (whole, (TILE, wide)), (whole, (1, wide)), (split, (wide, wide)), (split, (wide, wide)),
    ]
    results = pl.pallas_call(
        unpack_kernel,
        grid=(steps,),
        in_specs=[split(word_output.shape), split(grad_inputs.shape)] + [whole((width, width))] * 3 + [whole((1, width))]
        + [split(up.shape), split(down.shape), split(mix.shape), pl.BlockSpec((wide, TILE), lambda i: (0, 3)),
           pl.BlockSpec((1, per, wide), lambda i: (i // blocks, i % blocks, 0)), middle(mid.shape), whole(late.shape)],
        out_specs=[split(word_output.shape), split(grad_inputs.shape)] + [spec(shape) for spec, shape in outs],
        out_shape=[jax.ShapeDtypeStruct(word_output.shape, BF), jax.ShapeDtypeStruct(grad_inputs.shape, F32)]
        + [jax.ShapeDtypeStruct(shape, F32) for _, shape in outs],
        compiler_params=pltpu.CompilerParams(vmem_limit_bytes=60 << 20),
        name="unpack",
    )(word_output, grad_inputs, *weights, gain1[None, :], up, down, mix, mix, early, mid, late)

    def shaped(array):
        if array.ndim == 3:
            return array.reshape(-1, array.shape[2])
        return array[0] if array.shape[0] == 1 else array

    return tuple(shaped(array) for array in results)


def per_device(
    bits,
    char_inputs,
    char_counts,
    doc_ids,
    cotangent,
    char_norm_one,
    char_query,
    char_key,
    char_value,
    char_out,
    char_norm_two,
    char_up,
    char_down,
    char_proj,
    word_norm_one,
    word_query,
    word_key,
    word_value,
    word_out_proj,
    word_norm_two,
    word_up,
    word_down,
):
    char_qkv = (char_query, char_key, char_value)
    word_qkv = (word_query, word_key, word_value)
    vec, pooled, *saved, near, qkv_all, out_all, up_all, down_all = char_forward(
        char_inputs, char_counts, char_norm_one, char_qkv, char_out, char_norm_two, char_up, char_down, char_proj,
        word_qkv, word_out_proj, word_up, word_down,
    )
    word_output, grad_pooled, grad_proj, word_gains, *word_grads = word_layer(
        bits, vec, near, doc_ids, cotangent, qkv_all, out_all, up_all, down_all,
        word_norm_one, word_norm_two, char_proj, pooled,
    )
    grad_inputs, *sums = char_backward(
        bits, char_inputs, char_counts, char_norm_one, char_qkv, char_out, char_norm_two, char_up, char_down,
        grad_pooled, saved, grad_proj, word_gains, word_grads,
    )
    return unpack(word_output, grad_inputs, char_qkv, char_norm_one, sums, char_out.shape[0], char_up.shape[1])


def solution(mesh):
    in_specs = (
        P(("dp", "tensor"), None),
        P(("dp", "tensor")),
        P("dp", None),
        P("dp", None),
        P(),
        P(),
        P(),
        P(),
        P(),
        P(),
        P(),
        P(),
        P(),
        P(),
        P(None, "tensor"),
        P(None, "tensor"),
        P(None, "tensor"),
        P("tensor", None),
        P(),
        P(None, "tensor"),
        P("tensor", None),
    )
    out_specs = (
        P(("dp", "tensor"), None),
        P(("dp", "tensor"), None),
        P(),
        P(),
        P(),
        P(),
        P(),
        P(),
        P(),
        P(),
        P(),
        P(),
        P(None, "tensor"),
        P(None, "tensor"),
        P(None, "tensor"),
        P("tensor", None),
        P(),
        P(None, "tensor"),
        P("tensor", None),
    )
    assert mesh.shape["tensor"] == RANKS
    bits = mesh.shape["dp"].bit_length() - 1
    assert bits >= 3 and mesh.shape["dp"] == 1 << bits
    return jax.shard_map(
        functools.partial(per_device, bits), mesh=mesh, in_specs=in_specs, out_specs=out_specs, check_vma=False
    )
```
